32 devices in a mesh: dp: 4 (over z), vocab: 8 (over y, x, core).
Axes of the slice: x: 2, y: 2, z: 4, core: 2. Of those that a mesh axis runs over, the one named last changes fastest.
Arguments:
- packed_symbol_codes: int32 [32, 1024], P(('dp', 'vocab')), may hold values from 0 to 50256
- article_numbering: int32 [32, 1024], P(('dp', 'vocab')), may hold values from 0 to 19, never falling along the last dimension, each value on 1 to 256 neighbouring positions
- target_spots: int32 [32, 128], P(('dp', 'vocab')), may hold values from 0 to 1022
- answer_flags: int32 [32, 128], P(('dp', 'vocab')), may hold values 0 or 1
- shared_embedding: bfloat16 [50304, 1024], P('vocab'), may hold values from -0.6 to 0.6
- spot_embedding: bfloat16 [1024, 1024], replicated, may hold values from -0.359375 to 0.359375
- combined_qkv_weights: bfloat16 [1024, 3072], replicated, may hold values from -0.1875 to 0.1875
- attend_outgoing_weights: bfloat16 [1024, 1024], replicated, may hold values from -0.5 to 0.5
- dense_incoming_weights: bfloat16 [1024, 4096], replicated, may hold values from -0.1875 to 0.1875
- dense_outgoing_weights: bfloat16 [4096, 1024], replicated, may hold values from -0.09375 to 0.09375
- layernorm_affine: float32 [6, 1024], replicated, may hold values from -0.6 to 1.3, as said below
- bias_terms: float32 [9216], replicated, may hold values from -1.2 to 1.2
- adaptor_float_copies: float32 [73728], replicated, may hold values from -0.09375 to 0.09375
- average_moments: float32 [73728], replicated, may hold values from -1.2276159e-07 to 1.2276159e-07
- squared_moments: float32 [73728], replicated, may hold values from 1.3576945e-16 to 5.430778e-16
Outputs:
- refreshed_thin_pairs: float32 [73728], replicated
- updated_first_moment: float32 [73728], replicated
- updated_second_moment: float32 [73728], replicated
- gradient_global_norm: float32 [], replicated
- smoothed_entropy_cost: float32 [], replicated
The draws below stay inside these ranges and needn't reach their ends.
Inputs may be any that keep to these rules, and one draw needn't show every extreme that they name: `article_numbering`: within a slot the document numbers never fall, every document has 1 to 256 tokens. `layernorm_affine`: rows 0 to 2 are gains, rows 3 to 5 shifts.
All inputs are finite; a program needn't handle non-finite values. No bound on the sum of `answer_flags` on one device may be relied on, other than what follows from the above.
Results may differ from the reference program's by a relative error of at most 0.00085.
The reference program's roundings to bfloat16 on the way count: a program that leaves them out, or rounds other values in their place, can miss the bound.
Values may be sent and summed in bfloat16 or wider, within the bound.
A program may use at most 320 MiB of HBM per device.

```python
import math
import jax
import jax.numpy as jnp
import numpy as np
from jax import lax

MODEL_WIDTH = 1024
HEADS = 16
HEAD_DIM = 64
FEEDFWD_UNITS = 4096
VOCAB_SIZE = 50257
VOCAB_PADDED = 50304
RANK = 4
SEGMENT_SPAN = 1024
SCORED_SPOTS = 128
STEP = 10
SEGMENT_COUNT = 32
DOCS = 20
MOST = 256
NPAR = 73728


GRAD_CLIP = 0.0001


def draw_shared_embedding(key, part):
    noise = jnp.clip(jax.random.normal(jax.random.fold_in(key, 11), (VOCAB_PADDED, MODEL_WIDTH), jnp.float32), -3.0, 3.0)
    common = jnp.clip(jax.random.normal(jax.random.fold_in(key, 12), (MODEL_WIDTH,), jnp.float32), -3.0, 3.0)
    rows = jnp.arange(VOCAB_PADDED, dtype=jnp.float32) / VOCAB_PADDED
    level = 0.04 * (1.0 + 2.0 * rows)
    return (0.06 * noise + level[:, None] * common[None, :]).astype(jnp.bfloat16)


def draw_layernorm_affine(key, part):
    gains = 1.0 + 0.1 * jnp.clip(jax.random.normal(jax.random.fold_in(key, 1), (3, MODEL_WIDTH), jnp.float32), -3.0, 3.0)
    shifts = 0.2 * jnp.clip(jax.random.normal(jax.random.fold_in(key, 2), (3, MODEL_WIDTH), jnp.float32), -3.0, 3.0)
    return jnp.concatenate([gains, shifts], axis=0)


def draw_adaptor_float_copies(key, part):
    shapes = [((MODEL_WIDTH, 3 * RANK), MODEL_WIDTH), ((3, RANK, MODEL_WIDTH), 0), ((MODEL_WIDTH, RANK), MODEL_WIDTH), ((RANK, MODEL_WIDTH), 0), ((MODEL_WIDTH, RANK), MODEL_WIDTH), ((RANK, FEEDFWD_UNITS), 0), ((FEEDFWD_UNITS, RANK), FEEDFWD_UNITS), ((RANK, MODEL_WIDTH), 0)]
    pieces = []
    for index, (shape, fan) in enumerate(shapes):
        number = math.prod(shape)
        noise = jnp.clip(jax.random.normal(jax.random.fold_in(key, index), (number,), jnp.float32), -3.0, 3.0)
        scale = fan ** (-0.5) if fan else 0.02
        pieces.append(scale * noise)
    return jnp.concatenate(pieces)


def draw_average_moments(key, part):
    entry = GRAD_CLIP / math.sqrt(NPAR)
    noise = jnp.clip(jax.random.normal(key, (NPAR,), jnp.float32), -3.0, 3.0)
    return 0.1 / 0.9 * entry * noise


def draw_squared_moments(key, part):
    entry = GRAD_CLIP * GRAD_CLIP / NPAR
    factor = jax.random.uniform(key, (NPAR,), jnp.float32, 1.0, 4.0)
    return 0.001 / 0.999 * entry * factor


def touch_ends(array, own_key, smallest, high):
    index_at = [jax.random.randint(jax.random.fold_in(own_key, axis), (), 0, length) for axis, length in enumerate(array.shape)]
    widest = array.shape.index(max(array.shape))
    next_to = index_at[:widest] + [(index_at[widest] + 1) % array.shape[widest]] + index_at[widest + 1:]
    return array.at[tuple(index_at)].set(smallest).at[tuple(next_to)].set(high)


def rank_table(amount, slope):
    portions = [(1 << 20) // math.isqrt(grade ** slope) + 1 for grade in range(1, amount + 1)]
    deviation = 1 + sum(portions) // (1 << 30)
    return np.cumsum(np.array([max(1, weight // deviation) for weight in portions]))


def ranked(key, shape, number_of, lean):
    grid = rank_table(number_of, lean)
    pick = jax.random.randint(jax.random.fold_in(key, 1), shape, 0, int(grid[number_of - 1]))
    grade = jnp.searchsorted(jnp.asarray(grid, jnp.int32), pick, side="right")
    return jax.random.permutation(jax.random.fold_in(key, 2), number_of)[grade].astype(jnp.int32)


def split_up(count, total, bound, slope):
    portions = [(1 << 20) // math.isqrt(rank ** slope) + 1 for rank in range(2, count + 1)]
    rest, counts = total - bound - (count - 1), [1] * (count - 1)
    while rest > 0:
        candidates = [i for i in range(count - 1) if counts[i] < bound]
        whole, left = sum([portions[i] for i in candidates]), rest
        for i in candidates:
            more = min(bound - counts[i], max(1, left * portions[i] // whole), rest)
            counts[i] = counts[i] + more
            rest = rest - more
    return np.array([bound] + counts)


def ragged_sizes(stream_key, number_of, total, most, slope):
    if number_of == 2:
        one = jax.random.randint(stream_key, (), max(1, total - most), min(most, total - 1) + 1)
        return jnp.stack([one, total - one])
    lengths = jnp.asarray(split_up(number_of, total, most, slope), jnp.int32)
    couples = (number_of - 1) // 2
    donor, receiver = lengths[1:1 + 2 * couples:2], lengths[2:2 + 2 * couples:2]
    room = jnp.minimum(donor - 1, most - receiver)
    shifted = jax.random.randint(jax.random.fold_in(stream_key, 1), (couples,), 0, 1 << 20) % (room + 1)
    lengths = lengths.at[1:1 + 2 * couples:2].set(donor - shifted).at[2:2 + 2 * couples:2].set(receiver + shifted)
    return lengths[jax.random.permutation(jax.random.fold_in(stream_key, 2), number_of)]


def bell_draw(key, shape, deviation, bound, held_as=jnp.bfloat16):
    drawn = deviation * jax.random.normal(key, shape, jnp.float32)
    return jnp.clip(drawn, min=-bound, max=bound).astype(held_as)


def setup_inputs(seed: int = 0) -> dict:
    streams_of = jax.random.split(jax.random.key(seed), 16)
    return {
        "packed_symbol_codes": touch_ends(ranked(streams_of[0], (SEGMENT_COUNT, SEGMENT_SPAN), VOCAB_SIZE, 2), jax.random.fold_in(streams_of[0], 3), 0, VOCAB_SIZE - 1).astype(jnp.int32),
        "article_numbering": jax.vmap(lambda own: jnp.searchsorted(jnp.cumsum(ragged_sizes(own, DOCS, SEGMENT_SPAN, MOST, 1)), jnp.arange(SEGMENT_SPAN), side="right"))(jax.random.split(streams_of[1], SEGMENT_COUNT)).reshape((SEGMENT_COUNT, SEGMENT_SPAN)).astype(jnp.int32),
        "target_spots": touch_ends(jax.random.randint(streams_of[2], (SEGMENT_COUNT, SCORED_SPOTS), 0, SEGMENT_SPAN - 1), jax.random.fold_in(streams_of[2], 1), 0, (SEGMENT_SPAN - 1) - 1).astype(jnp.int32),
        "answer_flags": touch_ends((jax.random.randint(streams_of[3], (SEGMENT_COUNT, SCORED_SPOTS), 0, 4) < 3).astype(jnp.int32), jax.random.fold_in(streams_of[3], 1), 0, 1),
        "shared_embedding": draw_shared_embedding(jax.random.fold_in(streams_of[15], 71), 0),
        "spot_embedding": bell_draw(streams_of[5], (SEGMENT_SPAN, MODEL_WIDTH), 0.06, 0.359375),
        "combined_qkv_weights": bell_draw(streams_of[6], (MODEL_WIDTH, 3 * MODEL_WIDTH), MODEL_WIDTH ** -0.5, 0.1875),
        "attend_outgoing_weights": bell_draw(streams_of[7], (MODEL_WIDTH, MODEL_WIDTH), (MODEL_WIDTH // 8) ** -0.5, 0.5),
        "dense_incoming_weights": bell_draw(streams_of[8], (MODEL_WIDTH, FEEDFWD_UNITS), MODEL_WIDTH ** -0.5, 0.1875),
        "dense_outgoing_weights": bell_draw(streams_of[9], (FEEDFWD_UNITS, MODEL_WIDTH), FEEDFWD_UNITS ** -0.5, 0.09375),
        "layernorm_affine": draw_layernorm_affine(jax.random.fold_in(streams_of[15], 71), 0),
        "bias_terms": bell_draw(streams_of[11], (5 * MODEL_WIDTH + FEEDFWD_UNITS,), 0.2, 1.2, jnp.float32),
        "adaptor_float_copies": draw_adaptor_float_copies(jax.random.fold_in(streams_of[15], 71), 0),
        "average_moments": draw_average_moments(jax.random.fold_in(streams_of[15], 71), 0),
        "squared_moments": draw_squared_moments(jax.random.fold_in(streams_of[15], 71), 0),
    }


ADAPTER_SCALE = 8.0
NORM_EPS = 1e-05
GRAD_CLIP = 0.0001
STRIDE_LENGTH = 0.02
BETA_ONE = 0.9
BETA_TWO = 0.999
SHRINK_PENALTY = 0.01
STABILITY_FLOOR = 1e-08
MASKED = -1e+30
TOP_ACCURACY = lax.Precision.HIGHEST

@jax.custom_vjp
def lowrank_rows(v):
    return lax.optimization_barrier(v.astype(jnp.bfloat16)).astype(jnp.float32)

@jax.custom_vjp
def adaptor_reverse_sweep(v):
    return v

def low_keep(v):
    return (lowrank_rows(v), None)

def low_pass(kept, grad):
    return (grad,)

def back_keep(v):
    return (v, None)

def back_low(kept, grad):
    return (lowrank_rows(grad),)
lowrank_rows.defvjp(low_keep, low_pass)
adaptor_reverse_sweep.defvjp(back_keep, back_low)

def matrix_multiply(left, right):
    return jnp.dot(left, right, precision=TOP_ACCURACY, preferred_element_type=jnp.float32)

def layer_norm(stream, gain, shift):
    centred = stream - lax.optimization_barrier(jnp.mean(stream, axis=-1, keepdims=True))
    spread = lax.rsqrt(lax.optimization_barrier(jnp.mean(centred * centred, axis=-1, keepdims=True)) + NORM_EPS)
    return centred * spread * gain + shift

def positions(segments):
    steps_here = jnp.arange(segments.shape[0], dtype=jnp.int32)
    change = jnp.concatenate([jnp.ones((1,), bool), segments[1:] != segments[:-1]])
    starts = lax.cummax(jnp.where(change, steps_here, 0).astype(jnp.int32), axis=0)
    return steps_here - starts

def distinct_thin_pairs(stacked_samples):
    shapes = [(MODEL_WIDTH, 3 * RANK), (3, RANK, MODEL_WIDTH), (MODEL_WIDTH, RANK), (RANK, MODEL_WIDTH), (MODEL_WIDTH, RANK), (RANK, FEEDFWD_UNITS), (FEEDFWD_UNITS, RANK), (RANK, MODEL_WIDTH)]
    pieces = []
    offset = 0
    for shape in shapes:
        number = math.prod(shape)
        pieces.append(stacked_samples[offset:offset + number].reshape(shape))
        offset += number
    return pieces

def block_diagonal_mask(blocks):
    number, rank, width = blocks.shape
    eye = jnp.eye(number, dtype=blocks.dtype)
    return (eye[:, None, :, None] * blocks[:, :, None, :]).reshape(number * rank, number * width)

def segment_objective(stacked_samples, fixed_weights, packed_symbol_codes, article_numbering, target_spots, answer_flags):
    shared_embedding, spot_embedding, combined_qkv_weights, attend_outgoing_weights, dense_incoming_weights, dense_outgoing_weights, layernorm_affine, bias_terms = fixed_weights
    down_factor_attention, up_factor_attention, down_factor_output, up_factor_output, down_factor_feed, up_factor_feed, down_factor_projection, up_factor_projection = [lowrank_rows(lexicon_portion) for lexicon_portion in distinct_thin_pairs(stacked_samples)]
    places = positions(article_numbering)
    stream = shared_embedding[packed_symbol_codes] + spot_embedding[places]
    normalized_first = lowrank_rows(layer_norm(stream, layernorm_affine[0], layernorm_affine[3]))
    lowrank_attention = lowrank_rows(adaptor_reverse_sweep(matrix_multiply(normalized_first, down_factor_attention)))
    projected_rows = matrix_multiply(normalized_first, combined_qkv_weights) + bias_terms[:3 * MODEL_WIDTH] + ADAPTER_SCALE * matrix_multiply(lowrank_attention, block_diagonal_mask(up_factor_attention))
    projected_rows = lowrank_rows(adaptor_reverse_sweep(projected_rows)).reshape(SEGMENT_SPAN, 3, HEADS, HEAD_DIM)
    scores = jnp.einsum('qhd,khd->hqk', projected_rows[:, 0], projected_rows[:, 1], precision=TOP_ACCURACY) * HEAD_DIM ** (-0.5)
    scores = adaptor_reverse_sweep(scores)
    steps_here = jnp.arange(SEGMENT_SPAN, dtype=jnp.int32)
    allowed = (steps_here[None, :] <= steps_here[:, None]) & (article_numbering[None, :] == article_numbering[:, None])
    probs = lowrank_rows(jax.nn.softmax(jnp.where(allowed[None], scores, MASKED), axis=-1))
    attended_rows = jnp.einsum('hqk,khd->qhd', probs, projected_rows[:, 2], precision=TOP_ACCURACY).reshape(SEGMENT_SPAN, MODEL_WIDTH)
    attended_rows = lowrank_rows(adaptor_reverse_sweep(attended_rows))
    lowrank_output = lowrank_rows(adaptor_reverse_sweep(matrix_multiply(attended_rows, down_factor_output)))
    residual_branch = adaptor_reverse_sweep(matrix_multiply(attended_rows, attend_outgoing_weights) + bias_terms[3 * MODEL_WIDTH:4 * MODEL_WIDTH] + ADAPTER_SCALE * matrix_multiply(lowrank_output, up_factor_output))
    middle = stream + residual_branch
    normalized_second = lowrank_rows(layer_norm(middle, layernorm_affine[1], layernorm_affine[4]))
    lowrank_feed = lowrank_rows(adaptor_reverse_sweep(matrix_multiply(normalized_second, down_factor_feed)))
    preactivation_rows = adaptor_reverse_sweep(matrix_multiply(normalized_second, dense_incoming_weights) + bias_terms[4 * MODEL_WIDTH:4 * MODEL_WIDTH + FEEDFWD_UNITS] + ADAPTER_SCALE * matrix_multiply(lowrank_feed, up_factor_feed))
    activated_hidden = lowrank_rows(jax.nn.gelu(preactivation_rows, approximate=True))
    lowrank_projection = lowrank_rows(adaptor_reverse_sweep(matrix_multiply(activated_hidden, down_factor_projection)))
    residual_branch_second = adaptor_reverse_sweep(matrix_multiply(activated_hidden, dense_outgoing_weights) + bias_terms[4 * MODEL_WIDTH + FEEDFWD_UNITS:] + ADAPTER_SCALE * matrix_multiply(lowrank_projection, up_factor_projection))
    output = middle + residual_branch_second
    closing_result = lowrank_rows(layer_norm(output, layernorm_affine[2], layernorm_affine[5]))
    class_scores = adaptor_reverse_sweep(jnp.dot(closing_result[target_spots], shared_embedding.T, precision=TOP_ACCURACY))
    active_positions = jnp.arange(VOCAB_PADDED) < VOCAB_SIZE
    log_total = jax.nn.logsumexp(class_scores, axis=1, where=active_positions[None, :])
    smooth_sum = lax.optimization_barrier(jnp.sum(jnp.where(active_positions[None, :], class_scores, 0.0), axis=1))
    goal_label = packed_symbol_codes[target_spots + 1]
    target_logit = jnp.take_along_axis(class_scores, goal_label[:, None], axis=1)[:, 0]
    usable_flags = answer_flags * (article_numbering[target_spots] == article_numbering[target_spots + 1]).astype(jnp.int32)
    rows = log_total - 0.9 * target_logit - 0.1 * smooth_sum / VOCAB_SIZE
    return jnp.sum(usable_flags.astype(jnp.float32) * rows)

def reference(packed_symbol_codes, article_numbering, target_spots, answer_flags, shared_embedding, spot_embedding, combined_qkv_weights, attend_outgoing_weights, dense_incoming_weights, dense_outgoing_weights, layernorm_affine, bias_terms, adaptor_float_copies, average_moments, squared_moments):
    fixed_weights = tuple((a.astype(jnp.float32) for a in (shared_embedding, spot_embedding, combined_qkv_weights, attend_outgoing_weights, dense_incoming_weights, dense_outgoing_weights, layernorm_affine, bias_terms)))
    following_labels = jnp.take_along_axis(article_numbering, target_spots + 1, axis=1)
    present_items = jnp.take_along_axis(article_numbering, target_spots, axis=1)
    usable_flags = answer_flags * (present_items == following_labels).astype(jnp.int32)
    count = jnp.maximum(jnp.sum(usable_flags.astype(jnp.float32)), 1.0)
    checked = jax.checkpoint(segment_objective)

    def accumulated_sum(stacked_samples):

        def training_iteration(carry, item):
            return (carry + checked(stacked_samples, fixed_weights, *item), None)
        aggregated, ignored_item = lax.scan(training_iteration, jnp.zeros((), jnp.float32), (packed_symbol_codes, article_numbering, target_spots, answer_flags))
        return aggregated / count
    smoothed_entropy_cost, reverse_pass_lines = jax.vjp(accumulated_sum, adaptor_float_copies)
    grad, = reverse_pass_lines(jnp.ones((), jnp.float32))
    gradient_global_norm = jnp.sqrt(jnp.sum(grad * grad))
    capped_derivative = grad * (GRAD_CLIP / jnp.maximum(gradient_global_norm, GRAD_CLIP))
    updated_first_moment = BETA_ONE * average_moments + (1.0 - BETA_ONE) * capped_derivative
    updated_second_moment = BETA_TWO * squared_moments + (1.0 - BETA_TWO) * capped_derivative * capped_derivative
    debiased_mean_estimate = updated_first_moment / (1.0 - BETA_ONE ** STEP)
    debiased_variance_estimate = updated_second_moment / (1.0 - BETA_TWO ** STEP)
    refreshed_thin_pairs = adaptor_float_copies - STRIDE_LENGTH * (debiased_mean_estimate / (jnp.sqrt(debiased_variance_estimate) + STABILITY_FLOOR) + SHRINK_PENALTY * adaptor_float_copies)
    return (refreshed_thin_pairs, updated_first_moment, updated_second_moment, gradient_global_norm, smoothed_entropy_cost)
```

```python
from functools import partial
import math

import jax
import jax.numpy as jnp
from jax import lax
from jax.sharding import PartitionSpec as P

MODEL_WIDTH = 1024
HEADS = 16
FEEDFWD_UNITS = 4096
VOCAB_SIZE = 50257
RANK = 4
STEP = 10


ADAPTER_SCALE = 8.0
NORM_EPS = 1e-05
GRAD_CLIP = 0.0001
STRIDE_LENGTH = 0.02
BETA_ONE = 0.9
BETA_TWO = 0.999
SHRINK_PENALTY = 0.01
STABILITY_FLOOR = 1e-08
MASKED = -1e30


def matrix_multiply(left, right):
    return jnp.dot(left, right, preferred_element_type=jnp.float32)


def matrix_multiply_transposed_left(left, right):
    return lax.dot_general(
        left, right, (((0,), (0,)), ((), ())), preferred_element_type=jnp.float32
    )


def matrix_multiply_transposed_right(left, right):
    return lax.dot_general(
        left, right, (((1,), (1,)), ((), ())), preferred_element_type=jnp.float32
    )


def layer_norm(stream, gain, shift):
    centred = stream - jnp.mean(stream, axis=-1, keepdims=True)
    spread = lax.rsqrt(jnp.mean(centred * centred, axis=-1, keepdims=True) + NORM_EPS)
    return centred * spread * gain + shift


def positions(segments):
    steps_here = jnp.arange(segments.shape[0], dtype=jnp.int32)
    earlier = (segments[None, :] == segments[:, None]) & (steps_here[None, :] < steps_here[:, None])
    return jnp.sum(earlier.astype(jnp.int32), axis=1)


def distinct_thin_pairs(stacked_samples):
    shapes = [
        (MODEL_WIDTH, 3 * RANK),
        (3, RANK, MODEL_WIDTH),
        (MODEL_WIDTH, RANK),
        (RANK, MODEL_WIDTH),
        (MODEL_WIDTH, RANK),
        (RANK, FEEDFWD_UNITS),
        (FEEDFWD_UNITS, RANK),
        (RANK, MODEL_WIDTH),
    ]
    pieces = []
    offset = 0
    for shape in shapes:
        number = math.prod(shape)
        pieces.append(stacked_samples[offset : offset + number].reshape(shape))
        offset += number
    return pieces


def block_diagonal_mask(blocks):
    number, rank, width = blocks.shape
    eye = jnp.eye(number, dtype=blocks.dtype)
    return (eye[:, None, :, None] * blocks[:, :, None, :]).reshape(number * rank, number * width)


def select_rows(onehot, rows):
    return matrix_multiply(onehot, rows).astype(jnp.bfloat16)


def split_heads(rows):
    return rows.reshape(rows.shape[0], HEADS, rows.shape[1] // HEADS)


def logit_grads(masked_logits, log_total, hit, active_positions, row_weight, denom):
    grad_logits = (row_weight / denom)[:, None] * (
        jnp.exp(masked_logits - log_total[:, None])
        - 0.9 * hit.astype(jnp.float32)
        - 0.1 / VOCAB_SIZE * active_positions.astype(jnp.float32)[None, :]
    )
    return grad_logits.astype(jnp.bfloat16)


def adaptive_moment_update(grad, weight, first, second):
    first_new = BETA_ONE * first + (1.0 - BETA_ONE) * grad
    second_new = BETA_TWO * second + (1.0 - BETA_TWO) * grad * grad
    debiased_mean_estimate = first_new / (1.0 - BETA_ONE**STEP)
    debiased_variance_estimate = second_new / (1.0 - BETA_TWO**STEP)
    weight_new = weight - STRIDE_LENGTH * (
        debiased_mean_estimate / (jnp.sqrt(debiased_variance_estimate) + STABILITY_FLOOR)
        + SHRINK_PENALTY * weight
    )
    return (weight_new, first_new, second_new)


def local(
    packed_symbol_codes,
    article_numbering,
    target_spots,
    answer_flags,
    shared_embedding,
    spot_embedding,
    combined_qkv_weights,
    attend_outgoing_weights,
    dense_incoming_weights,
    dense_outgoing_weights,
    layernorm_affine,
    bias_terms,
    adaptor_float_copies,
    average_moments,
    squared_moments,
):
    tokens_here = packed_symbol_codes[0]
    segments = article_numbering[0]
    spot_objective = target_spots[0]
    rows_here = spot_objective.shape[0]
    shard_rows = shared_embedding.shape[0]
    table_base = lax.axis_index("vocab") * shard_rows
    all_tokens = lax.all_gather(packed_symbol_codes, "vocab", axis=0, tiled=True).reshape(-1)
    wanted = all_tokens - table_base
    inside = (wanted >= 0) & (wanted < shard_rows)
    picked = jnp.take(shared_embedding, jnp.clip(wanted, 0, shard_rows - 1), axis=0)
    embedded = lax.psum_scatter(
        jnp.where(inside[:, None], picked.astype(jnp.float32), 0.0).astype(jnp.bfloat16),
        "vocab",
        scatter_dimension=0,
        tiled=True,
    ).astype(jnp.float32)
    stream = embedded + jnp.take(spot_embedding, positions(segments), axis=0).astype(jnp.float32)
    (a_qkv, b_qkv, a_o, b_o, a_fc, b_fc, a_p, b_p) = [
        lexicon_portion.astype(jnp.bfloat16)
        for lexicon_portion in distinct_thin_pairs(adaptor_float_copies)
    ]
    width = stream.shape[1]
    hidden_width = dense_incoming_weights.shape[1]
    length = stream.shape[0]
    onehot = (spot_objective[:, None] == jnp.arange(length, dtype=jnp.int32)[None, :])
    pick = onehot.astype(jnp.bfloat16)
    h1 = layer_norm(stream, layernorm_affine[0], layernorm_affine[3]).astype(jnp.bfloat16)
    stream_rows = jnp.take(stream, spot_objective, axis=0)
    h1_rows = select_rows(pick, h1)
    u1 = matrix_multiply(h1, a_qkv).astype(jnp.bfloat16)
    u1_rows = select_rows(pick, u1)
    q = (
        matrix_multiply(h1_rows, combined_qkv_weights[:, :width])
        + bias_terms[:width]
        + ADAPTER_SCALE * matrix_multiply(u1_rows[:, :RANK], b_qkv[0])
    ).astype(jnp.bfloat16)
    kv = (
        matrix_multiply(h1, combined_qkv_weights[:, width:])
        + bias_terms[width : 3 * width]
        + ADAPTER_SCALE
        * matrix_multiply(u1[:, RANK:], block_diagonal_mask(b_qkv[1:]))
    ).astype(jnp.bfloat16)
    queries, keys_all, values_all = split_heads(q), split_heads(kv[:, :width]), split_heads(kv[:, width:])
    scale = queries.shape[2] ** (-0.5)
    there = jnp.arange(length, dtype=jnp.int32)[None, :]
    segment_rows = jnp.take(segments, spot_objective)
    allowed = (there <= spot_objective[:, None]) & (segment_rows[:, None] == segments[None, :])
    scores = (
        jnp.einsum("qhd,khd->hqk", queries, keys_all, preferred_element_type=jnp.float32) * scale
    )
    scores = jnp.where(allowed[None], scores, MASKED)
    top = jnp.max(scores, axis=2, keepdims=True)
    expd = jnp.exp(scores - top)
    probs = expd / jnp.sum(expd, axis=2, keepdims=True)
    probs_low = probs.astype(jnp.bfloat16)
    o = (
        jnp.einsum("hqk,khd->qhd", probs_low, values_all, preferred_element_type=jnp.float32)
        .reshape(rows_here, width)
        .astype(jnp.bfloat16)
    )
    uo = matrix_multiply(o, a_o).astype(jnp.bfloat16)
    middle = (
        stream_rows
        + matrix_multiply(o, attend_outgoing_weights)
        + bias_terms[3 * width : 4 * width]
        + ADAPTER_SCALE * matrix_multiply(uo, b_o)
    )
    h2, norm_two_back = jax.vjp(
        lambda value: layer_norm(value, layernorm_affine[1], layernorm_affine[4]), middle
    )
    h2 = h2.astype(jnp.bfloat16)
    uf = matrix_multiply(h2, a_fc).astype(jnp.bfloat16)
    pre = (
        matrix_multiply(h2, dense_incoming_weights)
        + bias_terms[4 * width : 4 * width + hidden_width]
        + ADAPTER_SCALE * matrix_multiply(uf, b_fc)
    )
    f, gelu_back = jax.vjp(partial(jax.nn.gelu, approximate=True), pre)
    f = f.astype(jnp.bfloat16)
    up = matrix_multiply(f, a_p).astype(jnp.bfloat16)
    output = (
        middle
        + matrix_multiply(f, dense_outgoing_weights)
        + bias_terms[4 * width + hidden_width :]
        + ADAPTER_SCALE * matrix_multiply(up, b_p)
    )
    closing_result, final_back = jax.vjp(
        lambda value: layer_norm(value, layernorm_affine[2], layernorm_affine[5]), output
    )
    final_rows = closing_result.astype(jnp.bfloat16)
    next_places = spot_objective + 1
    targets = jnp.take(tokens_here, next_places)
    weights_here = answer_flags[0] * (
        jnp.take(segments, spot_objective) == jnp.take(segments, next_places)
    ).astype(jnp.int32)
    all_labels = lax.all_gather(
        jnp.stack([targets, weights_here], axis=1), "vocab", axis=0, tiled=True
    )
    class_scores = matrix_multiply_transposed_right(
        lax.all_gather(final_rows, "vocab", axis=0, tiled=True), shared_embedding
    )
    vocab_ids = table_base + jnp.arange(shard_rows, dtype=jnp.int32)
    active_positions = vocab_ids < VOCAB_SIZE
    masked_logits = jnp.where(active_positions[None, :], class_scores, -jnp.inf)
    local_top = jnp.max(masked_logits, axis=1)
    smooth_local = jnp.sum(jnp.where(active_positions[None, :], class_scores, 0.0), axis=1)
    hit = vocab_ids[None, :] == all_labels[:, 0:1]
    target_local = jnp.sum(jnp.where(hit, class_scores, 0.0), axis=1)
    top = lax.pmax(local_top, "vocab")
    local_sum = jnp.sum(jnp.exp(masked_logits - top[:, None]), axis=1)
    exp_sum, smooth_sum, target_logit = lax.psum((local_sum, smooth_local, target_local), "vocab")
    log_total = top + jnp.log(exp_sum)
    row_weight = all_labels[:, 1].astype(jnp.float32)
    row_loss = log_total - 0.9 * target_logit - 0.1 * smooth_sum / VOCAB_SIZE
    loss_sum, weight_sum = lax.psum((jnp.sum(row_weight * row_loss), jnp.sum(row_weight)), "dp")
    denom = jnp.maximum(weight_sum, 1.0)
    smoothed_entropy_cost = loss_sum / denom
    grad_logits = logit_grads(masked_logits, log_total, hit, active_positions, row_weight, denom)
    grad_rows = lax.psum_scatter(
        matrix_multiply(
            lax.slice_in_dim(grad_logits, 0, rows_here * lax.axis_size("vocab"), axis=0),
            shared_embedding,
        ),
        "vocab",
        scatter_dimension=0,
        tiled=True,
    )
    same = spot_objective[:, None] == spot_objective[None, :]
    order = jnp.arange(rows_here, dtype=jnp.int32)
    repeat = jnp.any(same & (order[None, :] < order[:, None]), axis=1)
    merge = (same & ~repeat[:, None]).astype(jnp.float32)
    grad_final = jnp.dot(merge, grad_rows, precision=lax.Precision.HIGHEST)
    (dx3,) = final_back(grad_final)
    dm = dx3.astype(jnp.bfloat16)
    g_bp = ADAPTER_SCALE * matrix_multiply_transposed_left(up, dm)
    du_p = (ADAPTER_SCALE * matrix_multiply_transposed_right(dm, b_p)).astype(jnp.bfloat16)
    g_ap = matrix_multiply_transposed_left(f, du_p)
    df = matrix_multiply_transposed_right(
        dm, dense_outgoing_weights
    ) + matrix_multiply_transposed_right(du_p, a_p)
    (dpre,) = gelu_back(df)
    dpre = dpre.astype(jnp.bfloat16)
    g_bfc = ADAPTER_SCALE * matrix_multiply_transposed_left(uf, dpre)
    du_f = (ADAPTER_SCALE * matrix_multiply_transposed_right(dpre, b_fc)).astype(jnp.bfloat16)
    g_afc = matrix_multiply_transposed_left(h2, du_f)
    dh2 = matrix_multiply_transposed_right(
        dpre, dense_incoming_weights
    ) + matrix_multiply_transposed_right(du_f, a_fc)
    (grad_middle,) = norm_two_back(dh2)
    dx2 = dx3 + grad_middle
    da = dx2.astype(jnp.bfloat16)
    g_bo = ADAPTER_SCALE * matrix_multiply_transposed_left(uo, da)
    du_o = (ADAPTER_SCALE * matrix_multiply_transposed_right(da, b_o)).astype(jnp.bfloat16)
    g_ao = matrix_multiply_transposed_left(o, du_o)
    do = (
        matrix_multiply_transposed_right(da, attend_outgoing_weights)
        + matrix_multiply_transposed_right(du_o, a_o)
    ).astype(jnp.bfloat16)
    do = split_heads(do)
    dv = jnp.einsum("hqk,qhd->khd", probs_low, do, preferred_element_type=jnp.float32)
    dp = jnp.einsum("qhd,khd->hqk", do, values_all, preferred_element_type=jnp.float32)
    ds = (probs * (dp - jnp.sum(probs * dp, axis=2, keepdims=True))).astype(jnp.bfloat16)
    dq = jnp.einsum("hqk,khd->qhd", ds, keys_all, preferred_element_type=jnp.float32) * scale
    dk = jnp.einsum("hqk,qhd->khd", ds, queries, preferred_element_type=jnp.float32) * scale
    dq = dq.reshape(rows_here, width).astype(jnp.bfloat16)
    dk = dk.reshape(length, width).astype(jnp.bfloat16)
    dv = dv.reshape(length, width).astype(jnp.bfloat16)
    thirds = ((h1_rows, u1_rows, dq), (h1, u1, dk), (h1, u1, dv))
    g_bqkv = []
    g_aqkv = []
    for j, (normed, low, grad) in enumerate(thirds):
        low = low[:, j * RANK : (j + 1) * RANK]
        g_bqkv.append(ADAPTER_SCALE * matrix_multiply_transposed_left(low, grad))
        du = (ADAPTER_SCALE * matrix_multiply_transposed_right(grad, b_qkv[j])).astype(
            jnp.bfloat16
        )
        g_aqkv.append(matrix_multiply_transposed_left(normed, du))
    pieces = [
        jnp.concatenate(g_aqkv, axis=1),
        jnp.concatenate(g_bqkv, axis=0),
        g_ao,
        g_bo,
        g_afc,
        g_bfc,
        g_ap,
        g_bp,
    ]
    local_grad = jnp.concatenate([piece.reshape(-1) for piece in pieces])
    grad_total = lax.psum(local_grad, ("dp", "vocab"))
    gradient_global_norm = jnp.sqrt(jnp.sum(grad_total * grad_total))
    capped_derivative = grad_total * (GRAD_CLIP / jnp.maximum(gradient_global_norm, GRAD_CLIP))
    refreshed_thin_pairs, updated_first_moment, updated_second_moment = adaptive_moment_update(
        capped_derivative, adaptor_float_copies, average_moments, squared_moments
    )
    return (
        refreshed_thin_pairs,
        updated_first_moment,
        updated_second_moment,
        gradient_global_norm,
        smoothed_entropy_cost,
    )


def solution(mesh):
    return jax.shard_map(
        local,
        mesh=mesh,
        in_specs=(
            P(("dp", "vocab"), None),
            P(("dp", "vocab"), None),
            P(("dp", "vocab"), None),
            P(("dp", "vocab"), None),
            P("vocab", None),
            P(),
            P(),
            P(),
            P(),
            P(),
            P(),
            P(),
            P(),
            P(),
            P(),
        ),
        out_specs=(P(), P(), P(), P(), P()),
        check_vma=False,
    )
```

```python
from functools import partial
import math

import jax
import jax.numpy as jnp
from jax import lax
from jax.experimental import pallas as pl
from jax.experimental.pallas import tpu as pltpu
from jax.sharding import PartitionSpec as P

MODEL_WIDTH = 1024
HEADS = 16
FEEDFWD_UNITS = 4096
VOCAB_SIZE = 50257
RANK = 4
STEP = 10


ADAPTER_SCALE = 8.0
NORM_EPS = 1e-05
GRAD_CLIP = 0.0001
STRIDE_LENGTH = 0.02
BETA_ONE = 0.9
BETA_TWO = 0.999
SHRINK_PENALTY = 0.01
STABILITY_FLOOR = 1e-08
MASKED = -1e30
MESH = pl.DeviceIdType.MESH


def matrix_multiply(left, right):
    return jnp.dot(left, right, preferred_element_type=jnp.float32)


def matrix_multiply_transposed_left(left, right):
    return lax.dot_general(
        left, right, (((0,), (0,)), ((), ())), preferred_element_type=jnp.float32
    )


def matrix_multiply_transposed_right(left, right):
    return lax.dot_general(
        left, right, (((1,), (1,)), ((), ())), preferred_element_type=jnp.float32
    )


def layer_norm(stream, gain, shift):
    centred = stream - jnp.mean(stream, axis=-1, keepdims=True)
    spread = lax.rsqrt(jnp.mean(centred * centred, axis=-1, keepdims=True) + NORM_EPS)
    return centred * spread * gain + shift


def positions(segments):
    steps_here = jnp.arange(segments.shape[0], dtype=jnp.int32)
    earlier = (segments[None, :] == segments[:, None]) & (steps_here[None, :] < steps_here[:, None])
    return jnp.sum(earlier.astype(jnp.int32), axis=1)


def distinct_thin_pairs(stacked_samples):
    shapes = [
        (MODEL_WIDTH, 3 * RANK),
        (3, RANK, MODEL_WIDTH),
        (MODEL_WIDTH, RANK),
        (RANK, MODEL_WIDTH),
        (MODEL_WIDTH, RANK),
        (RANK, FEEDFWD_UNITS),
        (FEEDFWD_UNITS, RANK),
        (RANK, MODEL_WIDTH),
    ]
    pieces = []
    offset = 0
    for shape in shapes:
        number = math.prod(shape)
        pieces.append(stacked_samples[offset : offset + number].reshape(shape))
        offset += number
    return pieces


def block_diagonal_mask(blocks):
    number, rank, width = blocks.shape
    eye = jnp.eye(number, dtype=blocks.dtype)
    return (eye[:, None, :, None] * blocks[:, :, None, :]).reshape(number * rank, number * width)


def select_rows(onehot, rows):
    return matrix_multiply(onehot, rows).astype(jnp.bfloat16)


def split_heads(rows):
    return rows.reshape(rows.shape[0], HEADS, rows.shape[1] // HEADS)


def logit_grads(masked_logits, log_total, hit, active_positions, row_weight, denom):
    grad_logits = (row_weight / denom)[:, None] * (
        jnp.exp(masked_logits - log_total[:, None])
        - 0.9 * hit.astype(jnp.float32)
        - 0.1 / VOCAB_SIZE * active_positions.astype(jnp.float32)[None, :]
    )
    return grad_logits.astype(jnp.bfloat16)


def adaptive_moment_update(grad, weight, first, second):
    first_new = BETA_ONE * first + (1.0 - BETA_ONE) * grad
    second_new = BETA_TWO * second + (1.0 - BETA_TWO) * grad * grad
    debiased_mean_estimate = first_new / (1.0 - BETA_ONE**STEP)
    debiased_variance_estimate = second_new / (1.0 - BETA_TWO**STEP)
    weight_new = weight - STRIDE_LENGTH * (
        debiased_mean_estimate / (jnp.sqrt(debiased_variance_estimate) + STABILITY_FLOOR)
        + SHRINK_PENALTY * weight
    )
    return (weight_new, first_new, second_new)


def sum_and_step(dp_size, vocab_size, grad_ref, weight_ref, first_ref, second_ref,
                 weight_out, first_out, second_out, norm_out,
                 parts, planes, total, send_a, recv_a, send_b, recv_b, send_c, recv_c):
    my_plane = lax.axis_index("dp")
    me = lax.axis_index("vocab")

    def across(j):
        return (my_plane, lax.rem(me + j, vocab_size))

    def along(i):
        return (lax.rem(my_plane + i, dp_size), me)

    barrier = pltpu.get_barrier_semaphore()

    @pl.loop(1, vocab_size)
    def _(j):
        pl.semaphore_signal(barrier, inc=1, device_id=across(j), device_id_type=MESH)

    @pl.loop(1, dp_size)
    def _(i):
        pl.semaphore_signal(barrier, inc=1, device_id=along(i), device_id_type=MESH)

    pl.semaphore_wait(barrier, vocab_size + dp_size - 2)

    def part_copy(j):
        peer = across(j)
        return pltpu.make_async_remote_copy(
            src_ref=grad_ref.at[peer[1]], dst_ref=parts.at[me],
            send_sem=send_a.at[peer[1]], recv_sem=recv_a.at[me],
            device_id=peer, device_id_type=MESH)

    def part_arrival(j):
        peer = across(j)
        return pltpu.make_async_remote_copy(
            src_ref=grad_ref.at[peer[1]], dst_ref=parts.at[peer[1]],
            send_sem=send_a.at[peer[1]], recv_sem=recv_a.at[peer[1]],
            device_id=peer, device_id_type=MESH)

    def plane_copy(i):
        peer = along(i)
        return pltpu.make_async_remote_copy(
            src_ref=planes.at[my_plane], dst_ref=planes.at[my_plane],
            send_sem=send_b.at[peer[0]], recv_sem=recv_b.at[my_plane],
            device_id=peer, device_id_type=MESH)

    def plane_arrival(i):
        peer = along(i)
        return pltpu.make_async_remote_copy(
            src_ref=planes.at[my_plane], dst_ref=planes.at[peer[0]],
            send_sem=send_b.at[peer[0]], recv_sem=recv_b.at[peer[0]],
            device_id=peer, device_id_type=MESH)

    def total_copy(j):
        peer = across(j)
        return pltpu.make_async_remote_copy(
            src_ref=total.at[me], dst_ref=total.at[me],
            send_sem=send_c.at[peer[1]], recv_sem=recv_c.at[me],
            device_id=peer, device_id_type=MESH)

    def total_arrival(j):
        peer = across(j)
        return pltpu.make_async_remote_copy(
            src_ref=total.at[me], dst_ref=total.at[peer[1]],
            send_sem=send_c.at[peer[1]], recv_sem=recv_c.at[peer[1]],
            device_id=peer, device_id_type=MESH)

    @pl.loop(1, vocab_size)
    def _(j):
        part_copy(j).start()

    parts[me] = grad_ref[me]

    @pl.loop(1, vocab_size)
    def _(j):
        part_arrival(j).wait_recv()

    planes[my_plane] = lax.fori_loop(
        1, vocab_size, lambda j, held: held + parts[j], parts[0])

    @pl.loop(1, dp_size)
    def _(i):
        plane_copy(i).start()

    @pl.loop(1, dp_size)
    def _(i):
        plane_arrival(i).wait_recv()

    total[me] = lax.fori_loop(1, dp_size, lambda i, held: held + planes[i], planes[0])

    @pl.loop(1, vocab_size)
    def _(j):
        total_copy(j).start()

    @pl.loop(1, vocab_size)
    def _(j):
        part_copy(j).wait_send()

    @pl.loop(1, dp_size)
    def _(i):
        plane_copy(i).wait_send()

    @pl.loop(1, vocab_size)
    def _(j):
        total_arrival(j).wait_recv()

    @pl.loop(1, vocab_size)
    def _(j):
        total_copy(j).wait_send()

    def squares(j, held):
        piece = total[j]
        return held + piece * piece

    gathered = lax.fori_loop(0, vocab_size, squares, jnp.zeros(parts.shape[1:], jnp.float32))
    norm = jnp.sqrt(jnp.sum(gathered, keepdims=True))
    norm_out[...] = jnp.broadcast_to(norm, norm_out.shape)
    shrink = GRAD_CLIP / jnp.maximum(norm, GRAD_CLIP)

    @pl.loop(0, vocab_size)
    def _(j):
        weight, first, second = adaptive_moment_update(
            total[j] * shrink, weight_ref[j], first_ref[j], second_ref[j])
        weight_out[j] = weight
        first_out[j] = first
        second_out[j] = second


def reduce_and_update(mesh_sizes, local_grad, weights, first, second):
    dp_size, vocab_size = mesh_sizes
    number = local_grad.shape[0]
    rows = number // (128 * vocab_size)
    shape = (vocab_size, rows, 128)
    block = pltpu.VMEM(shape, jnp.float32)
    whole = pl.BlockSpec(memory_space=pltpu.VMEM)
    weight_new, first_new, second_new, norm = pl.pallas_call(
        partial(sum_and_step, dp_size, vocab_size),
        out_shape=[jax.ShapeDtypeStruct(shape, jnp.float32)] * 3
        + [jax.ShapeDtypeStruct((8, 128), jnp.float32)],
        in_specs=[whole] * 4,
        out_specs=[whole] * 4,
        scratch_shapes=[
            block,
            pltpu.VMEM((dp_size, rows, 128), jnp.float32),
            block,
            pltpu.SemaphoreType.DMA((vocab_size,)),
            pltpu.SemaphoreType.DMA((vocab_size,)),
            pltpu.SemaphoreType.DMA((dp_size,)),
            pltpu.SemaphoreType.DMA((dp_size,)),
            pltpu.SemaphoreType.DMA((vocab_size,)),
            pltpu.SemaphoreType.DMA((vocab_size,)),
        ],
        compiler_params=pltpu.CompilerParams(
            collective_id=5, has_side_effects=True, vmem_limit_bytes=24 << 20
        ),
        name="sum_and_step",
    )(*[piece.reshape(shape) for piece in (local_grad, weights, first, second)])
    flat = [piece.reshape(-1) for piece in (weight_new, first_new, second_new)]
    return (*flat, norm[0, 0])


def local(
    mesh_sizes,
    packed_symbol_codes,
    article_numbering,
    target_spots,
    answer_flags,
    shared_embedding,
    spot_embedding,
    combined_qkv_weights,
    attend_outgoing_weights,
    dense_incoming_weights,
    dense_outgoing_weights,
    layernorm_affine,
    bias_terms,
    adaptor_float_copies,
    average_moments,
    squared_moments,
):
    tokens_here = packed_symbol_codes[0]
    segments = article_numbering[0]
    spot_objective = target_spots[0]
    rows_here = spot_objective.shape[0]
    shard_rows = shared_embedding.shape[0]
    table_base = lax.axis_index("vocab") * shard_rows
    all_tokens = lax.all_gather(packed_symbol_codes, "vocab", axis=0, tiled=True).reshape(-1)
    wanted = all_tokens - table_base
    inside = (wanted >= 0) & (wanted < shard_rows)
    picked = jnp.take(shared_embedding, jnp.clip(wanted, 0, shard_rows - 1), axis=0)
    embedded = lax.psum_scatter(
        jnp.where(inside[:, None], picked.astype(jnp.float32), 0.0).astype(jnp.bfloat16),
        "vocab",
        scatter_dimension=0,
        tiled=True,
    ).astype(jnp.float32)
    stream = embedded + jnp.take(spot_embedding, positions(segments), axis=0).astype(jnp.float32)
    (a_qkv, b_qkv, a_o, b_o, a_fc, b_fc, a_p, b_p) = [
        lexicon_portion.astype(jnp.bfloat16)
        for lexicon_portion in distinct_thin_pairs(adaptor_float_copies)
    ]
    width = stream.shape[1]
    hidden_width = dense_incoming_weights.shape[1]
    length = stream.shape[0]
    onehot = (spot_objective[:, None] == jnp.arange(length, dtype=jnp.int32)[None, :])
    pick = onehot.astype(jnp.bfloat16)
    h1 = layer_norm(stream, layernorm_affine[0], layernorm_affine[3]).astype(jnp.bfloat16)
    stream_rows = jnp.take(stream, spot_objective, axis=0)
    h1_rows = select_rows(pick, h1)
    u1 = matrix_multiply(h1, a_qkv).astype(jnp.bfloat16)
    u1_rows = select_rows(pick, u1)
    q = (
        matrix_multiply(h1_rows, combined_qkv_weights[:, :width])
        + bias_terms[:width]
        + ADAPTER_SCALE * matrix_multiply(u1_rows[:, :RANK], b_qkv[0])
    ).astype(jnp.bfloat16)
    kv = (
        matrix_multiply(h1, combined_qkv_weights[:, width:])
        + bias_terms[width : 3 * width]
        + ADAPTER_SCALE
        * matrix_multiply(u1[:, RANK:], block_diagonal_mask(b_qkv[1:]))
    ).astype(jnp.bfloat16)
    queries, keys_all, values_all = split_heads(q), split_heads(kv[:, :width]), split_heads(kv[:, width:])
    scale = queries.shape[2] ** (-0.5)
    there = jnp.arange(length, dtype=jnp.int32)[None, :]
    segment_rows = jnp.take(segments, spot_objective)
    allowed = (there <= spot_objective[:, None]) & (segment_rows[:, None] == segments[None, :])
    scores = (
        jnp.einsum("qhd,khd->hqk", queries, keys_all, preferred_element_type=jnp.float32) * scale
    )
    scores = jnp.where(allowed[None], scores, MASKED)
    top = jnp.max(scores, axis=2, keepdims=True)
    expd = jnp.exp(scores - top)
    probs = expd / jnp.sum(expd, axis=2, keepdims=True)
    probs_low = probs.astype(jnp.bfloat16)
    o = (
        jnp.einsum("hqk,khd->qhd", probs_low, values_all, preferred_element_type=jnp.float32)
        .reshape(rows_here, width)
        .astype(jnp.bfloat16)
    )
    uo = matrix_multiply(o, a_o).astype(jnp.bfloat16)
    middle = (
        stream_rows
        + matrix_multiply(o, attend_outgoing_weights)
        + bias_terms[3 * width : 4 * width]
        + ADAPTER_SCALE * matrix_multiply(uo, b_o)
    )
    h2, norm_two_back = jax.vjp(
        lambda value: layer_norm(value, layernorm_affine[1], layernorm_affine[4]), middle
    )
    h2 = h2.astype(jnp.bfloat16)
    uf = matrix_multiply(h2, a_fc).astype(jnp.bfloat16)
    pre = (
        matrix_multiply(h2, dense_incoming_weights)
        + bias_terms[4 * width : 4 * width + hidden_width]
        + ADAPTER_SCALE * matrix_multiply(uf, b_fc)
    )
    f, gelu_back = jax.vjp(partial(jax.nn.gelu, approximate=True), pre)
    f = f.astype(jnp.bfloat16)
    up = matrix_multiply(f, a_p).astype(jnp.bfloat16)
    output = (
        middle
        + matrix_multiply(f, dense_outgoing_weights)
        + bias_terms[4 * width + hidden_width :]
        + ADAPTER_SCALE * matrix_multiply(up, b_p)
    )
    closing_result, final_back = jax.vjp(
        lambda value: layer_norm(value, layernorm_affine[2], layernorm_affine[5]), output
    )
    final_rows = closing_result.astype(jnp.bfloat16)
    next_places = spot_objective + 1
    targets = jnp.take(tokens_here, next_places)
    weights_here = answer_flags[0] * (
        jnp.take(segments, spot_objective) == jnp.take(segments, next_places)
    ).astype(jnp.int32)
    all_labels = lax.all_gather(
        jnp.stack([targets, weights_here], axis=1), "vocab", axis=0, tiled=True
    )
    class_scores = matrix_multiply_transposed_right(
        lax.all_gather(final_rows, "vocab", axis=0, tiled=True), shared_embedding
    )
    vocab_ids = table_base + jnp.arange(shard_rows, dtype=jnp.int32)
    active_positions = vocab_ids < VOCAB_SIZE
    masked_logits = jnp.where(active_positions[None, :], class_scores, -jnp.inf)
    local_top = jnp.max(masked_logits, axis=1)
    smooth_local = jnp.sum(jnp.where(active_positions[None, :], class_scores, 0.0), axis=1)
    hit = vocab_ids[None, :] == all_labels[:, 0:1]
    target_local = jnp.sum(jnp.where(hit, class_scores, 0.0), axis=1)
    top = lax.pmax(local_top, "vocab")
    local_sum = jnp.sum(jnp.exp(masked_logits - top[:, None]), axis=1)
    exp_sum, smooth_sum, target_logit = lax.psum((local_sum, smooth_local, target_local), "vocab")
    log_total = top + jnp.log(exp_sum)
    row_weight = all_labels[:, 1].astype(jnp.float32)
    row_loss = log_total - 0.9 * target_logit - 0.1 * smooth_sum / VOCAB_SIZE
    loss_sum, weight_sum = lax.psum((jnp.sum(row_weight * row_loss), jnp.sum(row_weight)), "dp")
    denom = jnp.maximum(weight_sum, 1.0)
    smoothed_entropy_cost = loss_sum / denom
    grad_logits = logit_grads(masked_logits, log_total, hit, active_positions, row_weight, denom)
    grad_rows = lax.psum_scatter(
        matrix_multiply(
            lax.slice_in_dim(grad_logits, 0, rows_here * lax.axis_size("vocab"), axis=0),
            shared_embedding,
        ),
        "vocab",
        scatter_dimension=0,
        tiled=True,
    )
    same = spot_objective[:, None] == spot_objective[None, :]
    order = jnp.arange(rows_here, dtype=jnp.int32)
    repeat = jnp.any(same & (order[None, :] < order[:, None]), axis=1)
    merge = (same & ~repeat[:, None]).astype(jnp.float32)
    grad_final = jnp.dot(merge, grad_rows, precision=lax.Precision.HIGHEST)
    (dx3,) = final_back(grad_final)
    dm = dx3.astype(jnp.bfloat16)
    g_bp = ADAPTER_SCALE * matrix_multiply_transposed_left(up, dm)
    du_p = (ADAPTER_SCALE * matrix_multiply_transposed_right(dm, b_p)).astype(jnp.bfloat16)
    g_ap = matrix_multiply_transposed_left(f, du_p)
    df = matrix_multiply_transposed_right(
        dm, dense_outgoing_weights
    ) + matrix_multiply_transposed_right(du_p, a_p)
    (dpre,) = gelu_back(df)
    dpre = dpre.astype(jnp.bfloat16)
    g_bfc = ADAPTER_SCALE * matrix_multiply_transposed_left(uf, dpre)
    du_f = (ADAPTER_SCALE * matrix_multiply_transposed_right(dpre, b_fc)).astype(jnp.bfloat16)
    g_afc = matrix_multiply_transposed_left(h2, du_f)
    dh2 = matrix_multiply_transposed_right(
        dpre, dense_incoming_weights
    ) + matrix_multiply_transposed_right(du_f, a_fc)
    (grad_middle,) = norm_two_back(dh2)
    dx2 = dx3 + grad_middle
    da = dx2.astype(jnp.bfloat16)
    g_bo = ADAPTER_SCALE * matrix_multiply_transposed_left(uo, da)
    du_o = (ADAPTER_SCALE * matrix_multiply_transposed_right(da, b_o)).astype(jnp.bfloat16)
    g_ao = matrix_multiply_transposed_left(o, du_o)
    do = (
        matrix_multiply_transposed_right(da, attend_outgoing_weights)
        + matrix_multiply_transposed_right(du_o, a_o)
    ).astype(jnp.bfloat16)
    do = split_heads(do)
    dv = jnp.einsum("hqk,qhd->khd", probs_low, do, preferred_element_type=jnp.float32)
    dp = jnp.einsum("qhd,khd->hqk", do, values_all, preferred_element_type=jnp.float32)
    ds = (probs * (dp - jnp.sum(probs * dp, axis=2, keepdims=True))).astype(jnp.bfloat16)
    dq = jnp.einsum("hqk,khd->qhd", ds, keys_all, preferred_element_type=jnp.float32) * scale
    dk = jnp.einsum("hqk,qhd->khd", ds, queries, preferred_element_type=jnp.float32) * scale
    dq = dq.reshape(rows_here, width).astype(jnp.bfloat16)
    dk = dk.reshape(length, width).astype(jnp.bfloat16)
    dv = dv.reshape(length, width).astype(jnp.bfloat16)
    thirds = ((h1_rows, u1_rows, dq), (h1, u1, dk), (h1, u1, dv))
    g_bqkv = []
    g_aqkv = []
    for j, (normed, low, grad) in enumerate(thirds):
        low = low[:, j * RANK : (j + 1) * RANK]
        g_bqkv.append(ADAPTER_SCALE * matrix_multiply_transposed_left(low, grad))
        du = (ADAPTER_SCALE * matrix_multiply_transposed_right(grad, b_qkv[j])).astype(
            jnp.bfloat16
        )
        g_aqkv.append(matrix_multiply_transposed_left(normed, du))
    pieces = [
        jnp.concatenate(g_aqkv, axis=1),
        jnp.concatenate(g_bqkv, axis=0),
        g_ao,
        g_bo,
        g_afc,
        g_bfc,
        g_ap,
        g_bp,
    ]
    local_grad = jnp.concatenate([piece.reshape(-1) for piece in pieces])
    (
        refreshed_thin_pairs,
        updated_first_moment,
        updated_second_moment,
        gradient_global_norm,
    ) = reduce_and_update(
        mesh_sizes, local_grad, adaptor_float_copies, average_moments, squared_moments
    )
    return (
        refreshed_thin_pairs,
        updated_first_moment,
        updated_second_moment,
        gradient_global_norm,
        smoothed_entropy_cost,
    )


def solution(mesh):
    return jax.shard_map(
        partial(local, (mesh.shape["dp"], mesh.shape["vocab"])),
        mesh=mesh,
        in_specs=(
            P(("dp", "vocab"), None),
            P(("dp", "vocab"), None),
            P(("dp", "vocab"), None),
            P(("dp", "vocab"), None),
            P("vocab", None),
            P(),
            P(),
            P(),
            P(),
            P(),
            P(),
            P(),
            P(),
            P(),
            P(),
        ),
        out_specs=(P(), P(), P(), P(), P()),
        check_vma=False,
    )
```

```python
from functools import partial
import math

import jax
import jax.numpy as jnp
from jax import lax
from jax.experimental import pallas as pl
from jax.experimental.pallas import tpu as pltpu
from jax.sharding import PartitionSpec as P

MODEL_WIDTH = 1024
HEADS = 16
FEEDFWD_UNITS = 4096
VOCAB_SIZE = 50257
RANK = 4
STEP = 10


ADAPTER_SCALE = 8.0
NORM_EPS = 1e-05
GRAD_CLIP = 0.0001
STRIDE_LENGTH = 0.02
BETA_ONE = 0.9
BETA_TWO = 0.999
SHRINK_PENALTY = 0.01
STABILITY_FLOOR = 1e-08
MASKED = -1e30
MESH = pl.DeviceIdType.MESH


def matrix_multiply(left, right):
    return jnp.dot(left, right, preferred_element_type=jnp.float32)


def matrix_multiply_transposed_left(left, right):
    return lax.dot_general(
        left, right, (((0,), (0,)), ((), ())), preferred_element_type=jnp.float32
    )


def matrix_multiply_transposed_right(left, right):
    return lax.dot_general(
        left, right, (((1,), (1,)), ((), ())), preferred_element_type=jnp.float32
    )


def layer_norm(stream, gain, shift):
    centred = stream - jnp.mean(stream, axis=-1, keepdims=True)
    spread = lax.rsqrt(jnp.mean(centred * centred, axis=-1, keepdims=True) + NORM_EPS)
    return centred * spread * gain + shift


def positions(segments):
    steps_here = jnp.arange(segments.shape[0], dtype=jnp.int32)
    earlier = (segments[None, :] == segments[:, None]) & (steps_here[None, :] < steps_here[:, None])
    return jnp.sum(earlier.astype(jnp.int32), axis=1)


def distinct_thin_pairs(stacked_samples):
    shapes = [
        (MODEL_WIDTH, 3 * RANK),
        (3, RANK, MODEL_WIDTH),
        (MODEL_WIDTH, RANK),
        (RANK, MODEL_WIDTH),
        (MODEL_WIDTH, RANK),
        (RANK, FEEDFWD_UNITS),
        (FEEDFWD_UNITS, RANK),
        (RANK, MODEL_WIDTH),
    ]
    pieces = []
    offset = 0
    for shape in shapes:
        number = math.prod(shape)
        pieces.append(stacked_samples[offset : offset + number].reshape(shape))
        offset += number
    return pieces


def block_diagonal_mask(blocks):
    number, rank, width = blocks.shape
    eye = jnp.eye(number, dtype=blocks.dtype)
    return (eye[:, None, :, None] * blocks[:, :, None, :]).reshape(number * rank, number * width)


def select_rows(onehot, rows):
    return matrix_multiply(onehot, rows).astype(jnp.bfloat16)


def split_heads(rows):
    return rows.reshape(rows.shape[0], HEADS, rows.shape[1] // HEADS)


def adaptive_moment_update(grad, weight, first, second):
    first_new = BETA_ONE * first + (1.0 - BETA_ONE) * grad
    second_new = BETA_TWO * second + (1.0 - BETA_TWO) * grad * grad
    debiased_mean_estimate = first_new / (1.0 - BETA_ONE**STEP)
    debiased_variance_estimate = second_new / (1.0 - BETA_TWO**STEP)
    weight_new = weight - STRIDE_LENGTH * (
        debiased_mean_estimate / (jnp.sqrt(debiased_variance_estimate) + STABILITY_FLOOR)
        + SHRINK_PENALTY * weight
    )
    return (weight_new, first_new, second_new)


def sum_and_step(dp_size, vocab_size, grad_ref, weight_ref, first_ref, second_ref,
                 weight_out, first_out, second_out, norm_out,
                 parts, planes, total, send_a, recv_a, send_b, recv_b, send_c, recv_c):
    my_plane = lax.axis_index("dp")
    me = lax.axis_index("vocab")

    def across(j):
        return (my_plane, lax.rem(me + j, vocab_size))

    def along(i):
        return (lax.rem(my_plane + i, dp_size), me)

    barrier = pltpu.get_barrier_semaphore()

    @pl.loop(1, vocab_size)
    def _(j):
        pl.semaphore_signal(barrier, inc=1, device_id=across(j), device_id_type=MESH)

    @pl.loop(1, dp_size)
    def _(i):
        pl.semaphore_signal(barrier, inc=1, device_id=along(i), device_id_type=MESH)

    pl.semaphore_wait(barrier, vocab_size + dp_size - 2)

    def part_copy(j):
        peer = across(j)
        return pltpu.make_async_remote_copy(
            src_ref=grad_ref.at[peer[1]], dst_ref=parts.at[me],
            send_sem=send_a.at[peer[1]], recv_sem=recv_a.at[me],
            device_id=peer, device_id_type=MESH)

    def part_arrival(j):
        peer = across(j)
        return pltpu.make_async_remote_copy(
            src_ref=grad_ref.at[peer[1]], dst_ref=parts.at[peer[1]],
            send_sem=send_a.at[peer[1]], recv_sem=recv_a.at[peer[1]],
            device_id=peer, device_id_type=MESH)

    def plane_copy(i):
        peer = along(i)
        return pltpu.make_async_remote_copy(
            src_ref=planes.at[my_plane], dst_ref=planes.at[my_plane],
            send_sem=send_b.at[peer[0]], recv_sem=recv_b.at[my_plane],
            device_id=peer, device_id_type=MESH)

    def plane_arrival(i):
        peer = along(i)
        return pltpu.make_async_remote_copy(
            src_ref=planes.at[my_plane], dst_ref=planes.at[peer[0]],
            send_sem=send_b.at[peer[0]], recv_sem=recv_b.at[peer[0]],
            device_id=peer, device_id_type=MESH)

    def total_copy(j):
        peer = across(j)
        return pltpu.make_async_remote_copy(
            src_ref=total.at[me], dst_ref=total.at[me],
            send_sem=send_c.at[peer[1]], recv_sem=recv_c.at[me],
            device_id=peer, device_id_type=MESH)

    def total_arrival(j):
        peer = across(j)
        return pltpu.make_async_remote_copy(
            src_ref=total.at[me], dst_ref=total.at[peer[1]],
            send_sem=send_c.at[peer[1]], recv_sem=recv_c.at[peer[1]],
            device_id=peer, device_id_type=MESH)

    @pl.loop(1, vocab_size)
    def _(j):
        part_copy(j).start()

    parts[me] = grad_ref[me]

    @pl.loop(1, vocab_size)
    def _(j):
        part_arrival(j).wait_recv()

    planes[my_plane] = lax.fori_loop(
        1, vocab_size, lambda j, held: held + parts[j], parts[0])

    @pl.loop(1, dp_size)
    def _(i):
        plane_copy(i).start()

    @pl.loop(1, dp_size)
    def _(i):
        plane_arrival(i).wait_recv()

    total[me] = lax.fori_loop(1, dp_size, lambda i, held: held + planes[i], planes[0])

    @pl.loop(1, vocab_size)
    def _(j):
        total_copy(j).start()

    @pl.loop(1, vocab_size)
    def _(j):
        part_copy(j).wait_send()

    @pl.loop(1, dp_size)
    def _(i):
        plane_copy(i).wait_send()

    @pl.loop(1, vocab_size)
    def _(j):
        total_arrival(j).wait_recv()

    @pl.loop(1, vocab_size)
    def _(j):
        total_copy(j).wait_send()

    def squares(j, held):
        piece = total[j]
        return held + piece * piece

    gathered = lax.fori_loop(0, vocab_size, squares, jnp.zeros(parts.shape[1:], jnp.float32))
    norm = jnp.sqrt(jnp.sum(gathered, keepdims=True))
    norm_out[...] = jnp.broadcast_to(norm, norm_out.shape)
    shrink = GRAD_CLIP / jnp.maximum(norm, GRAD_CLIP)

    @pl.loop(0, vocab_size)
    def _(j):
        weight, first, second = adaptive_moment_update(
            total[j] * shrink, weight_ref[j], first_ref[j], second_ref[j])
        weight_out[j] = weight
        first_out[j] = first
        second_out[j] = second


def reduce_and_update(mesh_sizes, local_grad, weights, first, second):
    dp_size, vocab_size = mesh_sizes
    number = local_grad.shape[0]
    rows = number // (128 * vocab_size)
    shape = (vocab_size, rows, 128)
    block = pltpu.VMEM(shape, jnp.float32)
    whole = pl.BlockSpec(memory_space=pltpu.VMEM)
    weight_new, first_new, second_new, norm = pl.pallas_call(
        partial(sum_and_step, dp_size, vocab_size),
        out_shape=[jax.ShapeDtypeStruct(shape, jnp.float32)] * 3
        + [jax.ShapeDtypeStruct((8, 128), jnp.float32)],
        in_specs=[whole] * 4,
        out_specs=[whole] * 4,
        scratch_shapes=[
            block,
            pltpu.VMEM((dp_size, rows, 128), jnp.float32),
            block,
            pltpu.SemaphoreType.DMA((vocab_size,)),
            pltpu.SemaphoreType.DMA((vocab_size,)),
            pltpu.SemaphoreType.DMA((dp_size,)),
            pltpu.SemaphoreType.DMA((dp_size,)),
            pltpu.SemaphoreType.DMA((vocab_size,)),
            pltpu.SemaphoreType.DMA((vocab_size,)),
        ],
        compiler_params=pltpu.CompilerParams(
            collective_id=5, has_side_effects=True, vmem_limit_bytes=24 << 20
        ),
        name="sum_and_step",
    )(*[piece.reshape(shape) for piece in (local_grad, weights, first, second)])
    flat = [piece.reshape(-1) for piece in (weight_new, first_new, second_new)]
    return (*flat, norm[0, 0])


def as_columns(rows, height):
    lanes = rows.shape[1]
    padded = jnp.concatenate([rows, jnp.zeros((128 - rows.shape[0], lanes), rows.dtype)], axis=0)
    return padded.T


def head_step(dp_size, vocab_size, block, hf_ref, label_ref, table_hbm, grad_out, loss_out,
              table, hf_all, label_all, exps, exps_rest, tops, acc, stats_all, count_all, loss_all,
              from_core, from_chip,
              table_sem, label_send, label_recv, hf_send, hf_recv, count_send, count_recv,
              stat_send, stat_recv, core_send, core_recv, chip_send, chip_recv, loss_send, loss_recv):
    plane = lax.axis_index("dp")
    me = lax.axis_index("vocab")
    chips = vocab_size // 2
    chip = me // 2
    core = lax.rem(me, 2)
    sibling = (plane, 2 * chip + 1 - core)
    held = table.shape[0]
    full = held // block
    rest = held - full * block
    base = me * held
    pair = 2 * hf_ref.shape[0]
    width = hf_ref.shape[1]

    def partner(k):
        out = 0
        bit = 1
        while bit < chips:
            out = out + lax.rem(chip // bit + (k // bit) % 2, 2) * bit
            bit *= 2
        return out

    def across(j):
        return (plane, lax.rem(me + j, vocab_size))

    def along(i):
        return (lax.rem(plane + i, dp_size), me)

    even = held % 16 == 0

    def table_copy(j, number):
        rows = pl.ds(pl.multiple_of(j * block, 16), number)
        return pltpu.make_async_copy(table_hbm.at[rows], table.at[rows], table_sem.at[j])

    def whole_copy():
        return pltpu.make_async_copy(table_hbm, table, table_sem.at[0])

    if even:
        @pl.loop(0, full)
        def _(j):
            table_copy(j, block).start()

        table_copy(full, rest).start()
    else:
        whole_copy().start()

    barrier = pltpu.get_barrier_semaphore()

    @pl.loop(1, vocab_size)
    def _(j):
        pl.semaphore_signal(barrier, inc=1, device_id=across(j), device_id_type=MESH)

    @pl.loop(1, dp_size)
    def _(i):
        pl.semaphore_signal(barrier, inc=1, device_id=along(i), device_id_type=MESH)

    pl.semaphore_wait(barrier, vocab_size + dp_size - 2)

    def remote(src, dst, send, recv, peer):
        return pltpu.make_async_remote_copy(
            src_ref=src, dst_ref=dst, send_sem=send, recv_sem=recv,
            device_id=peer, device_id_type=MESH)

    def hf_copy(k):
        peer = sibling if k == 0 else (plane, 2 * partner(k) + core)
        return remote(hf_ref, hf_all.at[me], hf_send.at[k], hf_recv.at[me], peer)

    def hf_arrival(k):
        source = 2 * chip + 1 - core if k == 0 else 2 * partner(k) + core
        return remote(hf_ref, hf_all.at[source], hf_send.at[k], hf_recv.at[source], sibling)

    def hf_forward(k):
        source = 2 * partner(k) + core
        return remote(hf_all.at[source], hf_all.at[source], hf_send.at[chips + k],
                      hf_recv.at[source], sibling)

    def hf_forwarded(k):
        source = 2 * partner(k) + 1 - core
        return remote(hf_ref, hf_all.at[source], hf_send.at[k], hf_recv.at[source], sibling)

    def label_copy(j):
        peer = across(j)
        return remote(label_ref, label_all.at[me], label_send.at[peer[1]], label_recv.at[me], peer)

    def label_arrival(j):
        source = across(j)[1]
        return remote(label_ref, label_all.at[source], label_send.at[source],
                      label_recv.at[source], across(j))

    tops[...] = jnp.zeros((pair, 128), jnp.float32)

    for k in range(chips):
        hf_copy(k).start()

    @pl.loop(1, vocab_size)
    def _(j):
        label_copy(j).start()

    hf_all[me] = hf_ref[...]
    label_all[me] = label_ref[...]

    @pl.loop(1, vocab_size)
    def _(j):
        label_arrival(j).wait_recv()

    def count_copy(i):
        peer = along(i)
        return remote(count_all.at[plane], count_all.at[plane], count_send.at[peer[0]],
                      count_recv.at[plane], peer)

    def count_arrival(i):
        source = along(i)[0]
        return remote(count_all.at[plane], count_all.at[source], count_send.at[source],
                      count_recv.at[source], along(i))

    weights = jnp.sum(label_all[:, 1:2, :].astype(jnp.float32), keepdims=True)
    count_all[plane] = jnp.broadcast_to(weights[0], count_all.shape[1:])

    @pl.loop(1, dp_size)
    def _(i):
        count_copy(i).start()

    lanes = lax.broadcasted_iota(jnp.int32, (pair, 128), 1)

    def targets_of(k):
        rows = label_all[pl.ds(2 * partner(k), 2), 0:1, :].astype(jnp.float32)
        columns = [as_columns(rows[i], 128)[:, 0:1] for i in range(2)]
        return jnp.concatenate(columns, axis=0).astype(jnp.int32) - base

    for k in range(chips):
        if k > 0:
            hf_arrival(k).wait_recv()
            hf_forward(k).start()
            hf_forwarded(k).wait_recv()
        else:
            hf_arrival(0).wait_recv()
            if not even:
                whole_copy().wait()
        hidden = hf_all[pl.ds(2 * partner(k), 2)].reshape(pair, width)
        target = targets_of(k)
        place = pl.ds(k * pair, pair)

        def scores_of(j, number, last):
            if k == 0 and even:
                table_copy(j, number).wait()
            rows = pl.ds(pl.multiple_of(j * block, 16), number)
            z = matrix_multiply_transposed_right(hidden, table[rows, :])
            where_to = lax.broadcasted_iota(jnp.int32, (pair, number), 1)
            hit = where_to == target - j * block
            if last:
                valid = where_to < VOCAB_SIZE - base - j * block
                shown = jnp.where(valid, z, 0.0)
                z = jnp.where(valid, z, MASKED)
            else:
                shown = z
            top = jnp.max(z, axis=1, keepdims=True)
            e = jnp.exp(z - top)
            return e, top, jnp.sum(e, axis=1, keepdims=True), jnp.sum(
                shown, axis=1, keepdims=True), jnp.sum(
                jnp.where(hit, shown, 0.0), axis=1, keepdims=True)

        def join(held_stats, new_stats):
            top, total, smooth, goal = held_stats
            new_top, new_total, new_smooth, new_goal = new_stats
            both = jnp.maximum(top, new_top)
            return (both, total * jnp.exp(top - both) + new_total * jnp.exp(new_top - both),
                    smooth + new_smooth, goal + new_goal)

        def one(j, carry):
            e, top, total, smooth, goal = scores_of(j, block, False)
            exps[j, place, :] = e
            tops[...] = jnp.where(lanes == k * (full + 1) + j, top, tops[...])
            return join(carry, (top, total, smooth, goal))

        nothing = jnp.zeros((pair, 1), jnp.float32)
        carry = lax.fori_loop(0, full, one, (nothing + MASKED, nothing, nothing, nothing))
        e, top, total, smooth, goal = scores_of(full, rest, True)
        exps_rest[place, :] = e
        tops[...] = jnp.where(lanes == k * (full + 1) + full, top, tops[...])
        top, total, smooth, goal = join(carry, (top, total, smooth, goal))
        packed = jnp.where(lanes == 0, top, 0.0)
        for i, piece in enumerate((total, smooth, goal)):
            packed = jnp.where(lanes == i + 1, piece, packed)
        stats_all[me, partner(k)] = packed.T[0:8, :]

    def stat_copy(j):
        peer = across(j)
        return remote(stats_all.at[me], stats_all.at[me], stat_send.at[peer[1]],
                      stat_recv.at[me], peer)

    def stat_arrival(j):
        source = across(j)[1]
        return remote(stats_all.at[me], stats_all.at[source], stat_send.at[source],
                      stat_recv.at[source], across(j))

    @pl.loop(1, vocab_size)
    def _(j):
        stat_copy(j).start()

    @pl.loop(1, dp_size)
    def _(i):
        count_arrival(i).wait_recv()

    count = jnp.maximum(jnp.sum(count_all[:, 0:1, 0:1], axis=0), 1.0)

    @pl.loop(1, vocab_size)
    def _(j):
        stat_arrival(j).wait_recv()

    def lse_of(c):
        here = stats_all[:, c]
        tops_here = here[:, 0:1, :]
        top = jnp.max(tops_here, axis=0)
        total = jnp.sum(here[:, 1:2, :] * jnp.exp(tops_here - top[None]), axis=0)
        return top + jnp.log(total), jnp.sum(here[:, 2:3, :], axis=0), jnp.sum(
            here[:, 3:4, :], axis=0)

    def weights_of(c):
        rows = label_all[pl.ds(2 * c, 2), 1:2, :].astype(jnp.float32)
        return jnp.concatenate([rows[0], rows[1]], axis=1)

    loss = jnp.zeros((1, pair), jnp.float32)
    for c in range(chips):
        lse, smooth, goal = lse_of(c)
        loss = loss + weights_of(c) * (lse - 0.9 * goal - 0.1 * smooth / VOCAB_SIZE)
    loss_all[plane] = jnp.broadcast_to(jnp.sum(loss, keepdims=True), loss_all.shape[1:])

    def loss_copy(i):
        peer = along(i)
        return remote(loss_all.at[plane], loss_all.at[plane], loss_send.at[peer[0]],
                      loss_recv.at[plane], peer)

    def loss_arrival(i):
        source = along(i)[0]
        return remote(loss_all.at[plane], loss_all.at[source], loss_send.at[source],
                      loss_recv.at[source], along(i))

    @pl.loop(1, dp_size)
    def _(i):
        loss_copy(i).start()

    rows_each = pair // 2

    def core_copy(k):
        half = pl.ds(pl.multiple_of((1 - core) * rows_each, rows_each), rows_each)
        return remote(acc.at[half], from_core.at[k], core_send.at[k], core_recv.at[k], sibling)

    def chip_copy(k):
        return remote(from_core.at[k], from_chip.at[k - 1], chip_send.at[k], chip_recv.at[k],
                      (plane, 2 * partner(k) + core))

    for k in range(chips - 1, -1, -1):
        c = partner(k)
        lse, _, _ = lse_of(c)
        share = weights_of(c) / count
        columns = as_columns(jnp.concatenate([lse, share], axis=0), pair)
        lse_col, share_col = columns[:, 0:1], columns[:, 1:2]
        target = targets_of(k)
        factors = share_col * jnp.exp(tops[...] - lse_col)
        low = share_col * (0.1 / VOCAB_SIZE)
        high = low + 0.9 * share_col
        place = pl.ds(k * pair, pair)

        def grads_of(j, number, last, e):
            factor = jnp.sum(jnp.where(lanes == k * (full + 1) + j, factors, 0.0), axis=1, keepdims=True)
            where_to = lax.broadcasted_iota(jnp.int32, (pair, number), 1)
            dz = e * factor - jnp.where(where_to == target - j * block, high, low)
            if last:
                dz = jnp.where(where_to < VOCAB_SIZE - base - j * block, dz, 0.0)
            rows = pl.ds(pl.multiple_of(j * block, 16), number)
            return matrix_multiply(dz.astype(jnp.bfloat16), table[rows, :])

        acc[...] = grads_of(full, rest, True, exps_rest[place, :])

        @pl.loop(0, full)
        def _(j):
            acc[...] += grads_of(j, block, False, exps[j, place, :])

        own = pl.multiple_of(core * rows_each, rows_each)
        core_copy(k).start()
        core_copy(k).wait()
        from_core[k] += acc[pl.ds(own, rows_each), :]
        if k > 0:
            chip_copy(k).start()

    total = from_core[0]
    for k in range(1, chips):
        chip_copy(k).wait_recv()
        total = total + from_chip[k - 1]
    grad_out[...] = total

    @pl.loop(1, dp_size)
    def _(i):
        loss_arrival(i).wait_recv()

    loss_out[...] = jnp.sum(loss_all[...], axis=0) / count

    for k in range(chips):
        hf_copy(k).wait_send()
        if k > 0:
            hf_forward(k).wait_send()
            chip_copy(k).wait_send()

    @pl.loop(1, vocab_size)
    def _(j):
        label_copy(j).wait_send()
        stat_copy(j).wait_send()

    @pl.loop(1, dp_size)
    def _(i):
        count_copy(i).wait_send()
        loss_copy(i).wait_send()


def head(mesh_sizes, final_rows, labels, table):
    dp_size, vocab_size = mesh_sizes
    rows, width = final_rows.shape
    held = table.shape[0]
    block = 1024
    full = held // block
    chips = vocab_size // 2
    whole = pl.BlockSpec(memory_space=pltpu.VMEM)
    dma = pltpu.SemaphoreType.DMA
    grad, loss = pl.pallas_call(
        partial(head_step, dp_size, vocab_size, block),
        out_shape=[
            jax.ShapeDtypeStruct((rows, width), jnp.float32),
            jax.ShapeDtypeStruct((8, 128), jnp.float32),
        ],
        in_specs=[whole, whole, pl.BlockSpec(memory_space=pl.ANY)],
        out_specs=[whole, whole],
        scratch_shapes=[
            pltpu.VMEM((held, width), jnp.bfloat16),
            pltpu.VMEM((vocab_size, rows, width), jnp.bfloat16),
            pltpu.VMEM((vocab_size, 8, rows), jnp.int32),
            pltpu.VMEM((full, vocab_size * rows, block), jnp.float32),
            pltpu.VMEM((vocab_size * rows, held - full * block), jnp.float32),
            pltpu.VMEM((2 * rows, 128), jnp.float32),
            pltpu.VMEM((2 * rows, width), jnp.float32),
            pltpu.VMEM((vocab_size, chips, 8, 2 * rows), jnp.float32),
            pltpu.VMEM((dp_size, 8, 128), jnp.float32),
            pltpu.VMEM((dp_size, 8, 128), jnp.float32),
            pltpu.VMEM((chips, rows, width), jnp.float32),
            pltpu.VMEM((chips - 1, rows, width), jnp.float32),
            dma((full + 1,)),
            dma((vocab_size,)),
            dma((vocab_size,)),
            dma((2 * chips,)),
            dma((vocab_size,)),
            dma((dp_size,)),
            dma((dp_size,)),
            dma((vocab_size,)),
            dma((vocab_size,)),
            dma((chips,)),
            dma((chips,)),
            dma((chips,)),
            dma((chips,)),
            dma((dp_size,)),
            dma((dp_size,)),
        ],
        compiler_params=pltpu.CompilerParams(
            collective_id=3, has_side_effects=True, vmem_limit_bytes=62 << 20
        ),
        name="head_step",
    )(final_rows, labels, table)
    return grad, loss[0, 0]


def local(
    mesh_sizes,
    packed_symbol_codes,
    article_numbering,
    target_spots,
    answer_flags,
    shared_embedding,
    spot_embedding,
    combined_qkv_weights,
    attend_outgoing_weights,
    dense_incoming_weights,
    dense_outgoing_weights,
    layernorm_affine,
    bias_terms,
    adaptor_float_copies,
    average_moments,
    squared_moments,
):
    tokens_here = packed_symbol_codes[0]
    segments = article_numbering[0]
    spot_objective = target_spots[0]
    rows_here = spot_objective.shape[0]
    shard_rows = shared_embedding.shape[0]
    table_base = lax.axis_index("vocab") * shard_rows
    all_tokens = lax.all_gather(packed_symbol_codes, "vocab", axis=0, tiled=True).reshape(-1)
    wanted = all_tokens - table_base
    inside = (wanted >= 0) & (wanted < shard_rows)
    picked = jnp.take(shared_embedding, jnp.clip(wanted, 0, shard_rows - 1), axis=0)
    embedded = lax.psum_scatter(
        jnp.where(inside[:, None], picked.astype(jnp.float32), 0.0).astype(jnp.bfloat16),
        "vocab",
        scatter_dimension=0,
        tiled=True,
    ).astype(jnp.float32)
    stream = embedded + jnp.take(spot_embedding, positions(segments), axis=0).astype(jnp.float32)
    (a_qkv, b_qkv, a_o, b_o, a_fc, b_fc, a_p, b_p) = [
        lexicon_portion.astype(jnp.bfloat16)
        for lexicon_portion in distinct_thin_pairs(adaptor_float_copies)
    ]
    width = stream.shape[1]
    hidden_width = dense_incoming_weights.shape[1]
    length = stream.shape[0]
    onehot = (spot_objective[:, None] == jnp.arange(length, dtype=jnp.int32)[None, :])
    pick = onehot.astype(jnp.bfloat16)
    h1 = layer_norm(stream, layernorm_affine[0], layernorm_affine[3]).astype(jnp.bfloat16)
    stream_rows = jnp.take(stream, spot_objective, axis=0)
    h1_rows = select_rows(pick, h1)
    u1 = matrix_multiply(h1, a_qkv).astype(jnp.bfloat16)
    u1_rows = select_rows(pick, u1)
    q = (
        matrix_multiply(h1_rows, combined_qkv_weights[:, :width])
        + bias_terms[:width]
        + ADAPTER_SCALE * matrix_multiply(u1_rows[:, :RANK], b_qkv[0])
    ).astype(jnp.bfloat16)
    kv = (
        matrix_multiply(h1, combined_qkv_weights[:, width:])
        + bias_terms[width : 3 * width]
        + ADAPTER_SCALE
        * matrix_multiply(u1[:, RANK:], block_diagonal_mask(b_qkv[1:]))
    ).astype(jnp.bfloat16)
    queries, keys_all, values_all = split_heads(q), split_heads(kv[:, :width]), split_heads(kv[:, width:])
    scale = queries.shape[2] ** (-0.5)
    there = jnp.arange(length, dtype=jnp.int32)[None, :]
    segment_rows = jnp.take(segments, spot_objective)
    allowed = (there <= spot_objective[:, None]) & (segment_rows[:, None] == segments[None, :])
    scores = (
        jnp.einsum("qhd,khd->hqk", queries, keys_all, preferred_element_type=jnp.float32) * scale
    )
    scores = jnp.where(allowed[None], scores, MASKED)
    top = jnp.max(scores, axis=2, keepdims=True)
    expd = jnp.exp(scores - top)
    probs = expd / jnp.sum(expd, axis=2, keepdims=True)
    probs_low = probs.astype(jnp.bfloat16)
    o = (
        jnp.einsum("hqk,khd->qhd", probs_low, values_all, preferred_element_type=jnp.float32)
        .reshape(rows_here, width)
        .astype(jnp.bfloat16)
    )
    uo = matrix_multiply(o, a_o).astype(jnp.bfloat16)
    middle = (
        stream_rows
        + matrix_multiply(o, attend_outgoing_weights)
        + bias_terms[3 * width : 4 * width]
        + ADAPTER_SCALE * matrix_multiply(uo, b_o)
    )
    h2, norm_two_back = jax.vjp(
        lambda value: layer_norm(value, layernorm_affine[1], layernorm_affine[4]), middle
    )
    h2 = h2.astype(jnp.bfloat16)
    uf = matrix_multiply(h2, a_fc).astype(jnp.bfloat16)
    pre = (
        matrix_multiply(h2, dense_incoming_weights)
        + bias_terms[4 * width : 4 * width + hidden_width]
        + ADAPTER_SCALE * matrix_multiply(uf, b_fc)
    )
    f, gelu_back = jax.vjp(partial(jax.nn.gelu, approximate=True), pre)
    f = f.astype(jnp.bfloat16)
    up = matrix_multiply(f, a_p).astype(jnp.bfloat16)
    output = (
        middle
        + matrix_multiply(f, dense_outgoing_weights)
        + bias_terms[4 * width + hidden_width :]
        + ADAPTER_SCALE * matrix_multiply(up, b_p)
    )
    closing_result, final_back = jax.vjp(
        lambda value: layer_norm(value, layernorm_affine[2], layernorm_affine[5]), output
    )
    final_rows = closing_result.astype(jnp.bfloat16)
    next_places = spot_objective + 1
    targets = jnp.take(tokens_here, next_places)
    weights_here = answer_flags[0] * (
        jnp.take(segments, spot_objective) == jnp.take(segments, next_places)
    ).astype(jnp.int32)
    labels = jnp.concatenate(
        [targets[None], weights_here[None], jnp.zeros((6, rows_here), jnp.int32)], axis=0
    )
    grad_rows, smoothed_entropy_cost = head(mesh_sizes, final_rows, labels, shared_embedding)
    same = spot_objective[:, None] == spot_objective[None, :]
    order = jnp.arange(rows_here, dtype=jnp.int32)
    repeat = jnp.any(same & (order[None, :] < order[:, None]), axis=1)
    merge = (same & ~repeat[:, None]).astype(jnp.float32)
    grad_final = jnp.dot(merge, grad_rows, precision=lax.Precision.HIGHEST)
    (dx3,) = final_back(grad_final)
    dm = dx3.astype(jnp.bfloat16)
    g_bp = ADAPTER_SCALE * matrix_multiply_transposed_left(up, dm)
    du_p = (ADAPTER_SCALE * matrix_multiply_transposed_right(dm, b_p)).astype(jnp.bfloat16)
    g_ap = matrix_multiply_transposed_left(f, du_p)
    df = matrix_multiply_transposed_right(
        dm, dense_outgoing_weights
    ) + matrix_multiply_transposed_right(du_p, a_p)
    (dpre,) = gelu_back(df)
    dpre = dpre.astype(jnp.bfloat16)
    g_bfc = ADAPTER_SCALE * matrix_multiply_transposed_left(uf, dpre)
    du_f = (ADAPTER_SCALE * matrix_multiply_transposed_right(dpre, b_fc)).astype(jnp.bfloat16)
    g_afc = matrix_multiply_transposed_left(h2, du_f)
    dh2 = matrix_multiply_transposed_right(
        dpre, dense_incoming_weights
    ) + matrix_multiply_transposed_right(du_f, a_fc)
    (grad_middle,) = norm_two_back(dh2)
    dx2 = dx3 + grad_middle
    da = dx2.astype(jnp.bfloat16)
    g_bo = ADAPTER_SCALE * matrix_multiply_transposed_left(uo, da)
    du_o = (ADAPTER_SCALE * matrix_multiply_transposed_right(da, b_o)).astype(jnp.bfloat16)
    g_ao = matrix_multiply_transposed_left(o, du_o)
    do = (
        matrix_multiply_transposed_right(da, attend_outgoing_weights)
        + matrix_multiply_transposed_right(du_o, a_o)
    ).astype(jnp.bfloat16)
    do = split_heads(do)
    dv = jnp.einsum("hqk,qhd->khd", probs_low, do, preferred_element_type=jnp.float32)
    dp = jnp.einsum("qhd,khd->hqk", do, values_all, preferred_element_type=jnp.float32)
    ds = (probs * (dp - jnp.sum(probs * dp, axis=2, keepdims=True))).astype(jnp.bfloat16)
    dq = jnp.einsum("hqk,khd->qhd", ds, keys_all, preferred_element_type=jnp.float32) * scale
    dk = jnp.einsum("hqk,qhd->khd", ds, queries, preferred_element_type=jnp.float32) * scale
    dq = dq.reshape(rows_here, width).astype(jnp.bfloat16)
    dk = dk.reshape(length, width).astype(jnp.bfloat16)
    dv = dv.reshape(length, width).astype(jnp.bfloat16)
    thirds = ((h1_rows, u1_rows, dq), (h1, u1, dk), (h1, u1, dv))
    g_bqkv = []
    g_aqkv = []
    for j, (normed, low, grad) in enumerate(thirds):
        low = low[:, j * RANK : (j + 1) * RANK]
        g_bqkv.append(ADAPTER_SCALE * matrix_multiply_transposed_left(low, grad))
        du = (ADAPTER_SCALE * matrix_multiply_transposed_right(grad, b_qkv[j])).astype(
            jnp.bfloat16
        )
        g_aqkv.append(matrix_multiply_transposed_left(normed, du))
    pieces = [
        jnp.concatenate(g_aqkv, axis=1),
        jnp.concatenate(g_bqkv, axis=0),
        g_ao,
        g_bo,
        g_afc,
        g_bfc,
        g_ap,
        g_bp,
    ]
    local_grad = jnp.concatenate([piece.reshape(-1) for piece in pieces])
    (
        refreshed_thin_pairs,
        updated_first_moment,
        updated_second_moment,
        gradient_global_norm,
    ) = reduce_and_update(
        mesh_sizes, local_grad, adaptor_float_copies, average_moments, squared_moments
    )
    return (
        refreshed_thin_pairs,
        updated_first_moment,
        updated_second_moment,
        gradient_global_norm,
        smoothed_entropy_cost,
    )


def solution(mesh):
    return jax.shard_map(
        partial(local, (mesh.shape["dp"], mesh.shape["vocab"])),
        mesh=mesh,
        in_specs=(
            P(("dp", "vocab"), None),
            P(("dp", "vocab"), None),
            P(("dp", "vocab"), None),
            P(("dp", "vocab"), None),
            P("vocab", None),
            P(),
            P(),
            P(),
            P(),
            P(),
            P(),
            P(),
            P(),
            P(),
            P(),
        ),
        out_specs=(P(), P(), P(), P(), P()),
        check_vma=False,
    )
```

```python
from functools import partial
import math

import jax
import jax.numpy as jnp
from jax import lax
from jax.experimental import pallas as pl
from jax.experimental.pallas import tpu as pltpu
from jax.sharding import PartitionSpec as P

MODEL_WIDTH = 1024
HEADS = 16
FEEDFWD_UNITS = 4096
VOCAB_SIZE = 50257
RANK = 4
STEP = 10


ADAPTER_SCALE = 8.0
NORM_EPS = 1e-05
GRAD_CLIP = 0.0001
STRIDE_LENGTH = 0.02
BETA_ONE = 0.9
BETA_TWO = 0.999
SHRINK_PENALTY = 0.01
STABILITY_FLOOR = 1e-08
MASKED = -1e30
MESH = pl.DeviceIdType.MESH


def matrix_multiply(left, right):
    return jnp.dot(left, right, preferred_element_type=jnp.float32)


def matrix_multiply_transposed_left(left, right):
    return lax.dot_general(
        left, right, (((0,), (0,)), ((), ())), preferred_element_type=jnp.float32
    )


def matrix_multiply_transposed_right(left, right):
    return lax.dot_general(
        left, right, (((1,), (1,)), ((), ())), preferred_element_type=jnp.float32
    )


def layer_norm(stream, gain, shift):
    centred = stream - jnp.mean(stream, axis=-1, keepdims=True)
    spread = lax.rsqrt(jnp.mean(centred * centred, axis=-1, keepdims=True) + NORM_EPS)
    return centred * spread * gain + shift


def positions(segments):
    steps_here = jnp.arange(segments.shape[0], dtype=jnp.int32)
    earlier = (segments[None, :] == segments[:, None]) & (steps_here[None, :] < steps_here[:, None])
    return jnp.sum(earlier.astype(jnp.int32), axis=1)


def distinct_thin_pairs(stacked_samples):
    shapes = [
        (MODEL_WIDTH, 3 * RANK),
        (3, RANK, MODEL_WIDTH),
        (MODEL_WIDTH, RANK),
        (RANK, MODEL_WIDTH),
        (MODEL_WIDTH, RANK),
        (RANK, FEEDFWD_UNITS),
        (FEEDFWD_UNITS, RANK),
        (RANK, MODEL_WIDTH),
    ]
    pieces = []
    offset = 0
    for shape in shapes:
        number = math.prod(shape)
        pieces.append(stacked_samples[offset : offset + number].reshape(shape))
        offset += number
    return pieces


def block_diagonal_mask(blocks):
    number, rank, width = blocks.shape
    eye = jnp.eye(number, dtype=blocks.dtype)
    return (eye[:, None, :, None] * blocks[:, :, None, :]).reshape(number * rank, number * width)


def select_rows(onehot, rows):
    return matrix_multiply(onehot, rows).astype(jnp.bfloat16)


def split_heads(rows):
    return rows.reshape(rows.shape[0], HEADS, rows.shape[1] // HEADS)


def adaptive_moment_update(grad, weight, first, second):
    first_new = BETA_ONE * first + (1.0 - BETA_ONE) * grad
    second_new = BETA_TWO * second + (1.0 - BETA_TWO) * grad * grad
    debiased_mean_estimate = first_new / (1.0 - BETA_ONE**STEP)
    debiased_variance_estimate = second_new / (1.0 - BETA_TWO**STEP)
    weight_new = weight - STRIDE_LENGTH * (
        debiased_mean_estimate / (jnp.sqrt(debiased_variance_estimate) + STABILITY_FLOOR)
        + SHRINK_PENALTY * weight
    )
    return (weight_new, first_new, second_new)


def sum_and_step(dp_size, vocab_size, grad_ref, weight_ref, first_ref, second_ref,
                 weight_out, first_out, second_out, norm_out,
                 parts, planes, total, send_a, recv_a, send_b, recv_b, send_c, recv_c):
    my_plane = lax.axis_index("dp")
    me = lax.axis_index("vocab")

    def across(j):
        return (my_plane, lax.rem(me + j, vocab_size))

    def along(i):
        return (lax.rem(my_plane + i, dp_size), me)

    barrier = pltpu.get_barrier_semaphore()

    @pl.loop(1, vocab_size)
    def _(j):
        pl.semaphore_signal(barrier, inc=1, device_id=across(j), device_id_type=MESH)

    @pl.loop(1, dp_size)
    def _(i):
        pl.semaphore_signal(barrier, inc=1, device_id=along(i), device_id_type=MESH)

    pl.semaphore_wait(barrier, vocab_size + dp_size - 2)

    def part_copy(j):
        peer = across(j)
        return pltpu.make_async_remote_copy(
            src_ref=grad_ref.at[peer[1]], dst_ref=parts.at[me],
            send_sem=send_a.at[peer[1]], recv_sem=recv_a.at[me],
            device_id=peer, device_id_type=MESH)

    def part_arrival(j):
        peer = across(j)
        return pltpu.make_async_remote_copy(
            src_ref=grad_ref.at[peer[1]], dst_ref=parts.at[peer[1]],
            send_sem=send_a.at[peer[1]], recv_sem=recv_a.at[peer[1]],
            device_id=peer, device_id_type=MESH)

    def plane_copy(i):
        peer = along(i)
        return pltpu.make_async_remote_copy(
            src_ref=planes.at[my_plane], dst_ref=planes.at[my_plane],
            send_sem=send_b.at[peer[0]], recv_sem=recv_b.at[my_plane],
            device_id=peer, device_id_type=MESH)

    def plane_arrival(i):
        peer = along(i)
        return pltpu.make_async_remote_copy(
            src_ref=planes.at[my_plane], dst_ref=planes.at[peer[0]],
            send_sem=send_b.at[peer[0]], recv_sem=recv_b.at[peer[0]],
            device_id=peer, device_id_type=MESH)

    def total_copy(j):
        peer = across(j)
        return pltpu.make_async_remote_copy(
            src_ref=total.at[me], dst_ref=total.at[me],
            send_sem=send_c.at[peer[1]], recv_sem=recv_c.at[me],
            device_id=peer, device_id_type=MESH)

    def total_arrival(j):
        peer = across(j)
        return pltpu.make_async_remote_copy(
            src_ref=total.at[me], dst_ref=total.at[peer[1]],
            send_sem=send_c.at[peer[1]], recv_sem=recv_c.at[peer[1]],
            device_id=peer, device_id_type=MESH)

    @pl.loop(1, vocab_size)
    def _(j):
        part_copy(j).start()

    parts[me] = grad_ref[me]

    @pl.loop(1, vocab_size)
    def _(j):
        part_arrival(j).wait_recv()

    planes[my_plane] = lax.fori_loop(
        1, vocab_size, lambda j, held: held + parts[j], parts[0])

    @pl.loop(1, dp_size)
    def _(i):
        plane_copy(i).start()

    @pl.loop(1, dp_size)
    def _(i):
        plane_arrival(i).wait_recv()

    total[me] = lax.fori_loop(1, dp_size, lambda i, held: held + planes[i], planes[0])

    @pl.loop(1, vocab_size)
    def _(j):
        total_copy(j).start()

    @pl.loop(1, vocab_size)
    def _(j):
        part_copy(j).wait_send()

    @pl.loop(1, dp_size)
    def _(i):
        plane_copy(i).wait_send()

    @pl.loop(1, vocab_size)
    def _(j):
        total_arrival(j).wait_recv()

    @pl.loop(1, vocab_size)
    def _(j):
        total_copy(j).wait_send()

    def squares(j, held):
        piece = total[j]
        return held + piece * piece

    gathered = lax.fori_loop(0, vocab_size, squares, jnp.zeros(parts.shape[1:], jnp.float32))
    norm = jnp.sqrt(jnp.sum(gathered, keepdims=True))
    norm_out[...] = jnp.broadcast_to(norm, norm_out.shape)
    shrink = GRAD_CLIP / jnp.maximum(norm, GRAD_CLIP)

    @pl.loop(0, vocab_size)
    def _(j):
        weight, first, second = adaptive_moment_update(
            total[j] * shrink, weight_ref[j], first_ref[j], second_ref[j])
        weight_out[j] = weight
        first_out[j] = first
        second_out[j] = second


def reduce_and_update(mesh_sizes, local_grad, weights, first, second):
    dp_size, vocab_size = mesh_sizes
    number = local_grad.shape[0]
    rows = number // (128 * vocab_size)
    shape = (vocab_size, rows, 128)
    block = pltpu.VMEM(shape, jnp.float32)
    whole = pl.BlockSpec(memory_space=pltpu.VMEM)
    weight_new, first_new, second_new, norm = pl.pallas_call(
        partial(sum_and_step, dp_size, vocab_size),
        out_shape=[jax.ShapeDtypeStruct(shape, jnp.float32)] * 3
        + [jax.ShapeDtypeStruct((8, 128), jnp.float32)],
        in_specs=[whole] * 4,
        out_specs=[whole] * 4,
        scratch_shapes=[
            block,
            pltpu.VMEM((dp_size, rows, 128), jnp.float32),
            block,
            pltpu.SemaphoreType.DMA((vocab_size,)),
            pltpu.SemaphoreType.DMA((vocab_size,)),
            pltpu.SemaphoreType.DMA((dp_size,)),
            pltpu.SemaphoreType.DMA((dp_size,)),
            pltpu.SemaphoreType.DMA((vocab_size,)),
            pltpu.SemaphoreType.DMA((vocab_size,)),
        ],
        compiler_params=pltpu.CompilerParams(
            collective_id=5, has_side_effects=True, vmem_limit_bytes=24 << 20
        ),
        name="sum_and_step",
    )(*[piece.reshape(shape) for piece in (local_grad, weights, first, second)])
    flat = [piece.reshape(-1) for piece in (weight_new, first_new, second_new)]
    return (*flat, norm[0, 0])


def as_columns(rows, height):
    lanes = rows.shape[1]
    padded = jnp.concatenate([rows, jnp.zeros((128 - rows.shape[0], lanes), rows.dtype)], axis=0)
    return padded.T


def head_step(dp_size, vocab_size, block, hf_ref, label_ref, table_hbm, grad_out, loss_out,
              table, hf_all, label_all, exps, exps_rest, tops, acc, stats_all, count_all, loss_all,
              from_core, from_chip,
              table_sem, label_send, label_recv, hf_send, hf_recv, count_send, count_recv,
              stat_send, stat_recv, core_send, core_recv, chip_send, chip_recv, loss_send, loss_recv):
    plane = lax.axis_index("dp")
    me = lax.axis_index("vocab")
    chips = vocab_size // 2
    chip = me // 2
    core = lax.rem(me, 2)
    sibling = (plane, 2 * chip + 1 - core)
    held = table.shape[0]
    full = held // block
    rest = held - full * block
    base = me * held
    pair = 2 * hf_ref.shape[0]
    width = hf_ref.shape[1]

    def partner(k):
        out = 0
        bit = 1
        while bit < chips:
            out = out + lax.rem(chip // bit + (k // bit) % 2, 2) * bit
            bit *= 2
        return out

    def across(j):
        return (plane, lax.rem(me + j, vocab_size))

    def along(i):
        return (lax.rem(plane + i, dp_size), me)

    even = held % 16 == 0

    def table_copy(j, number):
        rows = pl.ds(pl.multiple_of(j * block, 16), number)
        return pltpu.make_async_copy(table_hbm.at[rows], table.at[rows], table_sem.at[j])

    def whole_copy():
        return pltpu.make_async_copy(table_hbm, table, table_sem.at[0])

    if even:
        @pl.loop(0, full)
        def _(j):
            table_copy(j, block).start()

        table_copy(full, rest).start()
    else:
        whole_copy().start()

    barrier = pltpu.get_barrier_semaphore()

    @pl.loop(1, vocab_size)
    def _(j):
        pl.semaphore_signal(barrier, inc=1, device_id=across(j), device_id_type=MESH)

    @pl.loop(1, dp_size)
    def _(i):
        pl.semaphore_signal(barrier, inc=1, device_id=along(i), device_id_type=MESH)

    pl.semaphore_wait(barrier, vocab_size + dp_size - 2)

    def remote(src, dst, send, recv, peer):
        return pltpu.make_async_remote_copy(
            src_ref=src, dst_ref=dst, send_sem=send, recv_sem=recv,
            device_id=peer, device_id_type=MESH)

    def hf_copy(k):
        peer = sibling if k == 0 else (plane, 2 * partner(k) + core)
        return remote(hf_ref, hf_all.at[me], hf_send.at[k], hf_recv.at[me], peer)

    def hf_arrival(k):
        source = 2 * chip + 1 - core if k == 0 else 2 * partner(k) + core
        return remote(hf_ref, hf_all.at[source], hf_send.at[k], hf_recv.at[source], sibling)

    def hf_forward(k):
        source = 2 * partner(k) + core
        return remote(hf_all.at[source], hf_all.at[source], hf_send.at[chips + k],
                      hf_recv.at[source], sibling)

    def hf_forwarded(k):
        source = 2 * partner(k) + 1 - core
        return remote(hf_ref, hf_all.at[source], hf_send.at[k], hf_recv.at[source], sibling)

    def label_copy(j):
        peer = across(j)
        return remote(label_ref, label_all.at[me], label_send.at[peer[1]], label_recv.at[me], peer)

    def label_arrival(j):
        source = across(j)[1]
        return remote(label_ref, label_all.at[source], label_send.at[source],
                      label_recv.at[source], across(j))

    tops[...] = jnp.zeros((pair, 128), jnp.float32)

    for k in range(chips):
        hf_copy(k).start()

    @pl.loop(1, vocab_size)
    def _(j):
        label_copy(j).start()

    hf_all[me] = hf_ref[...]
    label_all[me] = label_ref[...]

    @pl.loop(1, vocab_size)
    def _(j):
        label_arrival(j).wait_recv()

    def count_copy(i):
        peer = along(i)
        return remote(count_all.at[plane], count_all.at[plane], count_send.at[peer[0]],
                      count_recv.at[plane], peer)

    def count_arrival(i):
        source = along(i)[0]
        return remote(count_all.at[plane], count_all.at[source], count_send.at[source],
                      count_recv.at[source], along(i))

    weights = jnp.sum(label_all[:, 1:2, :].astype(jnp.float32), keepdims=True)
    count_all[plane] = jnp.broadcast_to(weights[0], count_all.shape[1:])

    @pl.loop(1, dp_size)
    def _(i):
        count_copy(i).start()

    lanes = lax.broadcasted_iota(jnp.int32, (pair, 128), 1)

    def targets_of(k):
        rows = label_all[pl.ds(2 * partner(k), 2), 0:1, :].astype(jnp.float32)
        columns = [as_columns(rows[i], 128)[:, 0:1] for i in range(2)]
        return jnp.concatenate(columns, axis=0).astype(jnp.int32) - base

    for k in range(chips):
        if k > 0:
            hf_arrival(k).wait_recv()
            hf_forward(k).start()
            hf_forwarded(k).wait_recv()
        else:
            hf_arrival(0).wait_recv()
            if not even:
                whole_copy().wait()
        hidden = hf_all[pl.ds(2 * partner(k), 2)].reshape(pair, width)
        target = targets_of(k)
        place = pl.ds(k * pair, pair)

        def scores_of(j, number, last):
            if k == 0 and even:
                table_copy(j, number).wait()
            rows = pl.ds(pl.multiple_of(j * block, 16), number)
            z = matrix_multiply_transposed_right(hidden, table[rows, :])
            where_to = lax.broadcasted_iota(jnp.int32, (pair, number), 1)
            hit = where_to == target - j * block
            if last:
                valid = where_to < VOCAB_SIZE - base - j * block
                shown = jnp.where(valid, z, 0.0)
                z = jnp.where(valid, z, MASKED)
            else:
                shown = z
            top = jnp.max(z, axis=1, keepdims=True)
            e = jnp.exp(z - top)
            return e, top, jnp.sum(e, axis=1, keepdims=True), jnp.sum(
                shown, axis=1, keepdims=True), jnp.sum(
                jnp.where(hit, shown, 0.0), axis=1, keepdims=True)

        def join(held_stats, new_stats):
            top, total, smooth, goal = held_stats
            new_top, new_total, new_smooth, new_goal = new_stats
            both = jnp.maximum(top, new_top)
            return (both, total * jnp.exp(top - both) + new_total * jnp.exp(new_top - both),
                    smooth + new_smooth, goal + new_goal)

        def one(j, carry):
            e, top, total, smooth, goal = scores_of(j, block, False)
            exps[j, place, :] = e
            tops[...] = jnp.where(lanes == k * (full + 1) + j, top, tops[...])
            return join(carry, (top, total, smooth, goal))

        nothing = jnp.zeros((pair, 1), jnp.float32)
        carry = lax.fori_loop(0, full, one, (nothing + MASKED, nothing, nothing, nothing))
        e, top, total, smooth, goal = scores_of(full, rest, True)
        exps_rest[place, :] = e
        tops[...] = jnp.where(lanes == k * (full + 1) + full, top, tops[...])
        top, total, smooth, goal = join(carry, (top, total, smooth, goal))
        packed = jnp.where(lanes == 0, top, 0.0)
        for i, piece in enumerate((total, smooth, goal)):
            packed = jnp.where(lanes == i + 1, piece, packed)
        stats_all[me, partner(k)] = packed.T[0:8, :]

    def stat_copy(j):
        peer = across(j)
        return remote(stats_all.at[me], stats_all.at[me], stat_send.at[peer[1]],
                      stat_recv.at[me], peer)

    def stat_arrival(j):
        source = across(j)[1]
        return remote(stats_all.at[me], stats_all.at[source], stat_send.at[source],
                      stat_recv.at[source], across(j))

    @pl.loop(1, vocab_size)
    def _(j):
        stat_copy(j).start()

    @pl.loop(1, dp_size)
    def _(i):
        count_arrival(i).wait_recv()

    count = jnp.maximum(jnp.sum(count_all[:, 0:1, 0:1], axis=0), 1.0)

    @pl.loop(1, vocab_size)
    def _(j):
        stat_arrival(j).wait_recv()

    def lse_of(c):
        here = stats_all[:, c]
        tops_here = here[:, 0:1, :]
        top = jnp.max(tops_here, axis=0)
        total = jnp.sum(here[:, 1:2, :] * jnp.exp(tops_here - top[None]), axis=0)
        return top + jnp.log(total), jnp.sum(here[:, 2:3, :], axis=0), jnp.sum(
            here[:, 3:4, :], axis=0)

    def weights_of(c):
        rows = label_all[pl.ds(2 * c, 2), 1:2, :].astype(jnp.float32)
        return jnp.concatenate([rows[0], rows[1]], axis=1)

    loss = jnp.zeros((1, pair), jnp.float32)
    for c in range(chips):
        lse, smooth, goal = lse_of(c)
        loss = loss + weights_of(c) * (lse - 0.9 * goal - 0.1 * smooth / VOCAB_SIZE)
    loss_all[plane] = jnp.broadcast_to(jnp.sum(loss, keepdims=True), loss_all.shape[1:])

    def loss_copy(i):
        peer = along(i)
        return remote(loss_all.at[plane], loss_all.at[plane], loss_send.at[peer[0]],
                      loss_recv.at[plane], peer)

    def loss_arrival(i):
        source = along(i)[0]
        return remote(loss_all.at[plane], loss_all.at[source], loss_send.at[source],
                      loss_recv.at[source], along(i))

    @pl.loop(1, dp_size)
    def _(i):
        loss_copy(i).start()

    rows_each = pair // 2

    def core_copy(k):
        half = pl.ds(pl.multiple_of((1 - core) * rows_each, rows_each), rows_each)
        return remote(acc.at[half], from_core.at[k], core_send.at[k], core_recv.at[k], sibling)

    def chip_copy(k):
        return remote(from_core.at[k], from_chip.at[k - 1], chip_send.at[k], chip_recv.at[k],
                      (plane, 2 * partner(k) + core))

    for k in range(chips - 1, -1, -1):
        c = partner(k)
        lse, _, _ = lse_of(c)
        share = weights_of(c) / count
        columns = as_columns(jnp.concatenate([lse, share], axis=0), pair)
        lse_col, share_col = columns[:, 0:1], columns[:, 1:2]
        target = targets_of(k)
        factors = share_col * jnp.exp(tops[...] - lse_col)
        low = share_col * (0.1 / VOCAB_SIZE)
        high = low + 0.9 * share_col
        place = pl.ds(k * pair, pair)

        def grads_of(j, number, last, e):
            factor = jnp.sum(jnp.where(lanes == k * (full + 1) + j, factors, 0.0), axis=1, keepdims=True)
            where_to = lax.broadcasted_iota(jnp.int32, (pair, number), 1)
            dz = e * factor - jnp.where(where_to == target - j * block, high, low)
            if last:
                dz = jnp.where(where_to < VOCAB_SIZE - base - j * block, dz, 0.0)
            rows = pl.ds(pl.multiple_of(j * block, 16), number)
            return matrix_multiply(dz.astype(jnp.bfloat16), table[rows, :])

        acc[...] = grads_of(full, rest, True, exps_rest[place, :])

        @pl.loop(0, full)
        def _(j):
            acc[...] += grads_of(j, block, False, exps[j, place, :])

        own = pl.multiple_of(core * rows_each, rows_each)
        core_copy(k).start()
        core_copy(k).wait()
        from_core[k] += acc[pl.ds(own, rows_each), :]
        if k > 0:
            chip_copy(k).start()

    total = from_core[0]
    for k in range(1, chips):
        chip_copy(k).wait_recv()
        total = total + from_chip[k - 1]
    grad_out[...] = total

    @pl.loop(1, dp_size)
    def _(i):
        loss_arrival(i).wait_recv()

    loss_out[...] = jnp.sum(loss_all[...], axis=0) / count

    for k in range(chips):
        hf_copy(k).wait_send()
        if k > 0:
            hf_forward(k).wait_send()
            chip_copy(k).wait_send()

    @pl.loop(1, vocab_size)
    def _(j):
        label_copy(j).wait_send()
        stat_copy(j).wait_send()

    @pl.loop(1, dp_size)
    def _(i):
        count_copy(i).wait_send()
        loss_copy(i).wait_send()


def head(mesh_sizes, final_rows, labels, table):
    dp_size, vocab_size = mesh_sizes
    rows, width = final_rows.shape
    held = table.shape[0]
    block = 1024
    full = held // block
    chips = vocab_size // 2
    whole = pl.BlockSpec(memory_space=pltpu.VMEM)
    dma = pltpu.SemaphoreType.DMA
    grad, loss = pl.pallas_call(
        partial(head_step, dp_size, vocab_size, block),
        out_shape=[
            jax.ShapeDtypeStruct((rows, width), jnp.float32),
            jax.ShapeDtypeStruct((8, 128), jnp.float32),
        ],
        in_specs=[whole, whole, pl.BlockSpec(memory_space=pl.ANY)],
        out_specs=[whole, whole],
        scratch_shapes=[
            pltpu.VMEM((held, width), jnp.bfloat16),
            pltpu.VMEM((vocab_size, rows, width), jnp.bfloat16),
            pltpu.VMEM((vocab_size, 8, rows), jnp.int32),
            pltpu.VMEM((full, vocab_size * rows, block), jnp.float32),
            pltpu.VMEM((vocab_size * rows, held - full * block), jnp.float32),
            pltpu.VMEM((2 * rows, 128), jnp.float32),
            pltpu.VMEM((2 * rows, width), jnp.float32),
            pltpu.VMEM((vocab_size, chips, 8, 2 * rows), jnp.float32),
            pltpu.VMEM((dp_size, 8, 128), jnp.float32),
            pltpu.VMEM((dp_size, 8, 128), jnp.float32),
            pltpu.VMEM((chips, rows, width), jnp.float32),
            pltpu.VMEM((chips - 1, rows, width), jnp.float32),
            dma((full + 1,)),
            dma((vocab_size,)),
            dma((vocab_size,)),
            dma((2 * chips,)),
            dma((vocab_size,)),
            dma((dp_size,)),
            dma((dp_size,)),
            dma((vocab_size,)),
            dma((vocab_size,)),
            dma((chips,)),
            dma((chips,)),
            dma((chips,)),
            dma((chips,)),
            dma((dp_size,)),
            dma((dp_size,)),
        ],
        compiler_params=pltpu.CompilerParams(
            collective_id=3, has_side_effects=True, vmem_limit_bytes=62 << 20
        ),
        name="head_step",
    )(final_rows, labels, table)
    return grad, loss[0, 0]


def lane_columns(row):
    return jnp.broadcast_to(row, (128, row.shape[1])).T


def ones_where(condition):
    return jnp.where(condition, 1.0, 0.0)


def low_ones(condition):
    return ones_where(condition).astype(jnp.bfloat16)


def embed_step(dp_size, vocab_size, block, room, token_ref, segment_ref, spot_ref, flag_ref,
               place_hbm, affine_ref, table_hbm,
               h1_out, rows_out, label_out, full_out,
               table, place_table, key_cols, unique_cols, slot_cols, owners, asked, lists, lists_in,
               acc, leaving, arriving, stream, full_all,
               table_sem, place_sem, list_send, list_recv, row_send, row_recv, full_send, full_recv):
    plane = lax.axis_index("dp")
    me = lax.axis_index("vocab")
    chips = vocab_size // 2
    chip = me // 2
    held = table.shape[0]
    full = held // block
    rest = held - full * block
    even = held % 16 == 0
    length = token_ref.shape[1]
    width = table.shape[1]
    spots_here = spot_ref.shape[1]
    chunk = 128
    chunks = length // chunk

    def partner(k):
        out = 0
        bit = 1
        while bit < chips:
            out = out + lax.rem(chip // bit + (k // bit) % 2, 2) * bit
            bit *= 2
        return out

    def across(j):
        return (plane, lax.rem(me + j, vocab_size))

    def along(i):
        return (lax.rem(plane + i, dp_size), me)

    def remote(src, dst, send, recv, peer):
        return pltpu.make_async_remote_copy(
            src_ref=src, dst_ref=dst, send_sem=send, recv_sem=recv,
            device_id=peer, device_id_type=MESH)

    def table_copy(j, number):
        rows = pl.ds(pl.multiple_of(j * block, 16), number)
        return pltpu.make_async_copy(table_hbm.at[rows], table.at[rows], table_sem.at[j])

    def whole_copy():
        return pltpu.make_async_copy(table_hbm, table, table_sem.at[0])

    if even:
        @pl.loop(0, full)
        def _(j):
            table_copy(j, block).start()

        table_copy(full, rest).start()
    else:
        whole_copy().start()

    place_copy = pltpu.make_async_copy(
        place_hbm.at[pl.ds(0, place_table.shape[0])], place_table, place_sem)
    place_copy.start()
    barrier = pltpu.get_barrier_semaphore()

    @pl.loop(1, vocab_size)
    def _(j):
        pl.semaphore_signal(barrier, inc=1, device_id=across(j), device_id_type=MESH)

    @pl.loop(1, dp_size)
    def _(i):
        pl.semaphore_signal(barrier, inc=1, device_id=along(i), device_id_type=MESH)

    token = token_ref[...].astype(jnp.float32)
    segment = segment_ref[...].astype(jnp.float32)
    steps = lax.broadcasted_iota(jnp.int32, (1, length), 1).astype(jnp.float32)
    spot = lane_columns(spot_ref[...].astype(jnp.float32))[:, 0:1]
    flag = lane_columns(flag_ref[...].astype(jnp.float32))[:, 0:1]
    at_spot = steps == spot
    at_next = steps == spot + 1.0

    def picked(where_to, row):
        return jnp.sum(jnp.where(where_to, row, 0.0), axis=1, keepdims=True)

    segment_here = picked(at_spot, segment)
    weight = jnp.where(segment_here == picked(at_next, segment), flag, 0.0)
    target = picked(at_next, token)
    lanes = lax.broadcasted_iota(jnp.int32, (spots_here, 128), 1)
    label_tile = jnp.where(lanes == 0, target, jnp.where(lanes == 1, weight, 0.0))
    label_out[...] = label_tile.T[0:8, :].astype(jnp.int32)
    read = (steps <= spot) & (segment == segment_here) & (weight > 0.0)
    needed = jnp.max(ones_where(read), axis=0, keepdims=True) > 0.0

    key = jnp.where(needed, token, -1.0 - steps)
    key_cols[...] = lane_columns(key)

    def places(a):
        return (lax.broadcasted_iota(jnp.int32, (chunk, 1), 0) + a * chunk).astype(jnp.float32)

    def rows_at(a):
        return pl.ds(pl.multiple_of(a * chunk, chunk), chunk)

    def same(a):
        return key_cols[rows_at(a), 0:1] == key

    def seen(a, carry):
        return jnp.maximum(carry, jnp.max(
            ones_where(same(a) & (places(a) < steps)), axis=0, keepdims=True))

    again = lax.fori_loop(0, chunks, seen, jnp.zeros((1, length), jnp.float32))
    unique = ones_where(needed & (again == 0.0))
    unique_cols[...] = lane_columns(unique)
    owner = jnp.zeros((1, length), jnp.float32)
    for j in range(1, vocab_size):
        owner = owner + ones_where(token >= float(j * held))
    owner_ids = lax.broadcasted_iota(jnp.int32, (vocab_size, length), 0).astype(jnp.float32)
    mine = jnp.where(owner_ids == owner, unique, 0.0)
    owners[...] = mine

    def ahead(a, carry):
        before = low_ones(places(a) < steps)
        return carry + matrix_multiply(owners[:, rows_at(a)].astype(jnp.bfloat16), before)

    ranks = lax.fori_loop(0, chunks, ahead, jnp.zeros((vocab_size, length), jnp.float32))
    rank = jnp.sum(jnp.where(owner_ids == owner, ranks, 0.0), axis=0, keepdims=True)
    too_many = jnp.max(unique * ones_where(rank >= float(room)), axis=1, keepdims=True)
    local_id = token - owner * float(held)
    local_high = jnp.floor(local_id * (1.0 / 128.0))
    local_low = local_id - 128.0 * local_high
    row_ids = lax.broadcasted_iota(jnp.int32, (8, length), 0)

    def stacked(first, second):
        return jnp.where(row_ids == 0, first, jnp.where(row_ids == 1, second, 0.0))

    asked[...] = stacked(owner, jnp.minimum(rank, 127.0))

    def found(a, carry):
        match = low_ones(same(a) & (unique_cols[rows_at(a), 0:1] > 0.0))
        return carry + matrix_multiply(asked[:, rows_at(a)].astype(jnp.bfloat16), match)

    slots = lax.fori_loop(0, chunks, found, jnp.zeros((8, length), jnp.float32))
    slot = jnp.where(needed, slots[0:1, :] * 128.0 + slots[1:2, :], -1.0)
    slot_cols[...] = lane_columns(slot)
    local_parts = stacked(local_high, local_low).astype(jnp.bfloat16)
    rank_ids = lax.broadcasted_iota(jnp.int32, (128, length), 0).astype(jnp.float32)
    list_rows = lax.broadcasted_iota(jnp.int32, (8, 128), 0)

    @pl.loop(0, vocab_size)
    def _(j):
        theirs = (unique > 0.0) & (owner == j.astype(jnp.float32))
        chosen = low_ones(rank_ids == jnp.where(theirs, rank, -1.0))
        ids = matrix_multiply_transposed_right(local_parts, chosen)
        lists[j] = jnp.where(list_rows == 2, too_many, ids)

    @pl.loop(0, vocab_size)
    def _(j):
        arriving[j] = jnp.zeros(arriving.shape[1:], jnp.bfloat16)

    pl.semaphore_wait(barrier, vocab_size + dp_size - 2)

    def list_copy(j):
        peer = across(j)
        return remote(lists.at[peer[1]], lists_in.at[me], list_send.at[peer[1]],
                      list_recv.at[me], peer)

    def list_arrival(j):
        source = across(j)[1]
        return remote(lists.at[source], lists_in.at[source], list_send.at[source],
                      list_recv.at[source], across(j))

    @pl.loop(1, vocab_size)
    def _(j):
        list_copy(j).start()

    lists_in[me] = lists[me]

    ids = lax.broadcasted_iota(jnp.int32, (32, length), 0).astype(jnp.float32)
    starts = jnp.sum(ones_where(segment < ids), axis=1, keepdims=True)
    place = steps - jnp.sum(jnp.where(segment == ids, starts, 0.0), axis=0, keepdims=True)
    place_cols = lane_columns(place)[:, 0:1]
    span = place_table.shape[0]
    place_copy.wait()
    place_ids = lax.broadcasted_iota(jnp.int32, (length, span), 1).astype(jnp.float32)
    stream[...] = matrix_multiply(low_ones(place_ids == place_cols), place_table[...])
    spot_place = picked(at_spot, place)
    spot_slot = picked(at_spot, slot)

    @pl.loop(1, vocab_size)
    def _(j):
        list_arrival(j).wait_recv()

    full_all[plane] = jnp.broadcast_to(
        jnp.max(lists_in[:, 2:3, 0:1], axis=0), full_all.shape[1:])

    def full_copy(i):
        peer = along(i)
        return remote(full_all.at[plane], full_all.at[plane], full_send.at[peer[0]],
                      full_recv.at[plane], peer)

    def full_arrival(i):
        source = along(i)[0]
        return remote(full_all.at[plane], full_all.at[source], full_send.at[source],
                      full_recv.at[source], along(i))

    @pl.loop(1, dp_size)
    def _(i):
        full_copy(i).start()

    def row_copy(d):
        return remote(leaving.at[d], arriving.at[me, pl.ds(0, room)], row_send.at[d],
                      row_recv.at[me], (plane, d))

    def row_arrival(d):
        return remote(leaving.at[d], arriving.at[d, pl.ds(0, room)], row_send.at[d],
                      row_recv.at[d], (plane, d))

    def wanted(d):
        here = lists_in[d]
        return lane_columns(here[0:1, :] * 128.0 + here[1:2, :])[0:room, 0:1]

    first = True
    for k in range(chips - 1, -1, -1):
        c = partner(k)
        wanted_here = jnp.concatenate([wanted(2 * c), wanted(2 * c + 1)], axis=0)

        def rows_of(j, number):
            if first and even:
                table_copy(j, number).wait()
            ids_here = (lax.broadcasted_iota(jnp.int32, (2 * room, number), 1)
                        + j * block).astype(jnp.float32)
            rows = pl.ds(pl.multiple_of(j * block, 16), number)
            return matrix_multiply(low_ones(ids_here == wanted_here), table[rows, :])

        if first and not even:
            whole_copy().wait()
        acc[...] = rows_of(full, rest)

        @pl.loop(0, full)
        def _(j):
            acc[...] += rows_of(j, block)

        first = False
        for i in range(2):
            leaving[2 * c + i] = acc[pl.ds(i * room, room), :].astype(jnp.bfloat16)
        if k > 0:
            for i in range(2):
                row_copy(2 * c + i).start()
        else:
            row_copy(2 * c + 1 - lax.rem(me, 2)).start()
            arriving[me, pl.ds(0, room), :] = leaving[me]

    for k in range(chips):
        c = partner(k)
        if k > 0:
            for i in range(2):
                row_arrival(2 * c + i).wait_recv()
        else:
            row_arrival(2 * c + 1 - lax.rem(me, 2)).wait_recv()
        pair_rows = arriving[pl.ds(2 * c, 2)].reshape(256, width)
        offset = (2 * c * 128).astype(jnp.float32)

        def spread(column, ids_like):
            ids_here = lax.broadcasted_iota(jnp.int32, ids_like, 1).astype(jnp.float32)
            return low_ones(ids_here + offset == column)

        stream[...] += matrix_multiply(spread(slot_cols[:, 0:1], (length, 256)), pair_rows)
        spot_rows = matrix_multiply(spread(spot_slot, (spots_here, 256)), pair_rows)
        if k == 0:
            rows_out[...] = spot_rows
        else:
            rows_out[...] += spot_rows

    spot_ids = lax.broadcasted_iota(jnp.int32, (spots_here, span), 1).astype(jnp.float32)
    rows_out[...] += matrix_multiply(low_ones(spot_ids == spot_place), place_table[...])

    @pl.loop(0, length // 256)
    def _(a):
        rows = pl.ds(pl.multiple_of(a * 256, 256), 256)
        h1_out[rows, :] = layer_norm(
            stream[rows, :], affine_ref[0:1, :], affine_ref[3:4, :]).astype(jnp.bfloat16)

    @pl.loop(1, dp_size)
    def _(i):
        full_arrival(i).wait_recv()

    full_out[...] = jnp.max(full_all[...], axis=0)

    @pl.loop(1, vocab_size)
    def _(j):
        list_copy(j).wait_send()

    @pl.loop(1, dp_size)
    def _(i):
        full_copy(i).wait_send()

    for k in range(chips):
        if k > 0:
            for i in range(2):
                row_copy(2 * partner(k) + i).wait_send()
        else:
            row_copy(2 * chip + 1 - lax.rem(me, 2)).wait_send()


def embed(mesh_sizes, tokens, segments, spots, flags, place_table, affine, table):
    dp_size, vocab_size = mesh_sizes
    length = tokens.shape[1]
    spots_here = spots.shape[1]
    held, width = table.shape
    block = 1024
    full = held // block
    chips = vocab_size // 2
    room = 112 if vocab_size <= 8 else 64
    span = 256
    whole = pl.BlockSpec(memory_space=pltpu.VMEM)
    dma = pltpu.SemaphoreType.DMA
    return pl.pallas_call(
        partial(embed_step, dp_size, vocab_size, block, room),
        out_shape=[
            jax.ShapeDtypeStruct((length, width), jnp.bfloat16),
            jax.ShapeDtypeStruct((spots_here, width), jnp.float32),
            jax.ShapeDtypeStruct((8, spots_here), jnp.int32),
            jax.ShapeDtypeStruct((8, 128), jnp.float32),
        ],
        in_specs=[whole] * 4
        + [pl.BlockSpec(memory_space=pl.ANY), whole, pl.BlockSpec(memory_space=pl.ANY)],
        out_specs=[whole] * 4,
        scratch_shapes=[
            pltpu.VMEM((held, width), jnp.bfloat16),
            pltpu.VMEM((span, width), jnp.bfloat16),
            pltpu.VMEM((length, 128), jnp.float32),
            pltpu.VMEM((length, 128), jnp.float32),
            pltpu.VMEM((length, 128), jnp.float32),
            pltpu.VMEM((vocab_size, length), jnp.float32),
            pltpu.VMEM((8, length), jnp.float32),
            pltpu.VMEM((vocab_size, 8, 128), jnp.float32),
            pltpu.VMEM((vocab_size, 8, 128), jnp.float32),
            pltpu.VMEM((2 * room, width), jnp.float32),
            pltpu.VMEM((vocab_size, room, width), jnp.bfloat16),
            pltpu.VMEM((vocab_size, 128, width), jnp.bfloat16),
            pltpu.VMEM((length, width), jnp.float32),
            pltpu.VMEM((dp_size, 8, 128), jnp.float32),
            dma((full + 1,)),
            dma,
            dma((vocab_size,)),
            dma((vocab_size,)),
            dma((vocab_size,)),
            dma((vocab_size,)),
            dma((dp_size,)),
            dma((dp_size,)),
        ],
        compiler_params=pltpu.CompilerParams(
            collective_id=1, has_side_effects=True, vmem_limit_bytes=60 << 20
        ),
        name="embed_step",
    )(tokens, segments, spots, flags, place_table, affine, table)


def local(
    mesh_sizes,
    packed_symbol_codes,
    article_numbering,
    target_spots,
    answer_flags,
    shared_embedding,
    spot_embedding,
    combined_qkv_weights,
    attend_outgoing_weights,
    dense_incoming_weights,
    dense_outgoing_weights,
    layernorm_affine,
    bias_terms,
    adaptor_float_copies,
    average_moments,
    squared_moments,
):
    tokens_here = packed_symbol_codes[0]
    segments = article_numbering[0]
    spot_objective = target_spots[0]
    rows_here = spot_objective.shape[0]
    shard_rows = shared_embedding.shape[0]
    fast_h1, fast_rows, labels, crowded = embed(
        mesh_sizes,
        packed_symbol_codes,
        article_numbering,
        target_spots,
        answer_flags,
        spot_embedding,
        layernorm_affine,
        shared_embedding,
    )

    def every_row():
        table_base = lax.axis_index("vocab") * shard_rows
        all_tokens = lax.all_gather(packed_symbol_codes, "vocab", axis=0, tiled=True).reshape(-1)
        wanted = all_tokens - table_base
        inside = (wanted >= 0) & (wanted < shard_rows)
        picked = jnp.take(shared_embedding, jnp.clip(wanted, 0, shard_rows - 1), axis=0)
        embedded = lax.psum_scatter(
            jnp.where(inside[:, None], picked.astype(jnp.float32), 0.0).astype(jnp.bfloat16),
            "vocab",
            scatter_dimension=0,
            tiled=True,
        ).astype(jnp.float32)
        stream = embedded + jnp.take(spot_embedding, positions(segments), axis=0).astype(jnp.float32)
        normed = layer_norm(stream, layernorm_affine[0], layernorm_affine[3])
        return normed.astype(jnp.bfloat16), jnp.take(stream, spot_objective, axis=0)

    h1, stream_rows = lax.cond(
        crowded[0, 0] > 0.0, every_row, lambda: (fast_h1, fast_rows)
    )
    (a_qkv, b_qkv, a_o, b_o, a_fc, b_fc, a_p, b_p) = [
        lexicon_portion.astype(jnp.bfloat16)
        for lexicon_portion in distinct_thin_pairs(adaptor_float_copies)
    ]
    length, width = h1.shape
    hidden_width = dense_incoming_weights.shape[1]
    onehot = (spot_objective[:, None] == jnp.arange(length, dtype=jnp.int32)[None, :])
    pick = onehot.astype(jnp.bfloat16)
    h1_rows = select_rows(pick, h1)
    u1 = matrix_multiply(h1, a_qkv).astype(jnp.bfloat16)
    u1_rows = select_rows(pick, u1)
    q = (
        matrix_multiply(h1_rows, combined_qkv_weights[:, :width])
        + bias_terms[:width]
        + ADAPTER_SCALE * matrix_multiply(u1_rows[:, :RANK], b_qkv[0])
    ).astype(jnp.bfloat16)
    kv = (
        matrix_multiply(h1, combined_qkv_weights[:, width:])
        + bias_terms[width : 3 * width]
        + ADAPTER_SCALE
        * matrix_multiply(u1[:, RANK:], block_diagonal_mask(b_qkv[1:]))
    ).astype(jnp.bfloat16)
    queries, keys_all, values_all = split_heads(q), split_heads(kv[:, :width]), split_heads(kv[:, width:])
    scale = queries.shape[2] ** (-0.5)
    there = jnp.arange(length, dtype=jnp.int32)[None, :]
    segment_rows = jnp.take(segments, spot_objective)
    allowed = (there <= spot_objective[:, None]) & (segment_rows[:, None] == segments[None, :])
    scores = (
        jnp.einsum("qhd,khd->hqk", queries, keys_all, preferred_element_type=jnp.float32) * scale
    )
    scores = jnp.where(allowed[None], scores, MASKED)
    top = jnp.max(scores, axis=2, keepdims=True)
    expd = jnp.exp(scores - top)
    probs = expd / jnp.sum(expd, axis=2, keepdims=True)
    probs_low = probs.astype(jnp.bfloat16)
    o = (
        jnp.einsum("hqk,khd->qhd", probs_low, values_all, preferred_element_type=jnp.float32)
        .reshape(rows_here, width)
        .astype(jnp.bfloat16)
    )
    uo = matrix_multiply(o, a_o).astype(jnp.bfloat16)
    middle = (
        stream_rows
        + matrix_multiply(o, attend_outgoing_weights)
        + bias_terms[3 * width : 4 * width]
        + ADAPTER_SCALE * matrix_multiply(uo, b_o)
    )
    h2, norm_two_back = jax.vjp(
        lambda value: layer_norm(value, layernorm_affine[1], layernorm_affine[4]), middle
    )
    h2 = h2.astype(jnp.bfloat16)
    uf = matrix_multiply(h2, a_fc).astype(jnp.bfloat16)
    pre = (
        matrix_multiply(h2, dense_incoming_weights)
        + bias_terms[4 * width : 4 * width + hidden_width]
        + ADAPTER_SCALE * matrix_multiply(uf, b_fc)
    )
    f, gelu_back = jax.vjp(partial(jax.nn.gelu, approximate=True), pre)
    f = f.astype(jnp.bfloat16)
    up = matrix_multiply(f, a_p).astype(jnp.bfloat16)
    output = (
        middle
        + matrix_multiply(f, dense_outgoing_weights)
        + bias_terms[4 * width + hidden_width :]
        + ADAPTER_SCALE * matrix_multiply(up, b_p)
    )
    closing_result, final_back = jax.vjp(
        lambda value: layer_norm(value, layernorm_affine[2], layernorm_affine[5]), output
    )
    final_rows = closing_result.astype(jnp.bfloat16)
    grad_rows, smoothed_entropy_cost = head(mesh_sizes, final_rows, labels, shared_embedding)
    same = spot_objective[:, None] == spot_objective[None, :]
    order = jnp.arange(rows_here, dtype=jnp.int32)
    repeat = jnp.any(same & (order[None, :] < order[:, None]), axis=1)
    merge = (same & ~repeat[:, None]).astype(jnp.float32)
    grad_final = jnp.dot(merge, grad_rows, precision=lax.Precision.HIGHEST)
    (dx3,) = final_back(grad_final)
    dm = dx3.astype(jnp.bfloat16)
    g_bp = ADAPTER_SCALE * matrix_multiply_transposed_left(up, dm)
    du_p = (ADAPTER_SCALE * matrix_multiply_transposed_right(dm, b_p)).astype(jnp.bfloat16)
    g_ap = matrix_multiply_transposed_left(f, du_p)
    df = matrix_multiply_transposed_right(
        dm, dense_outgoing_weights
    ) + matrix_multiply_transposed_right(du_p, a_p)
    (dpre,) = gelu_back(df)
    dpre = dpre.astype(jnp.bfloat16)
    g_bfc = ADAPTER_SCALE * matrix_multiply_transposed_left(uf, dpre)
    du_f = (ADAPTER_SCALE * matrix_multiply_transposed_right(dpre, b_fc)).astype(jnp.bfloat16)
    g_afc = matrix_multiply_transposed_left(h2, du_f)
    dh2 = matrix_multiply_transposed_right(
        dpre, dense_incoming_weights
    ) + matrix_multiply_transposed_right(du_f, a_fc)
    (grad_middle,) = norm_two_back(dh2)
    dx2 = dx3 + grad_middle
    da = dx2.astype(jnp.bfloat16)
    g_bo = ADAPTER_SCALE * matrix_multiply_transposed_left(uo, da)
    du_o = (ADAPTER_SCALE * matrix_multiply_transposed_right(da, b_o)).astype(jnp.bfloat16)
    g_ao = matrix_multiply_transposed_left(o, du_o)
    do = (
        matrix_multiply_transposed_right(da, attend_outgoing_weights)
        + matrix_multiply_transposed_right(du_o, a_o)
    ).astype(jnp.bfloat16)
    do = split_heads(do)
    dv = jnp.einsum("hqk,qhd->khd", probs_low, do, preferred_element_type=jnp.float32)
    dp = jnp.einsum("qhd,khd->hqk", do, values_all, preferred_element_type=jnp.float32)
    ds = (probs * (dp - jnp.sum(probs * dp, axis=2, keepdims=True))).astype(jnp.bfloat16)
    dq = jnp.einsum("hqk,khd->qhd", ds, keys_all, preferred_element_type=jnp.float32) * scale
    dk = jnp.einsum("hqk,qhd->khd", ds, queries, preferred_element_type=jnp.float32) * scale
    dq = dq.reshape(rows_here, width).astype(jnp.bfloat16)
    dk = dk.reshape(length, width).astype(jnp.bfloat16)
    dv = dv.reshape(length, width).astype(jnp.bfloat16)
    thirds = ((h1_rows, u1_rows, dq), (h1, u1, dk), (h1, u1, dv))
    g_bqkv = []
    g_aqkv = []
    for j, (normed, low, grad) in enumerate(thirds):
        low = low[:, j * RANK : (j + 1) * RANK]
        g_bqkv.append(ADAPTER_SCALE * matrix_multiply_transposed_left(low, grad))
        du = (ADAPTER_SCALE * matrix_multiply_transposed_right(grad, b_qkv[j])).astype(
            jnp.bfloat16
        )
        g_aqkv.append(matrix_multiply_transposed_left(normed, du))
    pieces = [
        jnp.concatenate(g_aqkv, axis=1),
        jnp.concatenate(g_bqkv, axis=0),
        g_ao,
        g_bo,
        g_afc,
        g_bfc,
        g_ap,
        g_bp,
    ]
    local_grad = jnp.concatenate([piece.reshape(-1) for piece in pieces])
    (
        refreshed_thin_pairs,
        updated_first_moment,
        updated_second_moment,
        gradient_global_norm,
    ) = reduce_and_update(
        mesh_sizes, local_grad, adaptor_float_copies, average_moments, squared_moments
    )
    return (
        refreshed_thin_pairs,
        updated_first_moment,
        updated_second_moment,
        gradient_global_norm,
        smoothed_entropy_cost,
    )


def solution(mesh):
    return jax.shard_map(
        partial(local, (mesh.shape["dp"], mesh.shape["vocab"])),
        mesh=mesh,
        in_specs=(
            P(("dp", "vocab"), None),
            P(("dp", "vocab"), None),
            P(("dp", "vocab"), None),
            P(("dp", "vocab"), None),
            P("vocab", None),
            P(),
            P(),
            P(),
            P(),
            P(),
            P(),
            P(),
            P(),
            P(),
            P(),
        ),
        out_specs=(P(), P(), P(), P(), P()),
        check_vma=False,
    )
```

```python
from functools import partial
import math

import jax
import jax.numpy as jnp
from jax import lax
from jax.experimental import pallas as pl
from jax.experimental.pallas import tpu as pltpu
from jax.sharding import PartitionSpec as P

MODEL_WIDTH = 1024
HEADS = 16
FEEDFWD_UNITS = 4096
VOCAB_SIZE = 50257
RANK = 4
STEP = 10


ADAPTER_SCALE = 8.0
NORM_EPS = 1e-05
GRAD_CLIP = 0.0001
STRIDE_LENGTH = 0.02
BETA_ONE = 0.9
BETA_TWO = 0.999
SHRINK_PENALTY = 0.01
STABILITY_FLOOR = 1e-08
MASKED = -1e30
MESH = pl.DeviceIdType.MESH


def matrix_multiply(left, right):
    return jnp.dot(left, right, preferred_element_type=jnp.float32)


def matrix_multiply_transposed_left(left, right):
    return lax.dot_general(
        left, right, (((0,), (0,)), ((), ())), preferred_element_type=jnp.float32
    )


def matrix_multiply_transposed_right(left, right):
    return lax.dot_general(
        left, right, (((1,), (1,)), ((), ())), preferred_element_type=jnp.float32
    )


def layer_norm(stream, gain, shift):
    centred = stream - jnp.mean(stream, axis=-1, keepdims=True)
    spread = lax.rsqrt(jnp.mean(centred * centred, axis=-1, keepdims=True) + NORM_EPS)
    return centred * spread * gain + shift


def positions(segments):
    steps_here = jnp.arange(segments.shape[0], dtype=jnp.int32)
    earlier = (segments[None, :] == segments[:, None]) & (steps_here[None, :] < steps_here[:, None])
    return jnp.sum(earlier.astype(jnp.int32), axis=1)


def distinct_thin_pairs(stacked_samples):
    shapes = [
        (MODEL_WIDTH, 3 * RANK),
        (3, RANK, MODEL_WIDTH),
        (MODEL_WIDTH, RANK),
        (RANK, MODEL_WIDTH),
        (MODEL_WIDTH, RANK),
        (RANK, FEEDFWD_UNITS),
        (FEEDFWD_UNITS, RANK),
        (RANK, MODEL_WIDTH),
    ]
    pieces = []
    offset = 0
    for shape in shapes:
        number = math.prod(shape)
        pieces.append(stacked_samples[offset : offset + number].reshape(shape))
        offset += number
    return pieces


def adaptive_moment_update(grad, weight, first, second):
    first_new = BETA_ONE * first + (1.0 - BETA_ONE) * grad
    second_new = BETA_TWO * second + (1.0 - BETA_TWO) * grad * grad
    debiased_mean_estimate = first_new / (1.0 - BETA_ONE**STEP)
    debiased_variance_estimate = second_new / (1.0 - BETA_TWO**STEP)
    weight_new = weight - STRIDE_LENGTH * (
        debiased_mean_estimate / (jnp.sqrt(debiased_variance_estimate) + STABILITY_FLOOR)
        + SHRINK_PENALTY * weight
    )
    return (weight_new, first_new, second_new)


def sum_and_step(dp_size, vocab_size, grad_ref, weight_ref, first_ref, second_ref,
                 weight_out, first_out, second_out, norm_out,
                 parts, planes, total, send_a, recv_a, send_b, recv_b, send_c, recv_c):
    my_plane = lax.axis_index("dp")
    me = lax.axis_index("vocab")

    def across(j):
        return (my_plane, lax.rem(me + j, vocab_size))

    def along(i):
        return (lax.rem(my_plane + i, dp_size), me)

    barrier = pltpu.get_barrier_semaphore()

    @pl.loop(1, vocab_size)
    def _(j):
        pl.semaphore_signal(barrier, inc=1, device_id=across(j), device_id_type=MESH)

    @pl.loop(1, dp_size)
    def _(i):
        pl.semaphore_signal(barrier, inc=1, device_id=along(i), device_id_type=MESH)

    pl.semaphore_wait(barrier, vocab_size + dp_size - 2)

    def part_copy(j):
        peer = across(j)
        return pltpu.make_async_remote_copy(
            src_ref=grad_ref.at[peer[1]], dst_ref=parts.at[me],
            send_sem=send_a.at[peer[1]], recv_sem=recv_a.at[me],
            device_id=peer, device_id_type=MESH)

    def part_arrival(j):
        peer = across(j)
        return pltpu.make_async_remote_copy(
            src_ref=grad_ref.at[peer[1]], dst_ref=parts.at[peer[1]],
            send_sem=send_a.at[peer[1]], recv_sem=recv_a.at[peer[1]],
            device_id=peer, device_id_type=MESH)

    def plane_copy(i):
        peer = along(i)
        return pltpu.make_async_remote_copy(
            src_ref=planes.at[my_plane], dst_ref=planes.at[my_plane],
            send_sem=send_b.at[peer[0]], recv_sem=recv_b.at[my_plane],
            device_id=peer, device_id_type=MESH)

    def plane_arrival(i):
        peer = along(i)
        return pltpu.make_async_remote_copy(
            src_ref=planes.at[my_plane], dst_ref=planes.at[peer[0]],
            send_sem=send_b.at[peer[0]], recv_sem=recv_b.at[peer[0]],
            device_id=peer, device_id_type=MESH)

    def total_copy(j):
        peer = across(j)
        return pltpu.make_async_remote_copy(
            src_ref=total.at[me], dst_ref=total.at[me],
            send_sem=send_c.at[peer[1]], recv_sem=recv_c.at[me],
            device_id=peer, device_id_type=MESH)

    def total_arrival(j):
        peer = across(j)
        return pltpu.make_async_remote_copy(
            src_ref=total.at[me], dst_ref=total.at[peer[1]],
            send_sem=send_c.at[peer[1]], recv_sem=recv_c.at[peer[1]],
            device_id=peer, device_id_type=MESH)

    @pl.loop(1, vocab_size)
    def _(j):
        part_copy(j).start()

    parts[me] = grad_ref[me]

    @pl.loop(1, vocab_size)
    def _(j):
        part_arrival(j).wait_recv()

    planes[my_plane] = lax.fori_loop(
        1, vocab_size, lambda j, held: held + parts[j], parts[0])

    @pl.loop(1, dp_size)
    def _(i):
        plane_copy(i).start()

    @pl.loop(1, dp_size)
    def _(i):
        plane_arrival(i).wait_recv()

    total[me] = lax.fori_loop(1, dp_size, lambda i, held: held + planes[i], planes[0])

    @pl.loop(1, vocab_size)
    def _(j):
        total_copy(j).start()

    @pl.loop(1, vocab_size)
    def _(j):
        part_copy(j).wait_send()

    @pl.loop(1, dp_size)
    def _(i):
        plane_copy(i).wait_send()

    @pl.loop(1, vocab_size)
    def _(j):
        total_arrival(j).wait_recv()

    @pl.loop(1, vocab_size)
    def _(j):
        total_copy(j).wait_send()

    def squares(j, held):
        piece = total[j]
        return held + piece * piece

    gathered = lax.fori_loop(0, vocab_size, squares, jnp.zeros(parts.shape[1:], jnp.float32))
    norm = jnp.sqrt(jnp.sum(gathered, keepdims=True))
    norm_out[...] = jnp.broadcast_to(norm, norm_out.shape)
    shrink = GRAD_CLIP / jnp.maximum(norm, GRAD_CLIP)

    @pl.loop(0, vocab_size)
    def _(j):
        weight, first, second = adaptive_moment_update(
            total[j] * shrink, weight_ref[j], first_ref[j], second_ref[j])
        weight_out[j] = weight
        first_out[j] = first
        second_out[j] = second


def reduce_and_update(mesh_sizes, local_grad, weights, first, second):
    dp_size, vocab_size = mesh_sizes
    number = local_grad.shape[0]
    rows = number // (128 * vocab_size)
    shape = (vocab_size, rows, 128)
    block = pltpu.VMEM(shape, jnp.float32)
    whole = pl.BlockSpec(memory_space=pltpu.VMEM)
    weight_new, first_new, second_new, norm = pl.pallas_call(
        partial(sum_and_step, dp_size, vocab_size),
        out_shape=[jax.ShapeDtypeStruct(shape, jnp.float32)] * 3
        + [jax.ShapeDtypeStruct((8, 128), jnp.float32)],
        in_specs=[whole] * 4,
        out_specs=[whole] * 4,
        scratch_shapes=[
            block,
            pltpu.VMEM((dp_size, rows, 128), jnp.float32),
            block,
            pltpu.SemaphoreType.DMA((vocab_size,)),
            pltpu.SemaphoreType.DMA((vocab_size,)),
            pltpu.SemaphoreType.DMA((dp_size,)),
            pltpu.SemaphoreType.DMA((dp_size,)),
            pltpu.SemaphoreType.DMA((vocab_size,)),
            pltpu.SemaphoreType.DMA((vocab_size,)),
        ],
        compiler_params=pltpu.CompilerParams(
            collective_id=5, has_side_effects=True, vmem_limit_bytes=24 << 20
        ),
        name="sum_and_step",
    )(*[piece.reshape(shape) for piece in (local_grad, weights, first, second)])
    flat = [piece.reshape(-1) for piece in (weight_new, first_new, second_new)]
    return (*flat, norm[0, 0])


def as_columns(rows, height):
    lanes = rows.shape[1]
    padded = jnp.concatenate([rows, jnp.zeros((128 - rows.shape[0], lanes), rows.dtype)], axis=0)
    return padded.T


def head_step(dp_size, vocab_size, block, hf_ref, label_ref, table_hbm, grad_out, loss_out,
              table, hf_all, label_all, exps, exps_rest, tops, acc, stats_all, count_all, loss_all,
              from_core, from_chip,
              table_sem, label_send, label_recv, hf_send, hf_recv, count_send, count_recv,
              stat_send, stat_recv, core_send, core_recv, chip_send, chip_recv, loss_send, loss_recv):
    plane = lax.axis_index("dp")
    me = lax.axis_index("vocab")
    chips = vocab_size // 2
    chip = me // 2
    core = lax.rem(me, 2)
    sibling = (plane, 2 * chip + 1 - core)
    held = table.shape[0]
    full = held // block
    rest = held - full * block
    base = me * held
    pair = 2 * hf_ref.shape[0]
    width = hf_ref.shape[1]

    def partner(k):
        out = 0
        bit = 1
        while bit < chips:
            out = out + lax.rem(chip // bit + (k // bit) % 2, 2) * bit
            bit *= 2
        return out

    def across(j):
        return (plane, lax.rem(me + j, vocab_size))

    def along(i):
        return (lax.rem(plane + i, dp_size), me)

    even = held % 16 == 0

    def table_copy(j, number):
        rows = pl.ds(pl.multiple_of(j * block, 16), number)
        return pltpu.make_async_copy(table_hbm.at[rows], table.at[rows], table_sem.at[j])

    def whole_copy():
        return pltpu.make_async_copy(table_hbm, table, table_sem.at[0])

    if even:
        @pl.loop(0, full)
        def _(j):
            table_copy(j, block).start()

        table_copy(full, rest).start()
    else:
        whole_copy().start()

    barrier = pltpu.get_barrier_semaphore()

    @pl.loop(1, vocab_size)
    def _(j):
        pl.semaphore_signal(barrier, inc=1, device_id=across(j), device_id_type=MESH)

    @pl.loop(1, dp_size)
    def _(i):
        pl.semaphore_signal(barrier, inc=1, device_id=along(i), device_id_type=MESH)

    pl.semaphore_wait(barrier, vocab_size + dp_size - 2)

    def remote(src, dst, send, recv, peer):
        return pltpu.make_async_remote_copy(
            src_ref=src, dst_ref=dst, send_sem=send, recv_sem=recv,
            device_id=peer, device_id_type=MESH)

    def hf_copy(k):
        peer = sibling if k == 0 else (plane, 2 * partner(k) + core)
        return remote(hf_ref, hf_all.at[me], hf_send.at[k], hf_recv.at[me], peer)

    def hf_arrival(k):
        source = 2 * chip + 1 - core if k == 0 else 2 * partner(k) + core
        return remote(hf_ref, hf_all.at[source], hf_send.at[k], hf_recv.at[source], sibling)

    def hf_forward(k):
        source = 2 * partner(k) + core
        return remote(hf_all.at[source], hf_all.at[source], hf_send.at[chips + k],
                      hf_recv.at[source], sibling)

    def hf_forwarded(k):
        source = 2 * partner(k) + 1 - core
        return remote(hf_ref, hf_all.at[source], hf_send.at[k], hf_recv.at[source], sibling)

    def label_copy(j):
        peer = across(j)
        return remote(label_ref, label_all.at[me], label_send.at[peer[1]], label_recv.at[me], peer)

    def label_arrival(j):
        source = across(j)[1]
        return remote(label_ref, label_all.at[source], label_send.at[source],
                      label_recv.at[source], across(j))

    tops[...] = jnp.zeros((pair, 128), jnp.float32)

    for k in range(chips):
        hf_copy(k).start()

    @pl.loop(1, vocab_size)
    def _(j):
        label_copy(j).start()

    hf_all[me] = hf_ref[...]
    label_all[me] = label_ref[...]

    @pl.loop(1, vocab_size)
    def _(j):
        label_arrival(j).wait_recv()

    def count_copy(i):
        peer = along(i)
        return remote(count_all.at[plane], count_all.at[plane], count_send.at[peer[0]],
                      count_recv.at[plane], peer)

    def count_arrival(i):
        source = along(i)[0]
        return remote(count_all.at[plane], count_all.at[source], count_send.at[source],
                      count_recv.at[source], along(i))

    weights = jnp.sum(label_all[:, 1:2, :].astype(jnp.float32), keepdims=True)
    count_all[plane] = jnp.broadcast_to(weights[0], count_all.shape[1:])

    @pl.loop(1, dp_size)
    def _(i):
        count_copy(i).start()

    lanes = lax.broadcasted_iota(jnp.int32, (pair, 128), 1)

    def targets_of(k):
        rows = label_all[pl.ds(2 * partner(k), 2), 0:1, :].astype(jnp.float32)
        columns = [as_columns(rows[i], 128)[:, 0:1] for i in range(2)]
        return jnp.concatenate(columns, axis=0).astype(jnp.int32) - base

    for k in range(chips):
        if k > 0:
            hf_arrival(k).wait_recv()
            hf_forward(k).start()
            hf_forwarded(k).wait_recv()
        else:
            hf_arrival(0).wait_recv()
            if not even:
                whole_copy().wait()
        hidden = hf_all[pl.ds(2 * partner(k), 2)].reshape(pair, width)
        target = targets_of(k)
        place = pl.ds(k * pair, pair)

        def scores_of(j, number, last):
            if k == 0 and even:
                table_copy(j, number).wait()
            rows = pl.ds(pl.multiple_of(j * block, 16), number)
            z = matrix_multiply_transposed_right(hidden, table[rows, :])
            where_to = lax.broadcasted_iota(jnp.int32, (pair, number), 1)
            hit = where_to == target - j * block
            if last:
                valid = where_to < VOCAB_SIZE - base - j * block
                shown = jnp.where(valid, z, 0.0)
                z = jnp.where(valid, z, MASKED)
            else:
                shown = z
            top = jnp.max(z, axis=1, keepdims=True)
            e = jnp.exp(z - top)
            return e, top, jnp.sum(e, axis=1, keepdims=True), jnp.sum(
                shown, axis=1, keepdims=True), jnp.sum(
                jnp.where(hit, shown, 0.0), axis=1, keepdims=True)

        def join(held_stats, new_stats):
            top, total, smooth, goal = held_stats
            new_top, new_total, new_smooth, new_goal = new_stats
            both = jnp.maximum(top, new_top)
            return (both, total * jnp.exp(top - both) + new_total * jnp.exp(new_top - both),
                    smooth + new_smooth, goal + new_goal)

        def one(j, carry):
            e, top, total, smooth, goal = scores_of(j, block, False)
            exps[j, place, :] = e
            tops[...] = jnp.where(lanes == k * (full + 1) + j, top, tops[...])
            return join(carry, (top, total, smooth, goal))

        nothing = jnp.zeros((pair, 1), jnp.float32)
        carry = lax.fori_loop(0, full, one, (nothing + MASKED, nothing, nothing, nothing))
        e, top, total, smooth, goal = scores_of(full, rest, True)
        exps_rest[place, :] = e
        tops[...] = jnp.where(lanes == k * (full + 1) + full, top, tops[...])
        top, total, smooth, goal = join(carry, (top, total, smooth, goal))
        packed = jnp.where(lanes == 0, top, 0.0)
        for i, piece in enumerate((total, smooth, goal)):
            packed = jnp.where(lanes == i + 1, piece, packed)
        stats_all[me, partner(k)] = packed.T[0:8, :]

    def stat_copy(j):
        peer = across(j)
        return remote(stats_all.at[me], stats_all.at[me], stat_send.at[peer[1]],
                      stat_recv.at[me], peer)

    def stat_arrival(j):
        source = across(j)[1]
        return remote(stats_all.at[me], stats_all.at[source], stat_send.at[source],
                      stat_recv.at[source], across(j))

    @pl.loop(1, vocab_size)
    def _(j):
        stat_copy(j).start()

    @pl.loop(1, dp_size)
    def _(i):
        count_arrival(i).wait_recv()

    count = jnp.maximum(jnp.sum(count_all[:, 0:1, 0:1], axis=0), 1.0)

    @pl.loop(1, vocab_size)
    def _(j):
        stat_arrival(j).wait_recv()

    def lse_of(c):
        here = stats_all[:, c]
        tops_here = here[:, 0:1, :]
        top = jnp.max(tops_here, axis=0)
        total = jnp.sum(here[:, 1:2, :] * jnp.exp(tops_here - top[None]), axis=0)
        return top + jnp.log(total), jnp.sum(here[:, 2:3, :], axis=0), jnp.sum(
            here[:, 3:4, :], axis=0)

    def weights_of(c):
        rows = label_all[pl.ds(2 * c, 2), 1:2, :].astype(jnp.float32)
        return jnp.concatenate([rows[0], rows[1]], axis=1)

    loss = jnp.zeros((1, pair), jnp.float32)
    for c in range(chips):
        lse, smooth, goal = lse_of(c)
        loss = loss + weights_of(c) * (lse - 0.9 * goal - 0.1 * smooth / VOCAB_SIZE)
    loss_all[plane] = jnp.broadcast_to(jnp.sum(loss, keepdims=True), loss_all.shape[1:])

    def loss_copy(i):
        peer = along(i)
        return remote(loss_all.at[plane], loss_all.at[plane], loss_send.at[peer[0]],
                      loss_recv.at[plane], peer)

    def loss_arrival(i):
        source = along(i)[0]
        return remote(loss_all.at[plane], loss_all.at[source], loss_send.at[source],
                      loss_recv.at[source], along(i))

    @pl.loop(1, dp_size)
    def _(i):
        loss_copy(i).start()

    rows_each = pair // 2

    def core_copy(k):
        half = pl.ds(pl.multiple_of((1 - core) * rows_each, rows_each), rows_each)
        return remote(acc.at[half], from_core.at[k], core_send.at[k], core_recv.at[k], sibling)

    def chip_copy(k):
        return remote(from_core.at[k], from_chip.at[k - 1], chip_send.at[k], chip_recv.at[k],
                      (plane, 2 * partner(k) + core))

    for k in range(chips - 1, -1, -1):
        c = partner(k)
        lse, _, _ = lse_of(c)
        share = weights_of(c) / count
        columns = as_columns(jnp.concatenate([lse, share], axis=0), pair)
        lse_col, share_col = columns[:, 0:1], columns[:, 1:2]
        target = targets_of(k)
        factors = share_col * jnp.exp(tops[...] - lse_col)
        low = share_col * (0.1 / VOCAB_SIZE)
        high = low + 0.9 * share_col
        place = pl.ds(k * pair, pair)

        def grads_of(j, number, last, e):
            factor = jnp.sum(jnp.where(lanes == k * (full + 1) + j, factors, 0.0), axis=1, keepdims=True)
            where_to = lax.broadcasted_iota(jnp.int32, (pair, number), 1)
            dz = e * factor - jnp.where(where_to == target - j * block, high, low)
            if last:
                dz = jnp.where(where_to < VOCAB_SIZE - base - j * block, dz, 0.0)
            rows = pl.ds(pl.multiple_of(j * block, 16), number)
            return matrix_multiply(dz.astype(jnp.bfloat16), table[rows, :])

        acc[...] = grads_of(full, rest, True, exps_rest[place, :])

        @pl.loop(0, full)
        def _(j):
            acc[...] += grads_of(j, block, False, exps[j, place, :])

        own = pl.multiple_of(core * rows_each, rows_each)
        core_copy(k).start()
        core_copy(k).wait()
        from_core[k] += acc[pl.ds(own, rows_each), :]
        if k > 0:
            chip_copy(k).start()

    total = from_core[0]
    for k in range(1, chips):
        chip_copy(k).wait_recv()
        total = total + from_chip[k - 1]
    grad_out[...] = total

    @pl.loop(1, dp_size)
    def _(i):
        loss_arrival(i).wait_recv()

    loss_out[...] = jnp.sum(loss_all[...], axis=0) / count

    for k in range(chips):
        hf_copy(k).wait_send()
        if k > 0:
            hf_forward(k).wait_send()
            chip_copy(k).wait_send()

    @pl.loop(1, vocab_size)
    def _(j):
        label_copy(j).wait_send()
        stat_copy(j).wait_send()

    @pl.loop(1, dp_size)
    def _(i):
        count_copy(i).wait_send()
        loss_copy(i).wait_send()


def head(mesh_sizes, final_rows, labels, table):
    dp_size, vocab_size = mesh_sizes
    rows, width = final_rows.shape
    held = table.shape[0]
    block = 1024
    full = held // block
    chips = vocab_size // 2
    whole = pl.BlockSpec(memory_space=pltpu.VMEM)
    dma = pltpu.SemaphoreType.DMA
    grad, loss = pl.pallas_call(
        partial(head_step, dp_size, vocab_size, block),
        out_shape=[
            jax.ShapeDtypeStruct((rows, width), jnp.float32),
            jax.ShapeDtypeStruct((8, 128), jnp.float32),
        ],
        in_specs=[whole, whole, pl.BlockSpec(memory_space=pl.ANY)],
        out_specs=[whole, whole],
        scratch_shapes=[
            pltpu.VMEM((held, width), jnp.bfloat16),
            pltpu.VMEM((vocab_size, rows, width), jnp.bfloat16),
            pltpu.VMEM((vocab_size, 8, rows), jnp.int32),
            pltpu.VMEM((full, vocab_size * rows, block), jnp.float32),
            pltpu.VMEM((vocab_size * rows, held - full * block), jnp.float32),
            pltpu.VMEM((2 * rows, 128), jnp.float32),
            pltpu.VMEM((2 * rows, width), jnp.float32),
            pltpu.VMEM((vocab_size, chips, 8, 2 * rows), jnp.float32),
            pltpu.VMEM((dp_size, 8, 128), jnp.float32),
            pltpu.VMEM((dp_size, 8, 128), jnp.float32),
            pltpu.VMEM((chips, rows, width), jnp.float32),
            pltpu.VMEM((chips - 1, rows, width), jnp.float32),
            dma((full + 1,)),
            dma((vocab_size,)),
            dma((vocab_size,)),
            dma((2 * chips,)),
            dma((vocab_size,)),
            dma((dp_size,)),
            dma((dp_size,)),
            dma((vocab_size,)),
            dma((vocab_size,)),
            dma((chips,)),
            dma((chips,)),
            dma((chips,)),
            dma((chips,)),
            dma((dp_size,)),
            dma((dp_size,)),
        ],
        compiler_params=pltpu.CompilerParams(
            collective_id=3, has_side_effects=True, vmem_limit_bytes=62 << 20
        ),
        name="head_step",
    )(final_rows, labels, table)
    return grad, loss[0, 0]


def lane_columns(row):
    return jnp.broadcast_to(row, (128, row.shape[1])).T


def ones_where(condition):
    return jnp.where(condition, 1.0, 0.0)


def low_ones(condition):
    return ones_where(condition).astype(jnp.bfloat16)


def embed_step(dp_size, vocab_size, block, room, token_ref, segment_ref, spot_ref, flag_ref,
               place_hbm, affine_ref, table_hbm,
               h1_out, rows_out, label_out, full_out,
               table, place_table, key_cols, unique_cols, slot_cols, owners, asked, lists, lists_in,
               acc, leaving, arriving, stream, full_all,
               table_sem, place_sem, list_send, list_recv, row_send, row_recv, full_send, full_recv):
    plane = lax.axis_index("dp")
    me = lax.axis_index("vocab")
    chips = vocab_size // 2
    chip = me // 2
    held = table.shape[0]
    full = held // block
    rest = held - full * block
    even = held % 16 == 0
    length = token_ref.shape[1]
    width = table.shape[1]
    spots_here = spot_ref.shape[1]
    chunk = 128
    chunks = length // chunk

    def partner(k):
        out = 0
        bit = 1
        while bit < chips:
            out = out + lax.rem(chip // bit + (k // bit) % 2, 2) * bit
            bit *= 2
        return out

    def across(j):
        return (plane, lax.rem(me + j, vocab_size))

    def along(i):
        return (lax.rem(plane + i, dp_size), me)

    def remote(src, dst, send, recv, peer):
        return pltpu.make_async_remote_copy(
            src_ref=src, dst_ref=dst, send_sem=send, recv_sem=recv,
            device_id=peer, device_id_type=MESH)

    def table_copy(j, number):
        rows = pl.ds(pl.multiple_of(j * block, 16), number)
        return pltpu.make_async_copy(table_hbm.at[rows], table.at[rows], table_sem.at[j])

    def whole_copy():
        return pltpu.make_async_copy(table_hbm, table, table_sem.at[0])

    if even:
        @pl.loop(0, full)
        def _(j):
            table_copy(j, block).start()

        table_copy(full, rest).start()
    else:
        whole_copy().start()

    place_copy = pltpu.make_async_copy(
        place_hbm.at[pl.ds(0, place_table.shape[0])], place_table, place_sem)
    place_copy.start()
    barrier = pltpu.get_barrier_semaphore()

    @pl.loop(1, vocab_size)
    def _(j):
        pl.semaphore_signal(barrier, inc=1, device_id=across(j), device_id_type=MESH)

    @pl.loop(1, dp_size)
    def _(i):
        pl.semaphore_signal(barrier, inc=1, device_id=along(i), device_id_type=MESH)

    token = token_ref[...].astype(jnp.float32)
    segment = segment_ref[...].astype(jnp.float32)
    steps = lax.broadcasted_iota(jnp.int32, (1, length), 1).astype(jnp.float32)
    spot = lane_columns(spot_ref[...].astype(jnp.float32))[:, 0:1]
    flag = lane_columns(flag_ref[...].astype(jnp.float32))[:, 0:1]
    at_spot = steps == spot
    at_next = steps == spot + 1.0

    def picked(where_to, row):
        return jnp.sum(jnp.where(where_to, row, 0.0), axis=1, keepdims=True)

    segment_here = picked(at_spot, segment)
    weight = jnp.where(segment_here == picked(at_next, segment), flag, 0.0)
    target = picked(at_next, token)
    lanes = lax.broadcasted_iota(jnp.int32, (spots_here, 128), 1)
    label_tile = jnp.where(lanes == 0, target, jnp.where(lanes == 1, weight, 0.0))
    label_out[...] = label_tile.T[0:8, :].astype(jnp.int32)
    read = (steps <= spot) & (segment == segment_here) & (weight > 0.0)
    needed = jnp.max(ones_where(read), axis=0, keepdims=True) > 0.0

    key = jnp.where(needed, token, -1.0 - steps)
    key_cols[...] = lane_columns(key)

    def places(a):
        return (lax.broadcasted_iota(jnp.int32, (chunk, 1), 0) + a * chunk).astype(jnp.float32)

    def rows_at(a):
        return pl.ds(pl.multiple_of(a * chunk, chunk), chunk)

    def same(a):
        return key_cols[rows_at(a), 0:1] == key

    def seen(a, carry):
        return jnp.maximum(carry, jnp.max(
            ones_where(same(a) & (places(a) < steps)), axis=0, keepdims=True))

    again = lax.fori_loop(0, chunks, seen, jnp.zeros((1, length), jnp.float32))
    unique = ones_where(needed & (again == 0.0))
    unique_cols[...] = lane_columns(unique)
    owner = jnp.zeros((1, length), jnp.float32)
    for j in range(1, vocab_size):
        owner = owner + ones_where(token >= float(j * held))
    owner_ids = lax.broadcasted_iota(jnp.int32, (vocab_size, length), 0).astype(jnp.float32)
    mine = jnp.where(owner_ids == owner, unique, 0.0)
    owners[...] = mine

    def ahead(a, carry):
        before = low_ones(places(a) < steps)
        return carry + matrix_multiply(owners[:, rows_at(a)].astype(jnp.bfloat16), before)

    ranks = lax.fori_loop(0, chunks, ahead, jnp.zeros((vocab_size, length), jnp.float32))
    rank = jnp.sum(jnp.where(owner_ids == owner, ranks, 0.0), axis=0, keepdims=True)
    too_many = jnp.max(unique * ones_where(rank >= float(room)), axis=1, keepdims=True)
    local_id = token - owner * float(held)
    local_high = jnp.floor(local_id * (1.0 / 128.0))
    local_low = local_id - 128.0 * local_high
    row_ids = lax.broadcasted_iota(jnp.int32, (8, length), 0)

    def stacked(first, second):
        return jnp.where(row_ids == 0, first, jnp.where(row_ids == 1, second, 0.0))

    asked[...] = stacked(owner, jnp.minimum(rank, 127.0))

    def found(a, carry):
        match = low_ones(same(a) & (unique_cols[rows_at(a), 0:1] > 0.0))
        return carry + matrix_multiply(asked[:, rows_at(a)].astype(jnp.bfloat16), match)

    slots = lax.fori_loop(0, chunks, found, jnp.zeros((8, length), jnp.float32))
    slot = jnp.where(needed, slots[0:1, :] * 128.0 + slots[1:2, :], -1.0)
    slot_cols[...] = lane_columns(slot)
    local_parts = stacked(local_high, local_low).astype(jnp.bfloat16)
    rank_ids = lax.broadcasted_iota(jnp.int32, (128, length), 0).astype(jnp.float32)
    list_rows = lax.broadcasted_iota(jnp.int32, (8, 128), 0)

    @pl.loop(0, vocab_size)
    def _(j):
        theirs = (unique > 0.0) & (owner == j.astype(jnp.float32))
        chosen = low_ones(rank_ids == jnp.where(theirs, rank, -1.0))
        ids = matrix_multiply_transposed_right(local_parts, chosen)
        lists[j] = jnp.where(list_rows == 2, too_many, ids)

    @pl.loop(0, vocab_size)
    def _(j):
        arriving[j] = jnp.zeros(arriving.shape[1:], jnp.bfloat16)

    pl.semaphore_wait(barrier, vocab_size + dp_size - 2)

    def list_copy(j):
        peer = across(j)
        return remote(lists.at[peer[1]], lists_in.at[me], list_send.at[peer[1]],
                      list_recv.at[me], peer)

    def list_arrival(j):
        source = across(j)[1]
        return remote(lists.at[source], lists_in.at[source], list_send.at[source],
                      list_recv.at[source], across(j))

    @pl.loop(1, vocab_size)
    def _(j):
        list_copy(j).start()

    lists_in[me] = lists[me]

    ids = lax.broadcasted_iota(jnp.int32, (32, length), 0).astype(jnp.float32)
    starts = jnp.sum(ones_where(segment < ids), axis=1, keepdims=True)
    place = steps - jnp.sum(jnp.where(segment == ids, starts, 0.0), axis=0, keepdims=True)
    place_cols = lane_columns(place)[:, 0:1]
    span = place_table.shape[0]
    place_copy.wait()
    place_ids = lax.broadcasted_iota(jnp.int32, (length, span), 1).astype(jnp.float32)
    stream[...] = matrix_multiply(low_ones(place_ids == place_cols), place_table[...])
    spot_place = picked(at_spot, place)
    spot_slot = picked(at_spot, slot)

    @pl.loop(1, vocab_size)
    def _(j):
        list_arrival(j).wait_recv()

    full_all[plane] = jnp.broadcast_to(
        jnp.max(lists_in[:, 2:3, 0:1], axis=0), full_all.shape[1:])

    def full_copy(i):
        peer = along(i)
        return remote(full_all.at[plane], full_all.at[plane], full_send.at[peer[0]],
                      full_recv.at[plane], peer)

    def full_arrival(i):
        source = along(i)[0]
        return remote(full_all.at[plane], full_all.at[source], full_send.at[source],
                      full_recv.at[source], along(i))

    @pl.loop(1, dp_size)
    def _(i):
        full_copy(i).start()

    def row_copy(d):
        return remote(leaving.at[d], arriving.at[me, pl.ds(0, room)], row_send.at[d],
                      row_recv.at[me], (plane, d))

    def row_arrival(d):
        return remote(leaving.at[d], arriving.at[d, pl.ds(0, room)], row_send.at[d],
                      row_recv.at[d], (plane, d))

    def wanted(d):
        here = lists_in[d]
        return lane_columns(here[0:1, :] * 128.0 + here[1:2, :])[0:room, 0:1]

    first = True
    for k in range(chips - 1, -1, -1):
        c = partner(k)
        wanted_here = jnp.concatenate([wanted(2 * c), wanted(2 * c + 1)], axis=0)

        def rows_of(j, number):
            if first and even:
                table_copy(j, number).wait()
            ids_here = (lax.broadcasted_iota(jnp.int32, (2 * room, number), 1)
                        + j * block).astype(jnp.float32)
            rows = pl.ds(pl.multiple_of(j * block, 16), number)
            return matrix_multiply(low_ones(ids_here == wanted_here), table[rows, :])

        if first and not even:
            whole_copy().wait()
        acc[...] = rows_of(full, rest)

        @pl.loop(0, full)
        def _(j):
            acc[...] += rows_of(j, block)

        first = False
        for i in range(2):
            leaving[2 * c + i] = acc[pl.ds(i * room, room), :].astype(jnp.bfloat16)
        if k > 0:
            for i in range(2):
                row_copy(2 * c + i).start()
        else:
            row_copy(2 * c + 1 - lax.rem(me, 2)).start()
            arriving[me, pl.ds(0, room), :] = leaving[me]

    for k in range(chips):
        c = partner(k)
        if k > 0:
            for i in range(2):
                row_arrival(2 * c + i).wait_recv()
        else:
            row_arrival(2 * c + 1 - lax.rem(me, 2)).wait_recv()
        pair_rows = arriving[pl.ds(2 * c, 2)].reshape(256, width)
        offset = (2 * c * 128).astype(jnp.float32)

        def spread(column, ids_like):
            ids_here = lax.broadcasted_iota(jnp.int32, ids_like, 1).astype(jnp.float32)
            return low_ones(ids_here + offset == column)

        stream[...] += matrix_multiply(spread(slot_cols[:, 0:1], (length, 256)), pair_rows)
        spot_rows = matrix_multiply(spread(spot_slot, (spots_here, 256)), pair_rows)
        if k == 0:
            rows_out[...] = spot_rows
        else:
            rows_out[...] += spot_rows

    spot_ids = lax.broadcasted_iota(jnp.int32, (spots_here, span), 1).astype(jnp.float32)
    rows_out[...] += matrix_multiply(low_ones(spot_ids == spot_place), place_table[...])

    @pl.loop(0, length // 256)
    def _(a):
        rows = pl.ds(pl.multiple_of(a * 256, 256), 256)
        h1_out[rows, :] = layer_norm(
            stream[rows, :], affine_ref[0:1, :], affine_ref[3:4, :]).astype(jnp.bfloat16)

    @pl.loop(1, dp_size)
    def _(i):
        full_arrival(i).wait_recv()

    full_out[...] = jnp.max(full_all[...], axis=0)

    @pl.loop(1, vocab_size)
    def _(j):
        list_copy(j).wait_send()

    @pl.loop(1, dp_size)
    def _(i):
        full_copy(i).wait_send()

    for k in range(chips):
        if k > 0:
            for i in range(2):
                row_copy(2 * partner(k) + i).wait_send()
        else:
            row_copy(2 * chip + 1 - lax.rem(me, 2)).wait_send()


def embed(mesh_sizes, tokens, segments, spots, flags, place_table, affine, table):
    dp_size, vocab_size = mesh_sizes
    length = tokens.shape[1]
    spots_here = spots.shape[1]
    held, width = table.shape
    block = 1024
    full = held // block
    chips = vocab_size // 2
    room = 112 if vocab_size <= 8 else 64
    span = 256
    whole = pl.BlockSpec(memory_space=pltpu.VMEM)
    dma = pltpu.SemaphoreType.DMA
    return pl.pallas_call(
        partial(embed_step, dp_size, vocab_size, block, room),
        out_shape=[
            jax.ShapeDtypeStruct((length, width), jnp.bfloat16),
            jax.ShapeDtypeStruct((spots_here, width), jnp.float32),
            jax.ShapeDtypeStruct((8, spots_here), jnp.int32),
            jax.ShapeDtypeStruct((8, 128), jnp.float32),
        ],
        in_specs=[whole] * 4
        + [pl.BlockSpec(memory_space=pl.ANY), whole, pl.BlockSpec(memory_space=pl.ANY)],
        out_specs=[whole] * 4,
        scratch_shapes=[
            pltpu.VMEM((held, width), jnp.bfloat16),
            pltpu.VMEM((span, width), jnp.bfloat16),
            pltpu.VMEM((length, 128), jnp.float32),
            pltpu.VMEM((length, 128), jnp.float32),
            pltpu.VMEM((length, 128), jnp.float32),
            pltpu.VMEM((vocab_size, length), jnp.float32),
            pltpu.VMEM((8, length), jnp.float32),
            pltpu.VMEM((vocab_size, 8, 128), jnp.float32),
            pltpu.VMEM((vocab_size, 8, 128), jnp.float32),
            pltpu.VMEM((2 * room, width), jnp.float32),
            pltpu.VMEM((vocab_size, room, width), jnp.bfloat16),
            pltpu.VMEM((vocab_size, 128, width), jnp.bfloat16),
            pltpu.VMEM((length, width), jnp.float32),
            pltpu.VMEM((dp_size, 8, 128), jnp.float32),
            dma((full + 1,)),
            dma,
            dma((vocab_size,)),
            dma((vocab_size,)),
            dma((vocab_size,)),
            dma((vocab_size,)),
            dma((dp_size,)),
            dma((dp_size,)),
        ],
        compiler_params=pltpu.CompilerParams(
            collective_id=1, has_side_effects=True, vmem_limit_bytes=60 << 20
        ),
        name="embed_step",
    )(tokens, segments, spots, flags, place_table, affine, table)


NARROW = 16


def wide_loop(number, body):
    lax.fori_loop(0, number, lambda i, carry: (body(i), carry)[1], 0)


def norm_parts(rows):
    centred = rows - jnp.mean(rows, axis=-1, keepdims=True)
    return centred, lax.rsqrt(jnp.mean(centred * centred, axis=-1, keepdims=True) + NORM_EPS)


def norm_back(rows, gain, grad):
    centred, spread = norm_parts(rows)
    hat = centred * spread
    grad_hat = grad * gain
    return spread * (
        grad_hat
        - jnp.mean(grad_hat, axis=-1, keepdims=True)
        - hat * jnp.mean(grad_hat * hat, axis=-1, keepdims=True)
    )


GELU_RATE = math.sqrt(2.0 / math.pi)


def gelu_parts(pre):
    bend = jnp.tanh(GELU_RATE * (pre + 0.044715 * (pre * pre * pre)))
    return 0.5 * (1.0 + bend), bend


def gelu_slope(pre):
    half, bend = gelu_parts(pre)
    inner = GELU_RATE * (1.0 + 3.0 * 0.044715 * (pre * pre))
    return half + 0.5 * pre * (1.0 - bend * bend) * inner


def both_heads(pair):
    lanes = lax.broadcasted_iota(jnp.int32, pair.shape, 1)
    half = pair.shape[1] // 2
    wide = pair.astype(jnp.float32)
    return jnp.concatenate(
        [jnp.where(lanes < half, wide, 0.0), jnp.where(lanes < half, 0.0, wide)], axis=0
    ).astype(jnp.bfloat16)


def side_by_side(stacked):
    rows = stacked.shape[0] // 2
    lanes = lax.broadcasted_iota(jnp.int32, (rows, stacked.shape[1]), 1)
    return jnp.where(lanes < stacked.shape[1] // 2, stacked[:rows], stacked[rows:])


def third_of(rows, j):
    ids = lax.broadcasted_iota(jnp.int32, rows.shape, 0)
    wide = jnp.where((ids >= j * RANK) & (ids < (j + 1) * RANK), rows.astype(jnp.float32), 0.0)
    return wide.astype(jnp.bfloat16)


def attention_mask(spot_ref, segment_ref):
    spot = lane_columns(spot_ref[...].astype(jnp.float32))[:, 0:1]
    steps = lax.broadcasted_iota(jnp.int32, segment_ref.shape, 1).astype(jnp.float32)
    segment = segment_ref[...].astype(jnp.float32)
    here = jnp.sum(jnp.where(steps == spot, segment, 0.0), axis=1, keepdims=True)
    open_to = ones_where((steps <= spot) & (segment == here))
    return jnp.concatenate([open_to, open_to], axis=0)


def layer_up(h1_ref, rows_ref, segment_ref, spot_ref, affine_ref, bias_ref,
             a_qkv, b_qkv, a_o, b_o, a_fc, b_fc, a_p, b_p,
             qkv_hbm, o_hbm, in_hbm, out_hbm,
             final_ref, q_ref, k_ref, v_ref, u1_ref, u1_rows_ref, h1_rows_ref, lse_ref,
             o_ref, uo_ref, middle_ref, h2_ref, uf_ref, pre_ref, f_ref, up_ref, last_ref,
             wq, wk, wv, wo, win, wout, mask, sems):
    length, width = h1_ref.shape
    hidden = win.shape[1]
    quarter = hidden // 4

    def columns_of(source, j, number):
        return source.at[:, pl.ds(j * number, number)]

    copies = [
        pltpu.make_async_copy(columns_of(qkv_hbm, 1, width), wk, sems.at[0]),
        pltpu.make_async_copy(columns_of(qkv_hbm, 2, width), wv, sems.at[1]),
        pltpu.make_async_copy(columns_of(qkv_hbm, 0, width), wq, sems.at[2]),
        pltpu.make_async_copy(o_hbm, wo, sems.at[3]),
        pltpu.make_async_copy(in_hbm, win, sems.at[4]),
        pltpu.make_async_copy(out_hbm, wout, sems.at[5]),
    ]
    for copy in copies:
        copy.start()

    def bias(first, number):
        return bias_ref[0:1, first : first + number]

    mask[...] = attention_mask(spot_ref, segment_ref)
    h1_rows = layer_norm(rows_ref[...], affine_ref[0:1, :], affine_ref[3:4, :]).astype(
        jnp.bfloat16)
    h1_rows_ref[...] = h1_rows
    u1_ref[...] = matrix_multiply(h1_ref[...], a_qkv[...]).astype(jnp.bfloat16)
    u1_rows = matrix_multiply(h1_rows, a_qkv[...]).astype(jnp.bfloat16)
    u1_rows_ref[...] = u1_rows

    def project(normed, low, weight, j):
        return (
            matrix_multiply(normed, weight[...])
            + bias(j * width, width)
            + ADAPTER_SCALE * matrix_multiply(low, third_of(b_qkv[...], j))
        ).astype(jnp.bfloat16)

    chunk = 256
    for j, weight, out, copy in ((1, wk, k_ref, copies[0]), (2, wv, v_ref, copies[1])):
        copy.wait()

        def rows_of(i):
            rows = pl.ds(pl.multiple_of(i * chunk, chunk), chunk)
            out[rows, :] = project(h1_ref[rows, :], u1_ref[rows, :], weight, j)

        wide_loop(length // chunk, rows_of)
    copies[2].wait()
    q_ref[...] = project(h1_rows, u1_rows, wq, 0)
    scale = (width // HEADS) ** (-0.5)
    lanes = lax.broadcasted_iota(jnp.int32, lse_ref.shape, 1)
    lse_ref[...] = jnp.zeros(lse_ref.shape, jnp.float32)

    def heads(g):
        pair = pl.ds(pl.multiple_of(g * 128, 128), 128)
        scores = scale * matrix_multiply_transposed_right(both_heads(q_ref[:, pair]), k_ref[:, pair])
        scores = jnp.where(mask[...] > 0.0, scores, MASKED)
        top = jnp.max(scores, axis=1, keepdims=True)
        e = jnp.exp(scores - top)
        total = jnp.sum(e, axis=1, keepdims=True)
        probs = (e * (1.0 / total)).astype(jnp.bfloat16)
        o_ref[:, pair] = side_by_side(matrix_multiply(probs, v_ref[:, pair])).astype(jnp.bfloat16)
        lse_ref[...] = jnp.where(lanes == g, top + jnp.log(total), lse_ref[...])

    wide_loop(HEADS // 2, heads)
    o = o_ref[...]
    uo = matrix_multiply(o, a_o[...]).astype(jnp.bfloat16)
    uo_ref[...] = uo
    copies[3].wait()
    middle = (
        rows_ref[...]
        + matrix_multiply(o, wo[...])
        + bias(3 * width, width)
        + ADAPTER_SCALE * matrix_multiply(uo, b_o[...])
    )
    middle_ref[...] = middle
    h2 = layer_norm(middle, affine_ref[1:2, :], affine_ref[4:5, :]).astype(jnp.bfloat16)
    h2_ref[...] = h2
    uf = matrix_multiply(h2, a_fc[...]).astype(jnp.bfloat16)
    uf_ref[...] = uf
    copies[4].wait()
    for j in range(4):
        part = slice(j * quarter, (j + 1) * quarter)
        pre = (
            matrix_multiply(h2, win[:, part])
            + bias(4 * width + j * quarter, quarter)
            + ADAPTER_SCALE * matrix_multiply(uf, b_fc[:, part])
        )
        pre_ref[:, part] = pre
        f_ref[:, part] = (pre * gelu_parts(pre)[0]).astype(jnp.bfloat16)
    f = f_ref[...]
    up = matrix_multiply(f, a_p[...]).astype(jnp.bfloat16)
    up_ref[...] = up
    copies[5].wait()
    last = (
        middle
        + matrix_multiply(f, wout[...])
        + bias(4 * width + hidden, width)
        + ADAPTER_SCALE * matrix_multiply(up, b_p[...])
    )
    last_ref[...] = last
    final_ref[...] = layer_norm(last, affine_ref[2:3, :], affine_ref[5:6, :]).astype(jnp.bfloat16)


def layer_down(grad_ref, spot_ref, segment_ref, affine_ref, h1_ref,
               a_qkv, b_qkv, a_o, b_o, a_fc, b_fc, a_p, b_p,
               q_ref, k_ref, v_ref, u1_ref, u1_rows_ref, h1_rows_ref, lse_ref,
               o_ref, uo_ref, middle_ref, h2_ref, uf_ref, pre_ref, f_ref, up_ref, last_ref,
               o_hbm, in_hbm, out_hbm,
               ga_qkv, gb_qkv, ga_o, gb_o, ga_fc, gb_fc, ga_p, gb_p,
               wo, win, wout, mask, dpre_ref, do_ref, dq_ref, dk_ref, dv_ref, sems):
    length, width = h1_ref.shape
    hidden = win.shape[1]
    quarter = hidden // 4
    rows_here = grad_ref.shape[0]
    copies = [
        pltpu.make_async_copy(out_hbm, wout, sems.at[0]),
        pltpu.make_async_copy(in_hbm, win, sems.at[1]),
        pltpu.make_async_copy(o_hbm, wo, sems.at[2]),
    ]
    for copy in copies:
        copy.start()
    mask[...] = attention_mask(spot_ref, segment_ref)
    spot_row = spot_ref[...].astype(jnp.float32)
    spot = lane_columns(spot_row)[:, 0:1]
    order_row = lax.broadcasted_iota(jnp.int32, (1, rows_here), 1)
    order = lax.broadcasted_iota(jnp.int32, (rows_here, 1), 0)
    same = spot == spot_row
    repeat = jnp.max(ones_where(same & (order_row < order)), axis=1, keepdims=True)
    merge = ones_where(same) * (1.0 - repeat)
    grad_final = jnp.dot(
        merge, grad_ref[...], precision=lax.Precision.HIGHEST,
        preferred_element_type=jnp.float32)
    dx3 = norm_back(last_ref[...], affine_ref[2:3, :], grad_final)
    dm = dx3.astype(jnp.bfloat16)
    gb_p[...] = ADAPTER_SCALE * matrix_multiply_transposed_left(up_ref[...], dm)
    du_p = (ADAPTER_SCALE * matrix_multiply_transposed_right(dm, b_p[...])).astype(jnp.bfloat16)
    ga_p[...] = matrix_multiply_transposed_left(du_p, f_ref[...])
    copies[0].wait()
    for j in range(4):
        part = slice(j * quarter, (j + 1) * quarter)
        df = matrix_multiply_transposed_right(dm, wout[part, :]) + matrix_multiply_transposed_right(
            du_p, a_p[part, :])
        dpre_ref[:, part] = (df * gelu_slope(pre_ref[:, part])).astype(jnp.bfloat16)
    dpre = dpre_ref[...]
    gb_fc[...] = ADAPTER_SCALE * matrix_multiply_transposed_left(uf_ref[...], dpre)
    du_f = (ADAPTER_SCALE * matrix_multiply_transposed_right(dpre, b_fc[...])).astype(jnp.bfloat16)
    ga_fc[...] = matrix_multiply_transposed_left(du_f, h2_ref[...])
    copies[1].wait()
    dh2 = matrix_multiply_transposed_right(dpre, win[...]) + matrix_multiply_transposed_right(
        du_f, a_fc[...])
    dx2 = dx3 + norm_back(middle_ref[...], affine_ref[1:2, :], dh2)
    da = dx2.astype(jnp.bfloat16)
    gb_o[...] = ADAPTER_SCALE * matrix_multiply_transposed_left(uo_ref[...], da)
    du_o = (ADAPTER_SCALE * matrix_multiply_transposed_right(da, b_o[...])).astype(jnp.bfloat16)
    ga_o[...] = matrix_multiply_transposed_left(du_o, o_ref[...])
    copies[2].wait()
    do_ref[...] = (
        matrix_multiply_transposed_right(da, wo[...])
        + matrix_multiply_transposed_right(du_o, a_o[...])
    ).astype(jnp.bfloat16)
    scale = (width // HEADS) ** (-0.5)
    lanes = lax.broadcasted_iota(jnp.int32, lse_ref.shape, 1)

    def heads(g):
        pair = pl.ds(pl.multiple_of(g * 128, 128), 128)
        q = both_heads(q_ref[:, pair])
        do = both_heads(do_ref[:, pair])
        lse = jnp.sum(jnp.where(lanes == g, lse_ref[...], 0.0), axis=1, keepdims=True)
        scores = scale * matrix_multiply_transposed_right(q, k_ref[:, pair])
        probs = jnp.where(mask[...] > 0.0, jnp.exp(jnp.minimum(scores - lse, 0.0)), 0.0)
        dp = matrix_multiply_transposed_right(do, v_ref[:, pair])
        ds = (probs * (dp - jnp.sum(probs * dp, axis=1, keepdims=True))).astype(jnp.bfloat16)
        dv_ref[:, pair] = matrix_multiply_transposed_left(
            probs.astype(jnp.bfloat16), do).astype(jnp.bfloat16)
        dk_ref[:, pair] = (scale * matrix_multiply_transposed_left(ds, q)).astype(jnp.bfloat16)
        dq_ref[:, pair] = side_by_side(scale * matrix_multiply(ds, k_ref[:, pair])).astype(
            jnp.bfloat16)

    wide_loop(HEADS // 2, heads)
    b_all = b_qkv[...]
    gb = jnp.zeros(gb_qkv.shape, jnp.float32)
    ids = lax.broadcasted_iota(jnp.int32, gb_qkv.shape, 0)
    dus = []
    for j, low, grad in ((0, u1_rows_ref, dq_ref), (1, u1_ref, dk_ref), (2, u1_ref, dv_ref)):
        mine = (ids >= j * RANK) & (ids < (j + 1) * RANK)
        gb = jnp.where(mine, ADAPTER_SCALE * matrix_multiply_transposed_left(
            low[...], grad[...]), gb)
        dus.append(ADAPTER_SCALE * matrix_multiply_transposed_right(grad[...], third_of(b_all, j)))
    gb_qkv[...] = gb
    ga_qkv[...] = matrix_multiply_transposed_left(
        dus[0].astype(jnp.bfloat16), h1_rows_ref[...]
    ) + matrix_multiply_transposed_left((dus[1] + dus[2]).astype(jnp.bfloat16), h1_ref[...])


def narrow(matrix, axis):
    pads = [(0, 0), (0, 0)]
    pads[axis] = (0, NARROW - matrix.shape[axis])
    return jnp.pad(matrix.astype(jnp.bfloat16), pads)


def layer_kernels(rows_here, length, width, hidden):
    low, wide = jnp.bfloat16, jnp.float32
    whole = pl.BlockSpec(memory_space=pltpu.VMEM)
    away = pl.BlockSpec(memory_space=pl.ANY)
    dma = pltpu.SemaphoreType.DMA
    params = pltpu.CompilerParams(vmem_limit_bytes=60 << 20)
    kept = [
        ((rows_here, width), low),
        ((length, width), low),
        ((length, width), low),
        ((length, NARROW), low),
        ((rows_here, NARROW), low),
        ((rows_here, width), low),
        ((2 * rows_here, 128), wide),
        ((rows_here, width), low),
        ((rows_here, NARROW), low),
        ((rows_here, width), wide),
        ((rows_here, width), low),
        ((rows_here, NARROW), low),
        ((rows_here, hidden), wide),
        ((rows_here, hidden), low),
        ((rows_here, NARROW), low),
        ((rows_here, width), wide),
    ]
    up = pl.pallas_call(
        layer_up,
        out_shape=[jax.ShapeDtypeStruct(*k) for k in [((rows_here, width), low)] + kept],
        in_specs=[whole] * 14 + [away] * 4,
        out_specs=[whole] * 17,
        scratch_shapes=[pltpu.VMEM((width, width), low)] * 4
        + [
            pltpu.VMEM((width, hidden), low),
            pltpu.VMEM((hidden, width), low),
            pltpu.VMEM((2 * rows_here, length), wide),
            dma((6,)),
        ],
        compiler_params=params,
        name="layer_up",
    )
    grads = [
        (NARROW, width), (NARROW, width), (NARROW, width), (NARROW, width),
        (NARROW, width), (NARROW, hidden), (NARROW, hidden), (NARROW, width),
    ]
    down = pl.pallas_call(
        layer_down,
        out_shape=[jax.ShapeDtypeStruct(g, wide) for g in grads],
        in_specs=[whole] * 29 + [away] * 3,
        out_specs=[whole] * 8,
        scratch_shapes=[
            pltpu.VMEM((width, width), low),
            pltpu.VMEM((width, hidden), low),
            pltpu.VMEM((hidden, width), low),
            pltpu.VMEM((2 * rows_here, length), wide),
            pltpu.VMEM((rows_here, hidden), low),
            pltpu.VMEM((rows_here, width), low),
            pltpu.VMEM((rows_here, width), low),
            pltpu.VMEM((length, width), low),
            pltpu.VMEM((length, width), low),
            dma((3,)),
        ],
        compiler_params=params,
        name="layer_down",
    )
    return up, down


def local(
    mesh_sizes,
    packed_symbol_codes,
    article_numbering,
    target_spots,
    answer_flags,
    shared_embedding,
    spot_embedding,
    combined_qkv_weights,
    attend_outgoing_weights,
    dense_incoming_weights,
    dense_outgoing_weights,
    layernorm_affine,
    bias_terms,
    adaptor_float_copies,
    average_moments,
    squared_moments,
):
    spot_objective = target_spots[0]
    rows_here = spot_objective.shape[0]
    shard_rows = shared_embedding.shape[0]
    fast_h1, fast_rows, labels, crowded = embed(
        mesh_sizes,
        packed_symbol_codes,
        article_numbering,
        target_spots,
        answer_flags,
        spot_embedding,
        layernorm_affine,
        shared_embedding,
    )

    def every_row():
        sharers = mesh_sizes[1]
        base = lax.axis_index("vocab") * shard_rows

        def rows_held(tokens):
            wanted = tokens[0] - base
            inside = (wanted >= 0) & (wanted < shard_rows)
            picked = jnp.take(shared_embedding, jnp.clip(wanted, 0, shard_rows - 1), axis=0)
            return jnp.where(inside[:, None], picked, jnp.zeros((), jnp.bfloat16))

        embedded = rows_held(packed_symbol_codes).astype(jnp.float32)
        for j in range(1, sharers):
            there = [(i, (i + j) % sharers) for i in range(sharers)]
            back = [(i, (i - j) % sharers) for i in range(sharers)]
            theirs = lax.ppermute(packed_symbol_codes, "vocab", there)
            embedded = embedded + lax.ppermute(rows_held(theirs), "vocab", back)
        places = jnp.take(spot_embedding, positions(article_numbering[0]), axis=0)
        stream = embedded + places.astype(jnp.float32)
        normed = layer_norm(stream, layernorm_affine[0], layernorm_affine[3])
        return normed.astype(jnp.bfloat16), jnp.take(stream, spot_objective, axis=0)

    h1, stream_rows = lax.cond(
        crowded[0, 0] > 0.0, every_row, lambda: (fast_h1, fast_rows)
    )
    length, width = h1.shape
    hidden = dense_incoming_weights.shape[1]
    factors = distinct_thin_pairs(adaptor_float_copies)
    factors[1] = factors[1].reshape(3 * RANK, width)
    factors = [narrow(factor, 1 - i % 2) for i, factor in enumerate(factors)]
    layer_up_call, layer_down_call = layer_kernels(rows_here, length, width, hidden)
    final_rows, *kept = layer_up_call(
        h1,
        stream_rows,
        article_numbering,
        target_spots,
        layernorm_affine,
        bias_terms[None, :],
        *factors,
        combined_qkv_weights,
        attend_outgoing_weights,
        dense_incoming_weights,
        dense_outgoing_weights,
    )
    grad_rows, smoothed_entropy_cost = head(mesh_sizes, final_rows, labels, shared_embedding)
    ga_qkv, gb_qkv, ga_o, gb_o, ga_fc, gb_fc, ga_p, gb_p = layer_down_call(
        grad_rows,
        target_spots,
        article_numbering,
        layernorm_affine,
        h1,
        *factors,
        *kept,
        attend_outgoing_weights,
        dense_incoming_weights,
        dense_outgoing_weights,
    )
    pieces = [
        ga_qkv[: 3 * RANK].T,
        gb_qkv[: 3 * RANK],
        ga_o[:RANK].T,
        gb_o[:RANK],
        ga_fc[:RANK].T,
        gb_fc[:RANK],
        ga_p[:RANK].T,
        gb_p[:RANK],
    ]
    local_grad = jnp.concatenate([piece.reshape(-1) for piece in pieces])
    (
        refreshed_thin_pairs,
        updated_first_moment,
        updated_second_moment,
        gradient_global_norm,
    ) = reduce_and_update(
        mesh_sizes, local_grad, adaptor_float_copies, average_moments, squared_moments
    )
    return (
        refreshed_thin_pairs,
        updated_first_moment,
        updated_second_moment,
        gradient_global_norm,
        smoothed_entropy_cost,
    )


def solution(mesh):
    return jax.shard_map(
        partial(local, (mesh.shape["dp"], mesh.shape["vocab"])),
        mesh=mesh,
        in_specs=(
            P(("dp", "vocab"), None),
            P(("dp", "vocab"), None),
            P(("dp", "vocab"), None),
            P(("dp", "vocab"), None),
            P("vocab", None),
            P(),
            P(),
            P(),
            P(),
            P(),
            P(),
            P(),
            P(),
            P(),
            P(),
        ),
        out_specs=(P(), P(), P(), P(), P()),
        check_vma=False,
    )
```

```python
from functools import partial
import math

import jax
import jax.numpy as jnp
from jax import lax
from jax.experimental import pallas as pl
from jax.experimental.pallas import tpu as pltpu
from jax.sharding import PartitionSpec as P

MODEL_WIDTH = 1024
HEADS = 16
FEEDFWD_UNITS = 4096
VOCAB_SIZE = 50257
RANK = 4
STEP = 10


ADAPTER_SCALE = 8.0
NORM_EPS = 1e-05
GRAD_CLIP = 0.0001
STRIDE_LENGTH = 0.02
BETA_ONE = 0.9
BETA_TWO = 0.999
SHRINK_PENALTY = 0.01
STABILITY_FLOOR = 1e-08
MASKED = -1e30
MESH = pl.DeviceIdType.MESH


def matrix_multiply(left, right):
    return jnp.dot(left, right, preferred_element_type=jnp.float32)


def matrix_multiply_transposed_left(left, right):
    return lax.dot_general(
        left, right, (((0,), (0,)), ((), ())), preferred_element_type=jnp.float32
    )


def matrix_multiply_transposed_right(left, right):
    return lax.dot_general(
        left, right, (((1,), (1,)), ((), ())), preferred_element_type=jnp.float32
    )


def layer_norm(stream, gain, shift):
    centred = stream - jnp.mean(stream, axis=-1, keepdims=True)
    spread = lax.rsqrt(jnp.mean(centred * centred, axis=-1, keepdims=True) + NORM_EPS)
    return centred * spread * gain + shift


def positions(segments):
    steps_here = jnp.arange(segments.shape[0], dtype=jnp.int32)
    earlier = (segments[None, :] == segments[:, None]) & (steps_here[None, :] < steps_here[:, None])
    return jnp.sum(earlier.astype(jnp.int32), axis=1)


def distinct_thin_pairs(stacked_samples):
    shapes = [
        (MODEL_WIDTH, 3 * RANK),
        (3, RANK, MODEL_WIDTH),
        (MODEL_WIDTH, RANK),
        (RANK, MODEL_WIDTH),
        (MODEL_WIDTH, RANK),
        (RANK, FEEDFWD_UNITS),
        (FEEDFWD_UNITS, RANK),
        (RANK, MODEL_WIDTH),
    ]
    pieces = []
    offset = 0
    for shape in shapes:
        number = math.prod(shape)
        pieces.append(stacked_samples[offset : offset + number].reshape(shape))
        offset += number
    return pieces


def adaptive_moment_update(grad, weight, first, second):
    first_new = BETA_ONE * first + (1.0 - BETA_ONE) * grad
    second_new = BETA_TWO * second + (1.0 - BETA_TWO) * grad * grad
    debiased_mean_estimate = first_new / (1.0 - BETA_ONE**STEP)
    debiased_variance_estimate = second_new / (1.0 - BETA_TWO**STEP)
    weight_new = weight - STRIDE_LENGTH * (
        debiased_mean_estimate / (jnp.sqrt(debiased_variance_estimate) + STABILITY_FLOOR)
        + SHRINK_PENALTY * weight
    )
    return (weight_new, first_new, second_new)


def sum_and_step(dp_size, vocab_size, grad_ref, weight_ref, first_ref, second_ref, loss_ref,
                 weight_out, first_out, second_out, norm_out, loss_out,
                 parts, planes, total, losses, send_a, recv_a, send_b, recv_b, send_c, recv_c,
                 send_d, recv_d):
    my_plane = lax.axis_index("dp")
    me = lax.axis_index("vocab")

    def across(j):
        return (my_plane, lax.rem(me + j, vocab_size))

    def along(i):
        return (lax.rem(my_plane + i, dp_size), me)

    barrier = pltpu.get_barrier_semaphore()

    @pl.loop(1, vocab_size)
    def _(j):
        pl.semaphore_signal(barrier, inc=1, device_id=across(j), device_id_type=MESH)

    @pl.loop(1, dp_size)
    def _(i):
        pl.semaphore_signal(barrier, inc=1, device_id=along(i), device_id_type=MESH)

    pl.semaphore_wait(barrier, vocab_size + dp_size - 2)

    def part_copy(j):
        peer = across(j)
        return pltpu.make_async_remote_copy(
            src_ref=grad_ref.at[peer[1]], dst_ref=parts.at[me],
            send_sem=send_a.at[peer[1]], recv_sem=recv_a.at[me],
            device_id=peer, device_id_type=MESH)

    def part_arrival(j):
        peer = across(j)
        return pltpu.make_async_remote_copy(
            src_ref=grad_ref.at[peer[1]], dst_ref=parts.at[peer[1]],
            send_sem=send_a.at[peer[1]], recv_sem=recv_a.at[peer[1]],
            device_id=peer, device_id_type=MESH)

    def plane_copy(i):
        peer = along(i)
        return pltpu.make_async_remote_copy(
            src_ref=planes.at[my_plane], dst_ref=planes.at[my_plane],
            send_sem=send_b.at[peer[0]], recv_sem=recv_b.at[my_plane],
            device_id=peer, device_id_type=MESH)

    def plane_arrival(i):
        peer = along(i)
        return pltpu.make_async_remote_copy(
            src_ref=planes.at[my_plane], dst_ref=planes.at[peer[0]],
            send_sem=send_b.at[peer[0]], recv_sem=recv_b.at[peer[0]],
            device_id=peer, device_id_type=MESH)

    def loss_copy(i):
        peer = along(i)
        return pltpu.make_async_remote_copy(
            src_ref=loss_ref, dst_ref=losses.at[my_plane],
            send_sem=send_d.at[peer[0]], recv_sem=recv_d.at[my_plane],
            device_id=peer, device_id_type=MESH)

    def loss_arrival(i):
        peer = along(i)
        return pltpu.make_async_remote_copy(
            src_ref=loss_ref, dst_ref=losses.at[peer[0]],
            send_sem=send_d.at[peer[0]], recv_sem=recv_d.at[peer[0]],
            device_id=peer, device_id_type=MESH)

    def total_copy(j):
        peer = across(j)
        return pltpu.make_async_remote_copy(
            src_ref=total.at[me], dst_ref=total.at[me],
            send_sem=send_c.at[peer[1]], recv_sem=recv_c.at[me],
            device_id=peer, device_id_type=MESH)

    def total_arrival(j):
        peer = across(j)
        return pltpu.make_async_remote_copy(
            src_ref=total.at[me], dst_ref=total.at[peer[1]],
            send_sem=send_c.at[peer[1]], recv_sem=recv_c.at[peer[1]],
            device_id=peer, device_id_type=MESH)

    @pl.loop(1, vocab_size)
    def _(j):
        part_copy(j).start()

    @pl.loop(1, dp_size)
    def _(i):
        loss_copy(i).start()

    losses[my_plane] = loss_ref[...]
    parts[me] = grad_ref[me]

    @pl.loop(1, vocab_size)
    def _(j):
        part_arrival(j).wait_recv()

    planes[my_plane] = lax.fori_loop(
        1, vocab_size, lambda j, held: held + parts[j], parts[0])

    @pl.loop(1, dp_size)
    def _(i):
        plane_copy(i).start()

    @pl.loop(1, dp_size)
    def _(i):
        plane_arrival(i).wait_recv()

    total[me] = lax.fori_loop(1, dp_size, lambda i, held: held + planes[i], planes[0])

    @pl.loop(1, vocab_size)
    def _(j):
        total_copy(j).start()

    @pl.loop(1, vocab_size)
    def _(j):
        part_copy(j).wait_send()

    @pl.loop(1, dp_size)
    def _(i):
        plane_copy(i).wait_send()

    @pl.loop(1, vocab_size)
    def _(j):
        total_arrival(j).wait_recv()

    @pl.loop(1, vocab_size)
    def _(j):
        total_copy(j).wait_send()

    def squares(j, held):
        piece = total[j]
        return held + piece * piece

    gathered = lax.fori_loop(0, vocab_size, squares, jnp.zeros(parts.shape[1:], jnp.float32))
    norm = jnp.sqrt(jnp.sum(gathered, keepdims=True))
    norm_out[...] = norm

    @pl.loop(1, dp_size)
    def _(i):
        loss_arrival(i).wait_recv()
        loss_copy(i).wait_send()

    loss_out[...] = jnp.sum(losses[...], axis=0)[0:1, 0:1]
    shrink = GRAD_CLIP / jnp.maximum(norm, GRAD_CLIP)

    @pl.loop(0, vocab_size)
    def _(j):
        weight, first, second = adaptive_moment_update(
            total[j] * shrink, weight_ref[j], first_ref[j], second_ref[j])
        weight_out[j] = weight
        first_out[j] = first
        second_out[j] = second


def reduce_and_update(mesh_sizes, local_grad, weights, first, second, loss):
    dp_size, vocab_size = mesh_sizes
    number = local_grad.shape[0]
    rows = number // (128 * vocab_size)
    shape = (vocab_size, rows, 128)
    block = pltpu.VMEM(shape, jnp.float32)
    whole = pl.BlockSpec(memory_space=pltpu.VMEM)
    weight_new, first_new, second_new, norm, total_loss = pl.pallas_call(
        partial(sum_and_step, dp_size, vocab_size),
        out_shape=[jax.ShapeDtypeStruct(shape, jnp.float32)] * 3
        + [jax.ShapeDtypeStruct((1, 1), jnp.float32)] * 2,
        in_specs=[whole] * 5,
        out_specs=[whole] * 5,
        scratch_shapes=[
            block,
            pltpu.VMEM((dp_size, rows, 128), jnp.float32),
            block,
            pltpu.VMEM((dp_size, 8, 128), jnp.float32),
            pltpu.SemaphoreType.DMA((vocab_size,)),
            pltpu.SemaphoreType.DMA((vocab_size,)),
            pltpu.SemaphoreType.DMA((dp_size,)),
            pltpu.SemaphoreType.DMA((dp_size,)),
            pltpu.SemaphoreType.DMA((vocab_size,)),
            pltpu.SemaphoreType.DMA((vocab_size,)),
            pltpu.SemaphoreType.DMA((dp_size,)),
            pltpu.SemaphoreType.DMA((dp_size,)),
        ],
        compiler_params=pltpu.CompilerParams(
            collective_id=5, has_side_effects=True, vmem_limit_bytes=24 << 20
        ),
        name="sum_and_step",
    )(*[piece.reshape(shape) for piece in (local_grad, weights, first, second)], loss)
    flat = [piece.reshape(-1) for piece in (weight_new, first_new, second_new)]
    return (*flat, norm.reshape(()), total_loss.reshape(()))


TILE = 32


def head_step(dp_size, vocab_size, block, owned, hf_ref, label_ref, count_ref, table_hbm, grad_out, loss_out,
              table, hf_all, label_all, exps, exps_rest, tops, run_top, run_sum, run_smooth,
              run_goal, offset, z_even, z_odd, z_rest, dz_even, dz_odd, rest_even, rest_odd,
              acc_even, acc_odd, lse_tile, share_tile, stats_all,
              from_core, from_chip, leaving,
              table_sem, label_send, label_recv, hf_send, hf_recv,
              stat_send, stat_recv, core_send, core_recv, chip_send, chip_recv):
    plane = lax.axis_index("dp")
    me = lax.axis_index("vocab")
    chips = vocab_size // 2
    chip = me // 2
    core = lax.rem(me, 2)
    other = 2 * chip + 1 - core
    sibling = (plane, other)
    held = table_hbm.shape[0]
    full = held // block
    rest = held - full * block
    padded = table.shape[0] - full * block
    base = me * owned
    rows_each = hf_ref.shape[0]
    pair = 2 * rows_each
    width = hf_ref.shape[1]

    def partner(k):
        out = 0
        bit = 1
        while bit < chips:
            out = out + lax.rem(chip // bit + lax.rem(k // bit, 2), 2) * bit
            bit *= 2
        return out

    def across(j):
        return (plane, lax.rem(me + j, vocab_size))

    def table_copy(j, number):
        rows = pl.ds(pl.multiple_of(j * block, 16), number)
        return pltpu.make_async_copy(table_hbm.at[rows], table.at[rows], table_sem.at[j])

    @pl.loop(0, full)
    def _(j):
        table_copy(j, block).start()

    table_copy(full, rest).start()

    table[held:, :] = jnp.zeros((padded - rest, width), jnp.bfloat16)
    barrier = pltpu.get_barrier_semaphore()

    @pl.loop(1, vocab_size)
    def _(j):
        pl.semaphore_signal(barrier, inc=1, device_id=across(j), device_id_type=MESH)

    pl.semaphore_wait(barrier, vocab_size - 1)

    def remote(src, dst, send, recv, peer):
        return pltpu.make_async_remote_copy(
            src_ref=src, dst_ref=dst, send_sem=send, recv_sem=recv,
            device_id=peer, device_id_type=MESH)

    def hf_to_sibling():
        return remote(hf_ref, hf_all.at[me], hf_send.at[0], hf_recv.at[me], sibling)

    def hf_copy(k):
        return remote(hf_ref, hf_all.at[me], hf_send.at[k], hf_recv.at[me],
                      (plane, 2 * partner(k) + core))

    def hf_arrival(source):
        return remote(hf_ref, hf_all.at[source], hf_send.at[0], hf_recv.at[source], sibling)

    def hf_forward(k):
        source = 2 * partner(k) + core
        return remote(hf_all.at[source], hf_all.at[source], hf_send.at[chips + k],
                      hf_recv.at[source], sibling)

    def label_copy(j):
        peer = across(j)
        return remote(label_ref, label_all.at[me], label_send.at[peer[1]], label_recv.at[me], peer)

    def label_arrival(source):
        return remote(label_ref, label_all.at[source], label_send.at[source],
                      label_recv.at[source], sibling)

    near = min(3, chips)
    hf_to_sibling().start()

    @pl.loop(1, near)
    def _(k):
        hf_copy(k).start()

    @pl.loop(1, vocab_size)
    def _(j):
        label_copy(j).start()

    hf_all[me] = hf_ref[...]
    label_all[me] = label_ref[...]
    lanes = lax.broadcasted_iota(jnp.int32, (pair, 128), 1)

    def label_row(c, i):
        rows = label_all[pl.ds(2 * c, 2), i : i + 1, :].astype(jnp.float32)
        return jnp.concatenate([rows[0], rows[1]], axis=1)

    def set_offset(c):
        offset[...] = lane_columns(label_row(c, 0)).astype(jnp.int32) - base - lanes

    def folded(x):
        return sum(x[:, i * 128 : (i + 1) * 128] for i in range(1, x.shape[1] // 128)) + x[:, :128]

    def chunk_up(k, first):
        c = partner(k)
        if first:
            hf_arrival(other).wait_recv()
            label_arrival(other).wait_recv()
        else:
            hf_arrival(2 * c + core).wait_recv()
            hf_forward(k).start()
            label_arrival(2 * c).wait_recv()
            label_arrival(2 * c + 1).wait_recv()
            hf_arrival(2 * c + 1 - core).wait_recv()
        set_offset(c)
        run_top[...] = jnp.full((pair, 128), MASKED, jnp.float32)
        for ref in (run_sum, run_smooth, run_goal):
            ref[...] = jnp.zeros((pair, 128), jnp.float32)
        start = pl.multiple_of(k * pair, pair)

        def multiply(j, z_ref):
            if first:
                table_copy(j, rest if z_ref is z_rest else block).wait()
            rows = pl.ds(pl.multiple_of(j * block, 16), z_ref.shape[1])
            hidden = hf_all[pl.ds(2 * c, 2)].reshape(pair, width)
            z_ref[...] = matrix_multiply_transposed_right(hidden, table[rows, :])

        def reduce_full(j, z_ref):
            for r in range(pair // TILE):
                rows = slice(r * TILE, (r + 1) * TILE)
                there = pl.ds(start + r * TILE, TILE)
                z = z_ref[rows, :]
                old = run_top[rows, :]
                top = jnp.maximum(old, jnp.max(z, axis=1, keepdims=True))
                run_top[rows, :] = top
                tops[k, j, rows, :] = top
                gap = offset[rows, :] - j * block
                total = jnp.zeros((TILE, 128), jnp.float32)
                smooth = jnp.zeros((TILE, 128), jnp.float32)
                goal = jnp.zeros((TILE, 128), jnp.float32)
                for i in range(block // 128):
                    part = slice(i * 128, (i + 1) * 128)
                    piece = z[:, part]
                    e = jnp.exp(piece - top)
                    exps[j, there, part] = e
                    total = total + e
                    smooth = smooth + piece
                    goal = goal + jnp.where(gap == i * 128, piece, 0.0)
                run_sum[rows, :] = run_sum[rows, :] * jnp.exp(old - top) + total
                run_smooth[rows, :] = run_smooth[rows, :] + smooth
                run_goal[rows, :] = run_goal[rows, :] + goal

        def reduce_rest():
            for r in range(pair // TILE):
                rows = slice(r * TILE, (r + 1) * TILE)
                there = pl.ds(start + r * TILE, TILE)
                spot = lanes[rows, :]
                limit = jnp.minimum(VOCAB_SIZE - base, owned) - full * block - spot
                gap = offset[rows, :] - full * block
                pieces = []
                for i in range(padded // 128):
                    piece = z_rest[rows, i * 128 : (i + 1) * 128]
                    pieces.append((i * 128 < limit, piece))
                highest = jnp.where(pieces[0][0], pieces[0][1], MASKED)
                for valid, piece in pieces[1:]:
                    highest = jnp.maximum(highest, jnp.where(valid, piece, MASKED))
                old = run_top[rows, :]
                top = jnp.maximum(old, jnp.max(highest, axis=1, keepdims=True))
                run_top[rows, :] = top
                tops[k, full, rows, :] = top
                total = jnp.zeros((TILE, 128), jnp.float32)
                smooth = jnp.zeros((TILE, 128), jnp.float32)
                goal = jnp.zeros((TILE, 128), jnp.float32)
                for i, (valid, piece) in enumerate(pieces):
                    e = jnp.where(valid, jnp.exp(piece - top), 0.0)
                    exps_rest[there, i * 128 : (i + 1) * 128] = e
                    total = total + e
                    smooth = smooth + jnp.where(valid, piece, 0.0)
                    goal = goal + jnp.where(valid & (gap == i * 128), piece, 0.0)
                run_sum[rows, :] = run_sum[rows, :] * jnp.exp(old - top) + total
                run_smooth[rows, :] = run_smooth[rows, :] + smooth
                run_goal[rows, :] = run_goal[rows, :] + goal

        multiply(0, z_even)
        turns = (full - 1) // 2

        if turns > 0:
            @pl.loop(0, turns)
            def _(t):
                multiply(2 * t + 1, z_odd)
                reduce_full(2 * t, z_even)
                multiply(2 * t + 2, z_even)
                reduce_full(2 * t + 1, z_odd)

        if full - 2 * turns == 2:
            multiply(full - 1, z_odd)
            reduce_full(full - 2, z_even)
            multiply(full, z_rest)
            reduce_full(full - 1, z_odd)
        else:
            multiply(full, z_rest)
            reduce_full(full - 1, z_even)
        reduce_rest()

        def row_sum(ref):
            return jnp.sum(ref[...].T, axis=0, keepdims=True)

        ids = lax.broadcasted_iota(jnp.int32, (8, pair), 0)
        packed = jnp.where(ids == 0, run_top[...].T[0:1, :], 0.0)
        for i, ref in enumerate((run_sum, run_smooth, run_goal)):
            packed = jnp.where(ids == i + 1, row_sum(ref), packed)
        stats_all[me, c] = packed

    chunk_up(0, True)

    @pl.loop(near, chips)
    def _(k):
        hf_copy(k).start()

    @pl.loop(1, chips)
    def _(k):
        chunk_up(k, False)

    def stat_copy(j):
        peer = across(j)
        return remote(stats_all.at[me], stats_all.at[me], stat_send.at[peer[1]],
                      stat_recv.at[me], peer)

    def stat_arrival(j):
        source = across(j)[1]
        return remote(stats_all.at[me], stats_all.at[source], stat_send.at[source],
                      stat_recv.at[source], across(j))

    @pl.loop(1, vocab_size)
    def _(j):
        stat_copy(j).start()

    @pl.loop(1, vocab_size)
    def _(j):
        stat_arrival(j).wait_recv()

    count = jnp.maximum(count_ref[1:2, 0:1], 1.0)

    def totals_of(c):
        here = stats_all[:, c]
        tops_here = here[:, 0:1, :]
        top = jnp.max(tops_here, axis=0)
        total = jnp.sum(here[:, 1:2, :] * jnp.exp(tops_here - top[None]), axis=0)
        return top + jnp.log(total), jnp.sum(here[:, 2:3, :], axis=0), jnp.sum(
            here[:, 3:4, :], axis=0)

    def chunk_loss(c, held_loss):
        lse, smooth, goal = totals_of(c)
        return held_loss + label_row(c, 1) * (lse - 0.9 * goal - 0.1 * smooth / VOCAB_SIZE)

    slots = from_core.shape[0]
    columns_each = width // 4

    def core_copy(k, n, acc):
        half = pl.ds(pl.multiple_of((1 - core) * rows_each, rows_each), rows_each)
        part = pl.ds(pl.multiple_of(n * columns_each, columns_each), columns_each)
        return remote(acc.at[half, part], from_core.at[lax.rem(k, slots), :, part],
                      core_send.at[k, n], core_recv.at[k, n], sibling)

    def chip_copy(k):
        return remote(leaving.at[k - 1], from_chip.at[k - 1], chip_send.at[k], chip_recv.at[k],
                      (plane, 2 * partner(k) + core))

    def prepare(k):
        c = partner(k)
        lse, _, _ = totals_of(c)
        lse_tile[...] = lane_columns(lse)
        share_tile[...] = lane_columns(label_row(c, 1) / count)
        set_offset(c)

    quarter = pair // 4

    def grads(k, n, dz_ref, rest_ref):
        for r in range(quarter // TILE):
            first = pl.multiple_of(n * quarter + r * TILE, TILE)
            rows = pl.ds(first, TILE)
            there = pl.ds(pl.multiple_of(k * pair + first, TILE), TILE)
            share = share_tile[rows, :]
            lse = lse_tile[rows, :]
            low = share * (0.1 / VOCAB_SIZE)
            high = low + 0.9 * share
            gap = offset[rows, :]
            for j in range(full):
                factor = share * jnp.exp(tops[k, j, rows, :] - lse)
                for i in range(block // 128):
                    at = j * block + i * 128
                    e = exps[j, there, i * 128 : (i + 1) * 128]
                    dz = e * factor - jnp.where(gap == at, high, low)
                    dz_ref[rows, at : at + 128] = dz.astype(jnp.bfloat16)
            factor = share * jnp.exp(tops[k, full, rows, :] - lse)
            limit = jnp.minimum(VOCAB_SIZE - base, owned) - full * block - lanes[0:TILE, :]
            for i in range(padded // 128):
                part = slice(i * 128, (i + 1) * 128)
                at = full * block + i * 128
                dz = exps_rest[there, part] * factor - jnp.where(gap == at, high, low)
                rest_ref[rows, part] = jnp.where(i * 128 < limit, dz, 0.0).astype(jnp.bfloat16)

    def gather(k, n, dz_ref, rest_ref, acc):
        part = pl.ds(pl.multiple_of(n * columns_each, columns_each), columns_each)
        acc[:, part] = matrix_multiply(
            dz_ref[...], table[pl.ds(0, full * block), part]
        ) + matrix_multiply(rest_ref[...], table[pl.ds(full * block, padded), part])

    def finish(k, acc):
        for n in range(4):
            core_copy(k, n, acc).wait()
        own = pl.ds(pl.multiple_of(core * rows_each, rows_each), rows_each)
        return from_core[lax.rem(k, slots)] + acc[own, :]

    def stage(k, now, later, acc, acc_before, last):
        if later is not None:
            prepare(k - 1)

        @pl.loop(0, 4)
        def _(n):
            gather(k, n, *now, acc)
            if later is not None:
                grads(k - 1, n, *later)
            core_copy(k, n, acc).start()
            if acc_before is not None:
                @pl.when((n == 0) & (k < chips - 1))
                def _():
                    leaving[k] = finish(k + 1, acc_before).astype(jnp.bfloat16)
                    chip_copy(k + 1).start()

    evens = ((dz_even, rest_even), acc_even)
    odds = ((dz_odd, rest_odd), acc_odd)
    prepare(chips - 1)

    @pl.loop(0, 4)
    def _(n):
        grads(chips - 1, n, *odds[0])

    @pl.loop(0, chips // 2 - 1)
    def _(t):
        k = chips - 1 - 2 * t
        stage(k, odds[0], evens[0], acc_odd, acc_even, False)
        stage(k - 1, evens[0], odds[0], acc_even, acc_odd, False)

    stage(1, odds[0], evens[0], acc_odd, acc_even if chips > 2 else None, False)
    stage(0, evens[0], None, acc_even, acc_odd, True)

    loss = lax.fori_loop(0, chips, chunk_loss, jnp.zeros((1, pair), jnp.float32))
    loss_out[...] = jnp.broadcast_to(jnp.sum(loss, keepdims=True) / count, loss_out.shape)
    grad_out[...] = finish(0, acc_even)

    @pl.loop(1, chips)
    def _(k):
        chip_copy(k).wait_recv()
        grad_out[...] += from_chip[k - 1].astype(jnp.float32)

    hf_to_sibling().wait_send()

    @pl.loop(1, chips)
    def _(k):
        hf_copy(k).wait_send()
        hf_forward(k).wait_send()
        chip_copy(k).wait_send()

    @pl.loop(1, vocab_size)
    def _(j):
        label_copy(j).wait_send()
        stat_copy(j).wait_send()


def head(mesh_sizes, owned, final_rows, labels, counts, table):
    dp_size, vocab_size = mesh_sizes
    rows, width = final_rows.shape
    held = table.shape[0]
    block = 1024
    full = held // block
    rest = -(-(held - full * block) // 128) * 128
    chips = vocab_size // 2
    pair = 2 * rows
    low, wide = jnp.bfloat16, jnp.float32
    whole = pl.BlockSpec(memory_space=pltpu.VMEM)
    dma = pltpu.SemaphoreType.DMA
    tile = pltpu.VMEM((pair, 128), wide)
    grad, loss = pl.pallas_call(
        partial(head_step, dp_size, vocab_size, block, owned),
        out_shape=[
            jax.ShapeDtypeStruct((rows, width), wide),
            jax.ShapeDtypeStruct((8, 128), wide),
        ],
        in_specs=[whole, whole, whole, pl.BlockSpec(memory_space=pl.ANY)],
        out_specs=[whole, whole],
        scratch_shapes=[
            pltpu.VMEM((full * block + rest, width), low),
            pltpu.VMEM((vocab_size, rows, width), low),
            pltpu.VMEM((vocab_size, 8, rows), jnp.int32),
            pltpu.VMEM((full, vocab_size * rows, block), wide),
            pltpu.VMEM((vocab_size * rows, rest), wide),
            pltpu.VMEM((chips, full + 1, pair, 128), wide),
            tile,
            tile,
            tile,
            tile,
            pltpu.VMEM((pair, 128), jnp.int32),
            pltpu.VMEM((pair, block), wide),
            pltpu.VMEM((pair, block), wide),
            pltpu.VMEM((pair, rest), wide),
            pltpu.VMEM((pair, full * block), low),
            pltpu.VMEM((pair, full * block), low),
            pltpu.VMEM((pair, rest), low),
            pltpu.VMEM((pair, rest), low),
            pltpu.VMEM((pair, width), wide),
            pltpu.VMEM((pair, width), wide),
            tile,
            tile,
            pltpu.VMEM((vocab_size, chips, 8, pair), wide),
            pltpu.VMEM((3, rows, width), wide),
            pltpu.VMEM((chips - 1, rows, width), low),
            pltpu.VMEM((chips - 1, rows, width), low),
            dma((full + 1,)),
            dma((vocab_size,)),
            dma((vocab_size,)),
            dma((2 * chips,)),
            dma((vocab_size,)),
            dma((vocab_size,)),
            dma((vocab_size,)),
            dma((chips, 4)),
            dma((chips, 4)),
            dma((chips,)),
            dma((chips,)),
        ],
        compiler_params=pltpu.CompilerParams(
            collective_id=3, has_side_effects=True, vmem_limit_bytes=63 << 20
        ),
        name="head_step",
    )(final_rows, labels, counts, table)
    return grad, loss


def lane_columns(row):
    return jnp.broadcast_to(row, (128, row.shape[1])).T


def ones_where(condition):
    return jnp.where(condition, 1.0, 0.0)


def low_ones(condition):
    return ones_where(condition).astype(jnp.bfloat16)


def embed_step(dp_size, vocab_size, block, room, owned, token_ref, segment_ref, spot_ref, flag_ref,
               place_hbm, affine_ref, table_hbm,
               h1_out, rows_out, label_out, full_out,
               table, place_table, key_cols, unique_cols, slot_cols, owners, asked, lists, lists_in,
               acc, leaving, arriving, stream, full_all,
               table_sem, place_sem, list_send, list_recv, row_send, row_recv, full_send, full_recv):
    plane = lax.axis_index("dp")
    me = lax.axis_index("vocab")
    chips = vocab_size // 2
    chip = me // 2
    held = table.shape[0]
    full = held // block
    rest = held - full * block
    length = token_ref.shape[1]
    width = table.shape[1]
    spots_here = spot_ref.shape[1]
    chunk = 128
    chunks = length // chunk

    def partner(k):
        out = 0
        bit = 1
        while bit < chips:
            out = out + lax.rem(chip // bit + (k // bit) % 2, 2) * bit
            bit *= 2
        return out

    def across(j):
        return (plane, lax.rem(me + j, vocab_size))

    def along(i):
        return (lax.rem(plane + i, dp_size), me)

    def remote(src, dst, send, recv, peer):
        return pltpu.make_async_remote_copy(
            src_ref=src, dst_ref=dst, send_sem=send, recv_sem=recv,
            device_id=peer, device_id_type=MESH)

    def table_copy(j, number):
        rows = pl.ds(pl.multiple_of(j * block, 16), number)
        return pltpu.make_async_copy(table_hbm.at[rows], table.at[rows], table_sem.at[j])

    @pl.loop(0, full)
    def _(j):
        table_copy(j, block).start()

    table_copy(full, rest).start()

    place_copy = pltpu.make_async_copy(
        place_hbm.at[pl.ds(0, place_table.shape[0])], place_table, place_sem)
    place_copy.start()
    barrier = pltpu.get_barrier_semaphore()

    @pl.loop(1, vocab_size)
    def _(j):
        pl.semaphore_signal(barrier, inc=1, device_id=across(j), device_id_type=MESH)

    @pl.loop(1, dp_size)
    def _(i):
        pl.semaphore_signal(barrier, inc=1, device_id=along(i), device_id_type=MESH)

    token = token_ref[...].astype(jnp.float32)
    segment = segment_ref[...].astype(jnp.float32)
    steps = lax.broadcasted_iota(jnp.int32, (1, length), 1).astype(jnp.float32)
    spot = lane_columns(spot_ref[...].astype(jnp.float32))[:, 0:1]
    flag = lane_columns(flag_ref[...].astype(jnp.float32))[:, 0:1]
    at_spot = steps == spot
    at_next = steps == spot + 1.0

    def picked(where_to, row):
        return jnp.sum(jnp.where(where_to, row, 0.0), axis=1, keepdims=True)

    segment_here = picked(at_spot, segment)
    weight = jnp.where(segment_here == picked(at_next, segment), flag, 0.0)
    heavy = jnp.sum(weight, axis=0, keepdims=True)
    target = picked(at_next, token)
    lanes = lax.broadcasted_iota(jnp.int32, (spots_here, 128), 1)
    label_tile = jnp.where(lanes == 0, target, jnp.where(lanes == 1, weight, 0.0))
    label_out[...] = label_tile.T[0:8, :].astype(jnp.int32)
    read = (steps <= spot) & (segment == segment_here) & (weight > 0.0)
    needed = jnp.max(ones_where(read), axis=0, keepdims=True) > 0.0

    key = jnp.where(needed, token, -1.0 - steps)
    key_cols[...] = lane_columns(key)

    def places(a):
        return (lax.broadcasted_iota(jnp.int32, (chunk, 1), 0) + a * chunk).astype(jnp.float32)

    def rows_at(a):
        return pl.ds(pl.multiple_of(a * chunk, chunk), chunk)

    def same(a):
        return key_cols[rows_at(a), 0:1] == key

    def seen(a, carry):
        return jnp.maximum(carry, jnp.max(
            ones_where(same(a) & (places(a) < steps)), axis=0, keepdims=True))

    again = lax.fori_loop(0, chunks, seen, jnp.zeros((1, length), jnp.float32))
    unique = ones_where(needed & (again == 0.0))
    unique_cols[...] = lane_columns(unique)
    owner = jnp.zeros((1, length), jnp.float32)
    for j in range(1, vocab_size):
        owner = owner + ones_where(token >= float(j * owned))
    owner_ids = lax.broadcasted_iota(jnp.int32, (vocab_size, length), 0).astype(jnp.float32)
    mine = jnp.where(owner_ids == owner, unique, 0.0)
    owners[...] = mine

    def ahead(a, carry):
        before = low_ones(places(a) < steps)
        return carry + matrix_multiply(owners[:, rows_at(a)].astype(jnp.bfloat16), before)

    ranks = lax.fori_loop(0, chunks, ahead, jnp.zeros((vocab_size, length), jnp.float32))
    rank = jnp.sum(jnp.where(owner_ids == owner, ranks, 0.0), axis=0, keepdims=True)
    too_many = jnp.max(unique * ones_where(rank >= float(room)), axis=1, keepdims=True)
    local_id = token - owner * float(owned)
    local_high = jnp.floor(local_id * (1.0 / 128.0))
    local_low = local_id - 128.0 * local_high
    row_ids = lax.broadcasted_iota(jnp.int32, (8, length), 0)

    def stacked(first, second):
        return jnp.where(row_ids == 0, first, jnp.where(row_ids == 1, second, 0.0))

    asked[...] = stacked(owner, jnp.minimum(rank, 127.0))

    def found(a, carry):
        match = low_ones(same(a) & (unique_cols[rows_at(a), 0:1] > 0.0))
        return carry + matrix_multiply(asked[:, rows_at(a)].astype(jnp.bfloat16), match)

    slots = lax.fori_loop(0, chunks, found, jnp.zeros((8, length), jnp.float32))
    slot = jnp.where(needed, slots[0:1, :] * 128.0 + slots[1:2, :], -1.0)
    slot_cols[...] = lane_columns(slot)
    local_parts = stacked(local_high, local_low).astype(jnp.bfloat16)
    rank_ids = lax.broadcasted_iota(jnp.int32, (128, length), 0).astype(jnp.float32)
    list_rows = lax.broadcasted_iota(jnp.int32, (8, 128), 0)

    @pl.loop(0, vocab_size)
    def _(j):
        theirs = (unique > 0.0) & (owner == j.astype(jnp.float32))
        chosen = low_ones(rank_ids == jnp.where(theirs, rank, -1.0))
        ids = matrix_multiply_transposed_right(local_parts, chosen)
        lists[j] = jnp.where(list_rows == 2, too_many, jnp.where(list_rows == 3, heavy, ids))

    @pl.loop(0, vocab_size)
    def _(j):
        arriving[j] = jnp.zeros(arriving.shape[1:], jnp.bfloat16)

    pl.semaphore_wait(barrier, vocab_size + dp_size - 2)

    def list_copy(j):
        peer = across(j)
        return remote(lists.at[peer[1]], lists_in.at[me], list_send.at[peer[1]],
                      list_recv.at[me], peer)

    def list_arrival(j):
        source = across(j)[1]
        return remote(lists.at[source], lists_in.at[source], list_send.at[source],
                      list_recv.at[source], across(j))

    @pl.loop(1, vocab_size)
    def _(j):
        list_copy(j).start()

    lists_in[me] = lists[me]

    ids = lax.broadcasted_iota(jnp.int32, (32, length), 0).astype(jnp.float32)
    starts = jnp.sum(ones_where(segment < ids), axis=1, keepdims=True)
    place = steps - jnp.sum(jnp.where(segment == ids, starts, 0.0), axis=0, keepdims=True)
    place_cols = lane_columns(place)[:, 0:1]
    span = place_table.shape[0]
    place_copy.wait()
    place_ids = lax.broadcasted_iota(jnp.int32, (length, span), 1).astype(jnp.float32)
    stream[...] = matrix_multiply(low_ones(place_ids == place_cols), place_table[...])
    spot_place = picked(at_spot, place)
    spot_slot = picked(at_spot, slot)

    @pl.loop(1, vocab_size)
    def _(j):
        list_arrival(j).wait_recv()

    full_all[plane] = jnp.where(
        list_rows == 0, jnp.max(lists_in[:, 2:3, 0:1], axis=0),
        jnp.sum(lists_in[:, 3:4, 0:1], axis=0))

    def full_copy(i):
        peer = along(i)
        return remote(full_all.at[plane], full_all.at[plane], full_send.at[peer[0]],
                      full_recv.at[plane], peer)

    def full_arrival(i):
        source = along(i)[0]
        return remote(full_all.at[plane], full_all.at[source], full_send.at[source],
                      full_recv.at[source], along(i))

    @pl.loop(1, dp_size)
    def _(i):
        full_copy(i).start()

    def row_copy(d):
        return remote(leaving.at[d], arriving.at[me, pl.ds(0, room)], row_send.at[d],
                      row_recv.at[me], (plane, d))

    def row_arrival(d):
        return remote(leaving.at[d], arriving.at[d, pl.ds(0, room)], row_send.at[d],
                      row_recv.at[d], (plane, d))

    def wanted(d):
        here = lists_in[d]
        return lane_columns(here[0:1, :] * 128.0 + here[1:2, :])[0:room, 0:1]

    first = True
    for k in range(chips - 1, -1, -1):
        c = partner(k)
        wanted_here = jnp.concatenate([wanted(2 * c), wanted(2 * c + 1)], axis=0)

        def rows_of(j, number):
            if first:
                table_copy(j, number).wait()
            ids_here = (lax.broadcasted_iota(jnp.int32, (2 * room, number), 1)
                        + j * block).astype(jnp.float32)
            rows = pl.ds(pl.multiple_of(j * block, 16), number)
            return matrix_multiply(low_ones(ids_here == wanted_here), table[rows, :])

        acc[...] = rows_of(full, rest)

        @pl.loop(0, full)
        def _(j):
            acc[...] += rows_of(j, block)

        first = False
        for i in range(2):
            leaving[2 * c + i] = acc[pl.ds(i * room, room), :].astype(jnp.bfloat16)
        if k > 0:
            for i in range(2):
                row_copy(2 * c + i).start()
        else:
            row_copy(2 * c + 1 - lax.rem(me, 2)).start()
            arriving[me, pl.ds(0, room), :] = leaving[me]

    for k in range(chips):
        c = partner(k)
        if k > 0:
            for i in range(2):
                row_arrival(2 * c + i).wait_recv()
        else:
            row_arrival(2 * c + 1 - lax.rem(me, 2)).wait_recv()
        pair_rows = arriving[pl.ds(2 * c, 2)].reshape(256, width)
        offset = (2 * c * 128).astype(jnp.float32)

        def spread(column, ids_like):
            ids_here = lax.broadcasted_iota(jnp.int32, ids_like, 1).astype(jnp.float32)
            return low_ones(ids_here + offset == column)

        stream[...] += matrix_multiply(spread(slot_cols[:, 0:1], (length, 256)), pair_rows)
        spot_rows = matrix_multiply(spread(spot_slot, (spots_here, 256)), pair_rows)
        if k == 0:
            rows_out[...] = spot_rows
        else:
            rows_out[...] += spot_rows

    spot_ids = lax.broadcasted_iota(jnp.int32, (spots_here, span), 1).astype(jnp.float32)
    rows_out[...] += matrix_multiply(low_ones(spot_ids == spot_place), place_table[...])

    @pl.loop(0, length // 256)
    def _(a):
        rows = pl.ds(pl.multiple_of(a * 256, 256), 256)
        h1_out[rows, :] = layer_norm(
            stream[rows, :], affine_ref[0:1, :], affine_ref[3:4, :]).astype(jnp.bfloat16)

    @pl.loop(1, dp_size)
    def _(i):
        full_arrival(i).wait_recv()

    full_out[...] = jnp.where(
        list_rows == 0, jnp.max(full_all[...], axis=0), jnp.sum(full_all[...], axis=0))

    @pl.loop(1, vocab_size)
    def _(j):
        list_copy(j).wait_send()

    @pl.loop(1, dp_size)
    def _(i):
        full_copy(i).wait_send()

    for k in range(chips):
        if k > 0:
            for i in range(2):
                row_copy(2 * partner(k) + i).wait_send()
        else:
            row_copy(2 * chip + 1 - lax.rem(me, 2)).wait_send()


def embed(mesh_sizes, owned, tokens, segments, spots, flags, place_table, affine, table):
    dp_size, vocab_size = mesh_sizes
    length = tokens.shape[1]
    spots_here = spots.shape[1]
    held, width = table.shape
    block = 1024
    full = held // block
    chips = vocab_size // 2
    room = 112 if vocab_size <= 8 else 64
    span = 256
    whole = pl.BlockSpec(memory_space=pltpu.VMEM)
    dma = pltpu.SemaphoreType.DMA
    return pl.pallas_call(
        partial(embed_step, dp_size, vocab_size, block, room, owned),
        out_shape=[
            jax.ShapeDtypeStruct((length, width), jnp.bfloat16),
            jax.ShapeDtypeStruct((spots_here, width), jnp.float32),
            jax.ShapeDtypeStruct((8, spots_here), jnp.int32),
            jax.ShapeDtypeStruct((8, 128), jnp.float32),
        ],
        in_specs=[whole] * 4
        + [pl.BlockSpec(memory_space=pl.ANY), whole, pl.BlockSpec(memory_space=pl.ANY)],
        out_specs=[whole] * 4,
        scratch_shapes=[
            pltpu.VMEM((held, width), jnp.bfloat16),
            pltpu.VMEM((span, width), jnp.bfloat16),
            pltpu.VMEM((length, 128), jnp.float32),
            pltpu.VMEM((length, 128), jnp.float32),
            pltpu.VMEM((length, 128), jnp.float32),
            pltpu.VMEM((vocab_size, length), jnp.float32),
            pltpu.VMEM((8, length), jnp.float32),
            pltpu.VMEM((vocab_size, 8, 128), jnp.float32),
            pltpu.VMEM((vocab_size, 8, 128), jnp.float32),
            pltpu.VMEM((2 * room, width), jnp.float32),
            pltpu.VMEM((vocab_size, room, width), jnp.bfloat16),
            pltpu.VMEM((vocab_size, 128, width), jnp.bfloat16),
            pltpu.VMEM((length, width), jnp.float32),
            pltpu.VMEM((dp_size, 8, 128), jnp.float32),
            dma((full + 1,)),
            dma,
            dma((vocab_size,)),
            dma((vocab_size,)),
            dma((vocab_size,)),
            dma((vocab_size,)),
            dma((dp_size,)),
            dma((dp_size,)),
        ],
        compiler_params=pltpu.CompilerParams(
            collective_id=1, has_side_effects=True, vmem_limit_bytes=60 << 20
        ),
        name="embed_step",
    )(tokens, segments, spots, flags, place_table, affine, table)


NARROW = 16


def wide_loop(number, body):
    lax.fori_loop(0, number, lambda i, carry: (body(i), carry)[1], 0)


def norm_parts(rows):
    centred = rows - jnp.mean(rows, axis=-1, keepdims=True)
    return centred, lax.rsqrt(jnp.mean(centred * centred, axis=-1, keepdims=True) + NORM_EPS)


def norm_back(rows, gain, grad):
    centred, spread = norm_parts(rows)
    hat = centred * spread
    grad_hat = grad * gain
    return spread * (
        grad_hat
        - jnp.mean(grad_hat, axis=-1, keepdims=True)
        - hat * jnp.mean(grad_hat * hat, axis=-1, keepdims=True)
    )


GELU_RATE = math.sqrt(2.0 / math.pi)


def gelu_parts(pre):
    bend = jnp.tanh(GELU_RATE * (pre + 0.044715 * (pre * pre * pre)))
    return 0.5 * (1.0 + bend), bend


def gelu_slope(pre):
    half, bend = gelu_parts(pre)
    inner = GELU_RATE * (1.0 + 3.0 * 0.044715 * (pre * pre))
    return half + 0.5 * pre * (1.0 - bend * bend) * inner


def both_heads(pair):
    lanes = lax.broadcasted_iota(jnp.int32, pair.shape, 1)
    half = pair.shape[1] // 2
    wide = pair.astype(jnp.float32)
    return jnp.concatenate(
        [jnp.where(lanes < half, wide, 0.0), jnp.where(lanes < half, 0.0, wide)], axis=0
    ).astype(jnp.bfloat16)


def side_by_side(stacked):
    rows = stacked.shape[0] // 2
    lanes = lax.broadcasted_iota(jnp.int32, (rows, stacked.shape[1]), 1)
    return jnp.where(lanes < stacked.shape[1] // 2, stacked[:rows], stacked[rows:])


def third_of(rows, j):
    ids = lax.broadcasted_iota(jnp.int32, rows.shape, 0)
    wide = jnp.where((ids >= j * RANK) & (ids < (j + 1) * RANK), rows.astype(jnp.float32), 0.0)
    return wide.astype(jnp.bfloat16)


def attention_mask(spot_ref, segment_ref):
    spot = lane_columns(spot_ref[...].astype(jnp.float32))[:, 0:1]
    steps = lax.broadcasted_iota(jnp.int32, segment_ref.shape, 1).astype(jnp.float32)
    segment = segment_ref[...].astype(jnp.float32)
    here = jnp.sum(jnp.where(steps == spot, segment, 0.0), axis=1, keepdims=True)
    open_to = ones_where((steps <= spot) & (segment == here))
    return jnp.concatenate([open_to, open_to], axis=0)


def layer_up(h1_ref, rows_ref, segment_ref, spot_ref, affine_ref, bias_ref,
             a_qkv, b_qkv, a_o, b_o, a_fc, b_fc, a_p, b_p,
             qkv_hbm, o_hbm, in_hbm, out_hbm,
             final_ref, q_ref, k_ref, v_ref, u1_ref, u1_rows_ref, h1_rows_ref, lse_ref,
             o_ref, uo_ref, middle_ref, h2_ref, uf_ref, pre_ref, f_ref, up_ref, last_ref,
             wq, wk, wv, wo, win, wout, mask, sems):
    length, width = h1_ref.shape
    hidden = win.shape[1]
    quarter = hidden // 4

    def columns_of(source, j, number):
        return source.at[:, pl.ds(j * number, number)]

    copies = [
        pltpu.make_async_copy(columns_of(qkv_hbm, 1, width), wk, sems.at[0]),
        pltpu.make_async_copy(columns_of(qkv_hbm, 2, width), wv, sems.at[1]),
        pltpu.make_async_copy(columns_of(qkv_hbm, 0, width), wq, sems.at[2]),
        pltpu.make_async_copy(o_hbm, wo, sems.at[3]),
        pltpu.make_async_copy(in_hbm, win, sems.at[4]),
        pltpu.make_async_copy(out_hbm, wout, sems.at[5]),
    ]
    for copy in copies:
        copy.start()

    def bias(first, number):
        return bias_ref[0:1, first : first + number]

    mask[...] = attention_mask(spot_ref, segment_ref)
    h1_rows = layer_norm(rows_ref[...], affine_ref[0:1, :], affine_ref[3:4, :]).astype(
        jnp.bfloat16)
    h1_rows_ref[...] = h1_rows
    u1_ref[...] = matrix_multiply(h1_ref[...], a_qkv[...]).astype(jnp.bfloat16)
    u1_rows = matrix_multiply(h1_rows, a_qkv[...]).astype(jnp.bfloat16)
    u1_rows_ref[...] = u1_rows

    def project(normed, low, weight, j):
        return (
            matrix_multiply(normed, weight[...])
            + bias(j * width, width)
            + ADAPTER_SCALE * matrix_multiply(low, third_of(b_qkv[...], j))
        ).astype(jnp.bfloat16)

    chunk = 256
    for j, weight, out, copy in ((1, wk, k_ref, copies[0]), (2, wv, v_ref, copies[1])):
        copy.wait()

        def rows_of(i):
            rows = pl.ds(pl.multiple_of(i * chunk, chunk), chunk)
            out[rows, :] = project(h1_ref[rows, :], u1_ref[rows, :], weight, j)

        wide_loop(length // chunk, rows_of)
    copies[2].wait()
    q_ref[...] = project(h1_rows, u1_rows, wq, 0)
    scale = (width // HEADS) ** (-0.5)
    lanes = lax.broadcasted_iota(jnp.int32, lse_ref.shape, 1)
    lse_ref[...] = jnp.zeros(lse_ref.shape, jnp.float32)

    def heads(g):
        pair = pl.ds(pl.multiple_of(g * 128, 128), 128)
        scores = scale * matrix_multiply_transposed_right(both_heads(q_ref[:, pair]), k_ref[:, pair])
        scores = jnp.where(mask[...] > 0.0, scores, MASKED)
        top = jnp.max(scores, axis=1, keepdims=True)
        e = jnp.exp(scores - top)
        total = jnp.sum(e, axis=1, keepdims=True)
        probs = (e * (1.0 / total)).astype(jnp.bfloat16)
        o_ref[:, pair] = side_by_side(matrix_multiply(probs, v_ref[:, pair])).astype(jnp.bfloat16)
        lse_ref[...] = jnp.where(lanes == g, top + jnp.log(total), lse_ref[...])

    wide_loop(HEADS // 2, heads)
    o = o_ref[...]
    uo = matrix_multiply(o, a_o[...]).astype(jnp.bfloat16)
    uo_ref[...] = uo
    copies[3].wait()
    middle = (
        rows_ref[...]
        + matrix_multiply(o, wo[...])
        + bias(3 * width, width)
        + ADAPTER_SCALE * matrix_multiply(uo, b_o[...])
    )
    middle_ref[...] = middle
    h2 = layer_norm(middle, affine_ref[1:2, :], affine_ref[4:5, :]).astype(jnp.bfloat16)
    h2_ref[...] = h2
    uf = matrix_multiply(h2, a_fc[...]).astype(jnp.bfloat16)
    uf_ref[...] = uf
    copies[4].wait()
    for j in range(4):
        part = slice(j * quarter, (j + 1) * quarter)
        pre = (
            matrix_multiply(h2, win[:, part])
            + bias(4 * width + j * quarter, quarter)
            + ADAPTER_SCALE * matrix_multiply(uf, b_fc[:, part])
        )
        pre_ref[:, part] = pre
        f_ref[:, part] = (pre * gelu_parts(pre)[0]).astype(jnp.bfloat16)
    f = f_ref[...]
    up = matrix_multiply(f, a_p[...]).astype(jnp.bfloat16)
    up_ref[...] = up
    copies[5].wait()
    last = (
        middle
        + matrix_multiply(f, wout[...])
        + bias(4 * width + hidden, width)
        + ADAPTER_SCALE * matrix_multiply(up, b_p[...])
    )
    last_ref[...] = last
    final_ref[...] = layer_norm(last, affine_ref[2:3, :], affine_ref[5:6, :]).astype(jnp.bfloat16)


def layer_down(grad_ref, spot_ref, segment_ref, affine_ref, h1_ref,
               a_qkv, b_qkv, a_o, b_o, a_fc, b_fc, a_p, b_p,
               q_ref, k_ref, v_ref, u1_ref, u1_rows_ref, h1_rows_ref, lse_ref,
               o_ref, uo_ref, middle_ref, h2_ref, uf_ref, pre_ref, f_ref, up_ref, last_ref,
               o_hbm, in_hbm, out_hbm,
               ga_qkv, gb_qkv, ga_o, gb_o, ga_fc, gb_fc, ga_p, gb_p,
               wo, win, wout, mask, dpre_ref, do_ref, dq_ref, dk_ref, dv_ref, sems):
    length, width = h1_ref.shape
    hidden = win.shape[1]
    quarter = hidden // 4
    rows_here = grad_ref.shape[0]
    copies = [
        pltpu.make_async_copy(out_hbm, wout, sems.at[0]),
        pltpu.make_async_copy(in_hbm, win, sems.at[1]),
        pltpu.make_async_copy(o_hbm, wo, sems.at[2]),
    ]
    for copy in copies:
        copy.start()
    mask[...] = attention_mask(spot_ref, segment_ref)
    spot_row = spot_ref[...].astype(jnp.float32)
    spot = lane_columns(spot_row)[:, 0:1]
    order_row = lax.broadcasted_iota(jnp.int32, (1, rows_here), 1)
    order = lax.broadcasted_iota(jnp.int32, (rows_here, 1), 0)
    same = spot == spot_row
    repeat = jnp.max(ones_where(same & (order_row < order)), axis=1, keepdims=True)
    merge = ones_where(same) * (1.0 - repeat)
    grad_final = jnp.dot(
        merge, grad_ref[...], precision=lax.Precision.HIGHEST,
        preferred_element_type=jnp.float32)
    dx3 = norm_back(last_ref[...], affine_ref[2:3, :], grad_final)
    dm = dx3.astype(jnp.bfloat16)
    gb_p[...] = ADAPTER_SCALE * matrix_multiply_transposed_left(up_ref[...], dm)
    du_p = (ADAPTER_SCALE * matrix_multiply_transposed_right(dm, b_p[...])).astype(jnp.bfloat16)
    ga_p[...] = matrix_multiply_transposed_left(du_p, f_ref[...])
    copies[0].wait()
    for j in range(4):
        part = slice(j * quarter, (j + 1) * quarter)
        df = matrix_multiply_transposed_right(dm, wout[part, :]) + matrix_multiply_transposed_right(
            du_p, a_p[part, :])
        dpre_ref[:, part] = (df * gelu_slope(pre_ref[:, part])).astype(jnp.bfloat16)
    dpre = dpre_ref[...]
    gb_fc[...] = ADAPTER_SCALE * matrix_multiply_transposed_left(uf_ref[...], dpre)
    du_f = (ADAPTER_SCALE * matrix_multiply_transposed_right(dpre, b_fc[...])).astype(jnp.bfloat16)
    ga_fc[...] = matrix_multiply_transposed_left(du_f, h2_ref[...])
    copies[1].wait()
    dh2 = matrix_multiply_transposed_right(dpre, win[...]) + matrix_multiply_transposed_right(
        du_f, a_fc[...])
    dx2 = dx3 + norm_back(middle_ref[...], affine_ref[1:2, :], dh2)
    da = dx2.astype(jnp.bfloat16)
    gb_o[...] = ADAPTER_SCALE * matrix_multiply_transposed_left(uo_ref[...], da)
    du_o = (ADAPTER_SCALE * matrix_multiply_transposed_right(da, b_o[...])).astype(jnp.bfloat16)
    ga_o[...] = matrix_multiply_transposed_left(du_o, o_ref[...])
    copies[2].wait()
    do_ref[...] = (
        matrix_multiply_transposed_right(da, wo[...])
        + matrix_multiply_transposed_right(du_o, a_o[...])
    ).astype(jnp.bfloat16)
    scale = (width // HEADS) ** (-0.5)
    lanes = lax.broadcasted_iota(jnp.int32, lse_ref.shape, 1)

    def heads(g):
        pair = pl.ds(pl.multiple_of(g * 128, 128), 128)
        q = both_heads(q_ref[:, pair])
        do = both_heads(do_ref[:, pair])
        lse = jnp.sum(jnp.where(lanes == g, lse_ref[...], 0.0), axis=1, keepdims=True)
        scores = scale * matrix_multiply_transposed_right(q, k_ref[:, pair])
        probs = jnp.where(mask[...] > 0.0, jnp.exp(jnp.minimum(scores - lse, 0.0)), 0.0)
        dp = matrix_multiply_transposed_right(do, v_ref[:, pair])
        ds = (probs * (dp - jnp.sum(probs * dp, axis=1, keepdims=True))).astype(jnp.bfloat16)
        dv_ref[:, pair] = matrix_multiply_transposed_left(
            probs.astype(jnp.bfloat16), do).astype(jnp.bfloat16)
        dk_ref[:, pair] = (scale * matrix_multiply_transposed_left(ds, q)).astype(jnp.bfloat16)
        dq_ref[:, pair] = side_by_side(scale * matrix_multiply(ds, k_ref[:, pair])).astype(
            jnp.bfloat16)

    wide_loop(HEADS // 2, heads)
    b_all = b_qkv[...]
    gb = jnp.zeros(gb_qkv.shape, jnp.float32)
    ids = lax.broadcasted_iota(jnp.int32, gb_qkv.shape, 0)
    dus = []
    for j, low, grad in ((0, u1_rows_ref, dq_ref), (1, u1_ref, dk_ref), (2, u1_ref, dv_ref)):
        mine = (ids >= j * RANK) & (ids < (j + 1) * RANK)
        gb = jnp.where(mine, ADAPTER_SCALE * matrix_multiply_transposed_left(
            low[...], grad[...]), gb)
        dus.append(ADAPTER_SCALE * matrix_multiply_transposed_right(grad[...], third_of(b_all, j)))
    gb_qkv[...] = gb
    ga_qkv[...] = matrix_multiply_transposed_left(
        dus[0].astype(jnp.bfloat16), h1_rows_ref[...]
    ) + matrix_multiply_transposed_left((dus[1] + dus[2]).astype(jnp.bfloat16), h1_ref[...])


def narrow(matrix, axis):
    pads = [(0, 0), (0, 0)]
    pads[axis] = (0, NARROW - matrix.shape[axis])
    return jnp.pad(matrix.astype(jnp.bfloat16), pads)


def layer_kernels(rows_here, length, width, hidden):
    low, wide = jnp.bfloat16, jnp.float32
    whole = pl.BlockSpec(memory_space=pltpu.VMEM)
    away = pl.BlockSpec(memory_space=pl.ANY)
    dma = pltpu.SemaphoreType.DMA
    params = pltpu.CompilerParams(vmem_limit_bytes=60 << 20)
    kept = [
        ((rows_here, width), low),
        ((length, width), low),
        ((length, width), low),
        ((length, NARROW), low),
        ((rows_here, NARROW), low),
        ((rows_here, width), low),
        ((2 * rows_here, 128), wide),
        ((rows_here, width), low),
        ((rows_here, NARROW), low),
        ((rows_here, width), wide),
        ((rows_here, width), low),
        ((rows_here, NARROW), low),
        ((rows_here, hidden), wide),
        ((rows_here, hidden), low),
        ((rows_here, NARROW), low),
        ((rows_here, width), wide),
    ]
    up = pl.pallas_call(
        layer_up,
        out_shape=[jax.ShapeDtypeStruct(*k) for k in [((rows_here, width), low)] + kept],
        in_specs=[whole] * 14 + [away] * 4,
        out_specs=[whole] * 17,
        scratch_shapes=[pltpu.VMEM((width, width), low)] * 4
        + [
            pltpu.VMEM((width, hidden), low),
            pltpu.VMEM((hidden, width), low),
            pltpu.VMEM((2 * rows_here, length), wide),
            dma((6,)),
        ],
        compiler_params=params,
        name="layer_up",
    )
    grads = [
        (NARROW, width), (NARROW, width), (NARROW, width), (NARROW, width),
        (NARROW, width), (NARROW, hidden), (NARROW, hidden), (NARROW, width),
    ]
    down = pl.pallas_call(
        layer_down,
        out_shape=[jax.ShapeDtypeStruct(g, wide) for g in grads],
        in_specs=[whole] * 29 + [away] * 3,
        out_specs=[whole] * 8,
        scratch_shapes=[
            pltpu.VMEM((width, width), low),
            pltpu.VMEM((width, hidden), low),
            pltpu.VMEM((hidden, width), low),
            pltpu.VMEM((2 * rows_here, length), wide),
            pltpu.VMEM((rows_here, hidden), low),
            pltpu.VMEM((rows_here, width), low),
            pltpu.VMEM((rows_here, width), low),
            pltpu.VMEM((length, width), low),
            pltpu.VMEM((length, width), low),
            dma((3,)),
        ],
        compiler_params=params,
        name="layer_down",
    )
    return up, down


def local(
    mesh_sizes,
    packed_symbol_codes,
    article_numbering,
    target_spots,
    answer_flags,
    shared_embedding,
    spot_embedding,
    combined_qkv_weights,
    attend_outgoing_weights,
    dense_incoming_weights,
    dense_outgoing_weights,
    layernorm_affine,
    bias_terms,
    adaptor_float_copies,
    average_moments,
    squared_moments,
):
    spot_objective = target_spots[0]
    rows_here = spot_objective.shape[0]
    shard_rows = shared_embedding.shape[0]
    table = jnp.pad(shared_embedding, ((0, -shard_rows % 16), (0, 0)))
    fast_h1, fast_rows, labels, crowded = embed(
        mesh_sizes,
        shard_rows,
        packed_symbol_codes,
        article_numbering,
        target_spots,
        answer_flags,
        spot_embedding,
        layernorm_affine,
        table,
    )

    def every_row():
        sharers = mesh_sizes[1]
        base = lax.axis_index("vocab") * shard_rows

        def rows_held(tokens):
            wanted = tokens[0] - base
            inside = (wanted >= 0) & (wanted < shard_rows)
            picked = jnp.take(shared_embedding, jnp.clip(wanted, 0, shard_rows - 1), axis=0)
            return jnp.where(inside[:, None], picked, jnp.zeros((), jnp.bfloat16))

        embedded = rows_held(packed_symbol_codes).astype(jnp.float32)
        for j in range(1, sharers):
            there = [(i, (i + j) % sharers) for i in range(sharers)]
            back = [(i, (i - j) % sharers) for i in range(sharers)]
            theirs = lax.ppermute(packed_symbol_codes, "vocab", there)
            embedded = embedded + lax.ppermute(rows_held(theirs), "vocab", back)
        places = jnp.take(spot_embedding, positions(article_numbering[0]), axis=0)
        stream = embedded + places.astype(jnp.float32)
        normed = layer_norm(stream, layernorm_affine[0], layernorm_affine[3])
        return normed.astype(jnp.bfloat16), jnp.take(stream, spot_objective, axis=0)

    h1, stream_rows = lax.cond(
        crowded[0, 0] > 0.0, every_row, lambda: (fast_h1, fast_rows)
    )
    length, width = h1.shape
    hidden = dense_incoming_weights.shape[1]
    factors = distinct_thin_pairs(adaptor_float_copies)
    factors[1] = factors[1].reshape(3 * RANK, width)
    factors = [narrow(factor, 1 - i % 2) for i, factor in enumerate(factors)]
    layer_up_call, layer_down_call = layer_kernels(rows_here, length, width, hidden)
    final_rows, *kept = layer_up_call(
        h1,
        stream_rows,
        article_numbering,
        target_spots,
        layernorm_affine,
        bias_terms[None, :],
        *factors,
        combined_qkv_weights,
        attend_outgoing_weights,
        dense_incoming_weights,
        dense_outgoing_weights,
    )
    grad_rows, loss_part = head(
        mesh_sizes, shard_rows, final_rows, labels, crowded, table
    )
    ga_qkv, gb_qkv, ga_o, gb_o, ga_fc, gb_fc, ga_p, gb_p = layer_down_call(
        grad_rows,
        target_spots,
        article_numbering,
        layernorm_affine,
        h1,
        *factors,
        *kept,
        attend_outgoing_weights,
        dense_incoming_weights,
        dense_outgoing_weights,
    )
    pieces = [
        ga_qkv[: 3 * RANK].T,
        gb_qkv[: 3 * RANK],
        ga_o[:RANK].T,
        gb_o[:RANK],
        ga_fc[:RANK].T,
        gb_fc[:RANK],
        ga_p[:RANK].T,
        gb_p[:RANK],
    ]
    local_grad = jnp.concatenate([piece.reshape(-1) for piece in pieces])
    (
        refreshed_thin_pairs,
        updated_first_moment,
        updated_second_moment,
        gradient_global_norm,
        smoothed_entropy_cost,
    ) = reduce_and_update(
        mesh_sizes, local_grad, adaptor_float_copies, average_moments, squared_moments, loss_part
    )
    return (
        refreshed_thin_pairs,
        updated_first_moment,
        updated_second_moment,
        gradient_global_norm,
        smoothed_entropy_cost,
    )


def solution(mesh):
    return jax.shard_map(
        partial(local, (mesh.shape["dp"], mesh.shape["vocab"])),
        mesh=mesh,
        in_specs=(
            P(("dp", "vocab"), None),
            P(("dp", "vocab"), None),
            P(("dp", "vocab"), None),
            P(("dp", "vocab"), None),
            P("vocab", None),
            P(),
            P(),
            P(),
            P(),
            P(),
            P(),
            P(),
            P(),
            P(),
            P(),
        ),
        out_specs=(P(), P(), P(), P(), P()),
        check_vma=False,
    )
```

```python
from functools import partial
import math

import jax
import jax.numpy as jnp
from jax import lax
from jax.experimental import pallas as pl
from jax.experimental.pallas import tpu as pltpu
from jax.sharding import PartitionSpec as P

MODEL_WIDTH = 1024
HEADS = 16
FEEDFWD_UNITS = 4096
VOCAB_SIZE = 50257
RANK = 4
STEP = 10


ADAPTER_SCALE = 8.0
NORM_EPS = 1e-05
GRAD_CLIP = 0.0001
STRIDE_LENGTH = 0.02
BETA_ONE = 0.9
BETA_TWO = 0.999
SHRINK_PENALTY = 0.01
STABILITY_FLOOR = 1e-08
MASKED = -1e30
MESH = pl.DeviceIdType.MESH


def matrix_multiply(left, right):
    return jnp.dot(left, right, preferred_element_type=jnp.float32)


def matrix_multiply_transposed_left(left, right):
    return lax.dot_general(
        left, right, (((0,), (0,)), ((), ())), preferred_element_type=jnp.float32
    )


def matrix_multiply_transposed_right(left, right):
    return lax.dot_general(
        left, right, (((1,), (1,)), ((), ())), preferred_element_type=jnp.float32
    )


def layer_norm(stream, gain, shift):
    centred = stream - jnp.mean(stream, axis=-1, keepdims=True)
    spread = lax.rsqrt(jnp.mean(centred * centred, axis=-1, keepdims=True) + NORM_EPS)
    return centred * spread * gain + shift


def adaptive_moment_update(grad, weight, first, second):
    first_new = BETA_ONE * first + (1.0 - BETA_ONE) * grad
    second_new = BETA_TWO * second + (1.0 - BETA_TWO) * grad * grad
    debiased_mean_estimate = first_new / (1.0 - BETA_ONE**STEP)
    debiased_variance_estimate = second_new / (1.0 - BETA_TWO**STEP)
    weight_new = weight - STRIDE_LENGTH * (
        debiased_mean_estimate / (jnp.sqrt(debiased_variance_estimate) + STABILITY_FLOOR)
        + SHRINK_PENALTY * weight
    )
    return (weight_new, first_new, second_new)


def sum_and_step(dp_size, vocab_size, grad_ref, weight_ref, first_ref, second_ref, loss_ref,
                 weight_out, first_out, second_out, norm_out, loss_out,
                 parts, planes, total, losses, send_a, recv_a, send_b, recv_b, send_c, recv_c,
                 send_d, recv_d):
    my_plane = lax.axis_index("dp")
    me = lax.axis_index("vocab")

    def across(j):
        return (my_plane, lax.rem(me + j, vocab_size))

    def along(i):
        return (lax.rem(my_plane + i, dp_size), me)

    barrier = pltpu.get_barrier_semaphore()

    @pl.loop(1, vocab_size)
    def _(j):
        pl.semaphore_signal(barrier, inc=1, device_id=across(j), device_id_type=MESH)

    @pl.loop(1, dp_size)
    def _(i):
        pl.semaphore_signal(barrier, inc=1, device_id=along(i), device_id_type=MESH)

    pl.semaphore_wait(barrier, vocab_size + dp_size - 2)

    def part_copy(j):
        peer = across(j)
        return pltpu.make_async_remote_copy(
            src_ref=grad_ref.at[peer[1]], dst_ref=parts.at[me],
            send_sem=send_a.at[peer[1]], recv_sem=recv_a.at[me],
            device_id=peer, device_id_type=MESH)

    def part_arrival(j):
        peer = across(j)
        return pltpu.make_async_remote_copy(
            src_ref=grad_ref.at[peer[1]], dst_ref=parts.at[peer[1]],
            send_sem=send_a.at[peer[1]], recv_sem=recv_a.at[peer[1]],
            device_id=peer, device_id_type=MESH)

    def plane_copy(i):
        peer = along(i)
        return pltpu.make_async_remote_copy(
            src_ref=planes.at[my_plane], dst_ref=planes.at[my_plane],
            send_sem=send_b.at[peer[0]], recv_sem=recv_b.at[my_plane],
            device_id=peer, device_id_type=MESH)

    def plane_arrival(i):
        peer = along(i)
        return pltpu.make_async_remote_copy(
            src_ref=planes.at[my_plane], dst_ref=planes.at[peer[0]],
            send_sem=send_b.at[peer[0]], recv_sem=recv_b.at[peer[0]],
            device_id=peer, device_id_type=MESH)

    def loss_copy(i):
        peer = along(i)
        return pltpu.make_async_remote_copy(
            src_ref=loss_ref, dst_ref=losses.at[my_plane],
            send_sem=send_d.at[peer[0]], recv_sem=recv_d.at[my_plane],
            device_id=peer, device_id_type=MESH)

    def loss_arrival(i):
        peer = along(i)
        return pltpu.make_async_remote_copy(
            src_ref=loss_ref, dst_ref=losses.at[peer[0]],
            send_sem=send_d.at[peer[0]], recv_sem=recv_d.at[peer[0]],
            device_id=peer, device_id_type=MESH)

    def total_copy(j):
        peer = across(j)
        return pltpu.make_async_remote_copy(
            src_ref=total.at[me], dst_ref=total.at[me],
            send_sem=send_c.at[peer[1]], recv_sem=recv_c.at[me],
            device_id=peer, device_id_type=MESH)

    def total_arrival(j):
        peer = across(j)
        return pltpu.make_async_remote_copy(
            src_ref=total.at[me], dst_ref=total.at[peer[1]],
            send_sem=send_c.at[peer[1]], recv_sem=recv_c.at[peer[1]],
            device_id=peer, device_id_type=MESH)

    @pl.loop(1, vocab_size)
    def _(j):
        part_copy(j).start()

    @pl.loop(1, dp_size)
    def _(i):
        loss_copy(i).start()

    losses[my_plane] = loss_ref[...]
    parts[me] = grad_ref[me]

    @pl.loop(1, vocab_size)
    def _(j):
        part_arrival(j).wait_recv()

    planes[my_plane] = lax.fori_loop(
        1, vocab_size, lambda j, held: held + parts[j], parts[0])

    @pl.loop(1, dp_size)
    def _(i):
        plane_copy(i).start()

    @pl.loop(1, dp_size)
    def _(i):
        plane_arrival(i).wait_recv()

    total[me] = lax.fori_loop(1, dp_size, lambda i, held: held + planes[i], planes[0])

    @pl.loop(1, vocab_size)
    def _(j):
        total_copy(j).start()

    @pl.loop(1, vocab_size)
    def _(j):
        part_copy(j).wait_send()

    @pl.loop(1, dp_size)
    def _(i):
        plane_copy(i).wait_send()

    @pl.loop(1, vocab_size)
    def _(j):
        total_arrival(j).wait_recv()

    @pl.loop(1, vocab_size)
    def _(j):
        total_copy(j).wait_send()

    def squares(j, held):
        piece = total[j]
        return held + piece * piece

    gathered = lax.fori_loop(0, vocab_size, squares, jnp.zeros(parts.shape[1:], jnp.float32))
    norm = jnp.sqrt(jnp.sum(gathered, keepdims=True))
    norm_out[...] = norm

    @pl.loop(1, dp_size)
    def _(i):
        loss_arrival(i).wait_recv()
        loss_copy(i).wait_send()

    loss_out[...] = jnp.sum(losses[...], axis=0)[0:1, 0:1]
    shrink = GRAD_CLIP / jnp.maximum(norm, GRAD_CLIP)

    @pl.loop(0, vocab_size)
    def _(j):
        weight, first, second = adaptive_moment_update(
            total[j] * shrink, weight_ref[j], first_ref[j], second_ref[j])
        weight_out[j] = weight
        first_out[j] = first
        second_out[j] = second


def reduce_and_update(mesh_sizes, local_grad, weights, first, second, loss):
    dp_size, vocab_size = mesh_sizes
    number = local_grad.size
    rows = number // (128 * vocab_size)
    shape = (vocab_size, rows, 128)
    block = pltpu.VMEM(shape, jnp.float32)
    whole = pl.BlockSpec(memory_space=pltpu.VMEM)
    weight_new, first_new, second_new, norm, total_loss = pl.pallas_call(
        partial(sum_and_step, dp_size, vocab_size),
        out_shape=[jax.ShapeDtypeStruct(shape, jnp.float32)] * 3
        + [jax.ShapeDtypeStruct((1, 1), jnp.float32)] * 2,
        in_specs=[whole] * 5,
        out_specs=[whole] * 5,
        scratch_shapes=[
            block,
            pltpu.VMEM((dp_size, rows, 128), jnp.float32),
            block,
            pltpu.VMEM((dp_size, 8, 128), jnp.float32),
            pltpu.SemaphoreType.DMA((vocab_size,)),
            pltpu.SemaphoreType.DMA((vocab_size,)),
            pltpu.SemaphoreType.DMA((dp_size,)),
            pltpu.SemaphoreType.DMA((dp_size,)),
            pltpu.SemaphoreType.DMA((vocab_size,)),
            pltpu.SemaphoreType.DMA((vocab_size,)),
            pltpu.SemaphoreType.DMA((dp_size,)),
            pltpu.SemaphoreType.DMA((dp_size,)),
        ],
        compiler_params=pltpu.CompilerParams(
            collective_id=5, has_side_effects=True, vmem_limit_bytes=24 << 20
        ),
        name="sum_and_step",
    )(*[piece.reshape(shape) for piece in (local_grad, weights, first, second)], loss)
    flat = [piece.reshape(-1) for piece in (weight_new, first_new, second_new)]
    return (*flat, norm.reshape(()), total_loss.reshape(()))


TILE = 32


def head_step(dp_size, vocab_size, block, owned, hf_ref, label_ref, count_ref, table_hbm, grad_out, loss_out,
              table, hf_all, label_all, exps, exps_rest, tops, run_top, run_sum, run_smooth,
              run_goal, offset, z_even, z_odd, z_rest, dz_even, dz_odd, rest_even, rest_odd,
              acc_even, acc_odd, lse_tile, share_tile, stats_all,
              from_core, from_chip, leaving,
              table_sem, label_send, label_recv, hf_send, hf_recv,
              stat_send, stat_recv, core_send, core_recv, chip_send, chip_recv):
    plane = lax.axis_index("dp")
    me = lax.axis_index("vocab")
    chips = vocab_size // 2
    chip = me // 2
    core = lax.rem(me, 2)
    other = 2 * chip + 1 - core
    sibling = (plane, other)
    held = table_hbm.shape[0]
    full = held // block
    rest = held - full * block
    padded = table.shape[0] - full * block
    base = me * owned
    rows_each = hf_ref.shape[0]
    pair = 2 * rows_each
    width = hf_ref.shape[1]

    def partner(k):
        out = 0
        bit = 1
        while bit < chips:
            out = out + lax.rem(chip // bit + lax.rem(k // bit, 2), 2) * bit
            bit *= 2
        return out

    def across(j):
        return (plane, lax.rem(me + j, vocab_size))

    def table_copy(j, number):
        rows = pl.ds(pl.multiple_of(j * block, 16), number)
        return pltpu.make_async_copy(table_hbm.at[rows], table.at[rows], table_sem.at[j])

    @pl.loop(0, full)
    def _(j):
        table_copy(j, block).start()

    table_copy(full, rest).start()

    table[held:, :] = jnp.zeros((padded - rest, width), jnp.bfloat16)
    barrier = pltpu.get_barrier_semaphore()

    @pl.loop(1, vocab_size)
    def _(j):
        pl.semaphore_signal(barrier, inc=1, device_id=across(j), device_id_type=MESH)

    pl.semaphore_wait(barrier, vocab_size - 1)

    def remote(src, dst, send, recv, peer):
        return pltpu.make_async_remote_copy(
            src_ref=src, dst_ref=dst, send_sem=send, recv_sem=recv,
            device_id=peer, device_id_type=MESH)

    def hf_to_sibling():
        return remote(hf_ref, hf_all.at[me], hf_send.at[0], hf_recv.at[me], sibling)

    def hf_copy(k):
        return remote(hf_ref, hf_all.at[me], hf_send.at[k], hf_recv.at[me],
                      (plane, 2 * partner(k) + core))

    def hf_arrival(source):
        return remote(hf_ref, hf_all.at[source], hf_send.at[0], hf_recv.at[source], sibling)

    def hf_forward(k):
        source = 2 * partner(k) + core
        return remote(hf_all.at[source], hf_all.at[source], hf_send.at[chips + k],
                      hf_recv.at[source], sibling)

    def label_copy(j):
        peer = across(j)
        return remote(label_ref, label_all.at[me], label_send.at[peer[1]], label_recv.at[me], peer)

    def label_arrival(source):
        return remote(label_ref, label_all.at[source], label_send.at[source],
                      label_recv.at[source], sibling)

    near = min(3, chips)
    hf_to_sibling().start()

    @pl.loop(1, near)
    def _(k):
        hf_copy(k).start()

    @pl.loop(1, vocab_size)
    def _(j):
        label_copy(j).start()

    hf_all[me] = hf_ref[...]
    label_all[me] = label_ref[...]
    lanes = lax.broadcasted_iota(jnp.int32, (pair, 128), 1)

    def label_row(c, i):
        rows = label_all[pl.ds(2 * c, 2), i : i + 1, :].astype(jnp.float32)
        return jnp.concatenate([rows[0], rows[1]], axis=1)

    def set_offset(c):
        offset[...] = lane_columns(label_row(c, 0)).astype(jnp.int32) - base - lanes

    def folded(x):
        return sum(x[:, i * 128 : (i + 1) * 128] for i in range(1, x.shape[1] // 128)) + x[:, :128]

    def chunk_up(k, first):
        c = partner(k)
        if first:
            hf_arrival(other).wait_recv()
            label_arrival(other).wait_recv()
        else:
            hf_arrival(2 * c + core).wait_recv()
            hf_forward(k).start()
            label_arrival(2 * c).wait_recv()
            label_arrival(2 * c + 1).wait_recv()
            hf_arrival(2 * c + 1 - core).wait_recv()
        set_offset(c)
        run_top[...] = jnp.full((pair, 128), MASKED, jnp.float32)
        for ref in (run_sum, run_smooth, run_goal):
            ref[...] = jnp.zeros((pair, 128), jnp.float32)
        start = pl.multiple_of(k * pair, pair)

        def multiply(j, z_ref):
            if first:
                table_copy(j, rest if z_ref is z_rest else block).wait()
            rows = pl.ds(pl.multiple_of(j * block, 16), z_ref.shape[1])
            hidden = hf_all[pl.ds(2 * c, 2)].reshape(pair, width)
            z_ref[...] = matrix_multiply_transposed_right(hidden, table[rows, :])

        def reduce_full(j, z_ref):
            for r in range(pair // TILE):
                rows = slice(r * TILE, (r + 1) * TILE)
                there = pl.ds(start + r * TILE, TILE)
                z = z_ref[rows, :]
                old = run_top[rows, :]
                top = jnp.maximum(old, jnp.max(z, axis=1, keepdims=True))
                run_top[rows, :] = top
                tops[k, j, rows, :] = top
                gap = offset[rows, :] - j * block
                total = jnp.zeros((TILE, 128), jnp.float32)
                smooth = jnp.zeros((TILE, 128), jnp.float32)
                goal = jnp.zeros((TILE, 128), jnp.float32)
                for i in range(block // 128):
                    part = slice(i * 128, (i + 1) * 128)
                    piece = z[:, part]
                    e = jnp.exp(piece - top)
                    exps[j, there, part] = e
                    total = total + e
                    smooth = smooth + piece
                    goal = goal + jnp.where(gap == i * 128, piece, 0.0)
                run_sum[rows, :] = run_sum[rows, :] * jnp.exp(old - top) + total
                run_smooth[rows, :] = run_smooth[rows, :] + smooth
                run_goal[rows, :] = run_goal[rows, :] + goal

        def reduce_rest():
            for r in range(pair // TILE):
                rows = slice(r * TILE, (r + 1) * TILE)
                there = pl.ds(start + r * TILE, TILE)
                spot = lanes[rows, :]
                limit = jnp.minimum(VOCAB_SIZE - base, owned) - full * block - spot
                gap = offset[rows, :] - full * block
                pieces = []
                for i in range(padded // 128):
                    piece = z_rest[rows, i * 128 : (i + 1) * 128]
                    pieces.append((i * 128 < limit, piece))
                highest = jnp.where(pieces[0][0], pieces[0][1], MASKED)
                for valid, piece in pieces[1:]:
                    highest = jnp.maximum(highest, jnp.where(valid, piece, MASKED))
                old = run_top[rows, :]
                top = jnp.maximum(old, jnp.max(highest, axis=1, keepdims=True))
                run_top[rows, :] = top
                tops[k, full, rows, :] = top
                total = jnp.zeros((TILE, 128), jnp.float32)
                smooth = jnp.zeros((TILE, 128), jnp.float32)
                goal = jnp.zeros((TILE, 128), jnp.float32)
                for i, (valid, piece) in enumerate(pieces):
                    e = jnp.where(valid, jnp.exp(piece - top), 0.0)
                    exps_rest[there, i * 128 : (i + 1) * 128] = e
                    total = total + e
                    smooth = smooth + jnp.where(valid, piece, 0.0)
                    goal = goal + jnp.where(valid & (gap == i * 128), piece, 0.0)
                run_sum[rows, :] = run_sum[rows, :] * jnp.exp(old - top) + total
                run_smooth[rows, :] = run_smooth[rows, :] + smooth
                run_goal[rows, :] = run_goal[rows, :] + goal

        multiply(0, z_even)
        turns = (full - 1) // 2

        if turns > 0:
            @pl.loop(0, turns)
            def _(t):
                multiply(2 * t + 1, z_odd)
                reduce_full(2 * t, z_even)
                multiply(2 * t + 2, z_even)
                reduce_full(2 * t + 1, z_odd)

        if full - 2 * turns == 2:
            multiply(full - 1, z_odd)
            reduce_full(full - 2, z_even)
            multiply(full, z_rest)
            reduce_full(full - 1, z_odd)
        else:
            multiply(full, z_rest)
            reduce_full(full - 1, z_even)
        reduce_rest()

        def row_sum(ref):
            return jnp.sum(ref[...].T, axis=0, keepdims=True)

        ids = lax.broadcasted_iota(jnp.int32, (8, pair), 0)
        packed = jnp.where(ids == 0, run_top[...].T[0:1, :], 0.0)
        for i, ref in enumerate((run_sum, run_smooth, run_goal)):
            packed = jnp.where(ids == i + 1, row_sum(ref), packed)
        stats_all[me, c] = packed

    chunk_up(0, True)

    @pl.loop(near, chips)
    def _(k):
        hf_copy(k).start()

    @pl.loop(1, chips)
    def _(k):
        chunk_up(k, False)

    def stat_copy(j):
        peer = across(j)
        return remote(stats_all.at[me], stats_all.at[me], stat_send.at[peer[1]],
                      stat_recv.at[me], peer)

    def stat_arrival(j):
        source = across(j)[1]
        return remote(stats_all.at[me], stats_all.at[source], stat_send.at[source],
                      stat_recv.at[source], across(j))

    @pl.loop(1, vocab_size)
    def _(j):
        stat_copy(j).start()

    @pl.loop(1, vocab_size)
    def _(j):
        stat_arrival(j).wait_recv()

    count = jnp.maximum(count_ref[1:2, 0:1], 1.0)

    def totals_of(c):
        here = stats_all[:, c]
        tops_here = here[:, 0:1, :]
        top = jnp.max(tops_here, axis=0)
        total = jnp.sum(here[:, 1:2, :] * jnp.exp(tops_here - top[None]), axis=0)
        return top + jnp.log(total), jnp.sum(here[:, 2:3, :], axis=0), jnp.sum(
            here[:, 3:4, :], axis=0)

    def chunk_loss(c, held_loss):
        lse, smooth, goal = totals_of(c)
        return held_loss + label_row(c, 1) * (lse - 0.9 * goal - 0.1 * smooth / VOCAB_SIZE)

    slots = from_core.shape[0]
    columns_each = width // 4

    def core_copy(k, n, acc):
        half = pl.ds(pl.multiple_of((1 - core) * rows_each, rows_each), rows_each)
        part = pl.ds(pl.multiple_of(n * columns_each, columns_each), columns_each)
        return remote(acc.at[half, part], from_core.at[lax.rem(k, slots), :, part],
                      core_send.at[k, n], core_recv.at[k, n], sibling)

    def chip_copy(k):
        return remote(leaving.at[k - 1], from_chip.at[k - 1], chip_send.at[k], chip_recv.at[k],
                      (plane, 2 * partner(k) + core))

    def prepare(k):
        c = partner(k)
        lse, _, _ = totals_of(c)
        lse_tile[...] = lane_columns(lse)
        share_tile[...] = lane_columns(label_row(c, 1) / count)
        set_offset(c)

    quarter = pair // 4

    def grads(k, n, dz_ref, rest_ref):
        for r in range(quarter // TILE):
            first = pl.multiple_of(n * quarter + r * TILE, TILE)
            rows = pl.ds(first, TILE)
            there = pl.ds(pl.multiple_of(k * pair + first, TILE), TILE)
            share = share_tile[rows, :]
            lse = lse_tile[rows, :]
            low = share * (0.1 / VOCAB_SIZE)
            high = low + 0.9 * share
            gap = offset[rows, :]
            for j in range(full):
                factor = share * jnp.exp(tops[k, j, rows, :] - lse)
                for i in range(block // 128):
                    at = j * block + i * 128
                    e = exps[j, there, i * 128 : (i + 1) * 128]
                    dz = e * factor - jnp.where(gap == at, high, low)
                    dz_ref[rows, at : at + 128] = dz.astype(jnp.bfloat16)
            factor = share * jnp.exp(tops[k, full, rows, :] - lse)
            limit = jnp.minimum(VOCAB_SIZE - base, owned) - full * block - lanes[0:TILE, :]
            for i in range(padded // 128):
                part = slice(i * 128, (i + 1) * 128)
                at = full * block + i * 128
                dz = exps_rest[there, part] * factor - jnp.where(gap == at, high, low)
                rest_ref[rows, part] = jnp.where(i * 128 < limit, dz, 0.0).astype(jnp.bfloat16)

    def gather(k, n, dz_ref, rest_ref, acc):
        part = pl.ds(pl.multiple_of(n * columns_each, columns_each), columns_each)
        acc[:, part] = matrix_multiply(
            dz_ref[...], table[pl.ds(0, full * block), part]
        ) + matrix_multiply(rest_ref[...], table[pl.ds(full * block, padded), part])

    def finish(k, acc):
        for n in range(4):
            core_copy(k, n, acc).wait()
        own = pl.ds(pl.multiple_of(core * rows_each, rows_each), rows_each)
        return from_core[lax.rem(k, slots)] + acc[own, :]

    def stage(k, now, later, acc, acc_before, last):
        if later is not None:
            prepare(k - 1)

        @pl.loop(0, 4)
        def _(n):
            gather(k, n, *now, acc)
            if later is not None:
                grads(k - 1, n, *later)
            core_copy(k, n, acc).start()
            if acc_before is not None:
                @pl.when((n == 0) & (k < chips - 1))
                def _():
                    leaving[k] = finish(k + 1, acc_before).astype(jnp.bfloat16)
                    chip_copy(k + 1).start()

    evens = ((dz_even, rest_even), acc_even)
    odds = ((dz_odd, rest_odd), acc_odd)
    prepare(chips - 1)

    @pl.loop(0, 4)
    def _(n):
        grads(chips - 1, n, *odds[0])

    @pl.loop(0, chips // 2 - 1)
    def _(t):
        k = chips - 1 - 2 * t
        stage(k, odds[0], evens[0], acc_odd, acc_even, False)
        stage(k - 1, evens[0], odds[0], acc_even, acc_odd, False)

    stage(1, odds[0], evens[0], acc_odd, acc_even if chips > 2 else None, False)
    stage(0, evens[0], None, acc_even, acc_odd, True)

    loss = lax.fori_loop(0, chips, chunk_loss, jnp.zeros((1, pair), jnp.float32))
    loss_out[...] = jnp.broadcast_to(jnp.sum(loss, keepdims=True) / count, loss_out.shape)
    grad_out[...] = finish(0, acc_even)

    @pl.loop(1, chips)
    def _(k):
        chip_copy(k).wait_recv()
        grad_out[...] += from_chip[k - 1].astype(jnp.float32)

    hf_to_sibling().wait_send()

    @pl.loop(1, chips)
    def _(k):
        hf_copy(k).wait_send()
        hf_forward(k).wait_send()
        chip_copy(k).wait_send()

    @pl.loop(1, vocab_size)
    def _(j):
        label_copy(j).wait_send()
        stat_copy(j).wait_send()


def head(mesh_sizes, owned, final_rows, labels, counts, table):
    dp_size, vocab_size = mesh_sizes
    rows, width = final_rows.shape
    held = table.shape[0]
    block = 1024
    full = held // block
    rest = -(-(held - full * block) // 128) * 128
    chips = vocab_size // 2
    pair = 2 * rows
    low, wide = jnp.bfloat16, jnp.float32
    whole = pl.BlockSpec(memory_space=pltpu.VMEM)
    dma = pltpu.SemaphoreType.DMA
    tile = pltpu.VMEM((pair, 128), wide)
    grad, loss = pl.pallas_call(
        partial(head_step, dp_size, vocab_size, block, owned),
        out_shape=[
            jax.ShapeDtypeStruct((rows, width), wide),
            jax.ShapeDtypeStruct((8, 128), wide),
        ],
        in_specs=[whole, whole, whole, pl.BlockSpec(memory_space=pl.ANY)],
        out_specs=[whole, whole],
        scratch_shapes=[
            pltpu.VMEM((full * block + rest, width), low),
            pltpu.VMEM((vocab_size, rows, width), low),
            pltpu.VMEM((vocab_size, 8, rows), jnp.int32),
            pltpu.VMEM((full, vocab_size * rows, block), wide),
            pltpu.VMEM((vocab_size * rows, rest), wide),
            pltpu.VMEM((chips, full + 1, pair, 128), wide),
            tile,
            tile,
            tile,
            tile,
            pltpu.VMEM((pair, 128), jnp.int32),
            pltpu.VMEM((pair, block), wide),
            pltpu.VMEM((pair, block), wide),
            pltpu.VMEM((pair, rest), wide),
            pltpu.VMEM((pair, full * block), low),
            pltpu.VMEM((pair, full * block), low),
            pltpu.VMEM((pair, rest), low),
            pltpu.VMEM((pair, rest), low),
            pltpu.VMEM((pair, width), wide),
            pltpu.VMEM((pair, width), wide),
            tile,
            tile,
            pltpu.VMEM((vocab_size, chips, 8, pair), wide),
            pltpu.VMEM((3, rows, width), wide),
            pltpu.VMEM((chips - 1, rows, width), low),
            pltpu.VMEM((chips - 1, rows, width), low),
            dma((full + 1,)),
            dma((vocab_size,)),
            dma((vocab_size,)),
            dma((2 * chips,)),
            dma((vocab_size,)),
            dma((vocab_size,)),
            dma((vocab_size,)),
            dma((chips, 4)),
            dma((chips, 4)),
            dma((chips,)),
            dma((chips,)),
        ],
        compiler_params=pltpu.CompilerParams(
            collective_id=3, has_side_effects=True, vmem_limit_bytes=63 << 20
        ),
        name="head_step",
    )(final_rows, labels, counts, table)
    return grad, loss


NARROW = 16
PARTS = (0, 96, 192, 224, 256, 288, 416, 544, 576)


def floor_part(values, size):
    return jnp.floor((values + 0.5) * (1.0 / size))


def spread_places(ranks, slab):
    lanes = lax.broadcasted_iota(jnp.int32, (1024, 128), 1).astype(jnp.float32) + 128.0 * slab
    rows = lax.broadcasted_iota(jnp.int32, (1024, 128), 0).astype(jnp.float32)
    return floor_part(lanes, ranks) == rows - 32.0 * floor_part(rows, 32)


def unpack_down(flat_ref, first, ranks, out_ref, start):
    slabs = ranks // RANK
    total = None
    for slab in range(slabs):
        packed = flat_ref[pl.ds(first + slab, 32, stride=slabs), :]
        spread = jnp.broadcast_to(packed[:, None, :], (32, 32, 128)).reshape(1024, 128)
        spread = jnp.where(spread_places(ranks, slab), spread, 0.0).astype(jnp.bfloat16)
        lanes = lax.broadcasted_iota(jnp.int32, (128, NARROW), 0).astype(jnp.float32) + 128.0 * slab
        column = lax.broadcasted_iota(jnp.int32, (128, NARROW), 1).astype(jnp.float32)
        chosen = low_ones(lanes - ranks * floor_part(lanes, ranks) == column)
        part = matrix_multiply(spread, chosen)
        total = part if total is None else total + part
    out_ref[pl.ds(start, 1024), :] = total.astype(jnp.bfloat16)


def unpack_up(flat_ref, first, ranks, out_ref):
    wide = out_ref.shape[1] // 128
    for c in range(wide):
        rows = flat_ref[pl.ds(first + c, ranks, stride=wide), :]
        rows = jnp.concatenate([rows, jnp.zeros((NARROW - ranks, 128), jnp.float32)], axis=0)
        out_ref[:, c * 128 : (c + 1) * 128] = rows.astype(jnp.bfloat16)


def unpack(flat_ref, outs):
    for i, out_ref in enumerate(outs):
        ranks = 3 * RANK if i < 2 else RANK
        if i % 2:
            unpack_up(flat_ref, PARTS[i], ranks, out_ref)
        else:
            for b in range(out_ref.shape[0] // 1024):
                unpack_down(flat_ref, PARTS[i] + 32 * b, ranks, out_ref, 1024 * b)


def lane_columns(row):
    return jnp.broadcast_to(row, (128, row.shape[1])).T


def ones_where(condition):
    return jnp.where(condition, 1.0, 0.0)


def low_ones(condition):
    return ones_where(condition).astype(jnp.bfloat16)


def embed_step(dp_size, vocab_size, block, room, owned, token_ref, segment_ref, spot_ref, flag_ref,
               place_hbm, affine_ref, flat_ref, table_hbm,
               h1_out, rows_out, label_out, full_out, crowd_out,
               a_qkv, b_qkv, a_o, b_o, a_fc, b_fc, a_p, b_p,
               table, place_table, key_cols, unique_cols, slot_cols, owners, asked, lists, lists_in,
               acc, leaving, arriving, stream, full_all,
               table_sem, place_sem, list_send, list_recv, row_send, row_recv, full_send, full_recv):
    plane = lax.axis_index("dp")
    me = lax.axis_index("vocab")
    chips = vocab_size // 2
    chip = me // 2
    held = table.shape[0]
    full = held // block
    rest = held - full * block
    length = token_ref.shape[1]
    width = table.shape[1]
    spots_here = spot_ref.shape[1]
    chunk = 128
    chunks = length // chunk

    def partner(k):
        out = 0
        bit = 1
        while bit < chips:
            out = out + lax.rem(chip // bit + (k // bit) % 2, 2) * bit
            bit *= 2
        return out

    def across(j):
        return (plane, lax.rem(me + j, vocab_size))

    def along(i):
        return (lax.rem(plane + i, dp_size), me)

    def remote(src, dst, send, recv, peer):
        return pltpu.make_async_remote_copy(
            src_ref=src, dst_ref=dst, send_sem=send, recv_sem=recv,
            device_id=peer, device_id_type=MESH)

    def table_copy(j, number):
        rows = pl.ds(pl.multiple_of(j * block, 16), number)
        return pltpu.make_async_copy(table_hbm.at[rows], table.at[rows], table_sem.at[j])

    @pl.loop(0, full)
    def _(j):
        table_copy(j, block).start()

    table_copy(full, rest).start()

    place_copy = pltpu.make_async_copy(
        place_hbm.at[pl.ds(0, place_table.shape[0])], place_table, place_sem)
    place_copy.start()
    barrier = pltpu.get_barrier_semaphore()

    @pl.loop(1, vocab_size)
    def _(j):
        pl.semaphore_signal(barrier, inc=1, device_id=across(j), device_id_type=MESH)

    @pl.loop(1, dp_size)
    def _(i):
        pl.semaphore_signal(barrier, inc=1, device_id=along(i), device_id_type=MESH)

    token = token_ref[...].astype(jnp.float32)
    segment = segment_ref[...].astype(jnp.float32)
    steps = lax.broadcasted_iota(jnp.int32, (1, length), 1).astype(jnp.float32)
    spot = lane_columns(spot_ref[...].astype(jnp.float32))[:, 0:1]
    flag = lane_columns(flag_ref[...].astype(jnp.float32))[:, 0:1]
    at_spot = steps == spot
    at_next = steps == spot + 1.0

    def picked(where_to, row):
        return jnp.sum(jnp.where(where_to, row, 0.0), axis=1, keepdims=True)

    segment_here = picked(at_spot, segment)
    weight = jnp.where(segment_here == picked(at_next, segment), flag, 0.0)
    heavy = jnp.sum(weight, axis=0, keepdims=True)
    target = picked(at_next, token)
    lanes = lax.broadcasted_iota(jnp.int32, (spots_here, 128), 1)
    label_tile = jnp.where(lanes == 0, target, jnp.where(lanes == 1, weight, 0.0))
    label_out[...] = label_tile.T[0:8, :].astype(jnp.int32)
    read = (steps <= spot) & (segment == segment_here) & (weight > 0.0)
    needed = jnp.max(ones_where(read), axis=0, keepdims=True) > 0.0

    key = jnp.where(needed, token, -1.0 - steps)
    key_cols[...] = lane_columns(key)

    def places(a):
        return (lax.broadcasted_iota(jnp.int32, (chunk, 1), 0) + a * chunk).astype(jnp.float32)

    def rows_at(a):
        return pl.ds(pl.multiple_of(a * chunk, chunk), chunk)

    def same(a):
        return key_cols[rows_at(a), 0:1] == key

    def seen(a, carry):
        return jnp.maximum(carry, jnp.max(
            ones_where(same(a) & (places(a) < steps)), axis=0, keepdims=True))

    again = lax.fori_loop(0, chunks, seen, jnp.zeros((1, length), jnp.float32))
    unique = ones_where(needed & (again == 0.0))
    unique_cols[...] = lane_columns(unique)
    owner = jnp.zeros((1, length), jnp.float32)
    for j in range(1, vocab_size):
        owner = owner + ones_where(token >= float(j * owned))
    owner_ids = lax.broadcasted_iota(jnp.int32, (vocab_size, length), 0).astype(jnp.float32)
    mine = jnp.where(owner_ids == owner, unique, 0.0)
    owners[...] = mine

    def ahead(a, carry):
        before = low_ones(places(a) < steps)
        return carry + matrix_multiply(owners[:, rows_at(a)].astype(jnp.bfloat16), before)

    ranks = lax.fori_loop(0, chunks, ahead, jnp.zeros((vocab_size, length), jnp.float32))
    rank = jnp.sum(jnp.where(owner_ids == owner, ranks, 0.0), axis=0, keepdims=True)
    too_many = jnp.max(unique * ones_where(rank >= float(room)), axis=1, keepdims=True)
    local_id = token - owner * float(owned)
    local_high = jnp.floor(local_id * (1.0 / 128.0))
    local_low = local_id - 128.0 * local_high
    row_ids = lax.broadcasted_iota(jnp.int32, (8, length), 0)

    def stacked(first, second):
        return jnp.where(row_ids == 0, first, jnp.where(row_ids == 1, second, 0.0))

    asked[...] = stacked(owner, jnp.minimum(rank, 127.0))

    def found(a, carry):
        match = low_ones(same(a) & (unique_cols[rows_at(a), 0:1] > 0.0))
        return carry + matrix_multiply(asked[:, rows_at(a)].astype(jnp.bfloat16), match)

    slots = lax.fori_loop(0, chunks, found, jnp.zeros((8, length), jnp.float32))
    slot = jnp.where(needed, slots[0:1, :] * 128.0 + slots[1:2, :], -1.0)
    slot_cols[...] = lane_columns(slot)
    local_parts = stacked(local_high, local_low).astype(jnp.bfloat16)
    rank_ids = lax.broadcasted_iota(jnp.int32, (128, length), 0).astype(jnp.float32)
    list_rows = lax.broadcasted_iota(jnp.int32, (8, 128), 0)

    @pl.loop(0, vocab_size)
    def _(j):
        theirs = (unique > 0.0) & (owner == j.astype(jnp.float32))
        chosen = low_ones(rank_ids == jnp.where(theirs, rank, -1.0))
        ids = matrix_multiply_transposed_right(local_parts, chosen)
        lists[j] = jnp.where(list_rows == 2, too_many, jnp.where(list_rows == 3, heavy, ids))

    @pl.loop(0, vocab_size)
    def _(j):
        arriving[j] = jnp.zeros(arriving.shape[1:], jnp.bfloat16)

    pl.semaphore_wait(barrier, vocab_size + dp_size - 2)

    def list_copy(j):
        peer = across(j)
        return remote(lists.at[peer[1]], lists_in.at[me], list_send.at[peer[1]],
                      list_recv.at[me], peer)

    def list_arrival(j):
        source = across(j)[1]
        return remote(lists.at[source], lists_in.at[source], list_send.at[source],
                      list_recv.at[source], across(j))

    @pl.loop(1, vocab_size)
    def _(j):
        list_copy(j).start()

    lists_in[me] = lists[me]

    ids = lax.broadcasted_iota(jnp.int32, (32, length), 0).astype(jnp.float32)
    starts = jnp.sum(ones_where(segment < ids), axis=1, keepdims=True)
    place = steps - jnp.sum(jnp.where(segment == ids, starts, 0.0), axis=0, keepdims=True)
    place_cols = lane_columns(place)[:, 0:1]
    span = place_table.shape[0]
    place_copy.wait()
    place_ids = lax.broadcasted_iota(jnp.int32, (length, span), 1).astype(jnp.float32)
    stream[...] = matrix_multiply(low_ones(place_ids == place_cols), place_table[...])
    spot_place = picked(at_spot, place)
    spot_slot = picked(at_spot, slot)
    unpack(flat_ref, (a_qkv, b_qkv, a_o, b_o, a_fc, b_fc, a_p, b_p))

    @pl.loop(1, vocab_size)
    def _(j):
        list_arrival(j).wait_recv()

    full_all[plane] = jnp.where(
        list_rows == 0, jnp.max(lists_in[:, 2:3, 0:1], axis=0),
        jnp.sum(lists_in[:, 3:4, 0:1], axis=0))

    def full_copy(i):
        peer = along(i)
        return remote(full_all.at[plane], full_all.at[plane], full_send.at[peer[0]],
                      full_recv.at[plane], peer)

    def full_arrival(i):
        source = along(i)[0]
        return remote(full_all.at[plane], full_all.at[source], full_send.at[source],
                      full_recv.at[source], along(i))

    @pl.loop(1, dp_size)
    def _(i):
        full_copy(i).start()

    def row_copy(d):
        return remote(leaving.at[d], arriving.at[me, pl.ds(0, room)], row_send.at[d],
                      row_recv.at[me], (plane, d))

    def row_arrival(d):
        return remote(leaving.at[d], arriving.at[d, pl.ds(0, room)], row_send.at[d],
                      row_recv.at[d], (plane, d))

    def wanted(d):
        here = lists_in[d]
        return lane_columns(here[0:1, :] * 128.0 + here[1:2, :])[0:room, 0:1]

    first = True
    for k in range(chips - 1, -1, -1):
        c = partner(k)
        wanted_here = jnp.concatenate([wanted(2 * c), wanted(2 * c + 1)], axis=0)

        def rows_of(j, number):
            if first:
                table_copy(j, number).wait()
            ids_here = (lax.broadcasted_iota(jnp.int32, (2 * room, number), 1)
                        + j * block).astype(jnp.float32)
            rows = pl.ds(pl.multiple_of(j * block, 16), number)
            return matrix_multiply(low_ones(ids_here == wanted_here), table[rows, :])

        acc[...] = rows_of(full, rest)

        @pl.loop(0, full)
        def _(j):
            acc[...] += rows_of(j, block)

        first = False
        for i in range(2):
            leaving[2 * c + i] = acc[pl.ds(i * room, room), :].astype(jnp.bfloat16)
        if k > 0:
            for i in range(2):
                row_copy(2 * c + i).start()
        else:
            row_copy(2 * c + 1 - lax.rem(me, 2)).start()
            arriving[me, pl.ds(0, room), :] = leaving[me]

    for k in range(chips):
        c = partner(k)
        if k > 0:
            for i in range(2):
                row_arrival(2 * c + i).wait_recv()
        else:
            row_arrival(2 * c + 1 - lax.rem(me, 2)).wait_recv()
        pair_rows = arriving[pl.ds(2 * c, 2)].reshape(256, width)
        offset = (2 * c * 128).astype(jnp.float32)

        def spread(column, ids_like):
            ids_here = lax.broadcasted_iota(jnp.int32, ids_like, 1).astype(jnp.float32)
            return low_ones(ids_here + offset == column)

        stream[...] += matrix_multiply(spread(slot_cols[:, 0:1], (length, 256)), pair_rows)
        spot_rows = matrix_multiply(spread(spot_slot, (spots_here, 256)), pair_rows)
        if k == 0:
            rows_out[...] = spot_rows
        else:
            rows_out[...] += spot_rows

    spot_ids = lax.broadcasted_iota(jnp.int32, (spots_here, span), 1).astype(jnp.float32)
    rows_out[...] += matrix_multiply(low_ones(spot_ids == spot_place), place_table[...])

    @pl.loop(0, length // 256)
    def _(a):
        rows = pl.ds(pl.multiple_of(a * 256, 256), 256)
        h1_out[rows, :] = layer_norm(
            stream[rows, :], affine_ref[0:1, :], affine_ref[3:4, :]).astype(jnp.bfloat16)

    @pl.loop(1, dp_size)
    def _(i):
        full_arrival(i).wait_recv()

    counts = jnp.where(
        list_rows == 0, jnp.max(full_all[...], axis=0), jnp.sum(full_all[...], axis=0))
    full_out[...] = counts
    crowd_out[...] = counts[0:1, 0:1].astype(jnp.int32)

    @pl.loop(1, vocab_size)
    def _(j):
        list_copy(j).wait_send()

    @pl.loop(1, dp_size)
    def _(i):
        full_copy(i).wait_send()

    for k in range(chips):
        if k > 0:
            for i in range(2):
                row_copy(2 * partner(k) + i).wait_send()
        else:
            row_copy(2 * chip + 1 - lax.rem(me, 2)).wait_send()


def embed(mesh_sizes, owned, tokens, segments, spots, flags, place_table, affine, flat, table):
    dp_size, vocab_size = mesh_sizes
    length = tokens.shape[1]
    spots_here = spots.shape[1]
    held, width = table.shape
    block = 1024
    full = held // block
    chips = vocab_size // 2
    room = 112 if vocab_size <= 8 else 64
    span = 256
    whole = pl.BlockSpec(memory_space=pltpu.VMEM)
    dma = pltpu.SemaphoreType.DMA
    return pl.pallas_call(
        partial(embed_step, dp_size, vocab_size, block, room, owned),
        out_shape=[
            jax.ShapeDtypeStruct((length, width), jnp.bfloat16),
            jax.ShapeDtypeStruct((spots_here, width), jnp.float32),
            jax.ShapeDtypeStruct((8, spots_here), jnp.int32),
            jax.ShapeDtypeStruct((8, 128), jnp.float32),
            jax.ShapeDtypeStruct((1, 1), jnp.int32),
        ]
        + [
            jax.ShapeDtypeStruct(shape, jnp.bfloat16)
            for shape in (
                (width, NARROW), (NARROW, width), (width, NARROW), (NARROW, width),
                (width, NARROW), (NARROW, 4 * width), (4 * width, NARROW), (NARROW, width),
            )
        ],
        in_specs=[whole] * 4
        + [pl.BlockSpec(memory_space=pl.ANY), whole, whole, pl.BlockSpec(memory_space=pl.ANY)],
        out_specs=[whole] * 13,
        scratch_shapes=[
            pltpu.VMEM((held, width), jnp.bfloat16),
            pltpu.VMEM((span, width), jnp.bfloat16),
            pltpu.VMEM((length, 128), jnp.float32),
            pltpu.VMEM((length, 128), jnp.float32),
            pltpu.VMEM((length, 128), jnp.float32),
            pltpu.VMEM((vocab_size, length), jnp.float32),
            pltpu.VMEM((8, length), jnp.float32),
            pltpu.VMEM((vocab_size, 8, 128), jnp.float32),
            pltpu.VMEM((vocab_size, 8, 128), jnp.float32),
            pltpu.VMEM((2 * room, width), jnp.float32),
            pltpu.VMEM((vocab_size, room, width), jnp.bfloat16),
            pltpu.VMEM((vocab_size, 128, width), jnp.bfloat16),
            pltpu.VMEM((length, width), jnp.float32),
            pltpu.VMEM((dp_size, 8, 128), jnp.float32),
            dma((full + 1,)),
            dma,
            dma((vocab_size,)),
            dma((vocab_size,)),
            dma((vocab_size,)),
            dma((vocab_size,)),
            dma((dp_size,)),
            dma((dp_size,)),
        ],
        compiler_params=pltpu.CompilerParams(
            collective_id=1, has_side_effects=True, vmem_limit_bytes=60 << 20
        ),
        name="embed_step",
    )(tokens, segments, spots, flags, place_table, affine, flat.reshape(-1, 128), table)


def wide_loop(number, body):
    lax.fori_loop(0, number, lambda i, carry: (body(i), carry)[1], 0)


def norm_parts(rows):
    centred = rows - jnp.mean(rows, axis=-1, keepdims=True)
    return centred, lax.rsqrt(jnp.mean(centred * centred, axis=-1, keepdims=True) + NORM_EPS)


def norm_back(rows, gain, grad):
    centred, spread = norm_parts(rows)
    hat = centred * spread
    grad_hat = grad * gain
    return spread * (
        grad_hat
        - jnp.mean(grad_hat, axis=-1, keepdims=True)
        - hat * jnp.mean(grad_hat * hat, axis=-1, keepdims=True)
    )


GELU_RATE = math.sqrt(2.0 / math.pi)


def gelu_parts(pre):
    bend = jnp.tanh(GELU_RATE * (pre + 0.044715 * (pre * pre * pre)))
    return 0.5 * (1.0 + bend), bend


def gelu_slope(pre):
    half, bend = gelu_parts(pre)
    inner = GELU_RATE * (1.0 + 3.0 * 0.044715 * (pre * pre))
    return half + 0.5 * pre * (1.0 - bend * bend) * inner


def both_heads(pair):
    lanes = lax.broadcasted_iota(jnp.int32, pair.shape, 1)
    half = pair.shape[1] // 2
    wide = pair.astype(jnp.float32)
    return jnp.concatenate(
        [jnp.where(lanes < half, wide, 0.0), jnp.where(lanes < half, 0.0, wide)], axis=0
    ).astype(jnp.bfloat16)


def side_by_side(stacked):
    rows = stacked.shape[0] // 2
    lanes = lax.broadcasted_iota(jnp.int32, (rows, stacked.shape[1]), 1)
    return jnp.where(lanes < stacked.shape[1] // 2, stacked[:rows], stacked[rows:])


def third_of(rows, j):
    ids = lax.broadcasted_iota(jnp.int32, rows.shape, 0)
    wide = jnp.where((ids >= j * RANK) & (ids < (j + 1) * RANK), rows.astype(jnp.float32), 0.0)
    return wide.astype(jnp.bfloat16)


def attention_mask(spot_ref, segment_ref):
    spot = lane_columns(spot_ref[...].astype(jnp.float32))[:, 0:1]
    steps = lax.broadcasted_iota(jnp.int32, segment_ref.shape, 1).astype(jnp.float32)
    segment = segment_ref[...].astype(jnp.float32)
    here = jnp.sum(jnp.where(steps == spot, segment, 0.0), axis=1, keepdims=True)
    open_to = ones_where((steps <= spot) & (segment == here))
    return jnp.concatenate([open_to, open_to], axis=0)


def layer_up(h1_ref, rows_ref, segment_ref, spot_ref, affine_ref, bias_ref,
             a_qkv, b_qkv, a_o, b_o, a_fc, b_fc, a_p, b_p,
             qkv_hbm, o_hbm, in_hbm, out_hbm,
             final_ref, q_ref, k_ref, v_ref, u1_ref, u1_rows_ref, h1_rows_ref, lse_ref,
             o_ref, uo_ref, middle_ref, h2_ref, uf_ref, pre_ref, f_ref, up_ref, last_ref,
             wq, wk, wv, wo, win, wout, mask, sems):
    length, width = h1_ref.shape
    hidden = win.shape[1]
    quarter = hidden // 4

    def columns_of(source, j, number):
        return source.at[:, pl.ds(j * number, number)]

    copies = [
        pltpu.make_async_copy(columns_of(qkv_hbm, 1, width), wk, sems.at[0]),
        pltpu.make_async_copy(columns_of(qkv_hbm, 2, width), wv, sems.at[1]),
        pltpu.make_async_copy(columns_of(qkv_hbm, 0, width), wq, sems.at[2]),
        pltpu.make_async_copy(o_hbm, wo, sems.at[3]),
        pltpu.make_async_copy(in_hbm, win, sems.at[4]),
        pltpu.make_async_copy(out_hbm, wout, sems.at[5]),
    ]
    for copy in copies:
        copy.start()

    def bias(first, number):
        return bias_ref[0:1, first : first + number]

    mask[...] = attention_mask(spot_ref, segment_ref)
    h1_rows = layer_norm(rows_ref[...], affine_ref[0:1, :], affine_ref[3:4, :]).astype(
        jnp.bfloat16)
    h1_rows_ref[...] = h1_rows
    u1_ref[...] = matrix_multiply(h1_ref[...], a_qkv[...]).astype(jnp.bfloat16)
    u1_rows = matrix_multiply(h1_rows, a_qkv[...]).astype(jnp.bfloat16)
    u1_rows_ref[...] = u1_rows

    def project(normed, low, weight, j):
        return (
            matrix_multiply(normed, weight[...])
            + bias(j * width, width)
            + ADAPTER_SCALE * matrix_multiply(low, third_of(b_qkv[...], j))
        ).astype(jnp.bfloat16)

    chunk = 256
    for j, weight, out, copy in ((1, wk, k_ref, copies[0]), (2, wv, v_ref, copies[1])):
        copy.wait()

        def rows_of(i):
            rows = pl.ds(pl.multiple_of(i * chunk, chunk), chunk)
            out[rows, :] = project(h1_ref[rows, :], u1_ref[rows, :], weight, j)

        wide_loop(length // chunk, rows_of)
    copies[2].wait()
    q_ref[...] = project(h1_rows, u1_rows, wq, 0)
    scale = (width // HEADS) ** (-0.5)
    lanes = lax.broadcasted_iota(jnp.int32, lse_ref.shape, 1)
    lse_ref[...] = jnp.zeros(lse_ref.shape, jnp.float32)

    def heads(g):
        pair = pl.ds(pl.multiple_of(g * 128, 128), 128)
        scores = scale * matrix_multiply_transposed_right(both_heads(q_ref[:, pair]), k_ref[:, pair])
        scores = jnp.where(mask[...] > 0.0, scores, MASKED)
        top = jnp.max(scores, axis=1, keepdims=True)
        e = jnp.exp(scores - top)
        total = jnp.sum(e, axis=1, keepdims=True)
        probs = (e * (1.0 / total)).astype(jnp.bfloat16)
        o_ref[:, pair] = side_by_side(matrix_multiply(probs, v_ref[:, pair])).astype(jnp.bfloat16)
        lse_ref[...] = jnp.where(lanes == g, top + jnp.log(total), lse_ref[...])

    wide_loop(HEADS // 2, heads)
    o = o_ref[...]
    uo = matrix_multiply(o, a_o[...]).astype(jnp.bfloat16)
    uo_ref[...] = uo
    copies[3].wait()
    middle = (
        rows_ref[...]
        + matrix_multiply(o, wo[...])
        + bias(3 * width, width)
        + ADAPTER_SCALE * matrix_multiply(uo, b_o[...])
    )
    middle_ref[...] = middle
    h2 = layer_norm(middle, affine_ref[1:2, :], affine_ref[4:5, :]).astype(jnp.bfloat16)
    h2_ref[...] = h2
    uf = matrix_multiply(h2, a_fc[...]).astype(jnp.bfloat16)
    uf_ref[...] = uf
    copies[4].wait()
    for j in range(4):
        part = slice(j * quarter, (j + 1) * quarter)
        pre = (
            matrix_multiply(h2, win[:, part])
            + bias(4 * width + j * quarter, quarter)
            + ADAPTER_SCALE * matrix_multiply(uf, b_fc[:, part])
        )
        pre_ref[:, part] = pre
        f_ref[:, part] = (pre * gelu_parts(pre)[0]).astype(jnp.bfloat16)
    f = f_ref[...]
    up = matrix_multiply(f, a_p[...]).astype(jnp.bfloat16)
    up_ref[...] = up
    copies[5].wait()
    last = (
        middle
        + matrix_multiply(f, wout[...])
        + bias(4 * width + hidden, width)
        + ADAPTER_SCALE * matrix_multiply(up, b_p[...])
    )
    last_ref[...] = last
    final_ref[...] = layer_norm(last, affine_ref[2:3, :], affine_ref[5:6, :]).astype(jnp.bfloat16)


def pack_up(out_ref, part, grad):
    ranks = 3 * RANK if part < 2 else RANK
    wide = grad.shape[1] // 128
    for c in range(wide):
        rows = pl.ds(PARTS[part] + c, ranks, stride=wide)
        out_ref[rows, :] = grad[0:ranks, c * 128 : (c + 1) * 128]


def pack_down(out_ref, part, shift, grad):
    ranks = 3 * RANK if part < 2 else RANK
    slabs = ranks // RANK
    repeated = jnp.concatenate([grad[0:ranks]] * (128 * slabs // ranks), axis=0)
    for slab in range(slabs):
        spread = repeated[128 * slab : 128 * (slab + 1)].T
        spread = jnp.where(spread_places(ranks, slab), spread, 0.0)
        rows = pl.ds(PARTS[part] + shift + slab, 32, stride=slabs)
        out_ref[rows, :] = jnp.sum(spread.reshape(32, 32, 128), axis=1)


def layer_down(grad_ref, spot_ref, segment_ref, affine_ref, h1_ref,
               a_qkv, b_qkv, a_o, b_o, a_fc, b_fc, a_p, b_p,
               q_ref, k_ref, v_ref, u1_ref, u1_rows_ref, h1_rows_ref, lse_ref,
               o_ref, uo_ref, middle_ref, h2_ref, uf_ref, pre_ref, f_ref, up_ref, last_ref,
               o_hbm, in_hbm, out_hbm,
               grad_out,
               wo, win, wout, mask, dpre_ref, do_ref, dq_ref, dk_ref, dv_ref, sems):
    length, width = h1_ref.shape
    hidden = win.shape[1]
    quarter = hidden // 4
    rows_here = grad_ref.shape[0]
    copies = [
        pltpu.make_async_copy(out_hbm, wout, sems.at[0]),
        pltpu.make_async_copy(in_hbm, win, sems.at[1]),
        pltpu.make_async_copy(o_hbm, wo, sems.at[2]),
    ]
    for copy in copies:
        copy.start()
    mask[...] = attention_mask(spot_ref, segment_ref)
    spot_row = spot_ref[...].astype(jnp.float32)
    spot = lane_columns(spot_row)[:, 0:1]
    order_row = lax.broadcasted_iota(jnp.int32, (1, rows_here), 1)
    order = lax.broadcasted_iota(jnp.int32, (rows_here, 1), 0)
    same = spot == spot_row
    repeat = jnp.max(ones_where(same & (order_row < order)), axis=1, keepdims=True)
    merge = ones_where(same) * (1.0 - repeat)
    grad_final = jnp.dot(
        merge, grad_ref[...], precision=lax.Precision.HIGHEST,
        preferred_element_type=jnp.float32)
    dx3 = norm_back(last_ref[...], affine_ref[2:3, :], grad_final)
    dm = dx3.astype(jnp.bfloat16)
    pack_up(grad_out, 7, ADAPTER_SCALE * matrix_multiply_transposed_left(up_ref[...], dm))
    du_p = (ADAPTER_SCALE * matrix_multiply_transposed_right(dm, b_p[...])).astype(jnp.bfloat16)
    ga_p = matrix_multiply_transposed_left(du_p, f_ref[...])
    for b in range(hidden // 1024):
        pack_down(grad_out, 6, 32 * b, ga_p[:, 1024 * b : 1024 * (b + 1)])
    copies[0].wait()
    for j in range(4):
        part = slice(j * quarter, (j + 1) * quarter)
        df = matrix_multiply_transposed_right(dm, wout[part, :]) + matrix_multiply_transposed_right(
            du_p, a_p[part, :])
        dpre_ref[:, part] = (df * gelu_slope(pre_ref[:, part])).astype(jnp.bfloat16)
    dpre = dpre_ref[...]
    pack_up(grad_out, 5, ADAPTER_SCALE * matrix_multiply_transposed_left(uf_ref[...], dpre))
    du_f = (ADAPTER_SCALE * matrix_multiply_transposed_right(dpre, b_fc[...])).astype(jnp.bfloat16)
    pack_down(grad_out, 4, 0, matrix_multiply_transposed_left(du_f, h2_ref[...]))
    copies[1].wait()
    dh2 = matrix_multiply_transposed_right(dpre, win[...]) + matrix_multiply_transposed_right(
        du_f, a_fc[...])
    dx2 = dx3 + norm_back(middle_ref[...], affine_ref[1:2, :], dh2)
    da = dx2.astype(jnp.bfloat16)
    pack_up(grad_out, 3, ADAPTER_SCALE * matrix_multiply_transposed_left(uo_ref[...], da))
    du_o = (ADAPTER_SCALE * matrix_multiply_transposed_right(da, b_o[...])).astype(jnp.bfloat16)
    pack_down(grad_out, 2, 0, matrix_multiply_transposed_left(du_o, o_ref[...]))
    copies[2].wait()
    do_ref[...] = (
        matrix_multiply_transposed_right(da, wo[...])
        + matrix_multiply_transposed_right(du_o, a_o[...])
    ).astype(jnp.bfloat16)
    scale = (width // HEADS) ** (-0.5)
    lanes = lax.broadcasted_iota(jnp.int32, lse_ref.shape, 1)

    def heads(g):
        pair = pl.ds(pl.multiple_of(g * 128, 128), 128)
        q = both_heads(q_ref[:, pair])
        do = both_heads(do_ref[:, pair])
        lse = jnp.sum(jnp.where(lanes == g, lse_ref[...], 0.0), axis=1, keepdims=True)
        scores = scale * matrix_multiply_transposed_right(q, k_ref[:, pair])
        probs = jnp.where(mask[...] > 0.0, jnp.exp(jnp.minimum(scores - lse, 0.0)), 0.0)
        dp = matrix_multiply_transposed_right(do, v_ref[:, pair])
        ds = (probs * (dp - jnp.sum(probs * dp, axis=1, keepdims=True))).astype(jnp.bfloat16)
        dv_ref[:, pair] = matrix_multiply_transposed_left(
            probs.astype(jnp.bfloat16), do).astype(jnp.bfloat16)
        dk_ref[:, pair] = (scale * matrix_multiply_transposed_left(ds, q)).astype(jnp.bfloat16)
        dq_ref[:, pair] = side_by_side(scale * matrix_multiply(ds, k_ref[:, pair])).astype(
            jnp.bfloat16)

    wide_loop(HEADS // 2, heads)
    b_all = b_qkv[...]
    gb = jnp.zeros((NARROW, width), jnp.float32)
    ids = lax.broadcasted_iota(jnp.int32, gb.shape, 0)
    dus = []
    for j, low, grad in ((0, u1_rows_ref, dq_ref), (1, u1_ref, dk_ref), (2, u1_ref, dv_ref)):
        mine = (ids >= j * RANK) & (ids < (j + 1) * RANK)
        gb = jnp.where(mine, ADAPTER_SCALE * matrix_multiply_transposed_left(
            low[...], grad[...]), gb)
        dus.append(ADAPTER_SCALE * matrix_multiply_transposed_right(grad[...], third_of(b_all, j)))
    pack_up(grad_out, 1, gb)
    ga = matrix_multiply_transposed_left(
        dus[0].astype(jnp.bfloat16), h1_rows_ref[...]
    ) + matrix_multiply_transposed_left((dus[1] + dus[2]).astype(jnp.bfloat16), h1_ref[...])
    pack_down(grad_out, 0, 0, ga)


def layer_kernels(rows_here, length, width, hidden):
    low, wide = jnp.bfloat16, jnp.float32
    whole = pl.BlockSpec(memory_space=pltpu.VMEM)
    away = pl.BlockSpec(memory_space=pl.ANY)
    dma = pltpu.SemaphoreType.DMA
    params = pltpu.CompilerParams(vmem_limit_bytes=60 << 20)
    kept = [
        ((rows_here, width), low),
        ((length, width), low),
        ((length, width), low),
        ((length, NARROW), low),
        ((rows_here, NARROW), low),
        ((rows_here, width), low),
        ((2 * rows_here, 128), wide),
        ((rows_here, width), low),
        ((rows_here, NARROW), low),
        ((rows_here, width), wide),
        ((rows_here, width), low),
        ((rows_here, NARROW), low),
        ((rows_here, hidden), wide),
        ((rows_here, hidden), low),
        ((rows_here, NARROW), low),
        ((rows_here, width), wide),
    ]
    up = pl.pallas_call(
        layer_up,
        out_shape=[jax.ShapeDtypeStruct(*k) for k in [((rows_here, width), low)] + kept],
        in_specs=[whole] * 14 + [away] * 4,
        out_specs=[whole] * 17,
        scratch_shapes=[pltpu.VMEM((width, width), low)] * 4
        + [
            pltpu.VMEM((width, hidden), low),
            pltpu.VMEM((hidden, width), low),
            pltpu.VMEM((2 * rows_here, length), wide),
            dma((6,)),
        ],
        compiler_params=params,
        name="layer_up",
    )
    down = pl.pallas_call(
        layer_down,
        out_shape=jax.ShapeDtypeStruct((PARTS[-1], 128), wide),
        in_specs=[whole] * 29 + [away] * 3,
        out_specs=whole,
        scratch_shapes=[
            pltpu.VMEM((width, width), low),
            pltpu.VMEM((width, hidden), low),
            pltpu.VMEM((hidden, width), low),
            pltpu.VMEM((2 * rows_here, length), wide),
            pltpu.VMEM((rows_here, hidden), low),
            pltpu.VMEM((rows_here, width), low),
            pltpu.VMEM((rows_here, width), low),
            pltpu.VMEM((length, width), low),
            pltpu.VMEM((length, width), low),
            dma((3,)),
        ],
        compiler_params=params,
        name="layer_down",
    )
    return up, down


def settle_step(held_ref, segment_ref, spot_ref, place_ref, affine_ref, h1_out, rows_out, place_cols):
    length = segment_ref.shape[1]
    span = place_ref.shape[0]
    segment = segment_ref[...].astype(jnp.float32)
    steps = lax.broadcasted_iota(jnp.int32, (1, length), 1).astype(jnp.float32)
    ids = lax.broadcasted_iota(jnp.int32, (32, length), 0).astype(jnp.float32)
    starts = jnp.sum(ones_where(segment < ids), axis=1, keepdims=True)
    place = steps - jnp.sum(jnp.where(segment == ids, starts, 0.0), axis=0, keepdims=True)
    place_cols[...] = lane_columns(place)
    spot = lane_columns(spot_ref[...].astype(jnp.float32))[:, 0:1]
    at_spot = steps == spot
    spot_place = jnp.sum(jnp.where(at_spot, place, 0.0), axis=1, keepdims=True)

    def placed(column):
        ids_here = lax.broadcasted_iota(jnp.int32, (column.shape[0], span), 1).astype(jnp.float32)
        return matrix_multiply(low_ones(ids_here == column), place_ref[...])

    rows_out[...] = matrix_multiply(low_ones(at_spot), held_ref[...]) + placed(spot_place)

    @pl.loop(0, length // 128)
    def _(a):
        rows = pl.ds(pl.multiple_of(a * 128, 128), 128)
        stream = held_ref[rows, :].astype(jnp.float32) + placed(place_cols[rows, 0:1])
        h1_out[rows, :] = layer_norm(stream, affine_ref[0:1, :], affine_ref[3:4, :]).astype(
            jnp.bfloat16)


def settle_rows(held, segments, spots, place_table, affine):
    length, width = held.shape
    whole = pl.BlockSpec(memory_space=pltpu.VMEM)
    return pl.pallas_call(
        settle_step,
        out_shape=[
            jax.ShapeDtypeStruct((length, width), jnp.bfloat16),
            jax.ShapeDtypeStruct((spots.shape[1], width), jnp.float32),
        ],
        in_specs=[whole] * 5,
        out_specs=[whole] * 2,
        scratch_shapes=[pltpu.VMEM((length, 128), jnp.float32)],
        compiler_params=pltpu.CompilerParams(vmem_limit_bytes=32 << 20),
        name="settle_step",
    )(held, segments, spots, place_table[:256], affine)


def local(
    mesh_sizes,
    packed_symbol_codes,
    article_numbering,
    target_spots,
    answer_flags,
    shared_embedding,
    spot_embedding,
    combined_qkv_weights,
    attend_outgoing_weights,
    dense_incoming_weights,
    dense_outgoing_weights,
    layernorm_affine,
    bias_terms,
    adaptor_float_copies,
    average_moments,
    squared_moments,
):
    rows_here = target_spots.shape[1]
    shard_rows = shared_embedding.shape[0]
    table = jnp.pad(shared_embedding, ((0, -shard_rows % 16), (0, 0)))
    fast_h1, fast_rows, labels, counts, crowded, *factors = embed(
        mesh_sizes,
        shard_rows,
        packed_symbol_codes,
        article_numbering,
        target_spots,
        answer_flags,
        spot_embedding,
        layernorm_affine,
        adaptor_float_copies,
        table,
    )

    sharers = mesh_sizes[1]
    ring = [(j, (j + 1) % sharers) for j in range(sharers)]

    def visit(carry):
        turns, tokens, held = carry
        wanted = tokens[0] - lax.axis_index("vocab") * shard_rows
        inside = (wanted >= 0) & (wanted < shard_rows)
        picked = jnp.take(shared_embedding, jnp.clip(wanted, 0, shard_rows - 1), axis=0)
        kept = jnp.where(turns == sharers, jnp.zeros((), jnp.bfloat16), held)
        held = jnp.where(inside[:, None], picked, kept)
        return turns - 1, lax.ppermute(tokens, "vocab", ring), lax.ppermute(held, "vocab", ring)

    def settle(carry):
        _, held, _ = carry
        settled, rows = settle_rows(
            held, article_numbering, target_spots, spot_embedding, layernorm_affine
        )
        return jnp.zeros((), jnp.int32), settled, rows

    overflow = crowded.reshape(())
    _, _, held = lax.while_loop(
        lambda carry: carry[0] > 0, visit, (overflow * sharers, packed_symbol_codes, fast_h1)
    )
    _, h1, stream_rows = lax.while_loop(
        lambda carry: carry[0] > 0, settle, (overflow, held, fast_rows)
    )
    length, width = h1.shape
    hidden = dense_incoming_weights.shape[1]
    layer_up_call, layer_down_call = layer_kernels(rows_here, length, width, hidden)
    final_rows, *kept = layer_up_call(
        h1,
        stream_rows,
        article_numbering,
        target_spots,
        layernorm_affine,
        bias_terms[None, :],
        *factors,
        combined_qkv_weights,
        attend_outgoing_weights,
        dense_incoming_weights,
        dense_outgoing_weights,
    )
    grad_rows, loss_part = head(
        mesh_sizes, shard_rows, final_rows, labels, counts, table
    )
    local_grad = layer_down_call(
        grad_rows,
        target_spots,
        article_numbering,
        layernorm_affine,
        h1,
        *factors,
        *kept,
        attend_outgoing_weights,
        dense_incoming_weights,
        dense_outgoing_weights,
    )
    (
        refreshed_thin_pairs,
        updated_first_moment,
        updated_second_moment,
        gradient_global_norm,
        smoothed_entropy_cost,
    ) = reduce_and_update(
        mesh_sizes, local_grad, adaptor_float_copies, average_moments, squared_moments, loss_part
    )
    return (
        refreshed_thin_pairs,
        updated_first_moment,
        updated_second_moment,
        gradient_global_norm,
        smoothed_entropy_cost,
    )


def solution(mesh):
    return jax.shard_map(
        partial(local, (mesh.shape["dp"], mesh.shape["vocab"])),
        mesh=mesh,
        in_specs=(
            P(("dp", "vocab"), None),
            P(("dp", "vocab"), None),
            P(("dp", "vocab"), None),
            P(("dp", "vocab"), None),
            P("vocab", None),
            P(),
            P(),
            P(),
            P(),
            P(),
            P(),
            P(),
            P(),
            P(),
            P(),
        ),
        out_specs=(P(), P(), P(), P(), P()),
        check_vma=False,
    )
```

```python
from functools import partial
import math

import jax
import jax.numpy as jnp
from jax import lax
from jax.experimental import pallas as pl
from jax.experimental.pallas import tpu as pltpu
from jax.sharding import PartitionSpec as P

MODEL_WIDTH = 1024
HEADS = 16
FEEDFWD_UNITS = 4096
VOCAB_SIZE = 50257
RANK = 4
STEP = 10


ADAPTER_SCALE = 8.0
NORM_EPS = 1e-05
GRAD_CLIP = 0.0001
STRIDE_LENGTH = 0.02
BETA_ONE = 0.9
BETA_TWO = 0.999
SHRINK_PENALTY = 0.01
STABILITY_FLOOR = 1e-08
MASKED = -1e30
MESH = pl.DeviceIdType.MESH


def matrix_multiply(left, right):
    return jnp.dot(left, right, preferred_element_type=jnp.float32)


def matrix_multiply_transposed_left(left, right):
    return lax.dot_general(
        left, right, (((0,), (0,)), ((), ())), preferred_element_type=jnp.float32
    )


def matrix_multiply_transposed_right(left, right):
    return lax.dot_general(
        left, right, (((1,), (1,)), ((), ())), preferred_element_type=jnp.float32
    )


def layer_norm(stream, gain, shift):
    centred = stream - jnp.mean(stream, axis=-1, keepdims=True)
    spread = lax.rsqrt(jnp.mean(centred * centred, axis=-1, keepdims=True) + NORM_EPS)
    return centred * spread * gain + shift


def adaptive_moment_update(grad, weight, first, second):
    first_new = BETA_ONE * first + (1.0 - BETA_ONE) * grad
    second_new = BETA_TWO * second + (1.0 - BETA_TWO) * grad * grad
    debiased_mean_estimate = first_new / (1.0 - BETA_ONE**STEP)
    debiased_variance_estimate = second_new / (1.0 - BETA_TWO**STEP)
    weight_new = weight - STRIDE_LENGTH * (
        debiased_mean_estimate / (jnp.sqrt(debiased_variance_estimate) + STABILITY_FLOOR)
        + SHRINK_PENALTY * weight
    )
    return (weight_new, first_new, second_new)


def sum_and_step(dp_size, vocab_size, grad_ref, weight_ref, first_ref, second_ref, loss_ref,
                 weight_out, first_out, second_out, norm_out, loss_out,
                 parts, planes, total, losses, send_a, recv_a, send_b, recv_b, send_c, recv_c,
                 send_d, recv_d):
    my_plane = lax.axis_index("dp")
    me = lax.axis_index("vocab")

    def across(j):
        return (my_plane, lax.rem(me + j, vocab_size))

    def along(i):
        return (lax.rem(my_plane + i, dp_size), me)

    barrier = pltpu.get_barrier_semaphore()

    @pl.loop(1, vocab_size)
    def _(j):
        pl.semaphore_signal(barrier, inc=1, device_id=across(j), device_id_type=MESH)

    @pl.loop(1, dp_size)
    def _(i):
        pl.semaphore_signal(barrier, inc=1, device_id=along(i), device_id_type=MESH)

    pl.semaphore_wait(barrier, vocab_size + dp_size - 2)

    def part_copy(j):
        peer = across(j)
        return pltpu.make_async_remote_copy(
            src_ref=grad_ref.at[peer[1]], dst_ref=parts.at[me],
            send_sem=send_a.at[peer[1]], recv_sem=recv_a.at[me],
            device_id=peer, device_id_type=MESH)

    def part_arrival(j):
        peer = across(j)
        return pltpu.make_async_remote_copy(
            src_ref=grad_ref.at[peer[1]], dst_ref=parts.at[peer[1]],
            send_sem=send_a.at[peer[1]], recv_sem=recv_a.at[peer[1]],
            device_id=peer, device_id_type=MESH)

    def plane_copy(i):
        peer = along(i)
        return pltpu.make_async_remote_copy(
            src_ref=planes.at[my_plane], dst_ref=planes.at[my_plane],
            send_sem=send_b.at[peer[0]], recv_sem=recv_b.at[my_plane],
            device_id=peer, device_id_type=MESH)

    def plane_arrival(i):
        peer = along(i)
        return pltpu.make_async_remote_copy(
            src_ref=planes.at[my_plane], dst_ref=planes.at[peer[0]],
            send_sem=send_b.at[peer[0]], recv_sem=recv_b.at[peer[0]],
            device_id=peer, device_id_type=MESH)

    def loss_copy(i):
        peer = along(i)
        return pltpu.make_async_remote_copy(
            src_ref=loss_ref, dst_ref=losses.at[my_plane],
            send_sem=send_d.at[peer[0]], recv_sem=recv_d.at[my_plane],
            device_id=peer, device_id_type=MESH)

    def loss_arrival(i):
        peer = along(i)
        return pltpu.make_async_remote_copy(
            src_ref=loss_ref, dst_ref=losses.at[peer[0]],
            send_sem=send_d.at[peer[0]], recv_sem=recv_d.at[peer[0]],
            device_id=peer, device_id_type=MESH)

    def total_copy(j):
        peer = across(j)
        return pltpu.make_async_remote_copy(
            src_ref=total.at[me], dst_ref=total.at[me],
            send_sem=send_c.at[peer[1]], recv_sem=recv_c.at[me],
            device_id=peer, device_id_type=MESH)

    def total_arrival(j):
        peer = across(j)
        return pltpu.make_async_remote_copy(
            src_ref=total.at[me], dst_ref=total.at[peer[1]],
            send_sem=send_c.at[peer[1]], recv_sem=recv_c.at[peer[1]],
            device_id=peer, device_id_type=MESH)

    @pl.loop(1, vocab_size)
    def _(j):
        part_copy(j).start()

    @pl.loop(1, dp_size)
    def _(i):
        loss_copy(i).start()

    losses[my_plane] = loss_ref[...]
    parts[me] = grad_ref[me]

    @pl.loop(1, vocab_size)
    def _(j):
        part_arrival(j).wait_recv()

    planes[my_plane] = lax.fori_loop(
        1, vocab_size, lambda j, held: held + parts[j], parts[0])

    @pl.loop(1, dp_size)
    def _(i):
        plane_copy(i).start()

    @pl.loop(1, dp_size)
    def _(i):
        plane_arrival(i).wait_recv()

    total[me] = lax.fori_loop(1, dp_size, lambda i, held: held + planes[i], planes[0])

    @pl.loop(1, vocab_size)
    def _(j):
        total_copy(j).start()

    @pl.loop(1, vocab_size)
    def _(j):
        part_copy(j).wait_send()

    @pl.loop(1, dp_size)
    def _(i):
        plane_copy(i).wait_send()

    @pl.loop(1, vocab_size)
    def _(j):
        total_arrival(j).wait_recv()

    @pl.loop(1, vocab_size)
    def _(j):
        total_copy(j).wait_send()

    def squares(j, held):
        piece = total[j]
        return held + piece * piece

    gathered = lax.fori_loop(0, vocab_size, squares, jnp.zeros(parts.shape[1:], jnp.float32))
    norm = jnp.sqrt(jnp.sum(gathered, keepdims=True))
    norm_out[...] = norm

    @pl.loop(1, dp_size)
    def _(i):
        loss_arrival(i).wait_recv()
        loss_copy(i).wait_send()

    loss_out[...] = jnp.sum(losses[...], axis=0)[0:1, 0:1]
    shrink = GRAD_CLIP / jnp.maximum(norm, GRAD_CLIP)

    @pl.loop(0, vocab_size)
    def _(j):
        weight, first, second = adaptive_moment_update(
            total[j] * shrink, weight_ref[j], first_ref[j], second_ref[j])
        weight_out[j] = weight
        first_out[j] = first
        second_out[j] = second


def reduce_and_update(mesh_sizes, local_grad, weights, first, second, loss):
    dp_size, vocab_size = mesh_sizes
    number = local_grad.size
    rows = number // (128 * vocab_size)
    shape = (vocab_size, rows, 128)
    block = pltpu.VMEM(shape, jnp.float32)
    whole = pl.BlockSpec(memory_space=pltpu.VMEM)
    weight_new, first_new, second_new, norm, total_loss = pl.pallas_call(
        partial(sum_and_step, dp_size, vocab_size),
        out_shape=[jax.ShapeDtypeStruct(shape, jnp.float32)] * 3
        + [jax.ShapeDtypeStruct((1, 1), jnp.float32)] * 2,
        in_specs=[whole] * 5,
        out_specs=[whole] * 5,
        scratch_shapes=[
            block,
            pltpu.VMEM((dp_size, rows, 128), jnp.float32),
            block,
            pltpu.VMEM((dp_size, 8, 128), jnp.float32),
            pltpu.SemaphoreType.DMA((vocab_size,)),
            pltpu.SemaphoreType.DMA((vocab_size,)),
            pltpu.SemaphoreType.DMA((dp_size,)),
            pltpu.SemaphoreType.DMA((dp_size,)),
            pltpu.SemaphoreType.DMA((vocab_size,)),
            pltpu.SemaphoreType.DMA((vocab_size,)),
            pltpu.SemaphoreType.DMA((dp_size,)),
            pltpu.SemaphoreType.DMA((dp_size,)),
        ],
        compiler_params=pltpu.CompilerParams(
            collective_id=5, has_side_effects=True, vmem_limit_bytes=24 << 20
        ),
        name="sum_and_step",
    )(*[piece.reshape(shape) for piece in (local_grad, weights, first, second)], loss)
    flat = [piece.reshape(-1) for piece in (weight_new, first_new, second_new)]
    return (*flat, norm.reshape(()), total_loss.reshape(()))


TILE = 32


def head_step(dp_size, vocab_size, block, owned, hf_ref, label_ref, count_ref, table_hbm, grad_out, loss_out,
              table, hf_all, label_all, exps, exps_rest, tops, run_top, run_sum, run_smooth,
              run_goal, offset, z_even, z_odd, z_rest, dz_even, dz_odd, rest_even, rest_odd,
              acc_even, acc_odd, lse_tile, share_tile, stats_all,
              from_core, from_chip, leaving,
              table_sem, label_send, label_recv, hf_send, hf_recv,
              stat_send, stat_recv, core_send, core_recv, chip_send, chip_recv):
    plane = lax.axis_index("dp")
    me = lax.axis_index("vocab")
    chips = vocab_size // 2
    chip = me // 2
    core = lax.rem(me, 2)
    other = 2 * chip + 1 - core
    sibling = (plane, other)
    held = table_hbm.shape[0]
    full = held // block
    rest = held - full * block
    padded = table.shape[0] - full * block
    base = me * owned
    rows_each = hf_ref.shape[0]
    pair = 2 * rows_each
    width = hf_ref.shape[1]

    def partner(k):
        out = 0
        bit = 1
        while bit < chips:
            out = out + lax.rem(chip // bit + lax.rem(k // bit, 2), 2) * bit
            bit *= 2
        return out

    def across(j):
        return (plane, lax.rem(me + j, vocab_size))

    def table_copy(j, number):
        rows = pl.ds(pl.multiple_of(j * block, 16), number)
        return pltpu.make_async_copy(table_hbm.at[rows], table.at[rows], table_sem.at[j])

    @pl.loop(0, full)
    def _(j):
        table_copy(j, block).start()

    table_copy(full, rest).start()

    table[held:, :] = jnp.zeros((padded - rest, width), jnp.bfloat16)
    barrier = pltpu.get_barrier_semaphore()

    @pl.loop(1, vocab_size)
    def _(j):
        pl.semaphore_signal(barrier, inc=1, device_id=across(j), device_id_type=MESH)

    pl.semaphore_wait(barrier, vocab_size - 1)

    def remote(src, dst, send, recv, peer):
        return pltpu.make_async_remote_copy(
            src_ref=src, dst_ref=dst, send_sem=send, recv_sem=recv,
            device_id=peer, device_id_type=MESH)

    def hf_to_sibling():
        return remote(hf_ref, hf_all.at[me], hf_send.at[0], hf_recv.at[me], sibling)

    def hf_copy(k):
        return remote(hf_ref, hf_all.at[me], hf_send.at[k], hf_recv.at[me],
                      (plane, 2 * partner(k) + core))

    def hf_arrival(source):
        return remote(hf_ref, hf_all.at[source], hf_send.at[0], hf_recv.at[source], sibling)

    def hf_forward(k):
        source = 2 * partner(k) + core
        return remote(hf_all.at[source], hf_all.at[source], hf_send.at[chips + k],
                      hf_recv.at[source], sibling)

    def label_copy(j):
        peer = across(j)
        return remote(label_ref, label_all.at[me], label_send.at[peer[1]], label_recv.at[me], peer)

    def label_arrival(source):
        return remote(label_ref, label_all.at[source], label_send.at[source],
                      label_recv.at[source], sibling)

    near = min(3, chips)
    hf_to_sibling().start()

    @pl.loop(1, near)
    def _(k):
        hf_copy(k).start()

    @pl.loop(1, vocab_size)
    def _(j):
        label_copy(j).start()

    hf_all[me] = hf_ref[...]
    label_all[me] = label_ref[...]
    lanes = lax.broadcasted_iota(jnp.int32, (pair, 128), 1)

    def label_row(c, i):
        rows = label_all[pl.ds(2 * c, 2), i : i + 1, :].astype(jnp.float32)
        return jnp.concatenate([rows[0], rows[1]], axis=1)

    def set_offset(c):
        offset[...] = lane_columns(label_row(c, 0)).astype(jnp.int32) - base - lanes

    def folded(x):
        return sum(x[:, i * 128 : (i + 1) * 128] for i in range(1, x.shape[1] // 128)) + x[:, :128]

    def chunk_up(k, first):
        c = partner(k)
        if first:
            hf_arrival(other).wait_recv()
            label_arrival(other).wait_recv()
        else:
            hf_arrival(2 * c + core).wait_recv()
            hf_forward(k).start()
            label_arrival(2 * c).wait_recv()
            label_arrival(2 * c + 1).wait_recv()
            hf_arrival(2 * c + 1 - core).wait_recv()
        set_offset(c)
        run_top[...] = jnp.full((pair, 128), MASKED, jnp.float32)
        for ref in (run_sum, run_smooth, run_goal):
            ref[...] = jnp.zeros((pair, 128), jnp.float32)
        start = pl.multiple_of(k * pair, pair)

        def multiply(j, z_ref):
            if first:
                table_copy(j, rest if z_ref is z_rest else block).wait()
            rows = pl.ds(pl.multiple_of(j * block, 16), z_ref.shape[1])
            hidden = hf_all[pl.ds(2 * c, 2)].reshape(pair, width)
            z_ref[...] = matrix_multiply_transposed_right(hidden, table[rows, :])

        def reduce_full(j, z_ref):
            for r in range(pair // TILE):
                rows = slice(r * TILE, (r + 1) * TILE)
                there = pl.ds(start + r * TILE, TILE)
                z = z_ref[rows, :]
                old = run_top[rows, :]
                top = jnp.maximum(old, jnp.max(z, axis=1, keepdims=True))
                run_top[rows, :] = top
                tops[k, j, rows, :] = top
                gap = offset[rows, :] - j * block
                total = jnp.zeros((TILE, 128), jnp.float32)
                smooth = jnp.zeros((TILE, 128), jnp.float32)
                goal = jnp.zeros((TILE, 128), jnp.float32)
                for i in range(block // 128):
                    part = slice(i * 128, (i + 1) * 128)
                    piece = z[:, part]
                    e = jnp.exp(piece - top)
                    exps[j, there, part] = e
                    total = total + e
                    smooth = smooth + piece
                    goal = goal + jnp.where(gap == i * 128, piece, 0.0)
                run_sum[rows, :] = run_sum[rows, :] * jnp.exp(old - top) + total
                run_smooth[rows, :] = run_smooth[rows, :] + smooth
                run_goal[rows, :] = run_goal[rows, :] + goal

        def reduce_rest():
            for r in range(pair // TILE):
                rows = slice(r * TILE, (r + 1) * TILE)
                there = pl.ds(start + r * TILE, TILE)
                spot = lanes[rows, :]
                limit = jnp.minimum(VOCAB_SIZE - base, owned) - full * block - spot
                gap = offset[rows, :] - full * block
                pieces = []
                for i in range(padded // 128):
                    piece = z_rest[rows, i * 128 : (i + 1) * 128]
                    pieces.append((i * 128 < limit, piece))
                highest = jnp.where(pieces[0][0], pieces[0][1], MASKED)
                for valid, piece in pieces[1:]:
                    highest = jnp.maximum(highest, jnp.where(valid, piece, MASKED))
                old = run_top[rows, :]
                top = jnp.maximum(old, jnp.max(highest, axis=1, keepdims=True))
                run_top[rows, :] = top
                tops[k, full, rows, :] = top
                total = jnp.zeros((TILE, 128), jnp.float32)
                smooth = jnp.zeros((TILE, 128), jnp.float32)
                goal = jnp.zeros((TILE, 128), jnp.float32)
                for i, (valid, piece) in enumerate(pieces):
                    e = jnp.where(valid, jnp.exp(piece - top), 0.0)
                    exps_rest[there, i * 128 : (i + 1) * 128] = e
                    total = total + e
                    smooth = smooth + jnp.where(valid, piece, 0.0)
                    goal = goal + jnp.where(valid & (gap == i * 128), piece, 0.0)
                run_sum[rows, :] = run_sum[rows, :] * jnp.exp(old - top) + total
                run_smooth[rows, :] = run_smooth[rows, :] + smooth
                run_goal[rows, :] = run_goal[rows, :] + goal

        multiply(0, z_even)
        turns = (full - 1) // 2

        if turns > 0:
            @pl.loop(0, turns)
            def _(t):
                multiply(2 * t + 1, z_odd)
                reduce_full(2 * t, z_even)
                multiply(2 * t + 2, z_even)
                reduce_full(2 * t + 1, z_odd)

        if full - 2 * turns == 2:
            multiply(full - 1, z_odd)
            reduce_full(full - 2, z_even)
            multiply(full, z_rest)
            reduce_full(full - 1, z_odd)
        else:
            multiply(full, z_rest)
            reduce_full(full - 1, z_even)
        reduce_rest()

        def row_sum(ref):
            return jnp.sum(ref[...].T, axis=0, keepdims=True)

        ids = lax.broadcasted_iota(jnp.int32, (8, pair), 0)
        packed = jnp.where(ids == 0, run_top[...].T[0:1, :], 0.0)
        for i, ref in enumerate((run_sum, run_smooth, run_goal)):
            packed = jnp.where(ids == i + 1, row_sum(ref), packed)
        stats_all[me, c] = packed

    chunk_up(0, True)

    @pl.loop(near, chips)
    def _(k):
        hf_copy(k).start()

    @pl.loop(1, chips)
    def _(k):
        chunk_up(k, False)

    def stat_copy(j):
        peer = across(j)
        return remote(stats_all.at[me], stats_all.at[me], stat_send.at[peer[1]],
                      stat_recv.at[me], peer)

    def stat_arrival(j):
        source = across(j)[1]
        return remote(stats_all.at[me], stats_all.at[source], stat_send.at[source],
                      stat_recv.at[source], across(j))

    @pl.loop(1, vocab_size)
    def _(j):
        stat_copy(j).start()

    @pl.loop(1, vocab_size)
    def _(j):
        stat_arrival(j).wait_recv()

    count = jnp.maximum(count_ref[1:2, 0:1], 1.0)

    def totals_of(c):
        here = stats_all[:, c]
        tops_here = here[:, 0:1, :]
        top = jnp.max(tops_here, axis=0)
        total = jnp.sum(here[:, 1:2, :] * jnp.exp(tops_here - top[None]), axis=0)
        return top + jnp.log(total), jnp.sum(here[:, 2:3, :], axis=0), jnp.sum(
            here[:, 3:4, :], axis=0)

    def chunk_loss(c, held_loss):
        lse, smooth, goal = totals_of(c)
        return held_loss + label_row(c, 1) * (lse - 0.9 * goal - 0.1 * smooth / VOCAB_SIZE)

    slots = from_core.shape[0]
    columns_each = width // 4

    def core_copy(k, n, acc):
        half = pl.ds(pl.multiple_of((1 - core) * rows_each, rows_each), rows_each)
        part = pl.ds(pl.multiple_of(n * columns_each, columns_each), columns_each)
        return remote(acc.at[half, part], from_core.at[lax.rem(k, slots), :, part],
                      core_send.at[k, n], core_recv.at[k, n], sibling)

    def chip_copy(k):
        return remote(leaving.at[k - 1], from_chip.at[k - 1], chip_send.at[k], chip_recv.at[k],
                      (plane, 2 * partner(k) + core))

    def prepare(k):
        c = partner(k)
        lse, _, _ = totals_of(c)
        lse_tile[...] = lane_columns(lse)
        share_tile[...] = lane_columns(label_row(c, 1) / count)
        set_offset(c)

    quarter = pair // 4

    def grads(k, n, dz_ref, rest_ref):
        for r in range(quarter // TILE):
            first = pl.multiple_of(n * quarter + r * TILE, TILE)
            rows = pl.ds(first, TILE)
            there = pl.ds(pl.multiple_of(k * pair + first, TILE), TILE)
            share = share_tile[rows, :]
            lse = lse_tile[rows, :]
            low = share * (0.1 / VOCAB_SIZE)
            high = low + 0.9 * share
            gap = offset[rows, :]
            for j in range(full):
                factor = share * jnp.exp(tops[k, j, rows, :] - lse)
                for i in range(block // 128):
                    at = j * block + i * 128
                    e = exps[j, there, i * 128 : (i + 1) * 128]
                    dz = e * factor - jnp.where(gap == at, high, low)
                    dz_ref[rows, at : at + 128] = dz.astype(jnp.bfloat16)
            factor = share * jnp.exp(tops[k, full, rows, :] - lse)
            limit = jnp.minimum(VOCAB_SIZE - base, owned) - full * block - lanes[0:TILE, :]
            for i in range(padded // 128):
                part = slice(i * 128, (i + 1) * 128)
                at = full * block + i * 128
                dz = exps_rest[there, part] * factor - jnp.where(gap == at, high, low)
                rest_ref[rows, part] = jnp.where(i * 128 < limit, dz, 0.0).astype(jnp.bfloat16)

    def gather(k, n, dz_ref, rest_ref, acc):
        part = pl.ds(pl.multiple_of(n * columns_each, columns_each), columns_each)
        acc[:, part] = matrix_multiply(
            dz_ref[...], table[pl.ds(0, full * block), part]
        ) + matrix_multiply(rest_ref[...], table[pl.ds(full * block, padded), part])

    def finish(k, acc):
        for n in range(4):
            core_copy(k, n, acc).wait()
        own = pl.ds(pl.multiple_of(core * rows_each, rows_each), rows_each)
        return from_core[lax.rem(k, slots)] + acc[own, :]

    def stage(k, now, later, acc, acc_before, last):
        if later is not None:
            prepare(k - 1)

        @pl.loop(0, 4)
        def _(n):
            gather(k, n, *now, acc)
            if later is not None:
                grads(k - 1, n, *later)
            core_copy(k, n, acc).start()
            if acc_before is not None:
                @pl.when((n == 0) & (k < chips - 1))
                def _():
                    leaving[k] = finish(k + 1, acc_before).astype(jnp.bfloat16)
                    chip_copy(k + 1).start()

    evens = ((dz_even, rest_even), acc_even)
    odds = ((dz_odd, rest_odd), acc_odd)
    prepare(chips - 1)

    @pl.loop(0, 4)
    def _(n):
        grads(chips - 1, n, *odds[0])

    @pl.loop(0, chips // 2 - 1)
    def _(t):
        k = chips - 1 - 2 * t
        stage(k, odds[0], evens[0], acc_odd, acc_even, False)
        stage(k - 1, evens[0], odds[0], acc_even, acc_odd, False)

    stage(1, odds[0], evens[0], acc_odd, acc_even if chips > 2 else None, False)
    stage(0, evens[0], None, acc_even, acc_odd, True)

    loss = lax.fori_loop(0, chips, chunk_loss, jnp.zeros((1, pair), jnp.float32))
    loss_out[...] = jnp.broadcast_to(jnp.sum(loss, keepdims=True) / count, loss_out.shape)
    grad_out[...] = finish(0, acc_even)

    @pl.loop(1, chips)
    def _(k):
        chip_copy(k).wait_recv()
        grad_out[...] += from_chip[k - 1].astype(jnp.float32)

    hf_to_sibling().wait_send()

    @pl.loop(1, chips)
    def _(k):
        hf_copy(k).wait_send()
        hf_forward(k).wait_send()
        chip_copy(k).wait_send()

    @pl.loop(1, vocab_size)
    def _(j):
        label_copy(j).wait_send()
        stat_copy(j).wait_send()


def head(mesh_sizes, owned, final_rows, labels, counts, table):
    dp_size, vocab_size = mesh_sizes
    rows, width = final_rows.shape
    held = table.shape[0]
    block = 1024
    full = held // block
    rest = -(-(held - full * block) // 128) * 128
    chips = vocab_size // 2
    pair = 2 * rows
    low, wide = jnp.bfloat16, jnp.float32
    whole = pl.BlockSpec(memory_space=pltpu.VMEM)
    dma = pltpu.SemaphoreType.DMA
    tile = pltpu.VMEM((pair, 128), wide)
    grad, loss = pl.pallas_call(
        partial(head_step, dp_size, vocab_size, block, owned),
        out_shape=[
            jax.ShapeDtypeStruct((rows, width), wide),
            jax.ShapeDtypeStruct((8, 128), wide),
        ],
        in_specs=[whole, whole, whole, pl.BlockSpec(memory_space=pl.ANY)],
        out_specs=[whole, whole],
        scratch_shapes=[
            pltpu.VMEM((full * block + rest, width), low),
            pltpu.VMEM((vocab_size, rows, width), low),
            pltpu.VMEM((vocab_size, 8, rows), jnp.int32),
            pltpu.VMEM((full, vocab_size * rows, block), wide),
            pltpu.VMEM((vocab_size * rows, rest), wide),
            pltpu.VMEM((chips, full + 1, pair, 128), wide),
            tile,
            tile,
            tile,
            tile,
            pltpu.VMEM((pair, 128), jnp.int32),
            pltpu.VMEM((pair, block), wide),
            pltpu.VMEM((pair, block), wide),
            pltpu.VMEM((pair, rest), wide),
            pltpu.VMEM((pair, full * block), low),
            pltpu.VMEM((pair, full * block), low),
            pltpu.VMEM((pair, rest), low),
            pltpu.VMEM((pair, rest), low),
            pltpu.VMEM((pair, width), wide),
            pltpu.VMEM((pair, width), wide),
            tile,
            tile,
            pltpu.VMEM((vocab_size, chips, 8, pair), wide),
            pltpu.VMEM((3, rows, width), wide),
            pltpu.VMEM((chips - 1, rows, width), low),
            pltpu.VMEM((chips - 1, rows, width), low),
            dma((full + 1,)),
            dma((vocab_size,)),
            dma((vocab_size,)),
            dma((2 * chips,)),
            dma((vocab_size,)),
            dma((vocab_size,)),
            dma((vocab_size,)),
            dma((chips, 4)),
            dma((chips, 4)),
            dma((chips,)),
            dma((chips,)),
        ],
        compiler_params=pltpu.CompilerParams(
            collective_id=3, has_side_effects=True, vmem_limit_bytes=63 << 20
        ),
        name="head_step",
    )(final_rows, labels, counts, table)
    return grad, loss


NARROW = 16
PARTS = (0, 96, 192, 224, 256, 288, 416, 544, 576)


def floor_part(values, size):
    return jnp.floor((values + 0.5) * (1.0 / size))


def spread_places(ranks, slab):
    lanes = lax.broadcasted_iota(jnp.int32, (1024, 128), 1).astype(jnp.float32) + 128.0 * slab
    rows = lax.broadcasted_iota(jnp.int32, (1024, 128), 0).astype(jnp.float32)
    return floor_part(lanes, ranks) == rows - 32.0 * floor_part(rows, 32)


def unpack_down(flat_ref, first, ranks, out_ref, start):
    slabs = ranks // RANK
    total = None
    for slab in range(slabs):
        packed = flat_ref[pl.ds(first + slab, 32, stride=slabs), :]
        spread = jnp.broadcast_to(packed[:, None, :], (32, 32, 128)).reshape(1024, 128)
        spread = jnp.where(spread_places(ranks, slab), spread, 0.0).astype(jnp.bfloat16)
        lanes = lax.broadcasted_iota(jnp.int32, (128, NARROW), 0).astype(jnp.float32) + 128.0 * slab
        column = lax.broadcasted_iota(jnp.int32, (128, NARROW), 1).astype(jnp.float32)
        chosen = low_ones(lanes - ranks * floor_part(lanes, ranks) == column)
        part = matrix_multiply(spread, chosen)
        total = part if total is None else total + part
    out_ref[pl.ds(start, 1024), :] = total.astype(jnp.bfloat16)


def unpack_up(flat_ref, first, ranks, out_ref):
    wide = out_ref.shape[1] // 128
    for c in range(wide):
        rows = flat_ref[pl.ds(first + c, ranks, stride=wide), :]
        rows = jnp.concatenate([rows, jnp.zeros((NARROW - ranks, 128), jnp.float32)], axis=0)
        out_ref[:, c * 128 : (c + 1) * 128] = rows.astype(jnp.bfloat16)


def unpack(flat_ref, outs):
    for i, out_ref in enumerate(outs):
        ranks = 3 * RANK if i < 2 else RANK
        if i % 2:
            unpack_up(flat_ref, PARTS[i], ranks, out_ref)
        else:
            for b in range(out_ref.shape[0] // 1024):
                unpack_down(flat_ref, PARTS[i] + 32 * b, ranks, out_ref, 1024 * b)


def lane_columns(row):
    return jnp.broadcast_to(row, (128, row.shape[1])).T


def ones_where(condition):
    return jnp.where(condition, 1.0, 0.0)


def low_ones(condition):
    return ones_where(condition).astype(jnp.bfloat16)


def embed_step(dp_size, vocab_size, block, room, owned, token_ref, segment_ref, spot_ref, flag_ref,
               place_hbm, affine_ref, flat_ref, table_hbm,
               h1_out, rows_out, label_out, full_out, crowd_out,
               a_qkv, b_qkv, a_o, b_o, a_fc, b_fc, a_p, b_p,
               table, place_table, key_cols, unique_cols, slot_cols, owners, asked, lists, lists_in,
               acc, leaving, arriving, stream, full_all,
               table_sem, place_sem, list_send, list_recv, row_send, row_recv, full_send, full_recv):
    plane = lax.axis_index("dp")
    me = lax.axis_index("vocab")
    chips = vocab_size // 2
    chip = me // 2
    held = table.shape[0]
    full = held // block
    rest = held - full * block
    length = token_ref.shape[1]
    width = table.shape[1]
    spots_here = spot_ref.shape[1]
    chunk = 128
    chunks = length // chunk

    def partner(k):
        out = 0
        bit = 1
        while bit < chips:
            out = out + lax.rem(chip // bit + (k // bit) % 2, 2) * bit
            bit *= 2
        return out

    def across(j):
        return (plane, lax.rem(me + j, vocab_size))

    def along(i):
        return (lax.rem(plane + i, dp_size), me)

    def remote(src, dst, send, recv, peer):
        return pltpu.make_async_remote_copy(
            src_ref=src, dst_ref=dst, send_sem=send, recv_sem=recv,
            device_id=peer, device_id_type=MESH)

    def table_copy(j, number):
        rows = pl.ds(pl.multiple_of(j * block, 16), number)
        return pltpu.make_async_copy(table_hbm.at[rows], table.at[rows], table_sem.at[j])

    @pl.loop(0, full)
    def _(j):
        table_copy(j, block).start()

    table_copy(full, rest).start()

    place_copy = pltpu.make_async_copy(
        place_hbm.at[pl.ds(0, place_table.shape[0])], place_table, place_sem)
    place_copy.start()
    barrier = pltpu.get_barrier_semaphore()

    @pl.loop(1, vocab_size)
    def _(j):
        pl.semaphore_signal(barrier, inc=1, device_id=across(j), device_id_type=MESH)

    @pl.loop(1, dp_size)
    def _(i):
        pl.semaphore_signal(barrier, inc=1, device_id=along(i), device_id_type=MESH)

    token = token_ref[...].astype(jnp.float32)
    segment = segment_ref[...].astype(jnp.float32)
    steps = lax.broadcasted_iota(jnp.int32, (1, length), 1).astype(jnp.float32)
    spot = lane_columns(spot_ref[...].astype(jnp.float32))[:, 0:1]
    flag = lane_columns(flag_ref[...].astype(jnp.float32))[:, 0:1]
    at_spot = steps == spot
    at_next = steps == spot + 1.0

    def picked(where_to, row):
        return jnp.sum(jnp.where(where_to, row, 0.0), axis=1, keepdims=True)

    segment_here = picked(at_spot, segment)
    weight = jnp.where(segment_here == picked(at_next, segment), flag, 0.0)
    heavy = jnp.sum(weight, axis=0, keepdims=True)
    target = picked(at_next, token)
    lanes = lax.broadcasted_iota(jnp.int32, (spots_here, 128), 1)
    label_tile = jnp.where(lanes == 0, target, jnp.where(lanes == 1, weight, 0.0))
    label_out[...] = label_tile.T[0:8, :].astype(jnp.int32)
    read = (steps <= spot) & (segment == segment_here) & (weight > 0.0)
    needed = jnp.max(ones_where(read), axis=0, keepdims=True) > 0.0

    key = jnp.where(needed, token, -1.0 - steps)
    key_cols[...] = lane_columns(key)

    def places(a):
        return (lax.broadcasted_iota(jnp.int32, (chunk, 1), 0) + a * chunk).astype(jnp.float32)

    def rows_at(a):
        return pl.ds(pl.multiple_of(a * chunk, chunk), chunk)

    def same(a):
        return key_cols[rows_at(a), 0:1] == key

    def seen(a, carry):
        return jnp.maximum(carry, jnp.max(
            ones_where(same(a) & (places(a) < steps)), axis=0, keepdims=True))

    again = lax.fori_loop(0, chunks, seen, jnp.zeros((1, length), jnp.float32))
    unique = ones_where(needed & (again == 0.0))
    unique_cols[...] = lane_columns(unique)
    owner = jnp.zeros((1, length), jnp.float32)
    for j in range(1, vocab_size):
        owner = owner + ones_where(token >= float(j * owned))
    owner_ids = lax.broadcasted_iota(jnp.int32, (vocab_size, length), 0).astype(jnp.float32)
    mine = jnp.where(owner_ids == owner, unique, 0.0)
    owners[...] = mine

    def ahead(a, carry):
        before = low_ones(places(a) < steps)
        return carry + matrix_multiply(owners[:, rows_at(a)].astype(jnp.bfloat16), before)

    ranks = lax.fori_loop(0, chunks, ahead, jnp.zeros((vocab_size, length), jnp.float32))
    rank = jnp.sum(jnp.where(owner_ids == owner, ranks, 0.0), axis=0, keepdims=True)
    too_many = jnp.max(unique * ones_where(rank >= float(room)), axis=1, keepdims=True)
    local_id = token - owner * float(owned)
    local_high = jnp.floor(local_id * (1.0 / 128.0))
    local_low = local_id - 128.0 * local_high
    row_ids = lax.broadcasted_iota(jnp.int32, (8, length), 0)

    def stacked(first, second):
        return jnp.where(row_ids == 0, first, jnp.where(row_ids == 1, second, 0.0))

    asked[...] = stacked(owner, jnp.minimum(rank, 127.0))

    def found(a, carry):
        match = low_ones(same(a) & (unique_cols[rows_at(a), 0:1] > 0.0))
        return carry + matrix_multiply(asked[:, rows_at(a)].astype(jnp.bfloat16), match)

    slots = lax.fori_loop(0, chunks, found, jnp.zeros((8, length), jnp.float32))
    slot = jnp.where(needed, slots[0:1, :] * 128.0 + slots[1:2, :], -1.0)
    slot_cols[...] = lane_columns(slot)
    local_parts = stacked(local_high, local_low).astype(jnp.bfloat16)
    rank_ids = lax.broadcasted_iota(jnp.int32, (128, length), 0).astype(jnp.float32)
    list_rows = lax.broadcasted_iota(jnp.int32, (8, 128), 0)

    @pl.loop(0, vocab_size)
    def _(j):
        theirs = (unique > 0.0) & (owner == j.astype(jnp.float32))
        chosen = low_ones(rank_ids == jnp.where(theirs, rank, -1.0))
        ids = matrix_multiply_transposed_right(local_parts, chosen)
        lists[j] = jnp.where(list_rows == 2, too_many, jnp.where(list_rows == 3, heavy, ids))

    @pl.loop(0, vocab_size)
    def _(j):
        arriving[j] = jnp.zeros(arriving.shape[1:], jnp.bfloat16)

    pl.semaphore_wait(barrier, vocab_size + dp_size - 2)

    def list_copy(j):
        peer = across(j)
        return remote(lists.at[peer[1]], lists_in.at[me], list_send.at[peer[1]],
                      list_recv.at[me], peer)

    def list_arrival(j):
        source = across(j)[1]
        return remote(lists.at[source], lists_in.at[source], list_send.at[source],
                      list_recv.at[source], across(j))

    @pl.loop(1, vocab_size)
    def _(j):
        list_copy(j).start()

    lists_in[me] = lists[me]

    ids = lax.broadcasted_iota(jnp.int32, (32, length), 0).astype(jnp.float32)
    starts = jnp.sum(ones_where(segment < ids), axis=1, keepdims=True)
    place = steps - jnp.sum(jnp.where(segment == ids, starts, 0.0), axis=0, keepdims=True)
    place_cols = lane_columns(place)[:, 0:1]
    span = place_table.shape[0]
    place_copy.wait()
    place_ids = lax.broadcasted_iota(jnp.int32, (length, span), 1).astype(jnp.float32)
    stream[...] = matrix_multiply(low_ones(place_ids == place_cols), place_table[...])
    spot_place = picked(at_spot, place)
    spot_slot = picked(at_spot, slot)
    unpack(flat_ref, (a_qkv, b_qkv, a_o, b_o, a_fc, b_fc, a_p, b_p))

    @pl.loop(1, vocab_size)
    def _(j):
        list_arrival(j).wait_recv()

    full_all[plane] = jnp.where(
        list_rows == 0, jnp.max(lists_in[:, 2:3, 0:1], axis=0),
        jnp.sum(lists_in[:, 3:4, 0:1], axis=0))

    def full_copy(i):
        peer = along(i)
        return remote(full_all.at[plane], full_all.at[plane], full_send.at[peer[0]],
                      full_recv.at[plane], peer)

    def full_arrival(i):
        source = along(i)[0]
        return remote(full_all.at[plane], full_all.at[source], full_send.at[source],
                      full_recv.at[source], along(i))

    @pl.loop(1, dp_size)
    def _(i):
        full_copy(i).start()

    def row_copy(d):
        return remote(leaving.at[d], arriving.at[me, pl.ds(0, room)], row_send.at[d],
                      row_recv.at[me], (plane, d))

    def row_arrival(d):
        return remote(leaving.at[d], arriving.at[d, pl.ds(0, room)], row_send.at[d],
                      row_recv.at[d], (plane, d))

    def wanted(d):
        here = lists_in[d]
        return lane_columns(here[0:1, :] * 128.0 + here[1:2, :])[0:room, 0:1]

    first = True
    for k in range(chips - 1, -1, -1):
        c = partner(k)
        wanted_here = jnp.concatenate([wanted(2 * c), wanted(2 * c + 1)], axis=0)

        def rows_of(j, number):
            if first:
                table_copy(j, number).wait()
            ids_here = (lax.broadcasted_iota(jnp.int32, (2 * room, number), 1)
                        + j * block).astype(jnp.float32)
            rows = pl.ds(pl.multiple_of(j * block, 16), number)
            return matrix_multiply(low_ones(ids_here == wanted_here), table[rows, :])

        acc[...] = rows_of(full, rest)

        @pl.loop(0, full)
        def _(j):
            acc[...] += rows_of(j, block)

        first = False
        for i in range(2):
            leaving[2 * c + i] = acc[pl.ds(i * room, room), :].astype(jnp.bfloat16)
        if k > 0:
            for i in range(2):
                row_copy(2 * c + i).start()
        else:
            row_copy(2 * c + 1 - lax.rem(me, 2)).start()
            arriving[me, pl.ds(0, room), :] = leaving[me]

    for k in range(chips):
        c = partner(k)
        if k > 0:
            for i in range(2):
                row_arrival(2 * c + i).wait_recv()
        else:
            row_arrival(2 * c + 1 - lax.rem(me, 2)).wait_recv()
        pair_rows = arriving[pl.ds(2 * c, 2)].reshape(256, width)
        offset = (2 * c * 128).astype(jnp.float32)

        def spread(column, ids_like):
            ids_here = lax.broadcasted_iota(jnp.int32, ids_like, 1).astype(jnp.float32)
            return low_ones(ids_here + offset == column)

        stream[...] += matrix_multiply(spread(slot_cols[:, 0:1], (length, 256)), pair_rows)
        spot_rows = matrix_multiply(spread(spot_slot, (spots_here, 256)), pair_rows)
        if k == 0:
            rows_out[...] = spot_rows
        else:
            rows_out[...] += spot_rows

    spot_ids = lax.broadcasted_iota(jnp.int32, (spots_here, span), 1).astype(jnp.float32)
    rows_out[...] += matrix_multiply(low_ones(spot_ids == spot_place), place_table[...])

    @pl.loop(0, length // 256)
    def _(a):
        rows = pl.ds(pl.multiple_of(a * 256, 256), 256)
        h1_out[rows, :] = layer_norm(
            stream[rows, :], affine_ref[0:1, :], affine_ref[3:4, :]).astype(jnp.bfloat16)

    @pl.loop(1, dp_size)
    def _(i):
        full_arrival(i).wait_recv()

    counts = jnp.where(
        list_rows == 0, jnp.max(full_all[...], axis=0), jnp.sum(full_all[...], axis=0))
    full_out[...] = counts
    crowd_out[...] = counts[0:1, 0:1].astype(jnp.int32)

    @pl.loop(1, vocab_size)
    def _(j):
        list_copy(j).wait_send()

    @pl.loop(1, dp_size)
    def _(i):
        full_copy(i).wait_send()

    for k in range(chips):
        if k > 0:
            for i in range(2):
                row_copy(2 * partner(k) + i).wait_send()
        else:
            row_copy(2 * chip + 1 - lax.rem(me, 2)).wait_send()


def embed(mesh_sizes, owned, tokens, segments, spots, flags, place_table, affine, flat, table):
    dp_size, vocab_size = mesh_sizes
    length = tokens.shape[1]
    spots_here = spots.shape[1]
    held, width = table.shape
    block = 1024
    full = held // block
    chips = vocab_size // 2
    room = 112 if vocab_size <= 8 else 64
    span = 256
    whole = pl.BlockSpec(memory_space=pltpu.VMEM)
    dma = pltpu.SemaphoreType.DMA
    return pl.pallas_call(
        partial(embed_step, dp_size, vocab_size, block, room, owned),
        out_shape=[
            jax.ShapeDtypeStruct((length, width), jnp.bfloat16),
            jax.ShapeDtypeStruct((spots_here, width), jnp.float32),
            jax.ShapeDtypeStruct((8, spots_here), jnp.int32),
            jax.ShapeDtypeStruct((8, 128), jnp.float32),
            jax.ShapeDtypeStruct((1, 1), jnp.int32),
        ]
        + [
            jax.ShapeDtypeStruct(shape, jnp.bfloat16)
            for shape in (
                (width, NARROW), (NARROW, width), (width, NARROW), (NARROW, width),
                (width, NARROW), (NARROW, 4 * width), (4 * width, NARROW), (NARROW, width),
            )
        ],
        in_specs=[whole] * 4
        + [pl.BlockSpec(memory_space=pl.ANY), whole, whole, pl.BlockSpec(memory_space=pl.ANY)],
        out_specs=[whole] * 13,
        scratch_shapes=[
            pltpu.VMEM((held, width), jnp.bfloat16),
            pltpu.VMEM((span, width), jnp.bfloat16),
            pltpu.VMEM((length, 128), jnp.float32),
            pltpu.VMEM((length, 128), jnp.float32),
            pltpu.VMEM((length, 128), jnp.float32),
            pltpu.VMEM((vocab_size, length), jnp.float32),
            pltpu.VMEM((8, length), jnp.float32),
            pltpu.VMEM((vocab_size, 8, 128), jnp.float32),
            pltpu.VMEM((vocab_size, 8, 128), jnp.float32),
            pltpu.VMEM((2 * room, width), jnp.float32),
            pltpu.VMEM((vocab_size, room, width), jnp.bfloat16),
            pltpu.VMEM((vocab_size, 128, width), jnp.bfloat16),
            pltpu.VMEM((length, width), jnp.float32),
            pltpu.VMEM((dp_size, 8, 128), jnp.float32),
            dma((full + 1,)),
            dma,
            dma((vocab_size,)),
            dma((vocab_size,)),
            dma((vocab_size,)),
            dma((vocab_size,)),
            dma((dp_size,)),
            dma((dp_size,)),
        ],
        compiler_params=pltpu.CompilerParams(
            collective_id=1, has_side_effects=True, vmem_limit_bytes=60 << 20
        ),
        name="embed_step",
    )(tokens, segments, spots, flags, place_table, affine, flat.reshape(-1, 128), table)


def wide_loop(number, body):
    lax.fori_loop(0, number, lambda i, carry: (body(i), carry)[1], 0)


def norm_parts(rows):
    centred = rows - jnp.mean(rows, axis=-1, keepdims=True)
    return centred, lax.rsqrt(jnp.mean(centred * centred, axis=-1, keepdims=True) + NORM_EPS)


def norm_back(rows, gain, grad):
    centred, spread = norm_parts(rows)
    hat = centred * spread
    grad_hat = grad * gain
    return spread * (
        grad_hat
        - jnp.mean(grad_hat, axis=-1, keepdims=True)
        - hat * jnp.mean(grad_hat * hat, axis=-1, keepdims=True)
    )


GELU_RATE = math.sqrt(2.0 / math.pi)


def gelu_parts(pre):
    bend = jnp.tanh(GELU_RATE * (pre + 0.044715 * (pre * pre * pre)))
    return 0.5 * (1.0 + bend), bend


def gelu_slope(pre):
    half, bend = gelu_parts(pre)
    inner = GELU_RATE * (1.0 + 3.0 * 0.044715 * (pre * pre))
    return half + 0.5 * pre * (1.0 - bend * bend) * inner


def both_heads(pair):
    lanes = lax.broadcasted_iota(jnp.int32, pair.shape, 1)
    half = pair.shape[1] // 2
    wide = pair.astype(jnp.float32)
    return jnp.concatenate(
        [jnp.where(lanes < half, wide, 0.0), jnp.where(lanes < half, 0.0, wide)], axis=0
    ).astype(jnp.bfloat16)


def side_by_side(stacked):
    rows = stacked.shape[0] // 2
    lanes = lax.broadcasted_iota(jnp.int32, (rows, stacked.shape[1]), 1)
    return jnp.where(lanes < stacked.shape[1] // 2, stacked[:rows], stacked[rows:])


def third_of(rows, j):
    ids = lax.broadcasted_iota(jnp.int32, rows.shape, 0)
    wide = jnp.where((ids >= j * RANK) & (ids < (j + 1) * RANK), rows.astype(jnp.float32), 0.0)
    return wide.astype(jnp.bfloat16)


def attention_mask(spot_ref, segment_ref):
    spot = lane_columns(spot_ref[...].astype(jnp.float32))[:, 0:1]
    steps = lax.broadcasted_iota(jnp.int32, segment_ref.shape, 1).astype(jnp.float32)
    segment = segment_ref[...].astype(jnp.float32)
    here = jnp.sum(jnp.where(steps == spot, segment, 0.0), axis=1, keepdims=True)
    open_to = ones_where((steps <= spot) & (segment == here))
    return jnp.concatenate([open_to, open_to], axis=0)


def layer_up(h1_ref, rows_ref, segment_ref, spot_ref, affine_ref, bias_ref,
             a_qkv, b_qkv, a_o, b_o, a_fc, b_fc, a_p, b_p,
             qkv_hbm, o_hbm, in_hbm, out_hbm,
             final_ref, q_ref, k_ref, v_ref, u1_ref, u1_rows_ref, h1_rows_ref, lse_ref,
             o_ref, uo_ref, middle_ref, h2_ref, uf_ref, pre_ref, f_ref, up_ref, last_ref,
             wq, wk, wv, wo, win, wout, mask, sems):
    length, width = h1_ref.shape
    hidden = win.shape[1]
    quarter = hidden // 4

    def columns_of(source, j, number):
        return source.at[:, pl.ds(j * number, number)]

    copies = [
        pltpu.make_async_copy(columns_of(qkv_hbm, 1, width), wk, sems.at[0]),
        pltpu.make_async_copy(columns_of(qkv_hbm, 2, width), wv, sems.at[1]),
        pltpu.make_async_copy(columns_of(qkv_hbm, 0, width), wq, sems.at[2]),
        pltpu.make_async_copy(o_hbm, wo, sems.at[3]),
        pltpu.make_async_copy(in_hbm, win, sems.at[4]),
        pltpu.make_async_copy(out_hbm, wout, sems.at[5]),
    ]
    for copy in copies:
        copy.start()

    def bias(first, number):
        return bias_ref[0:1, first : first + number]

    mask[...] = attention_mask(spot_ref, segment_ref)
    h1_rows = layer_norm(rows_ref[...], affine_ref[0:1, :], affine_ref[3:4, :]).astype(
        jnp.bfloat16)
    h1_rows_ref[...] = h1_rows
    u1_ref[...] = matrix_multiply(h1_ref[...], a_qkv[...]).astype(jnp.bfloat16)
    u1_rows = matrix_multiply(h1_rows, a_qkv[...]).astype(jnp.bfloat16)
    u1_rows_ref[...] = u1_rows

    def project(normed, low, weight, j):
        return (
            matrix_multiply(normed, weight[...])
            + bias(j * width, width)
            + ADAPTER_SCALE * matrix_multiply(low, third_of(b_qkv[...], j))
        ).astype(jnp.bfloat16)

    chunk = 256
    for j, weight, out, copy in ((1, wk, k_ref, copies[0]), (2, wv, v_ref, copies[1])):
        copy.wait()

        def rows_of(i):
            rows = pl.ds(pl.multiple_of(i * chunk, chunk), chunk)
            out[rows, :] = project(h1_ref[rows, :], u1_ref[rows, :], weight, j)

        wide_loop(length // chunk, rows_of)
    copies[2].wait()
    q_ref[...] = project(h1_rows, u1_rows, wq, 0)
    scale = (width // HEADS) ** (-0.5)
    lanes = lax.broadcasted_iota(jnp.int32, lse_ref.shape, 1)
    lse_ref[...] = jnp.zeros(lse_ref.shape, jnp.float32)

    def heads(g):
        pair = pl.ds(pl.multiple_of(g * 128, 128), 128)
        scores = scale * matrix_multiply_transposed_right(both_heads(q_ref[:, pair]), k_ref[:, pair])
        scores = jnp.where(mask[...] > 0.0, scores, MASKED)
        top = jnp.max(scores, axis=1, keepdims=True)
        e = jnp.exp(scores - top)
        total = jnp.sum(e, axis=1, keepdims=True)
        probs = (e * (1.0 / total)).astype(jnp.bfloat16)
        o_ref[:, pair] = side_by_side(matrix_multiply(probs, v_ref[:, pair])).astype(jnp.bfloat16)
        lse_ref[...] = jnp.where(lanes == g, top + jnp.log(total), lse_ref[...])

    wide_loop(HEADS // 2, heads)
    o = o_ref[...]
    uo = matrix_multiply(o, a_o[...]).astype(jnp.bfloat16)
    uo_ref[...] = uo
    copies[3].wait()
    middle = (
        rows_ref[...]
        + matrix_multiply(o, wo[...])
        + bias(3 * width, width)
        + ADAPTER_SCALE * matrix_multiply(uo, b_o[...])
    )
    middle_ref[...] = middle
    h2 = layer_norm(middle, affine_ref[1:2, :], affine_ref[4:5, :]).astype(jnp.bfloat16)
    h2_ref[...] = h2
    uf = matrix_multiply(h2, a_fc[...]).astype(jnp.bfloat16)
    uf_ref[...] = uf
    copies[4].wait()
    for j in range(4):
        part = slice(j * quarter, (j + 1) * quarter)
        pre = (
            matrix_multiply(h2, win[:, part])
            + bias(4 * width + j * quarter, quarter)
            + ADAPTER_SCALE * matrix_multiply(uf, b_fc[:, part])
        )
        pre_ref[:, part] = pre
        f_ref[:, part] = (pre * gelu_parts(pre)[0]).astype(jnp.bfloat16)
    f = f_ref[...]
    up = matrix_multiply(f, a_p[...]).astype(jnp.bfloat16)
    up_ref[...] = up
    copies[5].wait()
    last = (
        middle
        + matrix_multiply(f, wout[...])
        + bias(4 * width + hidden, width)
        + ADAPTER_SCALE * matrix_multiply(up, b_p[...])
    )
    last_ref[...] = last
    final_ref[...] = layer_norm(last, affine_ref[2:3, :], affine_ref[5:6, :]).astype(jnp.bfloat16)


def pack_up(out_ref, part, grad):
    ranks = 3 * RANK if part < 2 else RANK
    wide = grad.shape[1] // 128
    for c in range(wide):
        rows = pl.ds(PARTS[part] + c, ranks, stride=wide)
        out_ref[rows, :] = grad[0:ranks, c * 128 : (c + 1) * 128]


def pack_down(out_ref, part, shift, grad):
    ranks = 3 * RANK if part < 2 else RANK
    slabs = ranks // RANK
    repeated = jnp.concatenate([grad[0:ranks]] * (128 * slabs // ranks), axis=0)
    for slab in range(slabs):
        spread = repeated[128 * slab : 128 * (slab + 1)].T
        spread = jnp.where(spread_places(ranks, slab), spread, 0.0)
        rows = pl.ds(PARTS[part] + shift + slab, 32, stride=slabs)
        out_ref[rows, :] = jnp.sum(spread.reshape(32, 32, 128), axis=1)


def layer_down(grad_ref, spot_ref, segment_ref, affine_ref, h1_ref,
               a_qkv, b_qkv, a_o, b_o, a_fc, b_fc, a_p, b_p,
               q_ref, k_ref, v_ref, u1_ref, u1_rows_ref, h1_rows_ref, lse_ref,
               o_ref, uo_ref, middle_ref, h2_ref, uf_ref, pre_ref, f_ref, up_ref, last_ref,
               o_hbm, in_hbm, out_hbm,
               grad_out,
               wo, win, wout, mask, dpre_ref, do_ref, dq_ref, dk_ref, dv_ref, sems):
    length, width = h1_ref.shape
    hidden = win.shape[1]
    quarter = hidden // 4
    rows_here = grad_ref.shape[0]
    copies = [
        pltpu.make_async_copy(out_hbm, wout, sems.at[0]),
        pltpu.make_async_copy(in_hbm, win, sems.at[1]),
        pltpu.make_async_copy(o_hbm, wo, sems.at[2]),
    ]
    for copy in copies:
        copy.start()
    mask[...] = attention_mask(spot_ref, segment_ref)
    spot_row = spot_ref[...].astype(jnp.float32)
    spot = lane_columns(spot_row)[:, 0:1]
    order_row = lax.broadcasted_iota(jnp.int32, (1, rows_here), 1)
    order = lax.broadcasted_iota(jnp.int32, (rows_here, 1), 0)
    same = spot == spot_row
    repeat = jnp.max(ones_where(same & (order_row < order)), axis=1, keepdims=True)
    merge = ones_where(same) * (1.0 - repeat)
    grad_final = jnp.dot(
        merge, grad_ref[...], precision=lax.Precision.HIGHEST,
        preferred_element_type=jnp.float32)
    dx3 = norm_back(last_ref[...], affine_ref[2:3, :], grad_final)
    dm = dx3.astype(jnp.bfloat16)
    pack_up(grad_out, 7, ADAPTER_SCALE * matrix_multiply_transposed_left(up_ref[...], dm))
    du_p = (ADAPTER_SCALE * matrix_multiply_transposed_right(dm, b_p[...])).astype(jnp.bfloat16)
    ga_p = matrix_multiply_transposed_left(du_p, f_ref[...])
    for b in range(hidden // 1024):
        pack_down(grad_out, 6, 32 * b, ga_p[:, 1024 * b : 1024 * (b + 1)])
    copies[0].wait()
    for j in range(4):
        part = slice(j * quarter, (j + 1) * quarter)
        df = matrix_multiply_transposed_right(dm, wout[part, :]) + matrix_multiply_transposed_right(
            du_p, a_p[part, :])
        dpre_ref[:, part] = (df * gelu_slope(pre_ref[:, part])).astype(jnp.bfloat16)
    dpre = dpre_ref[...]
    pack_up(grad_out, 5, ADAPTER_SCALE * matrix_multiply_transposed_left(uf_ref[...], dpre))
    du_f = (ADAPTER_SCALE * matrix_multiply_transposed_right(dpre, b_fc[...])).astype(jnp.bfloat16)
    pack_down(grad_out, 4, 0, matrix_multiply_transposed_left(du_f, h2_ref[...]))
    copies[1].wait()
    dh2 = matrix_multiply_transposed_right(dpre, win[...]) + matrix_multiply_transposed_right(
        du_f, a_fc[...])
    dx2 = dx3 + norm_back(middle_ref[...], affine_ref[1:2, :], dh2)
    da = dx2.astype(jnp.bfloat16)
    pack_up(grad_out, 3, ADAPTER_SCALE * matrix_multiply_transposed_left(uo_ref[...], da))
    du_o = (ADAPTER_SCALE * matrix_multiply_transposed_right(da, b_o[...])).astype(jnp.bfloat16)
    pack_down(grad_out, 2, 0, matrix_multiply_transposed_left(du_o, o_ref[...]))
    copies[2].wait()
    do_ref[...] = (
        matrix_multiply_transposed_right(da, wo[...])
        + matrix_multiply_transposed_right(du_o, a_o[...])
    ).astype(jnp.bfloat16)
    scale = (width // HEADS) ** (-0.5)
    lanes = lax.broadcasted_iota(jnp.int32, lse_ref.shape, 1)

    def heads(g):
        pair = pl.ds(pl.multiple_of(g * 128, 128), 128)
        q = both_heads(q_ref[:, pair])
        do = both_heads(do_ref[:, pair])
        lse = jnp.sum(jnp.where(lanes == g, lse_ref[...], 0.0), axis=1, keepdims=True)
        scores = scale * matrix_multiply_transposed_right(q, k_ref[:, pair])
        probs = jnp.where(mask[...] > 0.0, jnp.exp(jnp.minimum(scores - lse, 0.0)), 0.0)
        dp = matrix_multiply_transposed_right(do, v_ref[:, pair])
        ds = (probs * (dp - jnp.sum(probs * dp, axis=1, keepdims=True))).astype(jnp.bfloat16)
        dv_ref[:, pair] = matrix_multiply_transposed_left(
            probs.astype(jnp.bfloat16), do).astype(jnp.bfloat16)
        dk_ref[:, pair] = (scale * matrix_multiply_transposed_left(ds, q)).astype(jnp.bfloat16)
        dq_ref[:, pair] = side_by_side(scale * matrix_multiply(ds, k_ref[:, pair])).astype(
            jnp.bfloat16)

    wide_loop(HEADS // 2, heads)
    b_all = b_qkv[...]
    gb = jnp.zeros((NARROW, width), jnp.float32)
    ids = lax.broadcasted_iota(jnp.int32, gb.shape, 0)
    dus = []
    for j, low, grad in ((0, u1_rows_ref, dq_ref), (1, u1_ref, dk_ref), (2, u1_ref, dv_ref)):
        mine = (ids >= j * RANK) & (ids < (j + 1) * RANK)
        gb = jnp.where(mine, ADAPTER_SCALE * matrix_multiply_transposed_left(
            low[...], grad[...]), gb)
        dus.append(ADAPTER_SCALE * matrix_multiply_transposed_right(grad[...], third_of(b_all, j)))
    pack_up(grad_out, 1, gb)
    ga = matrix_multiply_transposed_left(
        dus[0].astype(jnp.bfloat16), h1_rows_ref[...]
    ) + matrix_multiply_transposed_left((dus[1] + dus[2]).astype(jnp.bfloat16), h1_ref[...])
    pack_down(grad_out, 0, 0, ga)


def layer_kernels(rows_here, length, width, hidden):
    low, wide = jnp.bfloat16, jnp.float32
    whole = pl.BlockSpec(memory_space=pltpu.VMEM)
    away = pl.BlockSpec(memory_space=pl.ANY)
    dma = pltpu.SemaphoreType.DMA
    params = pltpu.CompilerParams(vmem_limit_bytes=60 << 20)
    kept = [
        ((rows_here, width), low),
        ((length, width), low),
        ((length, width), low),
        ((length, NARROW), low),
        ((rows_here, NARROW), low),
        ((rows_here, width), low),
        ((2 * rows_here, 128), wide),
        ((rows_here, width), low),
        ((rows_here, NARROW), low),
        ((rows_here, width), wide),
        ((rows_here, width), low),
        ((rows_here, NARROW), low),
        ((rows_here, hidden), wide),
        ((rows_here, hidden), low),
        ((rows_here, NARROW), low),
        ((rows_here, width), wide),
    ]
    up = pl.pallas_call(
        layer_up,
        out_shape=[jax.ShapeDtypeStruct(*k) for k in [((rows_here, width), low)] + kept],
        in_specs=[whole] * 14 + [away] * 4,
        out_specs=[whole] * 17,
        scratch_shapes=[pltpu.VMEM((width, width), low)] * 4
        + [
            pltpu.VMEM((width, hidden), low),
            pltpu.VMEM((hidden, width), low),
            pltpu.VMEM((2 * rows_here, length), wide),
            dma((6,)),
        ],
        compiler_params=params,
        name="layer_up",
    )
    down = pl.pallas_call(
        layer_down,
        out_shape=jax.ShapeDtypeStruct((PARTS[-1], 128), wide),
        in_specs=[whole] * 29 + [away] * 3,
        out_specs=whole,
        scratch_shapes=[
            pltpu.VMEM((width, width), low),
            pltpu.VMEM((width, hidden), low),
            pltpu.VMEM((hidden, width), low),
            pltpu.VMEM((2 * rows_here, length), wide),
            pltpu.VMEM((rows_here, hidden), low),
            pltpu.VMEM((rows_here, width), low),
            pltpu.VMEM((rows_here, width), low),
            pltpu.VMEM((length, width), low),
            pltpu.VMEM((length, width), low),
            dma((3,)),
        ],
        compiler_params=params,
        name="layer_down",
    )
    return up, down


def settle_step(held_ref, segment_ref, spot_ref, place_ref, affine_ref, h1_out, rows_out, place_cols):
    length = segment_ref.shape[1]
    span = place_ref.shape[0]
    segment = segment_ref[...].astype(jnp.float32)
    steps = lax.broadcasted_iota(jnp.int32, (1, length), 1).astype(jnp.float32)
    ids = lax.broadcasted_iota(jnp.int32, (32, length), 0).astype(jnp.float32)
    starts = jnp.sum(ones_where(segment < ids), axis=1, keepdims=True)
    place = steps - jnp.sum(jnp.where(segment == ids, starts, 0.0), axis=0, keepdims=True)
    place_cols[...] = lane_columns(place)
    spot = lane_columns(spot_ref[...].astype(jnp.float32))[:, 0:1]
    at_spot = steps == spot
    spot_place = jnp.sum(jnp.where(at_spot, place, 0.0), axis=1, keepdims=True)

    def placed(column):
        ids_here = lax.broadcasted_iota(jnp.int32, (column.shape[0], span), 1).astype(jnp.float32)
        return matrix_multiply(low_ones(ids_here == column), place_ref[...])

    rows_out[...] = matrix_multiply(low_ones(at_spot), held_ref[...]) + placed(spot_place)

    @pl.loop(0, length // 128)
    def _(a):
        rows = pl.ds(pl.multiple_of(a * 128, 128), 128)
        stream = held_ref[rows, :].astype(jnp.float32) + placed(place_cols[rows, 0:1])
        h1_out[rows, :] = layer_norm(stream, affine_ref[0:1, :], affine_ref[3:4, :]).astype(
            jnp.bfloat16)


def settle_rows(held, segments, spots, place_table, affine):
    length, width = held.shape
    whole = pl.BlockSpec(memory_space=pltpu.VMEM)
    return pl.pallas_call(
        settle_step,
        out_shape=[
            jax.ShapeDtypeStruct((length, width), jnp.bfloat16),
            jax.ShapeDtypeStruct((spots.shape[1], width), jnp.float32),
        ],
        in_specs=[whole] * 5,
        out_specs=[whole] * 2,
        scratch_shapes=[pltpu.VMEM((length, 128), jnp.float32)],
        compiler_params=pltpu.CompilerParams(vmem_limit_bytes=32 << 20),
        name="settle_step",
    )(held, segments, spots, place_table[:256], affine)


def visit_step(block, wanted_ref, held_ref, table_hbm, out_ref, table, columns, acc, sem):
    copy = pltpu.make_async_copy(table_hbm, table, sem)
    copy.start()
    columns[...] = lane_columns(wanted_ref[...].astype(jnp.float32))
    rows_here = table.shape[0]
    full = rows_here // block
    copy.wait()

    @pl.loop(0, held_ref.shape[0] // 256)
    def _(a):
        rows = pl.ds(pl.multiple_of(a * 256, 256), 256)
        acc[...] = held_ref[rows, :].astype(jnp.float32)

        def add(first, number):
            ids = lax.broadcasted_iota(jnp.int32, (256, number), 1) + first
            chosen = low_ones(ids.astype(jnp.float32) == columns[rows, 0:1])
            acc[...] += matrix_multiply(chosen, table[pl.ds(first, number), :])

        @pl.loop(0, full)
        def _(j):
            add(pl.multiple_of(j * block, block), block)

        add(full * block, rows_here - full * block)
        out_ref[rows, :] = acc[...].astype(jnp.bfloat16)


def visit_rows(wanted, held, table):
    length, width = held.shape
    whole = pl.BlockSpec(memory_space=pltpu.VMEM)
    return pl.pallas_call(
        partial(visit_step, 256),
        out_shape=jax.ShapeDtypeStruct((length, width), jnp.bfloat16),
        in_specs=[whole, whole, pl.BlockSpec(memory_space=pl.ANY)],
        out_specs=whole,
        scratch_shapes=[
            pltpu.VMEM(table.shape, jnp.bfloat16),
            pltpu.VMEM((length, 128), jnp.float32),
            pltpu.VMEM((256, width), jnp.float32),
            pltpu.SemaphoreType.DMA,
        ],
        compiler_params=pltpu.CompilerParams(vmem_limit_bytes=40 << 20),
        name="visit_step",
    )(wanted, held, table)


def local(
    mesh_sizes,
    packed_symbol_codes,
    article_numbering,
    target_spots,
    answer_flags,
    shared_embedding,
    spot_embedding,
    combined_qkv_weights,
    attend_outgoing_weights,
    dense_incoming_weights,
    dense_outgoing_weights,
    layernorm_affine,
    bias_terms,
    adaptor_float_copies,
    average_moments,
    squared_moments,
):
    rows_here = target_spots.shape[1]
    shard_rows = shared_embedding.shape[0]
    table = jnp.pad(shared_embedding, ((0, -shard_rows % 16), (0, 0)))
    fast_h1, fast_rows, labels, counts, crowded, *factors = embed(
        mesh_sizes,
        shard_rows,
        packed_symbol_codes,
        article_numbering,
        target_spots,
        answer_flags,
        spot_embedding,
        layernorm_affine,
        adaptor_float_copies,
        table,
    )

    sharers = mesh_sizes[1]
    ring = [(j, (j + 1) % sharers) for j in range(sharers)]

    def visit(carry):
        turns, tokens, held = carry
        wanted = tokens - lax.axis_index("vocab") * shard_rows
        wanted = jnp.where((wanted >= 0) & (wanted < shard_rows), wanted, -1)
        kept = jnp.where(turns == sharers, jnp.zeros((), jnp.bfloat16), held)
        held = visit_rows(wanted, kept, table)
        return turns - 1, lax.ppermute(tokens, "vocab", ring), lax.ppermute(held, "vocab", ring)

    def settle(carry):
        _, held, _ = carry
        settled, rows = settle_rows(
            held, article_numbering, target_spots, spot_embedding, layernorm_affine
        )
        return jnp.zeros((), jnp.int32), settled, rows

    overflow = crowded.reshape(())
    _, _, held = lax.while_loop(
        lambda carry: carry[0] > 0, visit, (overflow * sharers, packed_symbol_codes, fast_h1)
    )
    _, h1, stream_rows = lax.while_loop(
        lambda carry: carry[0] > 0, settle, (overflow, held, fast_rows)
    )
    length, width = h1.shape
    hidden = dense_incoming_weights.shape[1]
    layer_up_call, layer_down_call = layer_kernels(rows_here, length, width, hidden)
    final_rows, *kept = layer_up_call(
        h1,
        stream_rows,
        article_numbering,
        target_spots,
        layernorm_affine,
        bias_terms[None, :],
        *factors,
        combined_qkv_weights,
        attend_outgoing_weights,
        dense_incoming_weights,
        dense_outgoing_weights,
    )
    grad_rows, loss_part = head(
        mesh_sizes, shard_rows, final_rows, labels, counts, table
    )
    local_grad = layer_down_call(
        grad_rows,
        target_spots,
        article_numbering,
        layernorm_affine,
        h1,
        *factors,
        *kept,
        attend_outgoing_weights,
        dense_incoming_weights,
        dense_outgoing_weights,
    )
    (
        refreshed_thin_pairs,
        updated_first_moment,
        updated_second_moment,
        gradient_global_norm,
        smoothed_entropy_cost,
    ) = reduce_and_update(
        mesh_sizes, local_grad, adaptor_float_copies, average_moments, squared_moments, loss_part
    )
    return (
        refreshed_thin_pairs,
        updated_first_moment,
        updated_second_moment,
        gradient_global_norm,
        smoothed_entropy_cost,
    )


def solution(mesh):
    return jax.shard_map(
        partial(local, (mesh.shape["dp"], mesh.shape["vocab"])),
        mesh=mesh,
        in_specs=(
            P(("dp", "vocab"), None),
            P(("dp", "vocab"), None),
            P(("dp", "vocab"), None),
            P(("dp", "vocab"), None),
            P("vocab", None),
            P(),
            P(),
            P(),
            P(),
            P(),
            P(),
            P(),
            P(),
            P(),
            P(),
        ),
        out_specs=(P(), P(), P(), P(), P()),
        check_vma=False,
    )
```

```python
from functools import partial
import math

import jax
import jax.numpy as jnp
from jax import lax
from jax.experimental import pallas as pl
from jax.experimental.pallas import tpu as pltpu
from jax.sharding import PartitionSpec as P

MODEL_WIDTH = 1024
HEADS = 16
FEEDFWD_UNITS = 4096
VOCAB_SIZE = 50257
RANK = 4
STEP = 10


ADAPTER_SCALE = 8.0
NORM_EPS = 1e-05
GRAD_CLIP = 0.0001
STRIDE_LENGTH = 0.02
BETA_ONE = 0.9
BETA_TWO = 0.999
SHRINK_PENALTY = 0.01
STABILITY_FLOOR = 1e-08
MASKED = -1e30
MESH = pl.DeviceIdType.MESH


def matrix_multiply(left, right):
    return jnp.dot(left, right, preferred_element_type=jnp.float32)


def matrix_multiply_transposed_left(left, right):
    return lax.dot_general(
        left, right, (((0,), (0,)), ((), ())), preferred_element_type=jnp.float32
    )


def matrix_multiply_transposed_right(left, right):
    return lax.dot_general(
        left, right, (((1,), (1,)), ((), ())), preferred_element_type=jnp.float32
    )


def layer_norm(stream, gain, shift):
    centred = stream - jnp.mean(stream, axis=-1, keepdims=True)
    spread = lax.rsqrt(jnp.mean(centred * centred, axis=-1, keepdims=True) + NORM_EPS)
    return centred * spread * gain + shift


def adaptive_moment_update(grad, weight, first, second):
    first_new = BETA_ONE * first + (1.0 - BETA_ONE) * grad
    second_new = BETA_TWO * second + (1.0 - BETA_TWO) * grad * grad
    debiased_mean_estimate = first_new / (1.0 - BETA_ONE**STEP)
    debiased_variance_estimate = second_new / (1.0 - BETA_TWO**STEP)
    weight_new = weight - STRIDE_LENGTH * (
        debiased_mean_estimate / (jnp.sqrt(debiased_variance_estimate) + STABILITY_FLOOR)
        + SHRINK_PENALTY * weight
    )
    return (weight_new, first_new, second_new)


def sum_and_step(dp_size, vocab_size, grad_ref, weight_ref, first_ref, second_ref, loss_ref,
                 weight_out, first_out, second_out, norm_out, loss_out,
                 parts, planes, total, losses, send_a, recv_a, send_b, recv_b, send_c, recv_c,
                 send_d, recv_d):
    my_plane = lax.axis_index("dp")
    me = lax.axis_index("vocab")

    def across(j):
        return (my_plane, lax.rem(me + j, vocab_size))

    def along(i):
        return (lax.rem(my_plane + i, dp_size), me)

    barrier = pltpu.get_barrier_semaphore()

    @pl.loop(1, vocab_size)
    def _(j):
        pl.semaphore_signal(barrier, inc=1, device_id=across(j), device_id_type=MESH)

    @pl.loop(1, dp_size)
    def _(i):
        pl.semaphore_signal(barrier, inc=1, device_id=along(i), device_id_type=MESH)

    pl.semaphore_wait(barrier, vocab_size + dp_size - 2)

    def part_copy(j):
        peer = across(j)
        return pltpu.make_async_remote_copy(
            src_ref=grad_ref.at[peer[1]], dst_ref=parts.at[me],
            send_sem=send_a.at[peer[1]], recv_sem=recv_a.at[me],
            device_id=peer, device_id_type=MESH)

    def part_arrival(j):
        peer = across(j)
        return pltpu.make_async_remote_copy(
            src_ref=grad_ref.at[peer[1]], dst_ref=parts.at[peer[1]],
            send_sem=send_a.at[peer[1]], recv_sem=recv_a.at[peer[1]],
            device_id=peer, device_id_type=MESH)

    def plane_copy(i):
        peer = along(i)
        return pltpu.make_async_remote_copy(
            src_ref=planes.at[my_plane], dst_ref=planes.at[my_plane],
            send_sem=send_b.at[peer[0]], recv_sem=recv_b.at[my_plane],
            device_id=peer, device_id_type=MESH)

    def plane_arrival(i):
        peer = along(i)
        return pltpu.make_async_remote_copy(
            src_ref=planes.at[my_plane], dst_ref=planes.at[peer[0]],
            send_sem=send_b.at[peer[0]], recv_sem=recv_b.at[peer[0]],
            device_id=peer, device_id_type=MESH)

    def loss_copy(i):
        peer = along(i)
        return pltpu.make_async_remote_copy(
            src_ref=loss_ref, dst_ref=losses.at[my_plane],
            send_sem=send_d.at[peer[0]], recv_sem=recv_d.at[my_plane],
            device_id=peer, device_id_type=MESH)

    def loss_arrival(i):
        peer = along(i)
        return pltpu.make_async_remote_copy(
            src_ref=loss_ref, dst_ref=losses.at[peer[0]],
            send_sem=send_d.at[peer[0]], recv_sem=recv_d.at[peer[0]],
            device_id=peer, device_id_type=MESH)

    def total_copy(j):
        peer = across(j)
        return pltpu.make_async_remote_copy(
            src_ref=total.at[me], dst_ref=total.at[me],
            send_sem=send_c.at[peer[1]], recv_sem=recv_c.at[me],
            device_id=peer, device_id_type=MESH)

    def total_arrival(j):
        peer = across(j)
        return pltpu.make_async_remote_copy(
            src_ref=total.at[me], dst_ref=total.at[peer[1]],
            send_sem=send_c.at[peer[1]], recv_sem=recv_c.at[peer[1]],
            device_id=peer, device_id_type=MESH)

    @pl.loop(1, vocab_size)
    def _(j):
        part_copy(j).start()

    @pl.loop(1, dp_size)
    def _(i):
        loss_copy(i).start()

    losses[my_plane] = loss_ref[...]
    parts[me] = grad_ref[me]

    @pl.loop(1, vocab_size)
    def _(j):
        part_arrival(j).wait_recv()

    planes[my_plane] = lax.fori_loop(
        1, vocab_size, lambda j, held: held + parts[j], parts[0])

    @pl.loop(1, dp_size)
    def _(i):
        plane_copy(i).start()

    @pl.loop(1, dp_size)
    def _(i):
        plane_arrival(i).wait_recv()

    total[me] = lax.fori_loop(1, dp_size, lambda i, held: held + planes[i], planes[0])

    @pl.loop(1, vocab_size)
    def _(j):
        total_copy(j).start()

    @pl.loop(1, vocab_size)
    def _(j):
        part_copy(j).wait_send()

    @pl.loop(1, dp_size)
    def _(i):
        plane_copy(i).wait_send()

    @pl.loop(1, vocab_size)
    def _(j):
        total_arrival(j).wait_recv()

    @pl.loop(1, vocab_size)
    def _(j):
        total_copy(j).wait_send()

    def squares(j, held):
        piece = total[j]
        return held + piece * piece

    gathered = lax.fori_loop(0, vocab_size, squares, jnp.zeros(parts.shape[1:], jnp.float32))
    norm = jnp.sqrt(jnp.sum(gathered, keepdims=True))
    norm_out[...] = norm

    @pl.loop(1, dp_size)
    def _(i):
        loss_arrival(i).wait_recv()
        loss_copy(i).wait_send()

    loss_out[...] = jnp.sum(losses[...], axis=0)[0:1, 0:1]
    shrink = GRAD_CLIP / jnp.maximum(norm, GRAD_CLIP)

    @pl.loop(0, vocab_size)
    def _(j):
        weight, first, second = adaptive_moment_update(
            total[j] * shrink, weight_ref[j], first_ref[j], second_ref[j])
        weight_out[j] = weight
        first_out[j] = first
        second_out[j] = second


def reduce_and_update(mesh_sizes, local_grad, weights, first, second, loss):
    dp_size, vocab_size = mesh_sizes
    number = local_grad.size
    rows = number // (128 * vocab_size)
    shape = (vocab_size, rows, 128)
    block = pltpu.VMEM(shape, jnp.float32)
    whole = pl.BlockSpec(memory_space=pltpu.VMEM)
    weight_new, first_new, second_new, norm, total_loss = pl.pallas_call(
        partial(sum_and_step, dp_size, vocab_size),
        out_shape=[jax.ShapeDtypeStruct(shape, jnp.float32)] * 3
        + [jax.ShapeDtypeStruct((1, 1), jnp.float32)] * 2,
        in_specs=[whole] * 5,
        out_specs=[whole] * 5,
        scratch_shapes=[
            block,
            pltpu.VMEM((dp_size, rows, 128), jnp.float32),
            block,
            pltpu.VMEM((dp_size, 8, 128), jnp.float32),
            pltpu.SemaphoreType.DMA((vocab_size,)),
            pltpu.SemaphoreType.DMA((vocab_size,)),
            pltpu.SemaphoreType.DMA((dp_size,)),
            pltpu.SemaphoreType.DMA((dp_size,)),
            pltpu.SemaphoreType.DMA((vocab_size,)),
            pltpu.SemaphoreType.DMA((vocab_size,)),
            pltpu.SemaphoreType.DMA((dp_size,)),
            pltpu.SemaphoreType.DMA((dp_size,)),
        ],
        compiler_params=pltpu.CompilerParams(
            collective_id=5, has_side_effects=True, vmem_limit_bytes=24 << 20
        ),
        name="sum_and_step",
    )(*[piece.reshape(shape) for piece in (local_grad, weights, first, second)], loss)
    flat = [piece.reshape(-1) for piece in (weight_new, first_new, second_new)]
    return (*flat, norm.reshape(()), total_loss.reshape(()))


TILE = 32


def head_step(dp_size, vocab_size, block, owned, hf_ref, label_ref, count_ref, table_hbm, grad_out, loss_out,
              table, hf_all, label_all, exps, exps_rest, tops, run_top, run_sum, run_smooth,
              run_goal, offset, z_even, z_odd, z_rest, dz_even, dz_odd, rest_even, rest_odd,
              acc_even, acc_odd, lse_tile, share_tile, stats_all,
              from_core, from_chip, leaving,
              table_sem, label_send, label_recv, hf_send, hf_recv,
              stat_send, stat_recv, core_send, core_recv, chip_send, chip_recv):
    plane = lax.axis_index("dp")
    me = lax.axis_index("vocab")
    chips = vocab_size // 2
    chip = me // 2
    core = lax.rem(me, 2)
    other = 2 * chip + 1 - core
    sibling = (plane, other)
    held = table_hbm.shape[0]
    full = held // block
    rest = held - full * block
    padded = table.shape[0] - full * block
    base = me * owned
    rows_each = hf_ref.shape[0]
    pair = 2 * rows_each
    width = hf_ref.shape[1]

    def partner(k):
        out = 0
        bit = 1
        while bit < chips:
            out = out + lax.rem(chip // bit + lax.rem(k // bit, 2), 2) * bit
            bit *= 2
        return out

    def across(j):
        return (plane, lax.rem(me + j, vocab_size))

    def table_copy(j, number):
        rows = pl.ds(pl.multiple_of(j * block, 16), number)
        return pltpu.make_async_copy(table_hbm.at[rows], table.at[rows], table_sem.at[j])

    @pl.loop(0, full)
    def _(j):
        table_copy(j, block).start()

    table_copy(full, rest).start()

    table[held:, :] = jnp.zeros((padded - rest, width), jnp.bfloat16)
    barrier = pltpu.get_barrier_semaphore()

    @pl.loop(1, vocab_size)
    def _(j):
        pl.semaphore_signal(barrier, inc=1, device_id=across(j), device_id_type=MESH)

    pl.semaphore_wait(barrier, vocab_size - 1)

    def remote(src, dst, send, recv, peer):
        return pltpu.make_async_remote_copy(
            src_ref=src, dst_ref=dst, send_sem=send, recv_sem=recv,
            device_id=peer, device_id_type=MESH)

    def hf_to_sibling():
        return remote(hf_ref, hf_all.at[me], hf_send.at[0], hf_recv.at[me], sibling)

    def hf_copy(k):
        return remote(hf_ref, hf_all.at[me], hf_send.at[k], hf_recv.at[me],
                      (plane, 2 * partner(k) + core))

    def hf_arrival(source):
        return remote(hf_ref, hf_all.at[source], hf_send.at[0], hf_recv.at[source], sibling)

    def hf_forward(k):
        source = 2 * partner(k) + core
        return remote(hf_all.at[source], hf_all.at[source], hf_send.at[chips + k],
                      hf_recv.at[source], sibling)

    def label_copy(j):
        peer = across(j)
        return remote(label_ref, label_all.at[me], label_send.at[peer[1]], label_recv.at[me], peer)

    def label_arrival(source):
        return remote(label_ref, label_all.at[source], label_send.at[source],
                      label_recv.at[source], sibling)

    near = min(3, chips)
    hf_to_sibling().start()

    @pl.loop(1, near)
    def _(k):
        hf_copy(k).start()

    @pl.loop(1, vocab_size)
    def _(j):
        label_copy(j).start()

    hf_all[me] = hf_ref[...]
    label_all[me] = label_ref[...]
    lanes = lax.broadcasted_iota(jnp.int32, (pair, 128), 1)

    def label_row(c, i):
        rows = label_all[pl.ds(2 * c, 2), i : i + 1, :].astype(jnp.float32)
        return jnp.concatenate([rows[0], rows[1]], axis=1)

    def set_offset(c):
        offset[...] = lane_columns(label_row(c, 0)).astype(jnp.int32) - base - lanes

    def folded(x):
        return sum(x[:, i * 128 : (i + 1) * 128] for i in range(1, x.shape[1] // 128)) + x[:, :128]

    def chunk_up(k, first):
        c = partner(k)
        if first:
            hf_arrival(other).wait_recv()
            label_arrival(other).wait_recv()
        else:
            hf_arrival(2 * c + core).wait_recv()
            hf_forward(k).start()
            label_arrival(2 * c).wait_recv()
            label_arrival(2 * c + 1).wait_recv()
            hf_arrival(2 * c + 1 - core).wait_recv()
        set_offset(c)
        run_top[...] = jnp.full((pair, 128), MASKED, jnp.float32)
        for ref in (run_sum, run_smooth, run_goal):
            ref[...] = jnp.zeros((pair, 128), jnp.float32)
        start = pl.multiple_of(k * pair, pair)

        def multiply(j, z_ref):
            if first:
                table_copy(j, rest if z_ref is z_rest else block).wait()
            rows = pl.ds(pl.multiple_of(j * block, 16), z_ref.shape[1])
            hidden = hf_all[pl.ds(2 * c, 2)].reshape(pair, width)
            z_ref[...] = matrix_multiply_transposed_right(hidden, table[rows, :])

        def reduce_full(j, z_ref):
            for r in range(pair // TILE):
                rows = slice(r * TILE, (r + 1) * TILE)
                there = pl.ds(start + r * TILE, TILE)
                z = z_ref[rows, :]
                old = run_top[rows, :]
                top = jnp.maximum(old, jnp.max(z, axis=1, keepdims=True))
                run_top[rows, :] = top
                tops[k, j, rows, :] = top
                gap = offset[rows, :] - j * block
                total = jnp.zeros((TILE, 128), jnp.float32)
                smooth = jnp.zeros((TILE, 128), jnp.float32)
                goal = jnp.zeros((TILE, 128), jnp.float32)
                for i in range(block // 128):
                    part = slice(i * 128, (i + 1) * 128)
                    piece = z[:, part]
                    e = jnp.exp(piece - top)
                    exps[j, there, part] = e
                    total = total + e
                    smooth = smooth + piece
                    goal = goal + jnp.where(gap == i * 128, piece, 0.0)
                run_sum[rows, :] = run_sum[rows, :] * jnp.exp(old - top) + total
                run_smooth[rows, :] = run_smooth[rows, :] + smooth
                run_goal[rows, :] = run_goal[rows, :] + goal

        def reduce_rest():
            for r in range(pair // TILE):
                rows = slice(r * TILE, (r + 1) * TILE)
                there = pl.ds(start + r * TILE, TILE)
                spot = lanes[rows, :]
                limit = jnp.minimum(VOCAB_SIZE - base, owned) - full * block - spot
                gap = offset[rows, :] - full * block
                pieces = []
                for i in range(padded // 128):
                    piece = z_rest[rows, i * 128 : (i + 1) * 128]
                    pieces.append((i * 128 < limit, piece))
                highest = jnp.where(pieces[0][0], pieces[0][1], MASKED)
                for valid, piece in pieces[1:]:
                    highest = jnp.maximum(highest, jnp.where(valid, piece, MASKED))
                old = run_top[rows, :]
                top = jnp.maximum(old, jnp.max(highest, axis=1, keepdims=True))
                run_top[rows, :] = top
                tops[k, full, rows, :] = top
                total = jnp.zeros((TILE, 128), jnp.float32)
                smooth = jnp.zeros((TILE, 128), jnp.float32)
                goal = jnp.zeros((TILE, 128), jnp.float32)
                for i, (valid, piece) in enumerate(pieces):
                    e = jnp.where(valid, jnp.exp(piece - top), 0.0)
                    exps_rest[there, i * 128 : (i + 1) * 128] = e
                    total = total + e
                    smooth = smooth + jnp.where(valid, piece, 0.0)
                    goal = goal + jnp.where(valid & (gap == i * 128), piece, 0.0)
                run_sum[rows, :] = run_sum[rows, :] * jnp.exp(old - top) + total
                run_smooth[rows, :] = run_smooth[rows, :] + smooth
                run_goal[rows, :] = run_goal[rows, :] + goal

        multiply(0, z_even)
        turns = (full - 1) // 2

        if turns > 0:
            @pl.loop(0, turns)
            def _(t):
                multiply(2 * t + 1, z_odd)
                reduce_full(2 * t, z_even)
                multiply(2 * t + 2, z_even)
                reduce_full(2 * t + 1, z_odd)

        if full - 2 * turns == 2:
            multiply(full - 1, z_odd)
            reduce_full(full - 2, z_even)
            multiply(full, z_rest)
            reduce_full(full - 1, z_odd)
        else:
            multiply(full, z_rest)
            reduce_full(full - 1, z_even)
        reduce_rest()

        def row_sum(ref):
            return jnp.sum(ref[...].T, axis=0, keepdims=True)

        ids = lax.broadcasted_iota(jnp.int32, (8, pair), 0)
        packed = jnp.where(ids == 0, run_top[...].T[0:1, :], 0.0)
        for i, ref in enumerate((run_sum, run_smooth, run_goal)):
            packed = jnp.where(ids == i + 1, row_sum(ref), packed)
        stats_all[me, c] = packed

    chunk_up(0, True)

    @pl.loop(near, chips)
    def _(k):
        hf_copy(k).start()

    @pl.loop(1, chips)
    def _(k):
        chunk_up(k, False)

    def stat_copy(j):
        peer = across(j)
        return remote(stats_all.at[me], stats_all.at[me], stat_send.at[peer[1]],
                      stat_recv.at[me], peer)

    def stat_arrival(j):
        source = across(j)[1]
        return remote(stats_all.at[me], stats_all.at[source], stat_send.at[source],
                      stat_recv.at[source], across(j))

    @pl.loop(1, vocab_size)
    def _(j):
        stat_copy(j).start()

    @pl.loop(1, vocab_size)
    def _(j):
        stat_arrival(j).wait_recv()

    count = jnp.maximum(count_ref[1:2, 0:1], 1.0)

    def totals_of(c):
        here = stats_all[:, c]
        tops_here = here[:, 0:1, :]
        top = jnp.max(tops_here, axis=0)
        total = jnp.sum(here[:, 1:2, :] * jnp.exp(tops_here - top[None]), axis=0)
        return top + jnp.log(total), jnp.sum(here[:, 2:3, :], axis=0), jnp.sum(
            here[:, 3:4, :], axis=0)

    def chunk_loss(c, held_loss):
        lse, smooth, goal = totals_of(c)
        return held_loss + label_row(c, 1) * (lse - 0.9 * goal - 0.1 * smooth / VOCAB_SIZE)

    slots = from_core.shape[0]
    columns_each = width // 4

    def core_copy(k, n, acc):
        half = pl.ds(pl.multiple_of((1 - core) * rows_each, rows_each), rows_each)
        part = pl.ds(pl.multiple_of(n * columns_each, columns_each), columns_each)
        return remote(acc.at[half, part], from_core.at[lax.rem(k, slots), :, part],
                      core_send.at[k, n], core_recv.at[k, n], sibling)

    def chip_copy(k, n):
        part = pl.ds(pl.multiple_of(n * columns_each, columns_each), columns_each)
        return remote(leaving.at[k - 1, :, part], from_chip.at[k - 1, :, part],
                      chip_send.at[k, n], chip_recv.at[k, n], (plane, 2 * partner(k) + core))

    def prepare(k):
        c = partner(k)
        lse, _, _ = totals_of(c)
        lse_tile[...] = lane_columns(lse)
        share_tile[...] = lane_columns(label_row(c, 1) / count)
        set_offset(c)

    quarter = pair // 4

    def grads(k, n, dz_ref, rest_ref):
        for r in range(quarter // TILE):
            first = pl.multiple_of(n * quarter + r * TILE, TILE)
            rows = pl.ds(first, TILE)
            there = pl.ds(pl.multiple_of(k * pair + first, TILE), TILE)
            share = share_tile[rows, :]
            lse = lse_tile[rows, :]
            low = share * (0.1 / VOCAB_SIZE)
            high = low + 0.9 * share
            gap = offset[rows, :]
            for j in range(full):
                factor = share * jnp.exp(tops[k, j, rows, :] - lse)
                for i in range(block // 128):
                    at = j * block + i * 128
                    e = exps[j, there, i * 128 : (i + 1) * 128]
                    dz = e * factor - jnp.where(gap == at, high, low)
                    dz_ref[rows, at : at + 128] = dz.astype(jnp.bfloat16)
            factor = share * jnp.exp(tops[k, full, rows, :] - lse)
            limit = jnp.minimum(VOCAB_SIZE - base, owned) - full * block - lanes[0:TILE, :]
            for i in range(padded // 128):
                part = slice(i * 128, (i + 1) * 128)
                at = full * block + i * 128
                dz = exps_rest[there, part] * factor - jnp.where(gap == at, high, low)
                rest_ref[rows, part] = jnp.where(i * 128 < limit, dz, 0.0).astype(jnp.bfloat16)

    def gather(k, n, dz_ref, rest_ref, acc):
        part = pl.ds(pl.multiple_of(n * columns_each, columns_each), columns_each)
        acc[:, part] = matrix_multiply(
            dz_ref[...], table[pl.ds(0, full * block), part]
        ) + matrix_multiply(rest_ref[...], table[pl.ds(full * block, padded), part])

    def finish(k, n, acc):
        core_copy(k, n, acc).wait()
        own = pl.ds(pl.multiple_of(core * rows_each, rows_each), rows_each)
        part = pl.ds(pl.multiple_of(n * columns_each, columns_each), columns_each)
        return from_core[lax.rem(k, slots), :, part] + acc[own, part]

    def ship(k, n, acc):
        part = pl.ds(pl.multiple_of(n * columns_each, columns_each), columns_each)
        leaving[k - 1, :, part] = finish(k, n, acc).astype(jnp.bfloat16)
        chip_copy(k, n).start()

    def stage(k, now, later, acc, acc_before):
        if later is not None:
            prepare(k - 1)

        @pl.loop(0, 4)
        def _(n):
            gather(k, n, *now, acc)
            if later is not None:
                grads(k - 1, n, *later)
            core_copy(k, n, acc).start()
            if later is not None:
                @pl.when(n > 0)
                def _():
                    ship(k, n - 1, acc)

            if acc_before is not None:
                @pl.when((n == 0) & (k < chips - 1))
                def _():
                    ship(k + 1, 3, acc_before)

    evens = ((dz_even, rest_even), acc_even)
    odds = ((dz_odd, rest_odd), acc_odd)
    prepare(chips - 1)

    @pl.loop(0, 4)
    def _(n):
        grads(chips - 1, n, *odds[0])

    @pl.loop(0, chips // 2 - 1)
    def _(t):
        k = chips - 1 - 2 * t
        stage(k, odds[0], evens[0], acc_odd, acc_even)
        stage(k - 1, evens[0], odds[0], acc_even, acc_odd)

    stage(1, odds[0], evens[0], acc_odd, acc_even if chips > 2 else None)
    stage(0, evens[0], None, acc_even, acc_odd)

    loss = lax.fori_loop(0, chips, chunk_loss, jnp.zeros((1, pair), jnp.float32))
    loss_out[...] = jnp.broadcast_to(jnp.sum(loss, keepdims=True) / count, loss_out.shape)
    for n in range(4):
        grad_out[:, n * columns_each : (n + 1) * columns_each] = finish(0, n, acc_even)

    @pl.loop(1, chips)
    def _(t):
        k = chips - t
        for n in range(4):
            chip_copy(k, n).wait_recv()
        grad_out[...] += from_chip[k - 1].astype(jnp.float32)

    hf_to_sibling().wait_send()

    @pl.loop(1, chips)
    def _(k):
        hf_copy(k).wait_send()
        hf_forward(k).wait_send()
        for n in range(4):
            chip_copy(k, n).wait_send()

    @pl.loop(1, vocab_size)
    def _(j):
        label_copy(j).wait_send()
        stat_copy(j).wait_send()


def head(mesh_sizes, owned, final_rows, labels, counts, table):
    dp_size, vocab_size = mesh_sizes
    rows, width = final_rows.shape
    held = table.shape[0]
    block = 1024
    full = held // block
    rest = -(-(held - full * block) // 128) * 128
    chips = vocab_size // 2
    pair = 2 * rows
    low, wide = jnp.bfloat16, jnp.float32
    whole = pl.BlockSpec(memory_space=pltpu.VMEM)
    dma = pltpu.SemaphoreType.DMA
    tile = pltpu.VMEM((pair, 128), wide)
    grad, loss = pl.pallas_call(
        partial(head_step, dp_size, vocab_size, block, owned),
        out_shape=[
            jax.ShapeDtypeStruct((rows, width), wide),
            jax.ShapeDtypeStruct((8, 128), wide),
        ],
        in_specs=[whole, whole, whole, pl.BlockSpec(memory_space=pl.ANY)],
        out_specs=[whole, whole],
        scratch_shapes=[
            pltpu.VMEM((full * block + rest, width), low),
            pltpu.VMEM((vocab_size, rows, width), low),
            pltpu.VMEM((vocab_size, 8, rows), jnp.int32),
            pltpu.VMEM((full, vocab_size * rows, block), wide),
            pltpu.VMEM((vocab_size * rows, rest), wide),
            pltpu.VMEM((chips, full + 1, pair, 128), wide),
            tile,
            tile,
            tile,
            tile,
            pltpu.VMEM((pair, 128), jnp.int32),
            pltpu.VMEM((pair, block), wide),
            pltpu.VMEM((pair, block), wide),
            pltpu.VMEM((pair, rest), wide),
            pltpu.VMEM((pair, full * block), low),
            pltpu.VMEM((pair, full * block), low),
            pltpu.VMEM((pair, rest), low),
            pltpu.VMEM((pair, rest), low),
            pltpu.VMEM((pair, width), wide),
            pltpu.VMEM((pair, width), wide),
            tile,
            tile,
            pltpu.VMEM((vocab_size, chips, 8, pair), wide),
            pltpu.VMEM((3, rows, width), wide),
            pltpu.VMEM((chips - 1, rows, width), low),
            pltpu.VMEM((chips - 1, rows, width), low),
            dma((full + 1,)),
            dma((vocab_size,)),
            dma((vocab_size,)),
            dma((2 * chips,)),
            dma((vocab_size,)),
            dma((vocab_size,)),
            dma((vocab_size,)),
            dma((chips, 4)),
            dma((chips, 4)),
            dma((chips, 4)),
            dma((chips, 4)),
        ],
        compiler_params=pltpu.CompilerParams(
            collective_id=3, has_side_effects=True, vmem_limit_bytes=63 << 20
        ),
        name="head_step",
    )(final_rows, labels, counts, table)
    return grad, loss


NARROW = 16
PARTS = (0, 96, 192, 224, 256, 288, 416, 544, 576)


def floor_part(values, size):
    return jnp.floor((values + 0.5) * (1.0 / size))


def spread_places(ranks, slab):
    lanes = lax.broadcasted_iota(jnp.int32, (1024, 128), 1).astype(jnp.float32) + 128.0 * slab
    rows = lax.broadcasted_iota(jnp.int32, (1024, 128), 0).astype(jnp.float32)
    return floor_part(lanes, ranks) == rows - 32.0 * floor_part(rows, 32)


def unpack_down(flat_ref, first, ranks, out_ref, start):
    slabs = ranks // RANK
    total = None
    for slab in range(slabs):
        packed = flat_ref[pl.ds(first + slab, 32, stride=slabs), :]
        spread = jnp.broadcast_to(packed[:, None, :], (32, 32, 128)).reshape(1024, 128)
        spread = jnp.where(spread_places(ranks, slab), spread, 0.0).astype(jnp.bfloat16)
        lanes = lax.broadcasted_iota(jnp.int32, (128, NARROW), 0).astype(jnp.float32) + 128.0 * slab
        column = lax.broadcasted_iota(jnp.int32, (128, NARROW), 1).astype(jnp.float32)
        chosen = low_ones(lanes - ranks * floor_part(lanes, ranks) == column)
        part = matrix_multiply(spread, chosen)
        total = part if total is None else total + part
    out_ref[pl.ds(start, 1024), :] = total.astype(jnp.bfloat16)


def unpack_up(flat_ref, first, ranks, out_ref):
    wide = out_ref.shape[1] // 128
    for c in range(wide):
        rows = flat_ref[pl.ds(first + c, ranks, stride=wide), :]
        rows = jnp.concatenate([rows, jnp.zeros((NARROW - ranks, 128), jnp.float32)], axis=0)
        out_ref[:, c * 128 : (c + 1) * 128] = rows.astype(jnp.bfloat16)


def unpack(flat_ref, outs):
    for i, out_ref in enumerate(outs):
        ranks = 3 * RANK if i < 2 else RANK
        if i % 2:
            unpack_up(flat_ref, PARTS[i], ranks, out_ref)
        else:
            for b in range(out_ref.shape[0] // 1024):
                unpack_down(flat_ref, PARTS[i] + 32 * b, ranks, out_ref, 1024 * b)


def lane_columns(row):
    return jnp.broadcast_to(row, (128, row.shape[1])).T


def ones_where(condition):
    return jnp.where(condition, 1.0, 0.0)


def low_ones(condition):
    return ones_where(condition).astype(jnp.bfloat16)


def embed_step(dp_size, vocab_size, block, room, owned, token_ref, segment_ref, spot_ref, flag_ref,
               place_hbm, affine_ref, flat_ref, table_hbm,
               h1_out, rows_out, label_out, full_out, crowd_out,
               a_qkv, b_qkv, a_o, b_o, a_fc, b_fc, a_p, b_p,
               table, place_table, key_cols, unique_cols, slot_cols, owners, asked, lists, lists_in,
               acc, leaving, arriving, stream, full_all,
               table_sem, place_sem, list_send, list_recv, row_send, row_recv, full_send, full_recv):
    plane = lax.axis_index("dp")
    me = lax.axis_index("vocab")
    chips = vocab_size // 2
    chip = me // 2
    held = table.shape[0]
    full = held // block
    rest = held - full * block
    length = token_ref.shape[1]
    width = table.shape[1]
    spots_here = spot_ref.shape[1]
    chunk = 128
    chunks = length // chunk

    def partner(k):
        out = 0
        bit = 1
        while bit < chips:
            out = out + lax.rem(chip // bit + (k // bit) % 2, 2) * bit
            bit *= 2
        return out

    def across(j):
        return (plane, lax.rem(me + j, vocab_size))

    def along(i):
        return (lax.rem(plane + i, dp_size), me)

    def remote(src, dst, send, recv, peer):
        return pltpu.make_async_remote_copy(
            src_ref=src, dst_ref=dst, send_sem=send, recv_sem=recv,
            device_id=peer, device_id_type=MESH)

    def table_copy(j, number):
        rows = pl.ds(pl.multiple_of(j * block, 16), number)
        return pltpu.make_async_copy(table_hbm.at[rows], table.at[rows], table_sem.at[j])

    @pl.loop(0, full)
    def _(j):
        table_copy(j, block).start()

    table_copy(full, rest).start()

    place_copy = pltpu.make_async_copy(
        place_hbm.at[pl.ds(0, place_table.shape[0])], place_table, place_sem)
    place_copy.start()
    barrier = pltpu.get_barrier_semaphore()

    @pl.loop(1, vocab_size)
    def _(j):
        pl.semaphore_signal(barrier, inc=1, device_id=across(j), device_id_type=MESH)

    @pl.loop(1, dp_size)
    def _(i):
        pl.semaphore_signal(barrier, inc=1, device_id=along(i), device_id_type=MESH)

    token = token_ref[...].astype(jnp.float32)
    segment = segment_ref[...].astype(jnp.float32)
    steps = lax.broadcasted_iota(jnp.int32, (1, length), 1).astype(jnp.float32)
    spot = lane_columns(spot_ref[...].astype(jnp.float32))[:, 0:1]
    flag = lane_columns(flag_ref[...].astype(jnp.float32))[:, 0:1]
    at_spot = steps == spot
    at_next = steps == spot + 1.0

    def picked(where_to, row):
        return jnp.sum(jnp.where(where_to, row, 0.0), axis=1, keepdims=True)

    segment_here = picked(at_spot, segment)
    weight = jnp.where(segment_here == picked(at_next, segment), flag, 0.0)
    heavy = jnp.sum(weight, axis=0, keepdims=True)
    target = picked(at_next, token)
    lanes = lax.broadcasted_iota(jnp.int32, (spots_here, 128), 1)
    label_tile = jnp.where(lanes == 0, target, jnp.where(lanes == 1, weight, 0.0))
    label_out[...] = label_tile.T[0:8, :].astype(jnp.int32)
    read = (steps <= spot) & (segment == segment_here) & (weight > 0.0)
    needed = jnp.max(ones_where(read), axis=0, keepdims=True) > 0.0

    key = jnp.where(needed, token, -1.0 - steps)
    key_cols[...] = lane_columns(key)

    def places(a):
        return (lax.broadcasted_iota(jnp.int32, (chunk, 1), 0) + a * chunk).astype(jnp.float32)

    def rows_at(a):
        return pl.ds(pl.multiple_of(a * chunk, chunk), chunk)

    def same(a):
        return key_cols[rows_at(a), 0:1] == key

    def seen(a, carry):
        return jnp.maximum(carry, jnp.max(
            ones_where(same(a) & (places(a) < steps)), axis=0, keepdims=True))

    again = lax.fori_loop(0, chunks, seen, jnp.zeros((1, length), jnp.float32))
    unique = ones_where(needed & (again == 0.0))
    unique_cols[...] = lane_columns(unique)
    owner = jnp.zeros((1, length), jnp.float32)
    for j in range(1, vocab_size):
        owner = owner + ones_where(token >= float(j * owned))
    owner_ids = lax.broadcasted_iota(jnp.int32, (vocab_size, length), 0).astype(jnp.float32)
    mine = jnp.where(owner_ids == owner, unique, 0.0)
    owners[...] = mine

    def ahead(a, carry):
        before = low_ones(places(a) < steps)
        return carry + matrix_multiply(owners[:, rows_at(a)].astype(jnp.bfloat16), before)

    ranks = lax.fori_loop(0, chunks, ahead, jnp.zeros((vocab_size, length), jnp.float32))
    rank = jnp.sum(jnp.where(owner_ids == owner, ranks, 0.0), axis=0, keepdims=True)
    too_many = jnp.max(unique * ones_where(rank >= float(room)), axis=1, keepdims=True)
    local_id = token - owner * float(owned)
    local_high = jnp.floor(local_id * (1.0 / 128.0))
    local_low = local_id - 128.0 * local_high
    row_ids = lax.broadcasted_iota(jnp.int32, (8, length), 0)

    def stacked(first, second):
        return jnp.where(row_ids == 0, first, jnp.where(row_ids == 1, second, 0.0))

    asked[...] = stacked(owner, jnp.minimum(rank, 127.0))

    def found(a, carry):
        match = low_ones(same(a) & (unique_cols[rows_at(a), 0:1] > 0.0))
        return carry + matrix_multiply(asked[:, rows_at(a)].astype(jnp.bfloat16), match)

    slots = lax.fori_loop(0, chunks, found, jnp.zeros((8, length), jnp.float32))
    slot = jnp.where(needed, slots[0:1, :] * 128.0 + slots[1:2, :], -1.0)
    slot_cols[...] = lane_columns(slot)
    local_parts = stacked(local_high, local_low).astype(jnp.bfloat16)
    rank_ids = lax.broadcasted_iota(jnp.int32, (128, length), 0).astype(jnp.float32)
    list_rows = lax.broadcasted_iota(jnp.int32, (8, 128), 0)

    @pl.loop(0, vocab_size)
    def _(j):
        theirs = (unique > 0.0) & (owner == j.astype(jnp.float32))
        chosen = low_ones(rank_ids == jnp.where(theirs, rank, -1.0))
        ids = matrix_multiply_transposed_right(local_parts, chosen)
        lists[j] = jnp.where(list_rows == 2, too_many, jnp.where(list_rows == 3, heavy, ids))

    @pl.loop(0, vocab_size)
    def _(j):
        arriving[j] = jnp.zeros(arriving.shape[1:], jnp.bfloat16)

    pl.semaphore_wait(barrier, vocab_size + dp_size - 2)

    def list_copy(j):
        peer = across(j)
        return remote(lists.at[peer[1]], lists_in.at[me], list_send.at[peer[1]],
                      list_recv.at[me], peer)

    def list_arrival(j):
        source = across(j)[1]
        return remote(lists.at[source], lists_in.at[source], list_send.at[source],
                      list_recv.at[source], across(j))

    @pl.loop(1, vocab_size)
    def _(j):
        list_copy(j).start()

    lists_in[me] = lists[me]

    ids = lax.broadcasted_iota(jnp.int32, (32, length), 0).astype(jnp.float32)
    starts = jnp.sum(ones_where(segment < ids), axis=1, keepdims=True)
    place = steps - jnp.sum(jnp.where(segment == ids, starts, 0.0), axis=0, keepdims=True)
    place_cols = lane_columns(place)[:, 0:1]
    span = place_table.shape[0]
    place_copy.wait()
    place_ids = lax.broadcasted_iota(jnp.int32, (length, span), 1).astype(jnp.float32)
    stream[...] = matrix_multiply(low_ones(place_ids == place_cols), place_table[...])
    spot_place = picked(at_spot, place)
    spot_slot = picked(at_spot, slot)
    unpack(flat_ref, (a_qkv, b_qkv, a_o, b_o, a_fc, b_fc, a_p, b_p))

    @pl.loop(1, vocab_size)
    def _(j):
        list_arrival(j).wait_recv()

    full_all[plane] = jnp.where(
        list_rows == 0, jnp.max(lists_in[:, 2:3, 0:1], axis=0),
        jnp.sum(lists_in[:, 3:4, 0:1], axis=0))

    def full_copy(i):
        peer = along(i)
        return remote(full_all.at[plane], full_all.at[plane], full_send.at[peer[0]],
                      full_recv.at[plane], peer)

    def full_arrival(i):
        source = along(i)[0]
        return remote(full_all.at[plane], full_all.at[source], full_send.at[source],
                      full_recv.at[source], along(i))

    @pl.loop(1, dp_size)
    def _(i):
        full_copy(i).start()

    def row_copy(d):
        return remote(leaving.at[d], arriving.at[me, pl.ds(0, room)], row_send.at[d],
                      row_recv.at[me], (plane, d))

    def row_arrival(d):
        return remote(leaving.at[d], arriving.at[d, pl.ds(0, room)], row_send.at[d],
                      row_recv.at[d], (plane, d))

    def wanted(d):
        here = lists_in[d]
        return lane_columns(here[0:1, :] * 128.0 + here[1:2, :])[0:room, 0:1]

    first = True
    for k in range(chips - 1, -1, -1):
        c = partner(k)
        wanted_here = jnp.concatenate([wanted(2 * c), wanted(2 * c + 1)], axis=0)

        def rows_of(j, number):
            if first:
                table_copy(j, number).wait()
            ids_here = (lax.broadcasted_iota(jnp.int32, (2 * room, number), 1)
                        + j * block).astype(jnp.float32)
            rows = pl.ds(pl.multiple_of(j * block, 16), number)
            return matrix_multiply(low_ones(ids_here == wanted_here), table[rows, :])

        acc[...] = rows_of(full, rest)

        @pl.loop(0, full)
        def _(j):
            acc[...] += rows_of(j, block)

        first = False
        for i in range(2):
            leaving[2 * c + i] = acc[pl.ds(i * room, room), :].astype(jnp.bfloat16)
        if k > 0:
            for i in range(2):
                row_copy(2 * c + i).start()
        else:
            row_copy(2 * c + 1 - lax.rem(me, 2)).start()
            arriving[me, pl.ds(0, room), :] = leaving[me]

    for k in range(chips):
        c = partner(k)
        if k > 0:
            for i in range(2):
                row_arrival(2 * c + i).wait_recv()
        else:
            row_arrival(2 * c + 1 - lax.rem(me, 2)).wait_recv()
        pair_rows = arriving[pl.ds(2 * c, 2)].reshape(256, width)
        offset = (2 * c * 128).astype(jnp.float32)

        def spread(column, ids_like):
            ids_here = lax.broadcasted_iota(jnp.int32, ids_like, 1).astype(jnp.float32)
            return low_ones(ids_here + offset == column)

        stream[...] += matrix_multiply(spread(slot_cols[:, 0:1], (length, 256)), pair_rows)
        spot_rows = matrix_multiply(spread(spot_slot, (spots_here, 256)), pair_rows)
        if k == 0:
            rows_out[...] = spot_rows
        else:
            rows_out[...] += spot_rows

    spot_ids = lax.broadcasted_iota(jnp.int32, (spots_here, span), 1).astype(jnp.float32)
    rows_out[...] += matrix_multiply(low_ones(spot_ids == spot_place), place_table[...])

    @pl.loop(0, length // 256)
    def _(a):
        rows = pl.ds(pl.multiple_of(a * 256, 256), 256)
        h1_out[rows, :] = layer_norm(
            stream[rows, :], affine_ref[0:1, :], affine_ref[3:4, :]).astype(jnp.bfloat16)

    @pl.loop(1, dp_size)
    def _(i):
        full_arrival(i).wait_recv()

    counts = jnp.where(
        list_rows == 0, jnp.max(full_all[...], axis=0), jnp.sum(full_all[...], axis=0))
    full_out[...] = counts
    crowd_out[...] = counts[0:1, 0:1].astype(jnp.int32)

    @pl.loop(1, vocab_size)
    def _(j):
        list_copy(j).wait_send()

    @pl.loop(1, dp_size)
    def _(i):
        full_copy(i).wait_send()

    for k in range(chips):
        if k > 0:
            for i in range(2):
                row_copy(2 * partner(k) + i).wait_send()
        else:
            row_copy(2 * chip + 1 - lax.rem(me, 2)).wait_send()


def embed(mesh_sizes, owned, tokens, segments, spots, flags, place_table, affine, flat, table):
    dp_size, vocab_size = mesh_sizes
    length = tokens.shape[1]
    spots_here = spots.shape[1]
    held, width = table.shape
    block = 1024
    full = held // block
    chips = vocab_size // 2
    room = 112 if vocab_size <= 8 else 64
    span = 256
    whole = pl.BlockSpec(memory_space=pltpu.VMEM)
    dma = pltpu.SemaphoreType.DMA
    return pl.pallas_call(
        partial(embed_step, dp_size, vocab_size, block, room, owned),
        out_shape=[
            jax.ShapeDtypeStruct((length, width), jnp.bfloat16),
            jax.ShapeDtypeStruct((spots_here, width), jnp.float32),
            jax.ShapeDtypeStruct((8, spots_here), jnp.int32),
            jax.ShapeDtypeStruct((8, 128), jnp.float32),
            jax.ShapeDtypeStruct((1, 1), jnp.int32),
        ]
        + [
            jax.ShapeDtypeStruct(shape, jnp.bfloat16)
            for shape in (
                (width, NARROW), (NARROW, width), (width, NARROW), (NARROW, width),
                (width, NARROW), (NARROW, 4 * width), (4 * width, NARROW), (NARROW, width),
            )
        ],
        in_specs=[whole] * 4
        + [pl.BlockSpec(memory_space=pl.ANY), whole, whole, pl.BlockSpec(memory_space=pl.ANY)],
        out_specs=[whole] * 13,
        scratch_shapes=[
            pltpu.VMEM((held, width), jnp.bfloat16),
            pltpu.VMEM((span, width), jnp.bfloat16),
            pltpu.VMEM((length, 128), jnp.float32),
            pltpu.VMEM((length, 128), jnp.float32),
            pltpu.VMEM((length, 128), jnp.float32),
            pltpu.VMEM((vocab_size, length), jnp.float32),
            pltpu.VMEM((8, length), jnp.float32),
            pltpu.VMEM((vocab_size, 8, 128), jnp.float32),
            pltpu.VMEM((vocab_size, 8, 128), jnp.float32),
            pltpu.VMEM((2 * room, width), jnp.float32),
            pltpu.VMEM((vocab_size, room, width), jnp.bfloat16),
            pltpu.VMEM((vocab_size, 128, width), jnp.bfloat16),
            pltpu.VMEM((length, width), jnp.float32),
            pltpu.VMEM((dp_size, 8, 128), jnp.float32),
            dma((full + 1,)),
            dma,
            dma((vocab_size,)),
            dma((vocab_size,)),
            dma((vocab_size,)),
            dma((vocab_size,)),
            dma((dp_size,)),
            dma((dp_size,)),
        ],
        compiler_params=pltpu.CompilerParams(
            collective_id=1, has_side_effects=True, vmem_limit_bytes=60 << 20
        ),
        name="embed_step",
    )(tokens, segments, spots, flags, place_table, affine, flat.reshape(-1, 128), table)


def wide_loop(number, body):
    lax.fori_loop(0, number, lambda i, carry: (body(i), carry)[1], 0)


def norm_parts(rows):
    centred = rows - jnp.mean(rows, axis=-1, keepdims=True)
    return centred, lax.rsqrt(jnp.mean(centred * centred, axis=-1, keepdims=True) + NORM_EPS)


def norm_back(rows, gain, grad):
    centred, spread = norm_parts(rows)
    hat = centred * spread
    grad_hat = grad * gain
    return spread * (
        grad_hat
        - jnp.mean(grad_hat, axis=-1, keepdims=True)
        - hat * jnp.mean(grad_hat * hat, axis=-1, keepdims=True)
    )


GELU_RATE = math.sqrt(2.0 / math.pi)


def gelu_parts(pre):
    bend = jnp.tanh(GELU_RATE * (pre + 0.044715 * (pre * pre * pre)))
    return 0.5 * (1.0 + bend), bend


def gelu_slope(pre):
    half, bend = gelu_parts(pre)
    inner = GELU_RATE * (1.0 + 3.0 * 0.044715 * (pre * pre))
    return half + 0.5 * pre * (1.0 - bend * bend) * inner


def both_heads(pair):
    lanes = lax.broadcasted_iota(jnp.int32, pair.shape, 1)
    half = pair.shape[1] // 2
    wide = pair.astype(jnp.float32)
    return jnp.concatenate(
        [jnp.where(lanes < half, wide, 0.0), jnp.where(lanes < half, 0.0, wide)], axis=0
    ).astype(jnp.bfloat16)


def side_by_side(stacked):
    rows = stacked.shape[0] // 2
    lanes = lax.broadcasted_iota(jnp.int32, (rows, stacked.shape[1]), 1)
    return jnp.where(lanes < stacked.shape[1] // 2, stacked[:rows], stacked[rows:])


def third_of(rows, j):
    ids = lax.broadcasted_iota(jnp.int32, rows.shape, 0)
    wide = jnp.where((ids >= j * RANK) & (ids < (j + 1) * RANK), rows.astype(jnp.float32), 0.0)
    return wide.astype(jnp.bfloat16)


def attention_mask(spot_ref, segment_ref):
    spot = lane_columns(spot_ref[...].astype(jnp.float32))[:, 0:1]
    steps = lax.broadcasted_iota(jnp.int32, segment_ref.shape, 1).astype(jnp.float32)
    segment = segment_ref[...].astype(jnp.float32)
    here = jnp.sum(jnp.where(steps == spot, segment, 0.0), axis=1, keepdims=True)
    open_to = ones_where((steps <= spot) & (segment == here))
    return jnp.concatenate([open_to, open_to], axis=0)


def layer_up(h1_ref, rows_ref, segment_ref, spot_ref, affine_ref, bias_ref,
             a_qkv, b_qkv, a_o, b_o, a_fc, b_fc, a_p, b_p,
             qkv_hbm, o_hbm, in_hbm, out_hbm,
             final_ref, q_ref, k_ref, v_ref, u1_ref, u1_rows_ref, h1_rows_ref, lse_ref,
             o_ref, uo_ref, middle_ref, h2_ref, uf_ref, pre_ref, f_ref, up_ref, last_ref,
             wq, wk, wv, wo, win, wout, mask, sems):
    length, width = h1_ref.shape
    hidden = win.shape[1]
    quarter = hidden // 4

    def columns_of(source, j, number):
        return source.at[:, pl.ds(j * number, number)]

    copies = [
        pltpu.make_async_copy(columns_of(qkv_hbm, 1, width), wk, sems.at[0]),
        pltpu.make_async_copy(columns_of(qkv_hbm, 2, width), wv, sems.at[1]),
        pltpu.make_async_copy(columns_of(qkv_hbm, 0, width), wq, sems.at[2]),
        pltpu.make_async_copy(o_hbm, wo, sems.at[3]),
        pltpu.make_async_copy(in_hbm, win, sems.at[4]),
        pltpu.make_async_copy(out_hbm, wout, sems.at[5]),
    ]
    for copy in copies:
        copy.start()

    def bias(first, number):
        return bias_ref[0:1, first : first + number]

    mask[...] = attention_mask(spot_ref, segment_ref)
    h1_rows = layer_norm(rows_ref[...], affine_ref[0:1, :], affine_ref[3:4, :]).astype(
        jnp.bfloat16)
    h1_rows_ref[...] = h1_rows
    u1_ref[...] = matrix_multiply(h1_ref[...], a_qkv[...]).astype(jnp.bfloat16)
    u1_rows = matrix_multiply(h1_rows, a_qkv[...]).astype(jnp.bfloat16)
    u1_rows_ref[...] = u1_rows

    def project(normed, low, weight, j):
        return (
            matrix_multiply(normed, weight[...])
            + bias(j * width, width)
            + ADAPTER_SCALE * matrix_multiply(low, third_of(b_qkv[...], j))
        ).astype(jnp.bfloat16)

    chunk = 256
    for j, weight, out, copy in ((1, wk, k_ref, copies[0]), (2, wv, v_ref, copies[1])):
        copy.wait()

        def rows_of(i):
            rows = pl.ds(pl.multiple_of(i * chunk, chunk), chunk)
            out[rows, :] = project(h1_ref[rows, :], u1_ref[rows, :], weight, j)

        wide_loop(length // chunk, rows_of)
    copies[2].wait()
    q_ref[...] = project(h1_rows, u1_rows, wq, 0)
    scale = (width // HEADS) ** (-0.5)
    lanes = lax.broadcasted_iota(jnp.int32, lse_ref.shape, 1)
    lse_ref[...] = jnp.zeros(lse_ref.shape, jnp.float32)

    def heads(g):
        pair = pl.ds(pl.multiple_of(g * 128, 128), 128)
        scores = scale * matrix_multiply_transposed_right(both_heads(q_ref[:, pair]), k_ref[:, pair])
        scores = jnp.where(mask[...] > 0.0, scores, MASKED)
        top = jnp.max(scores, axis=1, keepdims=True)
        e = jnp.exp(scores - top)
        total = jnp.sum(e, axis=1, keepdims=True)
        probs = (e * (1.0 / total)).astype(jnp.bfloat16)
        o_ref[:, pair] = side_by_side(matrix_multiply(probs, v_ref[:, pair])).astype(jnp.bfloat16)
        lse_ref[...] = jnp.where(lanes == g, top + jnp.log(total), lse_ref[...])

    wide_loop(HEADS // 2, heads)
    o = o_ref[...]
    uo = matrix_multiply(o, a_o[...]).astype(jnp.bfloat16)
    uo_ref[...] = uo
    copies[3].wait()
    middle = (
        rows_ref[...]
        + matrix_multiply(o, wo[...])
        + bias(3 * width, width)
        + ADAPTER_SCALE * matrix_multiply(uo, b_o[...])
    )
    middle_ref[...] = middle
    h2 = layer_norm(middle, affine_ref[1:2, :], affine_ref[4:5, :]).astype(jnp.bfloat16)
    h2_ref[...] = h2
    uf = matrix_multiply(h2, a_fc[...]).astype(jnp.bfloat16)
    uf_ref[...] = uf
    copies[4].wait()
    for j in range(4):
        part = slice(j * quarter, (j + 1) * quarter)
        pre = (
            matrix_multiply(h2, win[:, part])
            + bias(4 * width + j * quarter, quarter)
            + ADAPTER_SCALE * matrix_multiply(uf, b_fc[:, part])
        )
        pre_ref[:, part] = pre
        f_ref[:, part] = (pre * gelu_parts(pre)[0]).astype(jnp.bfloat16)
    f = f_ref[...]
    up = matrix_multiply(f, a_p[...]).astype(jnp.bfloat16)
    up_ref[...] = up
    copies[5].wait()
    last = (
        middle
        + matrix_multiply(f, wout[...])
        + bias(4 * width + hidden, width)
        + ADAPTER_SCALE * matrix_multiply(up, b_p[...])
    )
    last_ref[...] = last
    final_ref[...] = layer_norm(last, affine_ref[2:3, :], affine_ref[5:6, :]).astype(jnp.bfloat16)


def pack_up(out_ref, part, grad):
    ranks = 3 * RANK if part < 2 else RANK
    wide = grad.shape[1] // 128
    for c in range(wide):
        rows = pl.ds(PARTS[part] + c, ranks, stride=wide)
        out_ref[rows, :] = grad[0:ranks, c * 128 : (c + 1) * 128]


def pack_down(out_ref, part, shift, grad):
    ranks = 3 * RANK if part < 2 else RANK
    slabs = ranks // RANK
    repeated = jnp.concatenate([grad[0:ranks]] * (128 * slabs // ranks), axis=0)
    for slab in range(slabs):
        spread = repeated[128 * slab : 128 * (slab + 1)].T
        spread = jnp.where(spread_places(ranks, slab), spread, 0.0)
        rows = pl.ds(PARTS[part] + shift + slab, 32, stride=slabs)
        out_ref[rows, :] = jnp.sum(spread.reshape(32, 32, 128), axis=1)


def layer_down(grad_ref, spot_ref, segment_ref, affine_ref, h1_ref,
               a_qkv, b_qkv, a_o, b_o, a_fc, b_fc, a_p, b_p,
               q_ref, k_ref, v_ref, u1_ref, u1_rows_ref, h1_rows_ref, lse_ref,
               o_ref, uo_ref, middle_ref, h2_ref, uf_ref, pre_ref, f_ref, up_ref, last_ref,
               o_hbm, in_hbm, out_hbm,
               grad_out,
               wo, win, wout, mask, dpre_ref, do_ref, dq_ref, dk_ref, dv_ref, sems):
    length, width = h1_ref.shape
    hidden = win.shape[1]
    quarter = hidden // 4
    rows_here = grad_ref.shape[0]
    copies = [
        pltpu.make_async_copy(out_hbm, wout, sems.at[0]),
        pltpu.make_async_copy(in_hbm, win, sems.at[1]),
        pltpu.make_async_copy(o_hbm, wo, sems.at[2]),
    ]
    for copy in copies:
        copy.start()
    mask[...] = attention_mask(spot_ref, segment_ref)
    spot_row = spot_ref[...].astype(jnp.float32)
    spot = lane_columns(spot_row)[:, 0:1]
    order_row = lax.broadcasted_iota(jnp.int32, (1, rows_here), 1)
    order = lax.broadcasted_iota(jnp.int32, (rows_here, 1), 0)
    same = spot == spot_row
    repeat = jnp.max(ones_where(same & (order_row < order)), axis=1, keepdims=True)
    merge = ones_where(same) * (1.0 - repeat)
    grad_final = jnp.dot(
        merge, grad_ref[...], precision=lax.Precision.HIGHEST,
        preferred_element_type=jnp.float32)
    dx3 = norm_back(last_ref[...], affine_ref[2:3, :], grad_final)
    dm = dx3.astype(jnp.bfloat16)
    pack_up(grad_out, 7, ADAPTER_SCALE * matrix_multiply_transposed_left(up_ref[...], dm))
    du_p = (ADAPTER_SCALE * matrix_multiply_transposed_right(dm, b_p[...])).astype(jnp.bfloat16)
    ga_p = matrix_multiply_transposed_left(du_p, f_ref[...])
    for b in range(hidden // 1024):
        pack_down(grad_out, 6, 32 * b, ga_p[:, 1024 * b : 1024 * (b + 1)])
    copies[0].wait()
    for j in range(4):
        part = slice(j * quarter, (j + 1) * quarter)
        df = matrix_multiply_transposed_right(dm, wout[part, :]) + matrix_multiply_transposed_right(
            du_p, a_p[part, :])
        dpre_ref[:, part] = (df * gelu_slope(pre_ref[:, part])).astype(jnp.bfloat16)
    dpre = dpre_ref[...]
    pack_up(grad_out, 5, ADAPTER_SCALE * matrix_multiply_transposed_left(uf_ref[...], dpre))
    du_f = (ADAPTER_SCALE * matrix_multiply_transposed_right(dpre, b_fc[...])).astype(jnp.bfloat16)
    pack_down(grad_out, 4, 0, matrix_multiply_transposed_left(du_f, h2_ref[...]))
    copies[1].wait()
    dh2 = matrix_multiply_transposed_right(dpre, win[...]) + matrix_multiply_transposed_right(
        du_f, a_fc[...])
    dx2 = dx3 + norm_back(middle_ref[...], affine_ref[1:2, :], dh2)
    da = dx2.astype(jnp.bfloat16)
    pack_up(grad_out, 3, ADAPTER_SCALE * matrix_multiply_transposed_left(uo_ref[...], da))
    du_o = (ADAPTER_SCALE * matrix_multiply_transposed_right(da, b_o[...])).astype(jnp.bfloat16)
    pack_down(grad_out, 2, 0, matrix_multiply_transposed_left(du_o, o_ref[...]))
    copies[2].wait()
    do_ref[...] = (
        matrix_multiply_transposed_right(da, wo[...])
        + matrix_multiply_transposed_right(du_o, a_o[...])
    ).astype(jnp.bfloat16)
    scale = (width // HEADS) ** (-0.5)
    lanes = lax.broadcasted_iota(jnp.int32, lse_ref.shape, 1)

    def heads(g):
        pair = pl.ds(pl.multiple_of(g * 128, 128), 128)
        q = both_heads(q_ref[:, pair])
        do = both_heads(do_ref[:, pair])
        lse = jnp.sum(jnp.where(lanes == g, lse_ref[...], 0.0), axis=1, keepdims=True)
        scores = scale * matrix_multiply_transposed_right(q, k_ref[:, pair])
        probs = jnp.where(mask[...] > 0.0, jnp.exp(jnp.minimum(scores - lse, 0.0)), 0.0)
        dp = matrix_multiply_transposed_right(do, v_ref[:, pair])
        ds = (probs * (dp - jnp.sum(probs * dp, axis=1, keepdims=True))).astype(jnp.bfloat16)
        dv_ref[:, pair] = matrix_multiply_transposed_left(
            probs.astype(jnp.bfloat16), do).astype(jnp.bfloat16)
        dk_ref[:, pair] = (scale * matrix_multiply_transposed_left(ds, q)).astype(jnp.bfloat16)
        dq_ref[:, pair] = side_by_side(scale * matrix_multiply(ds, k_ref[:, pair])).astype(
            jnp.bfloat16)

    wide_loop(HEADS // 2, heads)
    b_all = b_qkv[...]
    gb = jnp.zeros((NARROW, width), jnp.float32)
    ids = lax.broadcasted_iota(jnp.int32, gb.shape, 0)
    dus = []
    for j, low, grad in ((0, u1_rows_ref, dq_ref), (1, u1_ref, dk_ref), (2, u1_ref, dv_ref)):
        mine = (ids >= j * RANK) & (ids < (j + 1) * RANK)
        gb = jnp.where(mine, ADAPTER_SCALE * matrix_multiply_transposed_left(
            low[...], grad[...]), gb)
        dus.append(ADAPTER_SCALE * matrix_multiply_transposed_right(grad[...], third_of(b_all, j)))
    pack_up(grad_out, 1, gb)
    ga = matrix_multiply_transposed_left(
        dus[0].astype(jnp.bfloat16), h1_rows_ref[...]
    ) + matrix_multiply_transposed_left((dus[1] + dus[2]).astype(jnp.bfloat16), h1_ref[...])
    pack_down(grad_out, 0, 0, ga)


def layer_kernels(rows_here, length, width, hidden):
    low, wide = jnp.bfloat16, jnp.float32
    whole = pl.BlockSpec(memory_space=pltpu.VMEM)
    away = pl.BlockSpec(memory_space=pl.ANY)
    dma = pltpu.SemaphoreType.DMA
    params = pltpu.CompilerParams(vmem_limit_bytes=60 << 20)
    kept = [
        ((rows_here, width), low),
        ((length, width), low),
        ((length, width), low),
        ((length, NARROW), low),
        ((rows_here, NARROW), low),
        ((rows_here, width), low),
        ((2 * rows_here, 128), wide),
        ((rows_here, width), low),
        ((rows_here, NARROW), low),
        ((rows_here, width), wide),
        ((rows_here, width), low),
        ((rows_here, NARROW), low),
        ((rows_here, hidden), wide),
        ((rows_here, hidden), low),
        ((rows_here, NARROW), low),
        ((rows_here, width), wide),
    ]
    up = pl.pallas_call(
        layer_up,
        out_shape=[jax.ShapeDtypeStruct(*k) for k in [((rows_here, width), low)] + kept],
        in_specs=[whole] * 14 + [away] * 4,
        out_specs=[whole] * 17,
        scratch_shapes=[pltpu.VMEM((width, width), low)] * 4
        + [
            pltpu.VMEM((width, hidden), low),
            pltpu.VMEM((hidden, width), low),
            pltpu.VMEM((2 * rows_here, length), wide),
            dma((6,)),
        ],
        compiler_params=params,
        name="layer_up",
    )
    down = pl.pallas_call(
        layer_down,
        out_shape=jax.ShapeDtypeStruct((PARTS[-1], 128), wide),
        in_specs=[whole] * 29 + [away] * 3,
        out_specs=whole,
        scratch_shapes=[
            pltpu.VMEM((width, width), low),
            pltpu.VMEM((width, hidden), low),
            pltpu.VMEM((hidden, width), low),
            pltpu.VMEM((2 * rows_here, length), wide),
            pltpu.VMEM((rows_here, hidden), low),
            pltpu.VMEM((rows_here, width), low),
            pltpu.VMEM((rows_here, width), low),
            pltpu.VMEM((length, width), low),
            pltpu.VMEM((length, width), low),
            dma((3,)),
        ],
        compiler_params=params,
        name="layer_down",
    )
    return up, down


def settle_step(held_ref, segment_ref, spot_ref, place_ref, affine_ref, h1_out, rows_out, place_cols):
    length = segment_ref.shape[1]
    span = place_ref.shape[0]
    segment = segment_ref[...].astype(jnp.float32)
    steps = lax.broadcasted_iota(jnp.int32, (1, length), 1).astype(jnp.float32)
    ids = lax.broadcasted_iota(jnp.int32, (32, length), 0).astype(jnp.float32)
    starts = jnp.sum(ones_where(segment < ids), axis=1, keepdims=True)
    place = steps - jnp.sum(jnp.where(segment == ids, starts, 0.0), axis=0, keepdims=True)
    place_cols[...] = lane_columns(place)
    spot = lane_columns(spot_ref[...].astype(jnp.float32))[:, 0:1]
    at_spot = steps == spot
    spot_place = jnp.sum(jnp.where(at_spot, place, 0.0), axis=1, keepdims=True)

    def placed(column):
        ids_here = lax.broadcasted_iota(jnp.int32, (column.shape[0], span), 1).astype(jnp.float32)
        return matrix_multiply(low_ones(ids_here == column), place_ref[...])

    rows_out[...] = matrix_multiply(low_ones(at_spot), held_ref[...]) + placed(spot_place)

    @pl.loop(0, length // 128)
    def _(a):
        rows = pl.ds(pl.multiple_of(a * 128, 128), 128)
        stream = held_ref[rows, :].astype(jnp.float32) + placed(place_cols[rows, 0:1])
        h1_out[rows, :] = layer_norm(stream, affine_ref[0:1, :], affine_ref[3:4, :]).astype(
            jnp.bfloat16)


def settle_rows(held, segments, spots, place_table, affine):
    length, width = held.shape
    whole = pl.BlockSpec(memory_space=pltpu.VMEM)
    return pl.pallas_call(
        settle_step,
        out_shape=[
            jax.ShapeDtypeStruct((length, width), jnp.bfloat16),
            jax.ShapeDtypeStruct((spots.shape[1], width), jnp.float32),
        ],
        in_specs=[whole] * 5,
        out_specs=[whole] * 2,
        scratch_shapes=[pltpu.VMEM((length, 128), jnp.float32)],
        compiler_params=pltpu.CompilerParams(vmem_limit_bytes=32 << 20),
        name="settle_step",
    )(held, segments, spots, place_table[:256], affine)


def visit_step(block, wanted_ref, held_ref, table_hbm, out_ref, table, columns, acc, sem):
    copy = pltpu.make_async_copy(table_hbm, table, sem)
    copy.start()
    columns[...] = lane_columns(wanted_ref[...].astype(jnp.float32))
    rows_here = table.shape[0]
    full = rows_here // block
    copy.wait()

    @pl.loop(0, held_ref.shape[0] // 256)
    def _(a):
        rows = pl.ds(pl.multiple_of(a * 256, 256), 256)
        acc[...] = held_ref[rows, :].astype(jnp.float32)

        def add(first, number):
            ids = lax.broadcasted_iota(jnp.int32, (256, number), 1) + first
            chosen = low_ones(ids.astype(jnp.float32) == columns[rows, 0:1])
            acc[...] += matrix_multiply(chosen, table[pl.ds(first, number), :])

        @pl.loop(0, full)
        def _(j):
            add(pl.multiple_of(j * block, block), block)

        add(full * block, rows_here - full * block)
        out_ref[rows, :] = acc[...].astype(jnp.bfloat16)


def visit_rows(wanted, held, table):
    length, width = held.shape
    whole = pl.BlockSpec(memory_space=pltpu.VMEM)
    return pl.pallas_call(
        partial(visit_step, 256),
        out_shape=jax.ShapeDtypeStruct((length, width), jnp.bfloat16),
        in_specs=[whole, whole, pl.BlockSpec(memory_space=pl.ANY)],
        out_specs=whole,
        scratch_shapes=[
            pltpu.VMEM(table.shape, jnp.bfloat16),
            pltpu.VMEM((length, 128), jnp.float32),
            pltpu.VMEM((256, width), jnp.float32),
            pltpu.SemaphoreType.DMA,
        ],
        compiler_params=pltpu.CompilerParams(vmem_limit_bytes=40 << 20),
        name="visit_step",
    )(wanted, held, table)


def local(
    mesh_sizes,
    packed_symbol_codes,
    article_numbering,
    target_spots,
    answer_flags,
    shared_embedding,
    spot_embedding,
    combined_qkv_weights,
    attend_outgoing_weights,
    dense_incoming_weights,
    dense_outgoing_weights,
    layernorm_affine,
    bias_terms,
    adaptor_float_copies,
    average_moments,
    squared_moments,
):
    rows_here = target_spots.shape[1]
    shard_rows = shared_embedding.shape[0]
    table = jnp.pad(shared_embedding, ((0, -shard_rows % 16), (0, 0)))
    fast_h1, fast_rows, labels, counts, crowded, *factors = embed(
        mesh_sizes,
        shard_rows,
        packed_symbol_codes,
        article_numbering,
        target_spots,
        answer_flags,
        spot_embedding,
        layernorm_affine,
        adaptor_float_copies,
        table,
    )

    sharers = mesh_sizes[1]
    ring = [(j, (j + 1) % sharers) for j in range(sharers)]

    def visit(carry):
        turns, tokens, held = carry
        wanted = tokens - lax.axis_index("vocab") * shard_rows
        wanted = jnp.where((wanted >= 0) & (wanted < shard_rows), wanted, -1)
        kept = jnp.where(turns == sharers, jnp.zeros((), jnp.bfloat16), held)
        held = visit_rows(wanted, kept, table)
        return turns - 1, lax.ppermute(tokens, "vocab", ring), lax.ppermute(held, "vocab", ring)

    def settle(carry):
        _, held, _ = carry
        settled, rows = settle_rows(
            held, article_numbering, target_spots, spot_embedding, layernorm_affine
        )
        return jnp.zeros((), jnp.int32), settled, rows

    overflow = crowded.reshape(())
    _, _, held = lax.while_loop(
        lambda carry: carry[0] > 0, visit, (overflow * sharers, packed_symbol_codes, fast_h1)
    )
    _, h1, stream_rows = lax.while_loop(
        lambda carry: carry[0] > 0, settle, (overflow, held, fast_rows)
    )
    length, width = h1.shape
    hidden = dense_incoming_weights.shape[1]
    layer_up_call, layer_down_call = layer_kernels(rows_here, length, width, hidden)
    final_rows, *kept = layer_up_call(
        h1,
        stream_rows,
        article_numbering,
        target_spots,
        layernorm_affine,
        bias_terms[None, :],
        *factors,
        combined_qkv_weights,
        attend_outgoing_weights,
        dense_incoming_weights,
        dense_outgoing_weights,
    )
    grad_rows, loss_part = head(
        mesh_sizes, shard_rows, final_rows, labels, counts, table
    )
    local_grad = layer_down_call(
        grad_rows,
        target_spots,
        article_numbering,
        layernorm_affine,
        h1,
        *factors,
        *kept,
        attend_outgoing_weights,
        dense_incoming_weights,
        dense_outgoing_weights,
    )
    (
        refreshed_thin_pairs,
        updated_first_moment,
        updated_second_moment,
        gradient_global_norm,
        smoothed_entropy_cost,
    ) = reduce_and_update(
        mesh_sizes, local_grad, adaptor_float_copies, average_moments, squared_moments, loss_part
    )
    return (
        refreshed_thin_pairs,
        updated_first_moment,
        updated_second_moment,
        gradient_global_norm,
        smoothed_entropy_cost,
    )


def solution(mesh):
    return jax.shard_map(
        partial(local, (mesh.shape["dp"], mesh.shape["vocab"])),
        mesh=mesh,
        in_specs=(
            P(("dp", "vocab"), None),
            P(("dp", "vocab"), None),
            P(("dp", "vocab"), None),
            P(("dp", "vocab"), None),
            P("vocab", None),
            P(),
            P(),
            P(),
            P(),
            P(),
            P(),
            P(),
            P(),
            P(),
            P(),
        ),
        out_specs=(P(), P(), P(), P(), P()),
        check_vma=False,
    )
```

```python
from functools import partial
import math

import jax
import jax.numpy as jnp
from jax import lax
from jax.experimental import pallas as pl
from jax.experimental.pallas import tpu as pltpu
from jax.sharding import PartitionSpec as P

MODEL_WIDTH = 1024
HEADS = 16
FEEDFWD_UNITS = 4096
VOCAB_SIZE = 50257
RANK = 4
STEP = 10


ADAPTER_SCALE = 8.0
NORM_EPS = 1e-05
GRAD_CLIP = 0.0001
STRIDE_LENGTH = 0.02
BETA_ONE = 0.9
BETA_TWO = 0.999
SHRINK_PENALTY = 0.01
STABILITY_FLOOR = 1e-08
MASKED = -1e30
MESH = pl.DeviceIdType.MESH


def matrix_multiply(left, right):
    return jnp.dot(left, right, preferred_element_type=jnp.float32)


def matrix_multiply_transposed_left(left, right):
    return lax.dot_general(
        left, right, (((0,), (0,)), ((), ())), preferred_element_type=jnp.float32
    )


def matrix_multiply_transposed_right(left, right):
    return lax.dot_general(
        left, right, (((1,), (1,)), ((), ())), preferred_element_type=jnp.float32
    )


def layer_norm(stream, gain, shift):
    centred = stream - jnp.mean(stream, axis=-1, keepdims=True)
    spread = lax.rsqrt(jnp.mean(centred * centred, axis=-1, keepdims=True) + NORM_EPS)
    return centred * spread * gain + shift


def adaptive_moment_update(grad, weight, first, second):
    first_new = BETA_ONE * first + (1.0 - BETA_ONE) * grad
    second_new = BETA_TWO * second + (1.0 - BETA_TWO) * grad * grad
    debiased_mean_estimate = first_new / (1.0 - BETA_ONE**STEP)
    debiased_variance_estimate = second_new / (1.0 - BETA_TWO**STEP)
    weight_new = weight - STRIDE_LENGTH * (
        debiased_mean_estimate / (jnp.sqrt(debiased_variance_estimate) + STABILITY_FLOOR)
        + SHRINK_PENALTY * weight
    )
    return (weight_new, first_new, second_new)


def sum_and_step(dp_size, vocab_size, grad_ref, weight_ref, first_ref, second_ref, loss_ref,
                 weight_out, first_out, second_out, norm_out, loss_out,
                 parts, planes, total, losses, send_a, recv_a, send_b, recv_b, send_c, recv_c,
                 send_d, recv_d):
    my_plane = lax.axis_index("dp")
    me = lax.axis_index("vocab")

    def across(j):
        return (my_plane, lax.rem(me + j, vocab_size))

    def along(i):
        return (lax.rem(my_plane + i, dp_size), me)

    barrier = pltpu.get_barrier_semaphore()

    @pl.loop(1, vocab_size)
    def _(j):
        pl.semaphore_signal(barrier, inc=1, device_id=across(j), device_id_type=MESH)

    @pl.loop(1, dp_size)
    def _(i):
        pl.semaphore_signal(barrier, inc=1, device_id=along(i), device_id_type=MESH)

    pl.semaphore_wait(barrier, vocab_size + dp_size - 2)

    def part_copy(j):
        peer = across(j)
        return pltpu.make_async_remote_copy(
            src_ref=grad_ref.at[peer[1]], dst_ref=parts.at[me],
            send_sem=send_a.at[peer[1]], recv_sem=recv_a.at[me],
            device_id=peer, device_id_type=MESH)

    def part_arrival(j):
        peer = across(j)
        return pltpu.make_async_remote_copy(
            src_ref=grad_ref.at[peer[1]], dst_ref=parts.at[peer[1]],
            send_sem=send_a.at[peer[1]], recv_sem=recv_a.at[peer[1]],
            device_id=peer, device_id_type=MESH)

    def plane_copy(i):
        peer = along(i)
        return pltpu.make_async_remote_copy(
            src_ref=planes.at[my_plane], dst_ref=planes.at[my_plane],
            send_sem=send_b.at[peer[0]], recv_sem=recv_b.at[my_plane],
            device_id=peer, device_id_type=MESH)

    def plane_arrival(i):
        peer = along(i)
        return pltpu.make_async_remote_copy(
            src_ref=planes.at[my_plane], dst_ref=planes.at[peer[0]],
            send_sem=send_b.at[peer[0]], recv_sem=recv_b.at[peer[0]],
            device_id=peer, device_id_type=MESH)

    def loss_copy(i):
        peer = along(i)
        return pltpu.make_async_remote_copy(
            src_ref=loss_ref, dst_ref=losses.at[my_plane],
            send_sem=send_d.at[peer[0]], recv_sem=recv_d.at[my_plane],
            device_id=peer, device_id_type=MESH)

    def loss_arrival(i):
        peer = along(i)
        return pltpu.make_async_remote_copy(
            src_ref=loss_ref, dst_ref=losses.at[peer[0]],
            send_sem=send_d.at[peer[0]], recv_sem=recv_d.at[peer[0]],
            device_id=peer, device_id_type=MESH)

    def total_copy(j):
        peer = across(j)
        return pltpu.make_async_remote_copy(
            src_ref=total.at[me], dst_ref=total.at[me],
            send_sem=send_c.at[peer[1]], recv_sem=recv_c.at[me],
            device_id=peer, device_id_type=MESH)

    def total_arrival(j):
        peer = across(j)
        return pltpu.make_async_remote_copy(
            src_ref=total.at[me], dst_ref=total.at[peer[1]],
            send_sem=send_c.at[peer[1]], recv_sem=recv_c.at[peer[1]],
            device_id=peer, device_id_type=MESH)

    @pl.loop(1, vocab_size)
    def _(j):
        part_copy(j).start()

    @pl.loop(1, dp_size)
    def _(i):
        loss_copy(i).start()

    losses[my_plane] = loss_ref[...]
    parts[me] = grad_ref[me]

    @pl.loop(1, vocab_size)
    def _(j):
        part_arrival(j).wait_recv()

    planes[my_plane] = lax.fori_loop(
        1, vocab_size, lambda j, held: held + parts[j], parts[0])

    @pl.loop(1, dp_size)
    def _(i):
        plane_copy(i).start()

    @pl.loop(1, dp_size)
    def _(i):
        plane_arrival(i).wait_recv()

    total[me] = lax.fori_loop(1, dp_size, lambda i, held: held + planes[i], planes[0])

    @pl.loop(1, vocab_size)
    def _(j):
        total_copy(j).start()

    @pl.loop(1, vocab_size)
    def _(j):
        part_copy(j).wait_send()

    @pl.loop(1, dp_size)
    def _(i):
        plane_copy(i).wait_send()

    @pl.loop(1, vocab_size)
    def _(j):
        total_arrival(j).wait_recv()

    @pl.loop(1, vocab_size)
    def _(j):
        total_copy(j).wait_send()

    def squares(j, held):
        piece = total[j]
        return held + piece * piece

    gathered = lax.fori_loop(0, vocab_size, squares, jnp.zeros(parts.shape[1:], jnp.float32))
    norm = jnp.sqrt(jnp.sum(gathered, keepdims=True))
    norm_out[...] = norm

    @pl.loop(1, dp_size)
    def _(i):
        loss_arrival(i).wait_recv()
        loss_copy(i).wait_send()

    loss_out[...] = jnp.sum(losses[...], axis=0)[0:1, 0:1]
    shrink = GRAD_CLIP / jnp.maximum(norm, GRAD_CLIP)

    @pl.loop(0, vocab_size)
    def _(j):
        weight, first, second = adaptive_moment_update(
            total[j] * shrink, weight_ref[j], first_ref[j], second_ref[j])
        weight_out[j] = weight
        first_out[j] = first
        second_out[j] = second


def reduce_and_update(mesh_sizes, local_grad, weights, first, second, loss):
    dp_size, vocab_size = mesh_sizes
    number = local_grad.size
    rows = number // (128 * vocab_size)
    shape = (vocab_size, rows, 128)
    block = pltpu.VMEM(shape, jnp.float32)
    whole = pl.BlockSpec(memory_space=pltpu.VMEM)
    weight_new, first_new, second_new, norm, total_loss = pl.pallas_call(
        partial(sum_and_step, dp_size, vocab_size),
        out_shape=[jax.ShapeDtypeStruct(shape, jnp.float32)] * 3
        + [jax.ShapeDtypeStruct((1, 1), jnp.float32)] * 2,
        in_specs=[whole] * 5,
        out_specs=[whole] * 5,
        scratch_shapes=[
            block,
            pltpu.VMEM((dp_size, rows, 128), jnp.float32),
            block,
            pltpu.VMEM((dp_size, 8, 128), jnp.float32),
            pltpu.SemaphoreType.DMA((vocab_size,)),
            pltpu.SemaphoreType.DMA((vocab_size,)),
            pltpu.SemaphoreType.DMA((dp_size,)),
            pltpu.SemaphoreType.DMA((dp_size,)),
            pltpu.SemaphoreType.DMA((vocab_size,)),
            pltpu.SemaphoreType.DMA((vocab_size,)),
            pltpu.SemaphoreType.DMA((dp_size,)),
            pltpu.SemaphoreType.DMA((dp_size,)),
        ],
        compiler_params=pltpu.CompilerParams(
            collective_id=5, has_side_effects=True, vmem_limit_bytes=24 << 20
        ),
        name="sum_and_step",
    )(*[piece.reshape(shape) for piece in (local_grad, weights, first, second)], loss)
    flat = [piece.reshape(-1) for piece in (weight_new, first_new, second_new)]
    return (*flat, norm.reshape(()), total_loss.reshape(()))


TILE = 32


def head_step(dp_size, vocab_size, block, owned, hf_ref, label_ref, count_ref, table_hbm, grad_out, loss_out,
              table, hf_all, label_all, exps, exps_rest, tops, run_top, run_sum, run_smooth,
              run_goal, offset, z_even, z_odd, z_rest, dz_even, dz_odd, rest_even, rest_odd,
              acc_even, acc_odd, lse_tile, share_tile, stats_all,
              from_core, from_chip, leaving,
              table_sem, label_send, label_recv, hf_send, hf_recv,
              stat_send, stat_recv, core_send, core_recv, chip_send, chip_recv):
    plane = lax.axis_index("dp")
    me = lax.axis_index("vocab")
    chips = vocab_size // 2
    chip = me // 2
    core = lax.rem(me, 2)
    other = 2 * chip + 1 - core
    sibling = (plane, other)
    held = table_hbm.shape[0]
    full = held // block
    rest = held - full * block
    padded = table.shape[0] - full * block
    base = me * owned
    rows_each = hf_ref.shape[0]
    pair = 2 * rows_each
    width = hf_ref.shape[1]

    def partner(k):
        out = 0
        bit = 1
        while bit < chips:
            out = out + lax.rem(chip // bit + lax.rem(k // bit, 2), 2) * bit
            bit *= 2
        return out

    def across(j):
        return (plane, lax.rem(me + j, vocab_size))

    def table_copy(j, number):
        rows = pl.ds(pl.multiple_of(j * block, 16), number)
        return pltpu.make_async_copy(table_hbm.at[rows], table.at[rows], table_sem.at[j])

    @pl.loop(0, full)
    def _(j):
        table_copy(j, block).start()

    table_copy(full, rest).start()

    table[held:, :] = jnp.zeros((padded - rest, width), jnp.bfloat16)
    barrier = pltpu.get_barrier_semaphore()

    @pl.loop(1, vocab_size)
    def _(j):
        pl.semaphore_signal(barrier, inc=1, device_id=across(j), device_id_type=MESH)

    pl.semaphore_wait(barrier, vocab_size - 1)

    def remote(src, dst, send, recv, peer):
        return pltpu.make_async_remote_copy(
            src_ref=src, dst_ref=dst, send_sem=send, recv_sem=recv,
            device_id=peer, device_id_type=MESH)

    def hf_to_sibling():
        return remote(hf_ref, hf_all.at[me], hf_send.at[0], hf_recv.at[me], sibling)

    def hf_copy(k):
        return remote(hf_ref, hf_all.at[me], hf_send.at[k], hf_recv.at[me],
                      (plane, 2 * partner(k) + core))

    def hf_arrival(source):
        return remote(hf_ref, hf_all.at[source], hf_send.at[0], hf_recv.at[source], sibling)

    def hf_forward(k):
        source = 2 * partner(k) + core
        return remote(hf_all.at[source], hf_all.at[source], hf_send.at[chips + k],
                      hf_recv.at[source], sibling)

    def label_copy(j):
        peer = across(j)
        return remote(label_ref, label_all.at[me], label_send.at[peer[1]], label_recv.at[me], peer)

    def label_arrival(source):
        return remote(label_ref, label_all.at[source], label_send.at[source],
                      label_recv.at[source], sibling)

    near = min(3, chips)
    hf_to_sibling().start()

    @pl.loop(1, near)
    def _(k):
        hf_copy(k).start()

    @pl.loop(1, vocab_size)
    def _(j):
        label_copy(j).start()

    hf_all[me] = hf_ref[...]
    label_all[me] = label_ref[...]
    lanes = lax.broadcasted_iota(jnp.int32, (pair, 128), 1)

    def label_row(c, i):
        rows = label_all[pl.ds(2 * c, 2), i : i + 1, :].astype(jnp.float32)
        return jnp.concatenate([rows[0], rows[1]], axis=1)

    def set_offset(c):
        offset[...] = lane_columns(label_row(c, 0)).astype(jnp.int32) - base - lanes

    def folded(x):
        return sum(x[:, i * 128 : (i + 1) * 128] for i in range(1, x.shape[1] // 128)) + x[:, :128]

    def chunk_up(k, first):
        c = partner(k)
        if first:
            hf_arrival(other).wait_recv()
            label_arrival(other).wait_recv()
        else:
            hf_arrival(2 * c + core).wait_recv()
            hf_forward(k).start()
            label_arrival(2 * c).wait_recv()
            label_arrival(2 * c + 1).wait_recv()
            hf_arrival(2 * c + 1 - core).wait_recv()
        set_offset(c)
        run_top[...] = jnp.full((pair, 128), MASKED, jnp.float32)
        for ref in (run_sum, run_smooth, run_goal):
            ref[...] = jnp.zeros((pair, 128), jnp.float32)
        start = pl.multiple_of(k * pair, pair)

        def multiply(j, z_ref):
            if first:
                table_copy(j, rest if z_ref is z_rest else block).wait()
            rows = pl.ds(pl.multiple_of(j * block, 16), z_ref.shape[1])
            hidden = hf_all[pl.ds(2 * c, 2)].reshape(pair, width)
            z_ref[...] = matrix_multiply_transposed_right(hidden, table[rows, :])

        def reduce_full(j, z_ref):
            for r in range(pair // TILE):
                rows = slice(r * TILE, (r + 1) * TILE)
                there = pl.ds(start + r * TILE, TILE)
                z = z_ref[rows, :]
                old = run_top[rows, :]
                top = jnp.maximum(old, jnp.max(z, axis=1, keepdims=True))
                run_top[rows, :] = top
                tops[k, j, rows, :] = top
                gap = offset[rows, :] - j * block
                total = jnp.zeros((TILE, 128), jnp.float32)
                smooth = jnp.zeros((TILE, 128), jnp.float32)
                goal = jnp.zeros((TILE, 128), jnp.float32)
                for i in range(block // 128):
                    part = slice(i * 128, (i + 1) * 128)
                    piece = z[:, part]
                    e = jnp.exp(piece - top)
                    exps[j, there, part] = e
                    total = total + e
                    smooth = smooth + piece
                    goal = goal + jnp.where(gap == i * 128, piece, 0.0)
                run_sum[rows, :] = run_sum[rows, :] * jnp.exp(old - top) + total
                run_smooth[rows, :] = run_smooth[rows, :] + smooth
                run_goal[rows, :] = run_goal[rows, :] + goal

        def reduce_rest():
            for r in range(pair // TILE):
                rows = slice(r * TILE, (r + 1) * TILE)
                there = pl.ds(start + r * TILE, TILE)
                spot = lanes[rows, :]
                limit = jnp.minimum(VOCAB_SIZE - base, owned) - full * block - spot
                gap = offset[rows, :] - full * block
                pieces = []
                for i in range(padded // 128):
                    piece = z_rest[rows, i * 128 : (i + 1) * 128]
                    pieces.append((i * 128 < limit, piece))
                highest = jnp.where(pieces[0][0], pieces[0][1], MASKED)
                for valid, piece in pieces[1:]:
                    highest = jnp.maximum(highest, jnp.where(valid, piece, MASKED))
                old = run_top[rows, :]
                top = jnp.maximum(old, jnp.max(highest, axis=1, keepdims=True))
                run_top[rows, :] = top
                tops[k, full, rows, :] = top
                total = jnp.zeros((TILE, 128), jnp.float32)
                smooth = jnp.zeros((TILE, 128), jnp.float32)
                goal = jnp.zeros((TILE, 128), jnp.float32)
                for i, (valid, piece) in enumerate(pieces):
                    e = jnp.where(valid, jnp.exp(piece - top), 0.0)
                    exps_rest[there, i * 128 : (i + 1) * 128] = e
                    total = total + e
                    smooth = smooth + jnp.where(valid, piece, 0.0)
                    goal = goal + jnp.where(valid & (gap == i * 128), piece, 0.0)
                run_sum[rows, :] = run_sum[rows, :] * jnp.exp(old - top) + total
                run_smooth[rows, :] = run_smooth[rows, :] + smooth
                run_goal[rows, :] = run_goal[rows, :] + goal

        multiply(0, z_even)
        turns = (full - 1) // 2

        if turns > 0:
            @pl.loop(0, turns)
            def _(t):
                multiply(2 * t + 1, z_odd)
                reduce_full(2 * t, z_even)
                multiply(2 * t + 2, z_even)
                reduce_full(2 * t + 1, z_odd)

        if full - 2 * turns == 2:
            multiply(full - 1, z_odd)
            reduce_full(full - 2, z_even)
            multiply(full, z_rest)
            reduce_full(full - 1, z_odd)
        else:
            multiply(full, z_rest)
            reduce_full(full - 1, z_even)
        reduce_rest()

        def row_sum(ref):
            return jnp.sum(ref[...].T, axis=0, keepdims=True)

        ids = lax.broadcasted_iota(jnp.int32, (8, pair), 0)
        packed = jnp.where(ids == 0, run_top[...].T[0:1, :], 0.0)
        for i, ref in enumerate((run_sum, run_smooth, run_goal)):
            packed = jnp.where(ids == i + 1, row_sum(ref), packed)
        stats_all[me, c] = packed

    chunk_up(0, True)

    @pl.loop(near, chips)
    def _(k):
        hf_copy(k).start()

    @pl.loop(1, chips)
    def _(k):
        chunk_up(k, False)

    def stat_copy(j):
        peer = across(j)
        return remote(stats_all.at[me], stats_all.at[me], stat_send.at[peer[1]],
                      stat_recv.at[me], peer)

    def stat_arrival(j):
        source = across(j)[1]
        return remote(stats_all.at[me], stats_all.at[source], stat_send.at[source],
                      stat_recv.at[source], across(j))

    @pl.loop(1, vocab_size)
    def _(j):
        stat_copy(j).start()

    @pl.loop(1, vocab_size)
    def _(j):
        stat_arrival(j).wait_recv()

    count = jnp.maximum(count_ref[1:2, 0:1], 1.0)

    def totals_of(c):
        here = stats_all[:, c]
        tops_here = here[:, 0:1, :]
        top = jnp.max(tops_here, axis=0)
        total = jnp.sum(here[:, 1:2, :] * jnp.exp(tops_here - top[None]), axis=0)
        return top + jnp.log(total), jnp.sum(here[:, 2:3, :], axis=0), jnp.sum(
            here[:, 3:4, :], axis=0)

    def chunk_loss(c, held_loss):
        lse, smooth, goal = totals_of(c)
        return held_loss + label_row(c, 1) * (lse - 0.9 * goal - 0.1 * smooth / VOCAB_SIZE)

    slots = from_core.shape[0]
    columns_each = width // 4

    def core_copy(k, n, acc):
        half = pl.ds(pl.multiple_of((1 - core) * rows_each, rows_each), rows_each)
        part = pl.ds(pl.multiple_of(n * columns_each, columns_each), columns_each)
        return remote(acc.at[half, part], from_core.at[lax.rem(k, slots), :, part],
                      core_send.at[k, n], core_recv.at[k, n], sibling)

    def chip_copy(k, n):
        part = pl.ds(pl.multiple_of(n * columns_each, columns_each), columns_each)
        return remote(leaving.at[k - 1, :, part], from_chip.at[k - 1, :, part],
                      chip_send.at[k, n], chip_recv.at[k, n], (plane, 2 * partner(k) + core))

    def prepare(k):
        c = partner(k)
        lse, _, _ = totals_of(c)
        lse_tile[...] = lane_columns(lse)
        share_tile[...] = lane_columns(label_row(c, 1) / count)
        set_offset(c)

    quarter = pair // 4

    def grads(k, n, dz_ref, rest_ref):
        for r in range(quarter // TILE):
            first = pl.multiple_of(n * quarter + r * TILE, TILE)
            rows = pl.ds(first, TILE)
            there = pl.ds(pl.multiple_of(k * pair + first, TILE), TILE)
            share = share_tile[rows, :]
            lse = lse_tile[rows, :]
            low = share * (0.1 / VOCAB_SIZE)
            high = low + 0.9 * share
            gap = offset[rows, :]
            for j in range(full):
                factor = share * jnp.exp(tops[k, j, rows, :] - lse)
                for i in range(block // 128):
                    at = j * block + i * 128
                    e = exps[j, there, i * 128 : (i + 1) * 128]
                    dz = e * factor - jnp.where(gap == at, high, low)
                    dz_ref[rows, at : at + 128] = dz.astype(jnp.bfloat16)
            factor = share * jnp.exp(tops[k, full, rows, :] - lse)
            limit = jnp.minimum(VOCAB_SIZE - base, owned) - full * block - lanes[0:TILE, :]
            for i in range(padded // 128):
                part = slice(i * 128, (i + 1) * 128)
                at = full * block + i * 128
                dz = exps_rest[there, part] * factor - jnp.where(gap == at, high, low)
                rest_ref[rows, part] = jnp.where(i * 128 < limit, dz, 0.0).astype(jnp.bfloat16)

    def gather(k, n, dz_ref, rest_ref, acc):
        part = pl.ds(pl.multiple_of(n * columns_each, columns_each), columns_each)
        acc[:, part] = matrix_multiply(
            dz_ref[...], table[pl.ds(0, full * block), part]
        ) + matrix_multiply(rest_ref[...], table[pl.ds(full * block, padded), part])

    def finish(k, n, acc):
        core_copy(k, n, acc).wait()
        own = pl.ds(pl.multiple_of(core * rows_each, rows_each), rows_each)
        part = pl.ds(pl.multiple_of(n * columns_each, columns_each), columns_each)
        return from_core[lax.rem(k, slots), :, part] + acc[own, part]

    def ship(k, n, acc):
        part = pl.ds(pl.multiple_of(n * columns_each, columns_each), columns_each)
        leaving[k - 1, :, part] = finish(k, n, acc).astype(jnp.bfloat16)
        chip_copy(k, n).start()

    def stage(k, now, later, acc, acc_before):
        if later is not None:
            prepare(k - 1)

        @pl.loop(0, 4)
        def _(n):
            gather(k, n, *now, acc)
            if later is not None:
                grads(k - 1, n, *later)
            core_copy(k, n, acc).start()
            if later is not None:
                @pl.when(n > 0)
                def _():
                    ship(k, n - 1, acc)

            if acc_before is not None:
                @pl.when((n == 0) & (k < chips - 1))
                def _():
                    ship(k + 1, 3, acc_before)

    evens = ((dz_even, rest_even), acc_even)
    odds = ((dz_odd, rest_odd), acc_odd)
    prepare(chips - 1)

    @pl.loop(0, 4)
    def _(n):
        grads(chips - 1, n, *odds[0])

    @pl.loop(0, chips // 2 - 1)
    def _(t):
        k = chips - 1 - 2 * t
        stage(k, odds[0], evens[0], acc_odd, acc_even)
        stage(k - 1, evens[0], odds[0], acc_even, acc_odd)

    stage(1, odds[0], evens[0], acc_odd, acc_even if chips > 2 else None)
    stage(0, evens[0], None, acc_even, acc_odd)

    loss = lax.fori_loop(0, chips, chunk_loss, jnp.zeros((1, pair), jnp.float32))
    loss_out[...] = jnp.broadcast_to(jnp.sum(loss, keepdims=True) / count, loss_out.shape)
    for n in range(4):
        grad_out[:, n * columns_each : (n + 1) * columns_each] = finish(0, n, acc_even)

    @pl.loop(1, chips)
    def _(t):
        k = chips - t
        for n in range(4):
            chip_copy(k, n).wait_recv()
        grad_out[...] += from_chip[k - 1].astype(jnp.float32)

    hf_to_sibling().wait_send()

    @pl.loop(1, chips)
    def _(k):
        hf_copy(k).wait_send()
        hf_forward(k).wait_send()
        for n in range(4):
            chip_copy(k, n).wait_send()

    @pl.loop(1, vocab_size)
    def _(j):
        label_copy(j).wait_send()
        stat_copy(j).wait_send()


def head(mesh_sizes, owned, final_rows, labels, counts, table):
    dp_size, vocab_size = mesh_sizes
    rows, width = final_rows.shape
    held = table.shape[0]
    block = 1024
    full = held // block
    rest = -(-(held - full * block) // 128) * 128
    chips = vocab_size // 2
    pair = 2 * rows
    low, wide = jnp.bfloat16, jnp.float32
    whole = pl.BlockSpec(memory_space=pltpu.VMEM)
    dma = pltpu.SemaphoreType.DMA
    tile = pltpu.VMEM((pair, 128), wide)
    grad, loss = pl.pallas_call(
        partial(head_step, dp_size, vocab_size, block, owned),
        out_shape=[
            jax.ShapeDtypeStruct((rows, width), wide),
            jax.ShapeDtypeStruct((8, 128), wide),
        ],
        in_specs=[whole, whole, whole, pl.BlockSpec(memory_space=pl.ANY)],
        out_specs=[whole, whole],
        scratch_shapes=[
            pltpu.VMEM((full * block + rest, width), low),
            pltpu.VMEM((vocab_size, rows, width), low),
            pltpu.VMEM((vocab_size, 8, rows), jnp.int32),
            pltpu.VMEM((full, vocab_size * rows, block), wide),
            pltpu.VMEM((vocab_size * rows, rest), wide),
            pltpu.VMEM((chips, full + 1, pair, 128), wide),
            tile,
            tile,
            tile,
            tile,
            pltpu.VMEM((pair, 128), jnp.int32),
            pltpu.VMEM((pair, block), wide),
            pltpu.VMEM((pair, block), wide),
            pltpu.VMEM((pair, rest), wide),
            pltpu.VMEM((pair, full * block), low),
            pltpu.VMEM((pair, full * block), low),
            pltpu.VMEM((pair, rest), low),
            pltpu.VMEM((pair, rest), low),
            pltpu.VMEM((pair, width), wide),
            pltpu.VMEM((pair, width), wide),
            tile,
            tile,
            pltpu.VMEM((vocab_size, chips, 8, pair), wide),
            pltpu.VMEM((3, rows, width), wide),
            pltpu.VMEM((chips - 1, rows, width), low),
            pltpu.VMEM((chips - 1, rows, width), low),
            dma((full + 1,)),
            dma((vocab_size,)),
            dma((vocab_size,)),
            dma((2 * chips,)),
            dma((vocab_size,)),
            dma((vocab_size,)),
            dma((vocab_size,)),
            dma((chips, 4)),
            dma((chips, 4)),
            dma((chips, 4)),
            dma((chips, 4)),
        ],
        compiler_params=pltpu.CompilerParams(
            collective_id=3, has_side_effects=True, vmem_limit_bytes=63 << 20
        ),
        name="head_step",
    )(final_rows, labels, counts, table)
    return grad, loss


NARROW = 16
PARTS = (0, 96, 192, 224, 256, 288, 416, 544, 576)


def floor_part(values, size):
    return jnp.floor((values + 0.5) * (1.0 / size))


def spread_places(ranks, slab):
    lanes = lax.broadcasted_iota(jnp.int32, (1024, 128), 1).astype(jnp.float32) + 128.0 * slab
    rows = lax.broadcasted_iota(jnp.int32, (1024, 128), 0).astype(jnp.float32)
    return floor_part(lanes, ranks) == rows - 32.0 * floor_part(rows, 32)


def unpack_down(flat_ref, first, ranks, out_ref, start):
    slabs = ranks // RANK
    total = None
    for slab in range(slabs):
        packed = flat_ref[pl.ds(first + slab, 32, stride=slabs), :]
        spread = jnp.broadcast_to(packed[:, None, :], (32, 32, 128)).reshape(1024, 128)
        spread = jnp.where(spread_places(ranks, slab), spread, 0.0).astype(jnp.bfloat16)
        lanes = lax.broadcasted_iota(jnp.int32, (128, NARROW), 0).astype(jnp.float32) + 128.0 * slab
        column = lax.broadcasted_iota(jnp.int32, (128, NARROW), 1).astype(jnp.float32)
        chosen = low_ones(lanes - ranks * floor_part(lanes, ranks) == column)
        part = matrix_multiply(spread, chosen)
        total = part if total is None else total + part
    out_ref[pl.ds(start, 1024), :] = total.astype(jnp.bfloat16)


def unpack_up(flat_ref, first, ranks, out_ref):
    wide = out_ref.shape[1] // 128
    for c in range(wide):
        rows = flat_ref[pl.ds(first + c, ranks, stride=wide), :]
        rows = jnp.concatenate([rows, jnp.zeros((NARROW - ranks, 128), jnp.float32)], axis=0)
        out_ref[:, c * 128 : (c + 1) * 128] = rows.astype(jnp.bfloat16)


def unpack(flat_ref, outs):
    for i, out_ref in enumerate(outs):
        ranks = 3 * RANK if i < 2 else RANK
        if i % 2:
            unpack_up(flat_ref, PARTS[i], ranks, out_ref)
        else:
            for b in range(out_ref.shape[0] // 1024):
                unpack_down(flat_ref, PARTS[i] + 32 * b, ranks, out_ref, 1024 * b)


def lane_columns(row):
    return jnp.broadcast_to(row, (128, row.shape[1])).T


def ones_where(condition):
    return jnp.where(condition, 1.0, 0.0)


def low_ones(condition):
    return ones_where(condition).astype(jnp.bfloat16)


def embed_step(dp_size, vocab_size, block, room, owned, token_ref, segment_ref, spot_ref, flag_ref,
               place_hbm, affine_ref, flat_ref, table_hbm,
               h1_out, rows_out, label_out, full_out, crowd_out,
               a_qkv, b_qkv, a_o, b_o, a_fc, b_fc, a_p, b_p,
               table, place_table, key_cols, unique_cols, slot_cols, owners, asked, lists, lists_in,
               acc, leaving, arriving, stream, full_all,
               table_sem, place_sem, list_send, list_recv, row_send, row_recv, full_send, full_recv):
    plane = lax.axis_index("dp")
    me = lax.axis_index("vocab")
    chips = vocab_size // 2
    chip = me // 2
    held = table.shape[0]
    full = held // block
    rest = held - full * block
    length = token_ref.shape[1]
    width = table.shape[1]
    spots_here = spot_ref.shape[1]
    chunk = 128
    chunks = length // chunk

    def partner(k):
        out = 0
        bit = 1
        while bit < chips:
            out = out + lax.rem(chip // bit + (k // bit) % 2, 2) * bit
            bit *= 2
        return out

    def across(j):
        return (plane, lax.rem(me + j, vocab_size))

    def along(i):
        return (lax.rem(plane + i, dp_size), me)

    def remote(src, dst, send, recv, peer):
        return pltpu.make_async_remote_copy(
            src_ref=src, dst_ref=dst, send_sem=send, recv_sem=recv,
            device_id=peer, device_id_type=MESH)

    def table_copy(j, number):
        rows = pl.ds(pl.multiple_of(j * block, 16), number)
        return pltpu.make_async_copy(table_hbm.at[rows], table.at[rows], table_sem.at[j])

    @pl.loop(0, full)
    def _(j):
        table_copy(j, block).start()

    table_copy(full, rest).start()

    place_copy = pltpu.make_async_copy(
        place_hbm.at[pl.ds(0, place_table.shape[0])], place_table, place_sem)
    place_copy.start()
    barrier = pltpu.get_barrier_semaphore()

    @pl.loop(1, vocab_size)
    def _(j):
        pl.semaphore_signal(barrier, inc=1, device_id=across(j), device_id_type=MESH)

    @pl.loop(1, dp_size)
    def _(i):
        pl.semaphore_signal(barrier, inc=1, device_id=along(i), device_id_type=MESH)

    token = token_ref[...].astype(jnp.float32)
    segment = segment_ref[...].astype(jnp.float32)
    steps = lax.broadcasted_iota(jnp.int32, (1, length), 1).astype(jnp.float32)
    spot = lane_columns(spot_ref[...].astype(jnp.float32))[:, 0:1]
    flag = lane_columns(flag_ref[...].astype(jnp.float32))[:, 0:1]
    at_spot = steps == spot
    at_next = steps == spot + 1.0

    def picked(where_to, row):
        return jnp.sum(jnp.where(where_to, row, 0.0), axis=1, keepdims=True)

    segment_here = picked(at_spot, segment)
    weight = jnp.where(segment_here == picked(at_next, segment), flag, 0.0)
    heavy = jnp.sum(weight, axis=0, keepdims=True)
    target = picked(at_next, token)
    lanes = lax.broadcasted_iota(jnp.int32, (spots_here, 128), 1)
    label_tile = jnp.where(lanes == 0, target, jnp.where(lanes == 1, weight, 0.0))
    label_out[...] = label_tile.T[0:8, :].astype(jnp.int32)
    read = (steps <= spot) & (segment == segment_here) & (weight > 0.0)
    needed = jnp.max(ones_where(read), axis=0, keepdims=True) > 0.0

    key = jnp.where(needed, token, -1.0 - steps)
    key_cols[...] = lane_columns(key)

    def places(a):
        return (lax.broadcasted_iota(jnp.int32, (chunk, 1), 0) + a * chunk).astype(jnp.float32)

    def rows_at(a):
        return pl.ds(pl.multiple_of(a * chunk, chunk), chunk)

    def same(a):
        return key_cols[rows_at(a), 0:1] == key

    def seen(a, carry):
        return jnp.maximum(carry, jnp.max(
            ones_where(same(a) & (places(a) < steps)), axis=0, keepdims=True))

    again = lax.fori_loop(0, chunks, seen, jnp.zeros((1, length), jnp.float32))
    unique = ones_where(needed & (again == 0.0))
    unique_cols[...] = lane_columns(unique)
    owner = jnp.zeros((1, length), jnp.float32)
    for j in range(1, vocab_size):
        owner = owner + ones_where(token >= float(j * owned))
    owner_ids = lax.broadcasted_iota(jnp.int32, (vocab_size, length), 0).astype(jnp.float32)
    mine = jnp.where(owner_ids == owner, unique, 0.0)
    owners[...] = mine

    def ahead(a, carry):
        before = low_ones(places(a) < steps)
        return carry + matrix_multiply(owners[:, rows_at(a)].astype(jnp.bfloat16), before)

    ranks = lax.fori_loop(0, chunks, ahead, jnp.zeros((vocab_size, length), jnp.float32))
    rank = jnp.sum(jnp.where(owner_ids == owner, ranks, 0.0), axis=0, keepdims=True)
    too_many = jnp.max(unique * ones_where(rank >= float(room)), axis=1, keepdims=True)
    local_id = token - owner * float(owned)
    local_high = jnp.floor(local_id * (1.0 / 128.0))
    local_low = local_id - 128.0 * local_high
    row_ids = lax.broadcasted_iota(jnp.int32, (8, length), 0)

    def stacked(first, second):
        return jnp.where(row_ids == 0, first, jnp.where(row_ids == 1, second, 0.0))

    asked[...] = stacked(owner, jnp.minimum(rank, 127.0))

    def found(a, carry):
        match = low_ones(same(a) & (unique_cols[rows_at(a), 0:1] > 0.0))
        return carry + matrix_multiply(asked[:, rows_at(a)].astype(jnp.bfloat16), match)

    slots = lax.fori_loop(0, chunks, found, jnp.zeros((8, length), jnp.float32))
    slot = jnp.where(needed, slots[0:1, :] * 128.0 + slots[1:2, :], -1.0)
    slot_cols[...] = lane_columns(slot)
    local_parts = stacked(local_high, local_low).astype(jnp.bfloat16)
    rank_ids = lax.broadcasted_iota(jnp.int32, (128, length), 0).astype(jnp.float32)
    list_rows = lax.broadcasted_iota(jnp.int32, (8, 128), 0)

    @pl.loop(0, vocab_size)
    def _(j):
        theirs = (unique > 0.0) & (owner == j.astype(jnp.float32))
        chosen = low_ones(rank_ids == jnp.where(theirs, rank, -1.0))
        ids = matrix_multiply_transposed_right(local_parts, chosen)
        lists[j] = jnp.where(list_rows == 2, too_many, jnp.where(list_rows == 3, heavy, ids))

    @pl.loop(0, vocab_size)
    def _(j):
        arriving[j] = jnp.zeros(arriving.shape[1:], jnp.bfloat16)

    pl.semaphore_wait(barrier, vocab_size + dp_size - 2)

    def list_copy(j):
        peer = across(j)
        return remote(lists.at[peer[1]], lists_in.at[me], list_send.at[peer[1]],
                      list_recv.at[me], peer)

    def list_arrival(j):
        source = across(j)[1]
        return remote(lists.at[source], lists_in.at[source], list_send.at[source],
                      list_recv.at[source], across(j))

    @pl.loop(1, vocab_size)
    def _(j):
        list_copy(j).start()

    lists_in[me] = lists[me]

    ids = lax.broadcasted_iota(jnp.int32, (32, length), 0).astype(jnp.float32)
    starts = jnp.sum(ones_where(segment < ids), axis=1, keepdims=True)
    place = steps - jnp.sum(jnp.where(segment == ids, starts, 0.0), axis=0, keepdims=True)
    place_cols = lane_columns(place)[:, 0:1]
    span = place_table.shape[0]
    place_copy.wait()
    place_ids = lax.broadcasted_iota(jnp.int32, (length, span), 1).astype(jnp.float32)
    stream[...] = matrix_multiply(low_ones(place_ids == place_cols), place_table[...])
    spot_place = picked(at_spot, place)
    spot_slot = picked(at_spot, slot)
    unpack(flat_ref, (a_qkv, b_qkv, a_o, b_o, a_fc, b_fc, a_p, b_p))

    @pl.loop(1, vocab_size)
    def _(j):
        list_arrival(j).wait_recv()

    full_all[plane] = jnp.where(
        list_rows == 0, jnp.max(lists_in[:, 2:3, 0:1], axis=0),
        jnp.sum(lists_in[:, 3:4, 0:1], axis=0))

    def full_copy(i):
        peer = along(i)
        return remote(full_all.at[plane], full_all.at[plane], full_send.at[peer[0]],
                      full_recv.at[plane], peer)

    def full_arrival(i):
        source = along(i)[0]
        return remote(full_all.at[plane], full_all.at[source], full_send.at[source],
                      full_recv.at[source], along(i))

    @pl.loop(1, dp_size)
    def _(i):
        full_copy(i).start()

    def row_copy(d):
        return remote(leaving.at[d], arriving.at[me, pl.ds(0, room)], row_send.at[d],
                      row_recv.at[me], (plane, d))

    def row_arrival(d):
        return remote(leaving.at[d], arriving.at[d, pl.ds(0, room)], row_send.at[d],
                      row_recv.at[d], (plane, d))

    def wanted(d):
        here = lists_in[d]
        return lane_columns(here[0:1, :] * 128.0 + here[1:2, :])[0:room, 0:1]

    first = True
    for k in range(chips - 1, -1, -1):
        c = partner(k)
        wanted_here = jnp.concatenate([wanted(2 * c), wanted(2 * c + 1)], axis=0)

        def rows_of(j, number):
            if first:
                table_copy(j, number).wait()
            ids_here = (lax.broadcasted_iota(jnp.int32, (2 * room, number), 1)
                        + j * block).astype(jnp.float32)
            rows = pl.ds(pl.multiple_of(j * block, 16), number)
            return matrix_multiply(low_ones(ids_here == wanted_here), table[rows, :])

        acc[...] = rows_of(full, rest)

        @pl.loop(0, full)
        def _(j):
            acc[...] += rows_of(j, block)

        first = False
        for i in range(2):
            leaving[2 * c + i] = acc[pl.ds(i * room, room), :].astype(jnp.bfloat16)
        if k > 0:
            for i in range(2):
                row_copy(2 * c + i).start()
        else:
            row_copy(2 * c + 1 - lax.rem(me, 2)).start()
            arriving[me, pl.ds(0, room), :] = leaving[me]

    for k in range(chips):
        c = partner(k)
        if k > 0:
            for i in range(2):
                row_arrival(2 * c + i).wait_recv()
        else:
            row_arrival(2 * c + 1 - lax.rem(me, 2)).wait_recv()
        pair_rows = arriving[pl.ds(2 * c, 2)].reshape(256, width)
        offset = (2 * c * 128).astype(jnp.float32)

        def spread(column, ids_like):
            ids_here = lax.broadcasted_iota(jnp.int32, ids_like, 1).astype(jnp.float32)
            return low_ones(ids_here + offset == column)

        stream[...] += matrix_multiply(spread(slot_cols[:, 0:1], (length, 256)), pair_rows)
        spot_rows = matrix_multiply(spread(spot_slot, (spots_here, 256)), pair_rows)
        if k == 0:
            rows_out[...] = spot_rows
        else:
            rows_out[...] += spot_rows

    spot_ids = lax.broadcasted_iota(jnp.int32, (spots_here, span), 1).astype(jnp.float32)
    rows_out[...] += matrix_multiply(low_ones(spot_ids == spot_place), place_table[...])

    @pl.loop(0, length // 256)
    def _(a):
        rows = pl.ds(pl.multiple_of(a * 256, 256), 256)
        h1_out[rows, :] = layer_norm(
            stream[rows, :], affine_ref[0:1, :], affine_ref[3:4, :]).astype(jnp.bfloat16)

    @pl.loop(1, dp_size)
    def _(i):
        full_arrival(i).wait_recv()

    counts = jnp.where(
        list_rows == 0, jnp.max(full_all[...], axis=0), jnp.sum(full_all[...], axis=0))
    full_out[...] = counts
    crowd_out[...] = counts[0:1, 0:1].astype(jnp.int32)

    @pl.loop(1, vocab_size)
    def _(j):
        list_copy(j).wait_send()

    @pl.loop(1, dp_size)
    def _(i):
        full_copy(i).wait_send()

    for k in range(chips):
        if k > 0:
            for i in range(2):
                row_copy(2 * partner(k) + i).wait_send()
        else:
            row_copy(2 * chip + 1 - lax.rem(me, 2)).wait_send()


def embed(mesh_sizes, owned, tokens, segments, spots, flags, place_table, affine, flat, table):
    dp_size, vocab_size = mesh_sizes
    length = tokens.shape[1]
    spots_here = spots.shape[1]
    held, width = table.shape
    block = 1024
    full = held // block
    chips = vocab_size // 2
    room = 112 if vocab_size <= 8 else 64
    span = 256
    whole = pl.BlockSpec(memory_space=pltpu.VMEM)
    dma = pltpu.SemaphoreType.DMA
    return pl.pallas_call(
        partial(embed_step, dp_size, vocab_size, block, room, owned),
        out_shape=[
            jax.ShapeDtypeStruct((length, width), jnp.bfloat16),
            jax.ShapeDtypeStruct((spots_here, width), jnp.float32),
            jax.ShapeDtypeStruct((8, spots_here), jnp.int32),
            jax.ShapeDtypeStruct((8, 128), jnp.float32),
            jax.ShapeDtypeStruct((1, 1), jnp.int32),
        ]
        + [
            jax.ShapeDtypeStruct(shape, jnp.bfloat16)
            for shape in (
                (width, NARROW), (NARROW, width), (width, NARROW), (NARROW, width),
                (width, NARROW), (NARROW, 4 * width), (4 * width, NARROW), (NARROW, width),
            )
        ],
        in_specs=[whole] * 4
        + [pl.BlockSpec(memory_space=pl.ANY), whole, whole, pl.BlockSpec(memory_space=pl.ANY)],
        out_specs=[whole] * 13,
        scratch_shapes=[
            pltpu.VMEM((held, width), jnp.bfloat16),
            pltpu.VMEM((span, width), jnp.bfloat16),
            pltpu.VMEM((length, 128), jnp.float32),
            pltpu.VMEM((length, 128), jnp.float32),
            pltpu.VMEM((length, 128), jnp.float32),
            pltpu.VMEM((vocab_size, length), jnp.float32),
            pltpu.VMEM((8, length), jnp.float32),
            pltpu.VMEM((vocab_size, 8, 128), jnp.float32),
            pltpu.VMEM((vocab_size, 8, 128), jnp.float32),
            pltpu.VMEM((2 * room, width), jnp.float32),
            pltpu.VMEM((vocab_size, room, width), jnp.bfloat16),
            pltpu.VMEM((vocab_size, 128, width), jnp.bfloat16),
            pltpu.VMEM((length, width), jnp.float32),
            pltpu.VMEM((dp_size, 8, 128), jnp.float32),
            dma((full + 1,)),
            dma,
            dma((vocab_size,)),
            dma((vocab_size,)),
            dma((vocab_size,)),
            dma((vocab_size,)),
            dma((dp_size,)),
            dma((dp_size,)),
        ],
        compiler_params=pltpu.CompilerParams(
            collective_id=1, has_side_effects=True, vmem_limit_bytes=60 << 20
        ),
        name="embed_step",
    )(tokens, segments, spots, flags, place_table, affine, flat.reshape(-1, 128), table)


def wide_loop(number, body):
    lax.fori_loop(0, number, lambda i, carry: (body(i), carry)[1], 0)


def norm_parts(rows):
    centred = rows - jnp.mean(rows, axis=-1, keepdims=True)
    return centred, lax.rsqrt(jnp.mean(centred * centred, axis=-1, keepdims=True) + NORM_EPS)


def norm_back(rows, gain, grad):
    centred, spread = norm_parts(rows)
    hat = centred * spread
    grad_hat = grad * gain
    return spread * (
        grad_hat
        - jnp.mean(grad_hat, axis=-1, keepdims=True)
        - hat * jnp.mean(grad_hat * hat, axis=-1, keepdims=True)
    )


GELU_RATE = math.sqrt(2.0 / math.pi)


def gelu_parts(pre):
    bend = jnp.tanh(GELU_RATE * (pre + 0.044715 * (pre * pre * pre)))
    return 0.5 * (1.0 + bend), bend


def gelu_slope(pre):
    half, bend = gelu_parts(pre)
    inner = GELU_RATE * (1.0 + 3.0 * 0.044715 * (pre * pre))
    return half + 0.5 * pre * (1.0 - bend * bend) * inner


def both_heads(pair):
    lanes = lax.broadcasted_iota(jnp.int32, pair.shape, 1)
    half = pair.shape[1] // 2
    wide = pair.astype(jnp.float32)
    return jnp.concatenate(
        [jnp.where(lanes < half, wide, 0.0), jnp.where(lanes < half, 0.0, wide)], axis=0
    ).astype(jnp.bfloat16)


def side_by_side(stacked):
    rows = stacked.shape[0] // 2
    lanes = lax.broadcasted_iota(jnp.int32, (rows, stacked.shape[1]), 1)
    return jnp.where(lanes < stacked.shape[1] // 2, stacked[:rows], stacked[rows:])


def third_of(rows, j):
    ids = lax.broadcasted_iota(jnp.int32, rows.shape, 0)
    wide = jnp.where((ids >= j * RANK) & (ids < (j + 1) * RANK), rows.astype(jnp.float32), 0.0)
    return wide.astype(jnp.bfloat16)


def attention_mask(spot_ref, segment_ref):
    spot = lane_columns(spot_ref[...].astype(jnp.float32))[:, 0:1]
    steps = lax.broadcasted_iota(jnp.int32, segment_ref.shape, 1).astype(jnp.float32)
    segment = segment_ref[...].astype(jnp.float32)
    here = jnp.sum(jnp.where(steps == spot, segment, 0.0), axis=1, keepdims=True)
    open_to = ones_where((steps <= spot) & (segment == here))
    return jnp.concatenate([open_to, open_to], axis=0)


def layer_up(h1_ref, rows_ref, segment_ref, spot_ref, affine_ref, bias_ref,
             a_qkv, b_qkv, a_o, b_o, a_fc, b_fc, a_p, b_p,
             qkv_hbm, o_hbm, in_hbm, out_hbm,
             final_ref, q_ref, k_ref, v_ref, u1_ref, u1_rows_ref, h1_rows_ref, lse_ref,
             o_ref, uo_ref, middle_ref, h2_ref, uf_ref, pre_ref, f_ref, up_ref, last_ref,
             wq, wk, wv, wo, win, wout, mask, sems):
    length, width = h1_ref.shape
    hidden = win.shape[1]
    quarter = hidden // 4

    def columns_of(source, j, number):
        return source.at[:, pl.ds(j * number, number)]

    copies = [
        pltpu.make_async_copy(columns_of(qkv_hbm, 1, width), wk, sems.at[0]),
        pltpu.make_async_copy(columns_of(qkv_hbm, 2, width), wv, sems.at[1]),
        pltpu.make_async_copy(columns_of(qkv_hbm, 0, width), wq, sems.at[2]),
        pltpu.make_async_copy(o_hbm, wo, sems.at[3]),
        pltpu.make_async_copy(in_hbm, win, sems.at[4]),
        pltpu.make_async_copy(out_hbm, wout, sems.at[5]),
    ]
    for copy in copies:
        copy.start()

    def bias(first, number):
        return bias_ref[0:1, first : first + number]

    mask[...] = attention_mask(spot_ref, segment_ref)
    h1_rows = layer_norm(rows_ref[...], affine_ref[0:1, :], affine_ref[3:4, :]).astype(
        jnp.bfloat16)
    h1_rows_ref[...] = h1_rows
    u1_ref[...] = matrix_multiply(h1_ref[...], a_qkv[...]).astype(jnp.bfloat16)
    u1_rows = matrix_multiply(h1_rows, a_qkv[...]).astype(jnp.bfloat16)
    u1_rows_ref[...] = u1_rows

    def project(normed, low, weight, j):
        return (
            matrix_multiply(normed, weight[...])
            + bias(j * width, width)
            + ADAPTER_SCALE * matrix_multiply(low, third_of(b_qkv[...], j))
        ).astype(jnp.bfloat16)

    chunk = 512
    for j, weight, out, copy in ((1, wk, k_ref, copies[0]), (2, wv, v_ref, copies[1])):
        copy.wait()

        def rows_of(i):
            rows = pl.ds(pl.multiple_of(i * chunk, chunk), chunk)
            out[rows, :] = project(h1_ref[rows, :], u1_ref[rows, :], weight, j)

        wide_loop(length // chunk, rows_of)
    copies[2].wait()
    q_ref[...] = project(h1_rows, u1_rows, wq, 0)
    scale = (width // HEADS) ** (-0.5)
    lanes = lax.broadcasted_iota(jnp.int32, lse_ref.shape, 1)
    lse_ref[...] = jnp.zeros(lse_ref.shape, jnp.float32)

    def heads(g):
        pair = pl.ds(pl.multiple_of(g * 128, 128), 128)
        scores = scale * matrix_multiply_transposed_right(both_heads(q_ref[:, pair]), k_ref[:, pair])
        scores = jnp.where(mask[...] > 0.0, scores, MASKED)
        top = jnp.max(scores, axis=1, keepdims=True)
        e = jnp.exp(scores - top)
        total = jnp.sum(e, axis=1, keepdims=True)
        probs = (e * (1.0 / total)).astype(jnp.bfloat16)
        o_ref[:, pair] = side_by_side(matrix_multiply(probs, v_ref[:, pair])).astype(jnp.bfloat16)
        lse_ref[...] = jnp.where(lanes == g, top + jnp.log(total), lse_ref[...])

    lax.fori_loop(0, HEADS // 2, lambda g, carry: (heads(g), carry)[1], 0, unroll=2)
    o = o_ref[...]
    uo = matrix_multiply(o, a_o[...]).astype(jnp.bfloat16)
    uo_ref[...] = uo
    copies[3].wait()
    middle = (
        rows_ref[...]
        + matrix_multiply(o, wo[...])
        + bias(3 * width, width)
        + ADAPTER_SCALE * matrix_multiply(uo, b_o[...])
    )
    middle_ref[...] = middle
    h2 = layer_norm(middle, affine_ref[1:2, :], affine_ref[4:5, :]).astype(jnp.bfloat16)
    h2_ref[...] = h2
    uf = matrix_multiply(h2, a_fc[...]).astype(jnp.bfloat16)
    uf_ref[...] = uf
    copies[4].wait()
    for j in range(4):
        part = slice(j * quarter, (j + 1) * quarter)
        pre = (
            matrix_multiply(h2, win[:, part])
            + bias(4 * width + j * quarter, quarter)
            + ADAPTER_SCALE * matrix_multiply(uf, b_fc[:, part])
        )
        pre_ref[:, part] = pre
        f_ref[:, part] = (pre * gelu_parts(pre)[0]).astype(jnp.bfloat16)
    f = f_ref[...]
    up = matrix_multiply(f, a_p[...]).astype(jnp.bfloat16)
    up_ref[...] = up
    copies[5].wait()
    last = (
        middle
        + matrix_multiply(f, wout[...])
        + bias(4 * width + hidden, width)
        + ADAPTER_SCALE * matrix_multiply(up, b_p[...])
    )
    last_ref[...] = last
    final_ref[...] = layer_norm(last, affine_ref[2:3, :], affine_ref[5:6, :]).astype(jnp.bfloat16)


def pack_up(out_ref, part, grad):
    ranks = 3 * RANK if part < 2 else RANK
    wide = grad.shape[1] // 128
    for c in range(wide):
        rows = pl.ds(PARTS[part] + c, ranks, stride=wide)
        out_ref[rows, :] = grad[0:ranks, c * 128 : (c + 1) * 128]


def pack_down(out_ref, part, shift, grad):
    ranks = 3 * RANK if part < 2 else RANK
    slabs = ranks // RANK
    repeated = jnp.concatenate([grad[0:ranks]] * (128 * slabs // ranks), axis=0)
    for slab in range(slabs):
        spread = repeated[128 * slab : 128 * (slab + 1)].T
        spread = jnp.where(spread_places(ranks, slab), spread, 0.0)
        rows = pl.ds(PARTS[part] + shift + slab, 32, stride=slabs)
        out_ref[rows, :] = jnp.sum(spread.reshape(32, 32, 128), axis=1)


def layer_down(grad_ref, spot_ref, segment_ref, affine_ref, h1_ref,
               a_qkv, b_qkv, a_o, b_o, a_fc, b_fc, a_p, b_p,
               q_ref, k_ref, v_ref, u1_ref, u1_rows_ref, h1_rows_ref, lse_ref,
               o_ref, uo_ref, middle_ref, h2_ref, uf_ref, pre_ref, f_ref, up_ref, last_ref,
               o_hbm, in_hbm, out_hbm,
               grad_out,
               wo, win, wout, mask, dpre_ref, do_ref, dq_ref, dk_ref, dv_ref, sems):
    length, width = h1_ref.shape
    hidden = win.shape[1]
    quarter = hidden // 4
    rows_here = grad_ref.shape[0]
    copies = [
        pltpu.make_async_copy(out_hbm, wout, sems.at[0]),
        pltpu.make_async_copy(in_hbm, win, sems.at[1]),
        pltpu.make_async_copy(o_hbm, wo, sems.at[2]),
    ]
    for copy in copies:
        copy.start()
    mask[...] = attention_mask(spot_ref, segment_ref)
    spot_row = spot_ref[...].astype(jnp.float32)
    spot = lane_columns(spot_row)[:, 0:1]
    order_row = lax.broadcasted_iota(jnp.int32, (1, rows_here), 1)
    order = lax.broadcasted_iota(jnp.int32, (rows_here, 1), 0)
    same = spot == spot_row
    repeat = jnp.max(ones_where(same & (order_row < order)), axis=1, keepdims=True)
    merge = ones_where(same) * (1.0 - repeat)
    grad_final = jnp.dot(
        merge, grad_ref[...], precision=lax.Precision.HIGHEST,
        preferred_element_type=jnp.float32)
    dx3 = norm_back(last_ref[...], affine_ref[2:3, :], grad_final)
    dm = dx3.astype(jnp.bfloat16)
    pack_up(grad_out, 7, ADAPTER_SCALE * matrix_multiply_transposed_left(up_ref[...], dm))
    du_p = (ADAPTER_SCALE * matrix_multiply_transposed_right(dm, b_p[...])).astype(jnp.bfloat16)
    ga_p = matrix_multiply_transposed_left(du_p, f_ref[...])
    for b in range(hidden // 1024):
        pack_down(grad_out, 6, 32 * b, ga_p[:, 1024 * b : 1024 * (b + 1)])
    copies[0].wait()
    for j in range(4):
        part = slice(j * quarter, (j + 1) * quarter)
        df = matrix_multiply_transposed_right(dm, wout[part, :]) + matrix_multiply_transposed_right(
            du_p, a_p[part, :])
        dpre_ref[:, part] = (df * gelu_slope(pre_ref[:, part])).astype(jnp.bfloat16)
    dpre = dpre_ref[...]
    pack_up(grad_out, 5, ADAPTER_SCALE * matrix_multiply_transposed_left(uf_ref[...], dpre))
    du_f = (ADAPTER_SCALE * matrix_multiply_transposed_right(dpre, b_fc[...])).astype(jnp.bfloat16)
    pack_down(grad_out, 4, 0, matrix_multiply_transposed_left(du_f, h2_ref[...]))
    copies[1].wait()
    dh2 = matrix_multiply_transposed_right(dpre, win[...]) + matrix_multiply_transposed_right(
        du_f, a_fc[...])
    dx2 = dx3 + norm_back(middle_ref[...], affine_ref[1:2, :], dh2)
    da = dx2.astype(jnp.bfloat16)
    pack_up(grad_out, 3, ADAPTER_SCALE * matrix_multiply_transposed_left(uo_ref[...], da))
    du_o = (ADAPTER_SCALE * matrix_multiply_transposed_right(da, b_o[...])).astype(jnp.bfloat16)
    pack_down(grad_out, 2, 0, matrix_multiply_transposed_left(du_o, o_ref[...]))
    copies[2].wait()
    do_ref[...] = (
        matrix_multiply_transposed_right(da, wo[...])
        + matrix_multiply_transposed_right(du_o, a_o[...])
    ).astype(jnp.bfloat16)
    scale = (width // HEADS) ** (-0.5)
    lanes = lax.broadcasted_iota(jnp.int32, lse_ref.shape, 1)

    def heads(g):
        pair = pl.ds(pl.multiple_of(g * 128, 128), 128)
        q = both_heads(q_ref[:, pair])
        do = both_heads(do_ref[:, pair])
        lse = jnp.sum(jnp.where(lanes == g, lse_ref[...], 0.0), axis=1, keepdims=True)
        scores = scale * matrix_multiply_transposed_right(q, k_ref[:, pair])
        probs = jnp.where(mask[...] > 0.0, jnp.exp(jnp.minimum(scores - lse, 0.0)), 0.0)
        dp = matrix_multiply_transposed_right(do, v_ref[:, pair])
        ds = (probs * (dp - jnp.sum(probs * dp, axis=1, keepdims=True))).astype(jnp.bfloat16)
        dv_ref[:, pair] = matrix_multiply_transposed_left(
            probs.astype(jnp.bfloat16), do).astype(jnp.bfloat16)
        dk_ref[:, pair] = (scale * matrix_multiply_transposed_left(ds, q)).astype(jnp.bfloat16)
        dq_ref[:, pair] = side_by_side(scale * matrix_multiply(ds, k_ref[:, pair])).astype(
            jnp.bfloat16)

    lax.fori_loop(0, HEADS // 2, lambda g, carry: (heads(g), carry)[1], 0, unroll=2)
    b_all = b_qkv[...]
    gb = jnp.zeros((NARROW, width), jnp.float32)
    ids = lax.broadcasted_iota(jnp.int32, gb.shape, 0)
    dus = []
    for j, low, grad in ((0, u1_rows_ref, dq_ref), (1, u1_ref, dk_ref), (2, u1_ref, dv_ref)):
        mine = (ids >= j * RANK) & (ids < (j + 1) * RANK)
        gb = jnp.where(mine, ADAPTER_SCALE * matrix_multiply_transposed_left(
            low[...], grad[...]), gb)
        dus.append(ADAPTER_SCALE * matrix_multiply_transposed_right(grad[...], third_of(b_all, j)))
    pack_up(grad_out, 1, gb)
    ga = matrix_multiply_transposed_left(
        dus[0].astype(jnp.bfloat16), h1_rows_ref[...]
    ) + matrix_multiply_transposed_left((dus[1] + dus[2]).astype(jnp.bfloat16), h1_ref[...])
    pack_down(grad_out, 0, 0, ga)


def layer_kernels(rows_here, length, width, hidden):
    low, wide = jnp.bfloat16, jnp.float32
    whole = pl.BlockSpec(memory_space=pltpu.VMEM)
    away = pl.BlockSpec(memory_space=pl.ANY)
    dma = pltpu.SemaphoreType.DMA
    params = pltpu.CompilerParams(vmem_limit_bytes=60 << 20)
    kept = [
        ((rows_here, width), low),
        ((length, width), low),
        ((length, width), low),
        ((length, NARROW), low),
        ((rows_here, NARROW), low),
        ((rows_here, width), low),
        ((2 * rows_here, 128), wide),
        ((rows_here, width), low),
        ((rows_here, NARROW), low),
        ((rows_here, width), wide),
        ((rows_here, width), low),
        ((rows_here, NARROW), low),
        ((rows_here, hidden), wide),
        ((rows_here, hidden), low),
        ((rows_here, NARROW), low),
        ((rows_here, width), wide),
    ]
    up = pl.pallas_call(
        layer_up,
        out_shape=[jax.ShapeDtypeStruct(*k) for k in [((rows_here, width), low)] + kept],
        in_specs=[whole] * 14 + [away] * 4,
        out_specs=[whole] * 17,
        scratch_shapes=[pltpu.VMEM((width, width), low)] * 4
        + [
            pltpu.VMEM((width, hidden), low),
            pltpu.VMEM((hidden, width), low),
            pltpu.VMEM((2 * rows_here, length), wide),
            dma((6,)),
        ],
        compiler_params=params,
        name="layer_up",
    )
    down = pl.pallas_call(
        layer_down,
        out_shape=jax.ShapeDtypeStruct((PARTS[-1], 128), wide),
        in_specs=[whole] * 29 + [away] * 3,
        out_specs=whole,
        scratch_shapes=[
            pltpu.VMEM((width, width), low),
            pltpu.VMEM((width, hidden), low),
            pltpu.VMEM((hidden, width), low),
            pltpu.VMEM((2 * rows_here, length), wide),
            pltpu.VMEM((rows_here, hidden), low),
            pltpu.VMEM((rows_here, width), low),
            pltpu.VMEM((rows_here, width), low),
            pltpu.VMEM((length, width), low),
            pltpu.VMEM((length, width), low),
            dma((3,)),
        ],
        compiler_params=params,
        name="layer_down",
    )
    return up, down


def settle_step(held_ref, segment_ref, spot_ref, place_ref, affine_ref, h1_out, rows_out, place_cols):
    length = segment_ref.shape[1]
    span = place_ref.shape[0]
    segment = segment_ref[...].astype(jnp.float32)
    steps = lax.broadcasted_iota(jnp.int32, (1, length), 1).astype(jnp.float32)
    ids = lax.broadcasted_iota(jnp.int32, (32, length), 0).astype(jnp.float32)
    starts = jnp.sum(ones_where(segment < ids), axis=1, keepdims=True)
    place = steps - jnp.sum(jnp.where(segment == ids, starts, 0.0), axis=0, keepdims=True)
    place_cols[...] = lane_columns(place)
    spot = lane_columns(spot_ref[...].astype(jnp.float32))[:, 0:1]
    at_spot = steps == spot
    spot_place = jnp.sum(jnp.where(at_spot, place, 0.0), axis=1, keepdims=True)

    def placed(column):
        ids_here = lax.broadcasted_iota(jnp.int32, (column.shape[0], span), 1).astype(jnp.float32)
        return matrix_multiply(low_ones(ids_here == column), place_ref[...])

    rows_out[...] = matrix_multiply(low_ones(at_spot), held_ref[...]) + placed(spot_place)

    @pl.loop(0, length // 128)
    def _(a):
        rows = pl.ds(pl.multiple_of(a * 128, 128), 128)
        stream = held_ref[rows, :].astype(jnp.float32) + placed(place_cols[rows, 0:1])
        h1_out[rows, :] = layer_norm(stream, affine_ref[0:1, :], affine_ref[3:4, :]).astype(
            jnp.bfloat16)


def settle_rows(held, segments, spots, place_table, affine):
    length, width = held.shape
    whole = pl.BlockSpec(memory_space=pltpu.VMEM)
    return pl.pallas_call(
        settle_step,
        out_shape=[
            jax.ShapeDtypeStruct((length, width), jnp.bfloat16),
            jax.ShapeDtypeStruct((spots.shape[1], width), jnp.float32),
        ],
        in_specs=[whole] * 5,
        out_specs=[whole] * 2,
        scratch_shapes=[pltpu.VMEM((length, 128), jnp.float32)],
        compiler_params=pltpu.CompilerParams(vmem_limit_bytes=32 << 20),
        name="settle_step",
    )(held, segments, spots, place_table[:256], affine)


def visit_step(block, wanted_ref, held_ref, table_hbm, out_ref, table, columns, acc, sem):
    copy = pltpu.make_async_copy(table_hbm, table, sem)
    copy.start()
    columns[...] = lane_columns(wanted_ref[...].astype(jnp.float32))
    rows_here = table.shape[0]
    full = rows_here // block
    copy.wait()

    @pl.loop(0, held_ref.shape[0] // 256)
    def _(a):
        rows = pl.ds(pl.multiple_of(a * 256, 256), 256)
        acc[...] = held_ref[rows, :].astype(jnp.float32)

        def add(first, number):
            ids = lax.broadcasted_iota(jnp.int32, (256, number), 1) + first
            chosen = low_ones(ids.astype(jnp.float32) == columns[rows, 0:1])
            acc[...] += matrix_multiply(chosen, table[pl.ds(first, number), :])

        @pl.loop(0, full)
        def _(j):
            add(pl.multiple_of(j * block, block), block)

        add(full * block, rows_here - full * block)
        out_ref[rows, :] = acc[...].astype(jnp.bfloat16)


def visit_rows(wanted, held, table):
    length, width = held.shape
    whole = pl.BlockSpec(memory_space=pltpu.VMEM)
    return pl.pallas_call(
        partial(visit_step, 256),
        out_shape=jax.ShapeDtypeStruct((length, width), jnp.bfloat16),
        in_specs=[whole, whole, pl.BlockSpec(memory_space=pl.ANY)],
        out_specs=whole,
        scratch_shapes=[
            pltpu.VMEM(table.shape, jnp.bfloat16),
            pltpu.VMEM((length, 128), jnp.float32),
            pltpu.VMEM((256, width), jnp.float32),
            pltpu.SemaphoreType.DMA,
        ],
        compiler_params=pltpu.CompilerParams(vmem_limit_bytes=40 << 20),
        name="visit_step",
    )(wanted, held, table)


def local(
    mesh_sizes,
    packed_symbol_codes,
    article_numbering,
    target_spots,
    answer_flags,
    shared_embedding,
    spot_embedding,
    combined_qkv_weights,
    attend_outgoing_weights,
    dense_incoming_weights,
    dense_outgoing_weights,
    layernorm_affine,
    bias_terms,
    adaptor_float_copies,
    average_moments,
    squared_moments,
):
    rows_here = target_spots.shape[1]
    shard_rows = shared_embedding.shape[0]
    table = jnp.pad(shared_embedding, ((0, -shard_rows % 16), (0, 0)))
    fast_h1, fast_rows, labels, counts, crowded, *factors = embed(
        mesh_sizes,
        shard_rows,
        packed_symbol_codes,
        article_numbering,
        target_spots,
        answer_flags,
        spot_embedding,
        layernorm_affine,
        adaptor_float_copies,
        table,
    )

    sharers = mesh_sizes[1]
    ring = [(j, (j + 1) % sharers) for j in range(sharers)]

    def visit(carry):
        turns, tokens, held = carry
        wanted = tokens - lax.axis_index("vocab") * shard_rows
        wanted = jnp.where((wanted >= 0) & (wanted < shard_rows), wanted, -1)
        kept = jnp.where(turns == sharers, jnp.zeros((), jnp.bfloat16), held)
        held = visit_rows(wanted, kept, table)
        return turns - 1, lax.ppermute(tokens, "vocab", ring), lax.ppermute(held, "vocab", ring)

    def settle(carry):
        _, held, _ = carry
        settled, rows = settle_rows(
            held, article_numbering, target_spots, spot_embedding, layernorm_affine
        )
        return jnp.zeros((), jnp.int32), settled, rows

    overflow = crowded.reshape(())
    _, _, held = lax.while_loop(
        lambda carry: carry[0] > 0, visit, (overflow * sharers, packed_symbol_codes, fast_h1)
    )
    _, h1, stream_rows = lax.while_loop(
        lambda carry: carry[0] > 0, settle, (overflow, held, fast_rows)
    )
    length, width = h1.shape
    hidden = dense_incoming_weights.shape[1]
    layer_up_call, layer_down_call = layer_kernels(rows_here, length, width, hidden)
    final_rows, *kept = layer_up_call(
        h1,
        stream_rows,
        article_numbering,
        target_spots,
        layernorm_affine,
        bias_terms[None, :],
        *factors,
        combined_qkv_weights,
        attend_outgoing_weights,
        dense_incoming_weights,
        dense_outgoing_weights,
    )
    grad_rows, loss_part = head(
        mesh_sizes, shard_rows, final_rows, labels, counts, table
    )
    local_grad = layer_down_call(
        grad_rows,
        target_spots,
        article_numbering,
        layernorm_affine,
        h1,
        *factors,
        *kept,
        attend_outgoing_weights,
        dense_incoming_weights,
        dense_outgoing_weights,
    )
    (
        refreshed_thin_pairs,
        updated_first_moment,
        updated_second_moment,
        gradient_global_norm,
        smoothed_entropy_cost,
    ) = reduce_and_update(
        mesh_sizes, local_grad, adaptor_float_copies, average_moments, squared_moments, loss_part
    )
    return (
        refreshed_thin_pairs,
        updated_first_moment,
        updated_second_moment,
        gradient_global_norm,
        smoothed_entropy_cost,
    )


def solution(mesh):
    return jax.shard_map(
        partial(local, (mesh.shape["dp"], mesh.shape["vocab"])),
        mesh=mesh,
        in_specs=(
            P(("dp", "vocab"), None),
            P(("dp", "vocab"), None),
            P(("dp", "vocab"), None),
            P(("dp", "vocab"), None),
            P("vocab", None),
            P(),
            P(),
            P(),
            P(),
            P(),
            P(),
            P(),
            P(),
            P(),
            P(),
        ),
        out_specs=(P(), P(), P(), P(), P()),
        check_vma=False,
    )
```

```python
from functools import partial
import math

import jax
import jax.numpy as jnp
from jax import lax
from jax.experimental import pallas as pl
from jax.experimental.pallas import tpu as pltpu
from jax.sharding import PartitionSpec as P

MODEL_WIDTH = 1024
HEADS = 16
FEEDFWD_UNITS = 4096
VOCAB_SIZE = 50257
RANK = 4
STEP = 10


ADAPTER_SCALE = 8.0
NORM_EPS = 1e-05
GRAD_CLIP = 0.0001
STRIDE_LENGTH = 0.02
BETA_ONE = 0.9
BETA_TWO = 0.999
SHRINK_PENALTY = 0.01
STABILITY_FLOOR = 1e-08
MASKED = -1e30
MESH = pl.DeviceIdType.MESH


def matrix_multiply(left, right):
    return jnp.dot(left, right, preferred_element_type=jnp.float32)


def matrix_multiply_transposed_left(left, right):
    return lax.dot_general(
        left, right, (((0,), (0,)), ((), ())), preferred_element_type=jnp.float32
    )


def matrix_multiply_transposed_right(left, right):
    return lax.dot_general(
        left, right, (((1,), (1,)), ((), ())), preferred_element_type=jnp.float32
    )


def layer_norm(stream, gain, shift):
    centred = stream - jnp.mean(stream, axis=-1, keepdims=True)
    spread = lax.rsqrt(jnp.mean(centred * centred, axis=-1, keepdims=True) + NORM_EPS)
    return centred * spread * gain + shift


def adaptive_moment_update(grad, weight, first, second):
    first_new = BETA_ONE * first + (1.0 - BETA_ONE) * grad
    second_new = BETA_TWO * second + (1.0 - BETA_TWO) * grad * grad
    debiased_mean_estimate = first_new / (1.0 - BETA_ONE**STEP)
    debiased_variance_estimate = second_new / (1.0 - BETA_TWO**STEP)
    weight_new = weight - STRIDE_LENGTH * (
        debiased_mean_estimate / (jnp.sqrt(debiased_variance_estimate) + STABILITY_FLOOR)
        + SHRINK_PENALTY * weight
    )
    return (weight_new, first_new, second_new)


def sum_and_step(dp_size, vocab_size, grad_ref, weight_ref, first_ref, second_ref, loss_ref,
                 weight_out, first_out, second_out, norm_out, loss_out,
                 parts, planes, total, losses, send_a, recv_a, send_b, recv_b, send_c, recv_c,
                 send_d, recv_d):
    my_plane = lax.axis_index("dp")
    me = lax.axis_index("vocab")

    def across(j):
        return (my_plane, lax.rem(me + j, vocab_size))

    def along(i):
        return (lax.rem(my_plane + i, dp_size), me)

    barrier = pltpu.get_barrier_semaphore()

    @pl.loop(1, vocab_size)
    def _(j):
        pl.semaphore_signal(barrier, inc=1, device_id=across(j), device_id_type=MESH)

    @pl.loop(1, dp_size)
    def _(i):
        pl.semaphore_signal(barrier, inc=1, device_id=along(i), device_id_type=MESH)

    pl.semaphore_wait(barrier, vocab_size + dp_size - 2)

    def part_copy(j):
        peer = across(j)
        return pltpu.make_async_remote_copy(
            src_ref=grad_ref.at[peer[1]], dst_ref=parts.at[me],
            send_sem=send_a.at[peer[1]], recv_sem=recv_a.at[me],
            device_id=peer, device_id_type=MESH)

    def part_arrival(j):
        peer = across(j)
        return pltpu.make_async_remote_copy(
            src_ref=grad_ref.at[peer[1]], dst_ref=parts.at[peer[1]],
            send_sem=send_a.at[peer[1]], recv_sem=recv_a.at[peer[1]],
            device_id=peer, device_id_type=MESH)

    def plane_copy(i):
        peer = along(i)
        return pltpu.make_async_remote_copy(
            src_ref=planes.at[my_plane], dst_ref=planes.at[my_plane],
            send_sem=send_b.at[peer[0]], recv_sem=recv_b.at[my_plane],
            device_id=peer, device_id_type=MESH)

    def plane_arrival(i):
        peer = along(i)
        return pltpu.make_async_remote_copy(
            src_ref=planes.at[my_plane], dst_ref=planes.at[peer[0]],
            send_sem=send_b.at[peer[0]], recv_sem=recv_b.at[peer[0]],
            device_id=peer, device_id_type=MESH)

    def loss_copy(i):
        peer = along(i)
        return pltpu.make_async_remote_copy(
            src_ref=loss_ref, dst_ref=losses.at[my_plane],
            send_sem=send_d.at[peer[0]], recv_sem=recv_d.at[my_plane],
            device_id=peer, device_id_type=MESH)

    def loss_arrival(i):
        peer = along(i)
        return pltpu.make_async_remote_copy(
            src_ref=loss_ref, dst_ref=losses.at[peer[0]],
            send_sem=send_d.at[peer[0]], recv_sem=recv_d.at[peer[0]],
            device_id=peer, device_id_type=MESH)

    def total_copy(j):
        peer = across(j)
        return pltpu.make_async_remote_copy(
            src_ref=total.at[me], dst_ref=total.at[me],
            send_sem=send_c.at[peer[1]], recv_sem=recv_c.at[me],
            device_id=peer, device_id_type=MESH)

    def total_arrival(j):
        peer = across(j)
        return pltpu.make_async_remote_copy(
            src_ref=total.at[me], dst_ref=total.at[peer[1]],
            send_sem=send_c.at[peer[1]], recv_sem=recv_c.at[peer[1]],
            device_id=peer, device_id_type=MESH)

    @pl.loop(1, vocab_size)
    def _(j):
        part_copy(j).start()

    @pl.loop(1, dp_size)
    def _(i):
        loss_copy(i).start()

    losses[my_plane] = loss_ref[...]
    parts[me] = grad_ref[me]

    @pl.loop(1, vocab_size)
    def _(j):
        part_arrival(j).wait_recv()

    planes[my_plane] = lax.fori_loop(
        1, vocab_size, lambda j, held: held + parts[j], parts[0])

    @pl.loop(1, dp_size)
    def _(i):
        plane_copy(i).start()

    @pl.loop(1, dp_size)
    def _(i):
        plane_arrival(i).wait_recv()

    total[me] = lax.fori_loop(1, dp_size, lambda i, held: held + planes[i], planes[0])

    @pl.loop(1, vocab_size)
    def _(j):
        total_copy(j).start()

    @pl.loop(1, vocab_size)
    def _(j):
        part_copy(j).wait_send()

    @pl.loop(1, dp_size)
    def _(i):
        plane_copy(i).wait_send()

    @pl.loop(1, vocab_size)
    def _(j):
        total_arrival(j).wait_recv()

    @pl.loop(1, vocab_size)
    def _(j):
        total_copy(j).wait_send()

    def squares(j, held):
        piece = total[j]
        return held + piece * piece

    gathered = lax.fori_loop(0, vocab_size, squares, jnp.zeros(parts.shape[1:], jnp.float32))
    norm = jnp.sqrt(jnp.sum(gathered, keepdims=True))
    norm_out[...] = norm

    @pl.loop(1, dp_size)
    def _(i):
        loss_arrival(i).wait_recv()
        loss_copy(i).wait_send()

    loss_out[...] = jnp.sum(losses[...], axis=0)[0:1, 0:1]
    shrink = GRAD_CLIP / jnp.maximum(norm, GRAD_CLIP)

    @pl.loop(0, vocab_size)
    def _(j):
        weight, first, second = adaptive_moment_update(
            total[j] * shrink, weight_ref[j], first_ref[j], second_ref[j])
        weight_out[j] = weight
        first_out[j] = first
        second_out[j] = second


def reduce_and_update(mesh_sizes, local_grad, weights, first, second, loss):
    dp_size, vocab_size = mesh_sizes
    number = local_grad.size
    rows = number // (128 * vocab_size)
    shape = (vocab_size, rows, 128)
    block = pltpu.VMEM(shape, jnp.float32)
    whole = pl.BlockSpec(memory_space=pltpu.VMEM)
    weight_new, first_new, second_new, norm, total_loss = pl.pallas_call(
        partial(sum_and_step, dp_size, vocab_size),
        out_shape=[jax.ShapeDtypeStruct(shape, jnp.float32)] * 3
        + [jax.ShapeDtypeStruct((1, 1), jnp.float32)] * 2,
        in_specs=[whole] * 5,
        out_specs=[whole] * 5,
        scratch_shapes=[
            block,
            pltpu.VMEM((dp_size, rows, 128), jnp.float32),
            block,
            pltpu.VMEM((dp_size, 8, 128), jnp.float32),
            pltpu.SemaphoreType.DMA((vocab_size,)),
            pltpu.SemaphoreType.DMA((vocab_size,)),
            pltpu.SemaphoreType.DMA((dp_size,)),
            pltpu.SemaphoreType.DMA((dp_size,)),
            pltpu.SemaphoreType.DMA((vocab_size,)),
            pltpu.SemaphoreType.DMA((vocab_size,)),
            pltpu.SemaphoreType.DMA((dp_size,)),
            pltpu.SemaphoreType.DMA((dp_size,)),
        ],
        compiler_params=pltpu.CompilerParams(
            collective_id=5, has_side_effects=True, vmem_limit_bytes=24 << 20
        ),
        name="sum_and_step",
    )(*[piece.reshape(shape) for piece in (local_grad, weights, first, second)], loss)
    flat = [piece.reshape(-1) for piece in (weight_new, first_new, second_new)]
    return (*flat, norm.reshape(()), total_loss.reshape(()))


TILE = 32


def head_step(dp_size, vocab_size, block, owned, hf_ref, label_ref, count_ref, table_hbm, grad_out, loss_out,
              table, hf_all, label_all, exps, exps_rest, tops, run_top, run_sum, run_smooth,
              run_goal, offset, z_even, z_odd, z_rest, dz_even, dz_odd, rest_even, rest_odd,
              acc_even, acc_odd, lse_tile, share_tile, stats_all,
              from_core, from_chip, leaving,
              table_sem, label_send, label_recv, hf_send, hf_recv,
              stat_send, stat_recv, core_send, core_recv, chip_send, chip_recv):
    plane = lax.axis_index("dp")
    me = lax.axis_index("vocab")
    chips = vocab_size // 2
    chip = me // 2
    core = lax.rem(me, 2)
    other = 2 * chip + 1 - core
    sibling = (plane, other)
    held = table_hbm.shape[0]
    full = held // block
    rest = held - full * block
    padded = table.shape[0] - full * block
    base = me * owned
    rows_each = hf_ref.shape[0]
    pair = 2 * rows_each
    width = hf_ref.shape[1]

    def partner(k):
        out = 0
        bit = 1
        while bit < chips:
            out = out + lax.rem(chip // bit + lax.rem(k // bit, 2), 2) * bit
            bit *= 2
        return out

    def across(j):
        return (plane, lax.rem(me + j, vocab_size))

    def table_copy(j, number):
        rows = pl.ds(pl.multiple_of(j * block, 16), number)
        return pltpu.make_async_copy(table_hbm.at[rows], table.at[rows], table_sem.at[j])

    @pl.loop(0, full)
    def _(j):
        table_copy(j, block).start()

    table_copy(full, rest).start()

    table[held:, :] = jnp.zeros((padded - rest, width), jnp.bfloat16)
    barrier = pltpu.get_barrier_semaphore()

    @pl.loop(1, vocab_size)
    def _(j):
        pl.semaphore_signal(barrier, inc=1, device_id=across(j), device_id_type=MESH)

    pl.semaphore_wait(barrier, vocab_size - 1)

    def remote(src, dst, send, recv, peer):
        return pltpu.make_async_remote_copy(
            src_ref=src, dst_ref=dst, send_sem=send, recv_sem=recv,
            device_id=peer, device_id_type=MESH)

    def hf_to_sibling():
        return remote(hf_ref, hf_all.at[me], hf_send.at[0], hf_recv.at[me], sibling)

    def hf_copy(k):
        return remote(hf_ref, hf_all.at[me], hf_send.at[k], hf_recv.at[me],
                      (plane, 2 * partner(k) + core))

    def hf_arrival(source):
        return remote(hf_ref, hf_all.at[source], hf_send.at[0], hf_recv.at[source], sibling)

    def hf_forward(k):
        source = 2 * partner(k) + core
        return remote(hf_all.at[source], hf_all.at[source], hf_send.at[chips + k],
                      hf_recv.at[source], sibling)

    def label_copy(j):
        peer = across(j)
        return remote(label_ref, label_all.at[me], label_send.at[peer[1]], label_recv.at[me], peer)

    def label_arrival(source):
        return remote(label_ref, label_all.at[source], label_send.at[source],
                      label_recv.at[source], sibling)

    near = min(3, chips)
    hf_to_sibling().start()

    @pl.loop(1, near)
    def _(k):
        hf_copy(k).start()

    @pl.loop(1, vocab_size)
    def _(j):
        label_copy(j).start()

    hf_all[me] = hf_ref[...]
    label_all[me] = label_ref[...]
    lanes = lax.broadcasted_iota(jnp.int32, (pair, 128), 1)

    def label_row(c, i):
        rows = label_all[pl.ds(2 * c, 2), i : i + 1, :].astype(jnp.float32)
        return jnp.concatenate([rows[0], rows[1]], axis=1)

    def set_offset(c):
        offset[...] = lane_columns(label_row(c, 0)).astype(jnp.int32) - base - lanes

    def folded(x):
        return sum(x[:, i * 128 : (i + 1) * 128] for i in range(1, x.shape[1] // 128)) + x[:, :128]

    def chunk_up(k, first):
        c = partner(k)
        if first:
            hf_arrival(other).wait_recv()
            label_arrival(other).wait_recv()
        else:
            hf_arrival(2 * c + core).wait_recv()
            hf_forward(k).start()
            label_arrival(2 * c).wait_recv()
            label_arrival(2 * c + 1).wait_recv()
            hf_arrival(2 * c + 1 - core).wait_recv()
        set_offset(c)
        run_top[...] = jnp.full((pair, 128), MASKED, jnp.float32)
        for ref in (run_sum, run_smooth, run_goal):
            ref[...] = jnp.zeros((pair, 128), jnp.float32)
        start = pl.multiple_of(k * pair, pair)

        def multiply(j, z_ref):
            if first:
                table_copy(j, rest if z_ref is z_rest else block).wait()
            rows = pl.ds(pl.multiple_of(j * block, 16), z_ref.shape[1])
            hidden = hf_all[pl.ds(2 * c, 2)].reshape(pair, width)
            z_ref[...] = matrix_multiply_transposed_right(hidden, table[rows, :])

        def reduce_full(j, z_ref):
            for r in range(pair // TILE):
                rows = slice(r * TILE, (r + 1) * TILE)
                there = pl.ds(start + r * TILE, TILE)
                z = z_ref[rows, :]
                old = run_top[rows, :]
                top = jnp.maximum(old, jnp.max(z, axis=1, keepdims=True))
                run_top[rows, :] = top
                tops[k, j, rows, :] = top
                gap = offset[rows, :] - j * block
                total = jnp.zeros((TILE, 128), jnp.float32)
                smooth = jnp.zeros((TILE, 128), jnp.float32)
                goal = jnp.zeros((TILE, 128), jnp.float32)
                for i in range(block // 128):
                    part = slice(i * 128, (i + 1) * 128)
                    piece = z[:, part]
                    e = jnp.exp(piece - top)
                    exps[j, there, part] = e
                    total = total + e
                    smooth = smooth + piece
                    goal = goal + jnp.where(gap == i * 128, piece, 0.0)
                run_sum[rows, :] = run_sum[rows, :] * jnp.exp(old - top) + total
                run_smooth[rows, :] = run_smooth[rows, :] + smooth
                run_goal[rows, :] = run_goal[rows, :] + goal

        def reduce_rest():
            for r in range(pair // TILE):
                rows = slice(r * TILE, (r + 1) * TILE)
                there = pl.ds(start + r * TILE, TILE)
                spot = lanes[rows, :]
                limit = jnp.minimum(VOCAB_SIZE - base, owned) - full * block - spot
                gap = offset[rows, :] - full * block
                pieces = []
                for i in range(padded // 128):
                    piece = z_rest[rows, i * 128 : (i + 1) * 128]
                    pieces.append((i * 128 < limit, piece))
                highest = jnp.where(pieces[0][0], pieces[0][1], MASKED)
                for valid, piece in pieces[1:]:
                    highest = jnp.maximum(highest, jnp.where(valid, piece, MASKED))
                old = run_top[rows, :]
                top = jnp.maximum(old, jnp.max(highest, axis=1, keepdims=True))
                run_top[rows, :] = top
                tops[k, full, rows, :] = top
                total = jnp.zeros((TILE, 128), jnp.float32)
                smooth = jnp.zeros((TILE, 128), jnp.float32)
                goal = jnp.zeros((TILE, 128), jnp.float32)
                for i, (valid, piece) in enumerate(pieces):
                    e = jnp.where(valid, jnp.exp(piece - top), 0.0)
                    exps_rest[there, i * 128 : (i + 1) * 128] = e
                    total = total + e
                    smooth = smooth + jnp.where(valid, piece, 0.0)
                    goal = goal + jnp.where(valid & (gap == i * 128), piece, 0.0)
                run_sum[rows, :] = run_sum[rows, :] * jnp.exp(old - top) + total
                run_smooth[rows, :] = run_smooth[rows, :] + smooth
                run_goal[rows, :] = run_goal[rows, :] + goal

        multiply(0, z_even)
        turns = (full - 1) // 2

        if turns > 0:
            @pl.loop(0, turns)
            def _(t):
                multiply(2 * t + 1, z_odd)
                reduce_full(2 * t, z_even)
                multiply(2 * t + 2, z_even)
                reduce_full(2 * t + 1, z_odd)

        if full - 2 * turns == 2:
            multiply(full - 1, z_odd)
            reduce_full(full - 2, z_even)
            multiply(full, z_rest)
            reduce_full(full - 1, z_odd)
        else:
            multiply(full, z_rest)
            reduce_full(full - 1, z_even)
        reduce_rest()

        def row_sum(ref):
            return jnp.sum(ref[...].T, axis=0, keepdims=True)

        ids = lax.broadcasted_iota(jnp.int32, (8, pair), 0)
        packed = jnp.where(ids == 0, run_top[...].T[0:1, :], 0.0)
        for i, ref in enumerate((run_sum, run_smooth, run_goal)):
            packed = jnp.where(ids == i + 1, row_sum(ref), packed)
        stats_all[me, c] = packed

    chunk_up(0, True)

    @pl.loop(near, chips)
    def _(k):
        hf_copy(k).start()

    @pl.loop(1, chips)
    def _(k):
        chunk_up(k, False)

    def stat_copy(j):
        peer = across(j)
        return remote(stats_all.at[me], stats_all.at[me], stat_send.at[peer[1]],
                      stat_recv.at[me], peer)

    def stat_arrival(j):
        source = across(j)[1]
        return remote(stats_all.at[me], stats_all.at[source], stat_send.at[source],
                      stat_recv.at[source], across(j))

    @pl.loop(1, vocab_size)
    def _(j):
        stat_copy(j).start()

    @pl.loop(1, vocab_size)
    def _(j):
        stat_arrival(j).wait_recv()

    count = jnp.maximum(count_ref[1:2, 0:1], 1.0)

    def totals_of(c):
        here = stats_all[:, c]
        tops_here = here[:, 0:1, :]
        top = jnp.max(tops_here, axis=0)
        total = jnp.sum(here[:, 1:2, :] * jnp.exp(tops_here - top[None]), axis=0)
        return top + jnp.log(total), jnp.sum(here[:, 2:3, :], axis=0), jnp.sum(
            here[:, 3:4, :], axis=0)

    def chunk_loss(c, held_loss):
        lse, smooth, goal = totals_of(c)
        return held_loss + label_row(c, 1) * (lse - 0.9 * goal - 0.1 * smooth / VOCAB_SIZE)

    slots = from_core.shape[0]
    columns_each = width // 4

    def core_copy(k, n, acc):
        half = pl.ds(pl.multiple_of((1 - core) * rows_each, rows_each), rows_each)
        part = pl.ds(pl.multiple_of(n * columns_each, columns_each), columns_each)
        return remote(acc.at[half, part], from_core.at[lax.rem(k, slots), :, part],
                      core_send.at[k, n], core_recv.at[k, n], sibling)

    def chip_copy(k, n):
        part = pl.ds(pl.multiple_of(n * columns_each, columns_each), columns_each)
        return remote(leaving.at[k - 1, :, part], from_chip.at[k - 1, :, part],
                      chip_send.at[k, n], chip_recv.at[k, n], (plane, 2 * partner(k) + core))

    def prepare(k):
        c = partner(k)
        lse, _, _ = totals_of(c)
        lse_tile[...] = lane_columns(lse)
        share_tile[...] = lane_columns(label_row(c, 1) / count)
        set_offset(c)

    quarter = pair // 4

    def grads(k, n, dz_ref, rest_ref):
        for r in range(quarter // TILE):
            first = pl.multiple_of(n * quarter + r * TILE, TILE)
            rows = pl.ds(first, TILE)
            there = pl.ds(pl.multiple_of(k * pair + first, TILE), TILE)
            share = share_tile[rows, :]
            lse = lse_tile[rows, :]
            low = share * (0.1 / VOCAB_SIZE)
            high = low + 0.9 * share
            gap = offset[rows, :]
            for j in range(full):
                factor = share * jnp.exp(tops[k, j, rows, :] - lse)
                for i in range(block // 128):
                    at = j * block + i * 128
                    e = exps[j, there, i * 128 : (i + 1) * 128]
                    dz = e * factor - jnp.where(gap == at, high, low)
                    dz_ref[rows, at : at + 128] = dz.astype(jnp.bfloat16)
            factor = share * jnp.exp(tops[k, full, rows, :] - lse)
            limit = jnp.minimum(VOCAB_SIZE - base, owned) - full * block - lanes[0:TILE, :]
            for i in range(padded // 128):
                part = slice(i * 128, (i + 1) * 128)
                at = full * block + i * 128
                dz = exps_rest[there, part] * factor - jnp.where(gap == at, high, low)
                rest_ref[rows, part] = jnp.where(i * 128 < limit, dz, 0.0).astype(jnp.bfloat16)

    def gather(k, n, dz_ref, rest_ref, acc):
        part = pl.ds(pl.multiple_of(n * columns_each, columns_each), columns_each)
        acc[:, part] = matrix_multiply(
            dz_ref[...], table[pl.ds(0, full * block), part]
        ) + matrix_multiply(rest_ref[...], table[pl.ds(full * block, padded), part])

    def finish(k, n, acc):
        core_copy(k, n, acc).wait()
        own = pl.ds(pl.multiple_of(core * rows_each, rows_each), rows_each)
        part = pl.ds(pl.multiple_of(n * columns_each, columns_each), columns_each)
        return from_core[lax.rem(k, slots), :, part] + acc[own, part]

    def ship(k, n, acc):
        part = pl.ds(pl.multiple_of(n * columns_each, columns_each), columns_each)
        leaving[k - 1, :, part] = finish(k, n, acc).astype(jnp.bfloat16)
        chip_copy(k, n).start()

    def stage(k, now, later, acc, acc_before):
        if later is not None:
            prepare(k - 1)

        @pl.loop(0, 4)
        def _(n):
            gather(k, n, *now, acc)
            if later is not None:
                grads(k - 1, n, *later)
            core_copy(k, n, acc).start()
            if later is not None:
                @pl.when(n > 0)
                def _():
                    ship(k, n - 1, acc)

            if acc_before is not None:
                @pl.when((n == 0) & (k < chips - 1))
                def _():
                    ship(k + 1, 3, acc_before)

    evens = ((dz_even, rest_even), acc_even)
    odds = ((dz_odd, rest_odd), acc_odd)
    prepare(chips - 1)

    @pl.loop(0, 4)
    def _(n):
        grads(chips - 1, n, *odds[0])

    @pl.loop(0, chips // 2 - 1)
    def _(t):
        k = chips - 1 - 2 * t
        stage(k, odds[0], evens[0], acc_odd, acc_even)
        stage(k - 1, evens[0], odds[0], acc_even, acc_odd)

    stage(1, odds[0], evens[0], acc_odd, acc_even if chips > 2 else None)
    stage(0, evens[0], None, acc_even, acc_odd)

    loss = lax.fori_loop(0, chips, chunk_loss, jnp.zeros((1, pair), jnp.float32))
    loss_out[...] = jnp.broadcast_to(jnp.sum(loss, keepdims=True) / count, loss_out.shape)
    for n in range(4):
        grad_out[:, n * columns_each : (n + 1) * columns_each] = finish(0, n, acc_even)

    @pl.loop(1, chips)
    def _(t):
        k = chips - t
        for n in range(4):
            chip_copy(k, n).wait_recv()
        grad_out[...] += from_chip[k - 1].astype(jnp.float32)

    hf_to_sibling().wait_send()

    @pl.loop(1, chips)
    def _(k):
        hf_copy(k).wait_send()
        hf_forward(k).wait_send()
        for n in range(4):
            chip_copy(k, n).wait_send()

    @pl.loop(1, vocab_size)
    def _(j):
        label_copy(j).wait_send()
        stat_copy(j).wait_send()


def head(mesh_sizes, owned, final_rows, labels, counts, table):
    dp_size, vocab_size = mesh_sizes
    rows, width = final_rows.shape
    held = table.shape[0]
    block = 1024
    full = held // block
    rest = -(-(held - full * block) // 128) * 128
    chips = vocab_size // 2
    pair = 2 * rows
    low, wide = jnp.bfloat16, jnp.float32
    whole = pl.BlockSpec(memory_space=pltpu.VMEM)
    dma = pltpu.SemaphoreType.DMA
    tile = pltpu.VMEM((pair, 128), wide)
    grad, loss = pl.pallas_call(
        partial(head_step, dp_size, vocab_size, block, owned),
        out_shape=[
            jax.ShapeDtypeStruct((rows, width), wide),
            jax.ShapeDtypeStruct((8, 128), wide),
        ],
        in_specs=[whole, whole, whole, pl.BlockSpec(memory_space=pl.ANY)],
        out_specs=[whole, whole],
        scratch_shapes=[
            pltpu.VMEM((full * block + rest, width), low),
            pltpu.VMEM((vocab_size, rows, width), low),
            pltpu.VMEM((vocab_size, 8, rows), jnp.int32),
            pltpu.VMEM((full, vocab_size * rows, block), wide),
            pltpu.VMEM((vocab_size * rows, rest), wide),
            pltpu.VMEM((chips, full + 1, pair, 128), wide),
            tile,
            tile,
            tile,
            tile,
            pltpu.VMEM((pair, 128), jnp.int32),
            pltpu.VMEM((pair, block), wide),
            pltpu.VMEM((pair, block), wide),
            pltpu.VMEM((pair, rest), wide),
            pltpu.VMEM((pair, full * block), low),
            pltpu.VMEM((pair, full * block), low),
            pltpu.VMEM((pair, rest), low),
            pltpu.VMEM((pair, rest), low),
            pltpu.VMEM((pair, width), wide),
            pltpu.VMEM((pair, width), wide),
            tile,
            tile,
            pltpu.VMEM((vocab_size, chips, 8, pair), wide),
            pltpu.VMEM((3, rows, width), wide),
            pltpu.VMEM((chips - 1, rows, width), low),
            pltpu.VMEM((chips - 1, rows, width), low),
            dma((full + 1,)),
            dma((vocab_size,)),
            dma((vocab_size,)),
            dma((2 * chips,)),
            dma((vocab_size,)),
            dma((vocab_size,)),
            dma((vocab_size,)),
            dma((chips, 4)),
            dma((chips, 4)),
            dma((chips, 4)),
            dma((chips, 4)),
        ],
        compiler_params=pltpu.CompilerParams(
            collective_id=3, has_side_effects=True, vmem_limit_bytes=63 << 20
        ),
        name="head_step",
    )(final_rows, labels, counts, table)
    return grad, loss


NARROW = 16
PARTS = (0, 96, 192, 224, 256, 288, 416, 544, 576)


def floor_part(values, size):
    return jnp.floor((values + 0.5) * (1.0 / size))


def spread_places(ranks, slab):
    lanes = lax.broadcasted_iota(jnp.int32, (1024, 128), 1).astype(jnp.float32) + 128.0 * slab
    rows = lax.broadcasted_iota(jnp.int32, (1024, 128), 0).astype(jnp.float32)
    return floor_part(lanes, ranks) == rows - 32.0 * floor_part(rows, 32)


def unpack_down(flat_ref, first, ranks, out_ref, start):
    slabs = ranks // RANK
    total = None
    for slab in range(slabs):
        packed = flat_ref[pl.ds(first + slab, 32, stride=slabs), :]
        spread = jnp.broadcast_to(packed[:, None, :], (32, 32, 128)).reshape(1024, 128)
        spread = jnp.where(spread_places(ranks, slab), spread, 0.0).astype(jnp.bfloat16)
        lanes = lax.broadcasted_iota(jnp.int32, (128, NARROW), 0).astype(jnp.float32) + 128.0 * slab
        column = lax.broadcasted_iota(jnp.int32, (128, NARROW), 1).astype(jnp.float32)
        chosen = low_ones(lanes - ranks * floor_part(lanes, ranks) == column)
        part = matrix_multiply(spread, chosen)
        total = part if total is None else total + part
    out_ref[pl.ds(start, 1024), :] = total.astype(jnp.bfloat16)


def unpack_up(flat_ref, first, ranks, out_ref):
    wide = out_ref.shape[1] // 128
    for c in range(wide):
        if wide == 8 and ranks == RANK:
            rows = jnp.concatenate(
                [flat_ref[first + wide * r + c : first + wide * r + c + 1, :] for r in range(ranks)],
                axis=0)
        else:
            rows = flat_ref[pl.ds(first + c, ranks, stride=wide), :]
        rows = jnp.concatenate([rows, jnp.zeros((NARROW - ranks, 128), jnp.float32)], axis=0)
        out_ref[:, c * 128 : (c + 1) * 128] = rows.astype(jnp.bfloat16)


def unpack(flat_ref, outs):
    for i, out_ref in enumerate(outs):
        ranks = 3 * RANK if i < 2 else RANK
        if i % 2:
            unpack_up(flat_ref, PARTS[i], ranks, out_ref)
        else:
            for b in range(out_ref.shape[0] // 1024):
                unpack_down(flat_ref, PARTS[i] + 32 * b, ranks, out_ref, 1024 * b)


def lane_columns(row):
    return jnp.broadcast_to(row, (128, row.shape[1])).T


def ones_where(condition):
    return jnp.where(condition, 1.0, 0.0)


def low_ones(condition):
    return ones_where(condition).astype(jnp.bfloat16)


def embed_step(dp_size, vocab_size, block, room, owned, token_ref, segment_ref, spot_ref, flag_ref,
               place_hbm, affine_ref, flat_ref, table_hbm,
               h1_out, rows_out, label_out, full_out, crowd_out,
               a_qkv, b_qkv, a_o, b_o, a_fc, b_fc, a_p, b_p,
               table, place_table, key_cols, unique_cols, slot_cols, owners, asked, lists, lists_in,
               acc, leaving, arriving, stream, full_all,
               table_sem, place_sem, list_send, list_recv, row_send, row_recv, full_send, full_recv):
    plane = lax.axis_index("dp")
    me = lax.axis_index("vocab")
    chips = vocab_size // 2
    chip = me // 2
    held = table.shape[0]
    full = held // block
    rest = held - full * block
    length = token_ref.shape[1]
    width = table.shape[1]
    spots_here = spot_ref.shape[1]
    chunk = 128
    chunks = length // chunk

    def partner(k):
        out = 0
        bit = 1
        while bit < chips:
            out = out + lax.rem(chip // bit + (k // bit) % 2, 2) * bit
            bit *= 2
        return out

    def across(j):
        return (plane, lax.rem(me + j, vocab_size))

    def along(i):
        return (lax.rem(plane + i, dp_size), me)

    def remote(src, dst, send, recv, peer):
        return pltpu.make_async_remote_copy(
            src_ref=src, dst_ref=dst, send_sem=send, recv_sem=recv,
            device_id=peer, device_id_type=MESH)

    def table_copy(j, number):
        rows = pl.ds(pl.multiple_of(j * block, 16), number)
        return pltpu.make_async_copy(table_hbm.at[rows], table.at[rows], table_sem.at[j])

    @pl.loop(0, full)
    def _(j):
        table_copy(j, block).start()

    table_copy(full, rest).start()

    place_copy = pltpu.make_async_copy(
        place_hbm.at[pl.ds(0, place_table.shape[0])], place_table, place_sem)
    place_copy.start()
    barrier = pltpu.get_barrier_semaphore()

    @pl.loop(1, vocab_size)
    def _(j):
        pl.semaphore_signal(barrier, inc=1, device_id=across(j), device_id_type=MESH)

    @pl.loop(1, dp_size)
    def _(i):
        pl.semaphore_signal(barrier, inc=1, device_id=along(i), device_id_type=MESH)

    token = token_ref[...].astype(jnp.float32)
    segment = segment_ref[...].astype(jnp.float32)
    steps = lax.broadcasted_iota(jnp.int32, (1, length), 1).astype(jnp.float32)
    spot = lane_columns(spot_ref[...].astype(jnp.float32))[:, 0:1]
    flag = lane_columns(flag_ref[...].astype(jnp.float32))[:, 0:1]
    at_spot = steps == spot
    at_next = steps == spot + 1.0

    def picked(where_to, row):
        return jnp.sum(jnp.where(where_to, row, 0.0), axis=1, keepdims=True)

    segment_here = picked(at_spot, segment)
    weight = jnp.where(segment_here == picked(at_next, segment), flag, 0.0)
    heavy = jnp.sum(weight, axis=0, keepdims=True)
    target = picked(at_next, token)
    lanes = lax.broadcasted_iota(jnp.int32, (spots_here, 128), 1)
    label_tile = jnp.where(lanes == 0, target, jnp.where(lanes == 1, weight, 0.0))
    label_out[...] = label_tile.T[0:8, :].astype(jnp.int32)
    read = (steps <= spot) & (segment == segment_here) & (weight > 0.0)
    needed = jnp.max(ones_where(read), axis=0, keepdims=True) > 0.0

    key = jnp.where(needed, token, -1.0 - steps)
    key_cols[...] = lane_columns(key)

    def places(a):
        return (lax.broadcasted_iota(jnp.int32, (chunk, 1), 0) + a * chunk).astype(jnp.float32)

    def rows_at(a):
        return pl.ds(pl.multiple_of(a * chunk, chunk), chunk)

    def same(a):
        return key_cols[rows_at(a), 0:1] == key

    def seen(a, carry):
        return jnp.maximum(carry, jnp.max(
            ones_where(same(a) & (places(a) < steps)), axis=0, keepdims=True))

    again = lax.fori_loop(0, chunks, seen, jnp.zeros((1, length), jnp.float32))
    unique = ones_where(needed & (again == 0.0))
    unique_cols[...] = lane_columns(unique)
    owner = jnp.zeros((1, length), jnp.float32)
    for j in range(1, vocab_size):
        owner = owner + ones_where(token >= float(j * owned))
    owner_ids = lax.broadcasted_iota(jnp.int32, (vocab_size, length), 0).astype(jnp.float32)
    mine = jnp.where(owner_ids == owner, unique, 0.0)
    owners[...] = mine

    def ahead(a, carry):
        before = low_ones(places(a) < steps)
        return carry + matrix_multiply(owners[:, rows_at(a)].astype(jnp.bfloat16), before)

    ranks = lax.fori_loop(0, chunks, ahead, jnp.zeros((vocab_size, length), jnp.float32))
    rank = jnp.sum(jnp.where(owner_ids == owner, ranks, 0.0), axis=0, keepdims=True)
    too_many = jnp.max(unique * ones_where(rank >= float(room)), axis=1, keepdims=True)
    local_id = token - owner * float(owned)
    local_high = jnp.floor(local_id * (1.0 / 128.0))
    local_low = local_id - 128.0 * local_high
    row_ids = lax.broadcasted_iota(jnp.int32, (8, length), 0)

    def stacked(first, second):
        return jnp.where(row_ids == 0, first, jnp.where(row_ids == 1, second, 0.0))

    asked[...] = stacked(owner, jnp.minimum(rank, 127.0))

    def found(a, carry):
        match = low_ones(same(a) & (unique_cols[rows_at(a), 0:1] > 0.0))
        return carry + matrix_multiply(asked[:, rows_at(a)].astype(jnp.bfloat16), match)

    slots = lax.fori_loop(0, chunks, found, jnp.zeros((8, length), jnp.float32))
    slot = jnp.where(needed, slots[0:1, :] * 128.0 + slots[1:2, :], -1.0)
    slot_cols[...] = lane_columns(slot)
    local_parts = stacked(local_high, local_low).astype(jnp.bfloat16)
    rank_ids = lax.broadcasted_iota(jnp.int32, (128, length), 0).astype(jnp.float32)
    list_rows = lax.broadcasted_iota(jnp.int32, (8, 128), 0)

    @pl.loop(0, vocab_size)
    def _(j):
        theirs = (unique > 0.0) & (owner == j.astype(jnp.float32))
        chosen = low_ones(rank_ids == jnp.where(theirs, rank, -1.0))
        ids = matrix_multiply_transposed_right(local_parts, chosen)
        lists[j] = jnp.where(list_rows == 2, too_many, jnp.where(list_rows == 3, heavy, ids))

    @pl.loop(0, vocab_size)
    def _(j):
        arriving[j] = jnp.zeros(arriving.shape[1:], jnp.bfloat16)

    pl.semaphore_wait(barrier, vocab_size + dp_size - 2)

    def list_copy(j):
        peer = across(j)
        return remote(lists.at[peer[1]], lists_in.at[me], list_send.at[peer[1]],
                      list_recv.at[me], peer)

    def list_arrival(j):
        source = across(j)[1]
        return remote(lists.at[source], lists_in.at[source], list_send.at[source],
                      list_recv.at[source], across(j))

    @pl.loop(1, vocab_size)
    def _(j):
        list_copy(j).start()

    lists_in[me] = lists[me]

    ids = lax.broadcasted_iota(jnp.int32, (32, length), 0).astype(jnp.float32)
    starts = jnp.sum(ones_where(segment < ids), axis=1, keepdims=True)
    place = steps - jnp.sum(jnp.where(segment == ids, starts, 0.0), axis=0, keepdims=True)
    place_cols = lane_columns(place)[:, 0:1]
    span = place_table.shape[0]
    place_copy.wait()
    place_ids = lax.broadcasted_iota(jnp.int32, (length, span), 1).astype(jnp.float32)
    stream[...] = matrix_multiply(low_ones(place_ids == place_cols), place_table[...])
    spot_place = picked(at_spot, place)
    spot_slot = picked(at_spot, slot)
    unpack(flat_ref, (a_qkv, b_qkv, a_o, b_o, a_fc, b_fc, a_p, b_p))

    @pl.loop(1, vocab_size)
    def _(j):
        list_arrival(j).wait_recv()

    full_all[plane] = jnp.where(
        list_rows == 0, jnp.max(lists_in[:, 2:3, 0:1], axis=0),
        jnp.sum(lists_in[:, 3:4, 0:1], axis=0))

    def full_copy(i):
        peer = along(i)
        return remote(full_all.at[plane], full_all.at[plane], full_send.at[peer[0]],
                      full_recv.at[plane], peer)

    def full_arrival(i):
        source = along(i)[0]
        return remote(full_all.at[plane], full_all.at[source], full_send.at[source],
                      full_recv.at[source], along(i))

    @pl.loop(1, dp_size)
    def _(i):
        full_copy(i).start()

    def row_copy(d):
        return remote(leaving.at[d], arriving.at[me, pl.ds(0, room)], row_send.at[d],
                      row_recv.at[me], (plane, d))

    def row_arrival(d):
        return remote(leaving.at[d], arriving.at[d, pl.ds(0, room)], row_send.at[d],
                      row_recv.at[d], (plane, d))

    def wanted(d):
        here = lists_in[d]
        return lane_columns(here[0:1, :] * 128.0 + here[1:2, :])[0:room, 0:1]

    first = True
    for k in range(chips - 1, -1, -1):
        c = partner(k)
        wanted_here = jnp.concatenate([wanted(2 * c), wanted(2 * c + 1)], axis=0)

        def rows_of(j, number):
            if first:
                table_copy(j, number).wait()
            ids_here = (lax.broadcasted_iota(jnp.int32, (2 * room, number), 1)
                        + j * block).astype(jnp.float32)
            rows = pl.ds(pl.multiple_of(j * block, 16), number)
            return matrix_multiply(low_ones(ids_here == wanted_here), table[rows, :])

        acc[...] = rows_of(full, rest)

        @pl.loop(0, full)
        def _(j):
            acc[...] += rows_of(j, block)

        first = False
        for i in range(2):
            leaving[2 * c + i] = acc[pl.ds(i * room, room), :].astype(jnp.bfloat16)
        if k > 0:
            for i in range(2):
                row_copy(2 * c + i).start()
        else:
            row_copy(2 * c + 1 - lax.rem(me, 2)).start()
            arriving[me, pl.ds(0, room), :] = leaving[me]

    for k in range(chips):
        c = partner(k)
        if k > 0:
            for i in range(2):
                row_arrival(2 * c + i).wait_recv()
        else:
            row_arrival(2 * c + 1 - lax.rem(me, 2)).wait_recv()
        pair_rows = arriving[pl.ds(2 * c, 2)].reshape(256, width)
        offset = (2 * c * 128).astype(jnp.float32)

        def spread(column, ids_like):
            ids_here = lax.broadcasted_iota(jnp.int32, ids_like, 1).astype(jnp.float32)
            return low_ones(ids_here + offset == column)

        stream[...] += matrix_multiply(spread(slot_cols[:, 0:1], (length, 256)), pair_rows)
        spot_rows = matrix_multiply(spread(spot_slot, (spots_here, 256)), pair_rows)
        if k == 0:
            rows_out[...] = spot_rows
        else:
            rows_out[...] += spot_rows

    spot_ids = lax.broadcasted_iota(jnp.int32, (spots_here, span), 1).astype(jnp.float32)
    rows_out[...] += matrix_multiply(low_ones(spot_ids == spot_place), place_table[...])

    @pl.loop(0, length // 256)
    def _(a):
        rows = pl.ds(pl.multiple_of(a * 256, 256), 256)
        h1_out[rows, :] = layer_norm(
            stream[rows, :], affine_ref[0:1, :], affine_ref[3:4, :]).astype(jnp.bfloat16)

    @pl.loop(1, dp_size)
    def _(i):
        full_arrival(i).wait_recv()

    counts = jnp.where(
        list_rows == 0, jnp.max(full_all[...], axis=0), jnp.sum(full_all[...], axis=0))
    full_out[...] = counts
    crowd_out[...] = counts[0:1, 0:1].astype(jnp.int32)

    @pl.loop(1, vocab_size)
    def _(j):
        list_copy(j).wait_send()

    @pl.loop(1, dp_size)
    def _(i):
        full_copy(i).wait_send()

    for k in range(chips):
        if k > 0:
            for i in range(2):
                row_copy(2 * partner(k) + i).wait_send()
        else:
            row_copy(2 * chip + 1 - lax.rem(me, 2)).wait_send()


def embed(mesh_sizes, owned, tokens, segments, spots, flags, place_table, affine, flat, table):
    dp_size, vocab_size = mesh_sizes
    length = tokens.shape[1]
    spots_here = spots.shape[1]
    held, width = table.shape
    block = 1024
    full = held // block
    chips = vocab_size // 2
    room = 112 if vocab_size <= 8 else 64
    span = 256
    whole = pl.BlockSpec(memory_space=pltpu.VMEM)
    dma = pltpu.SemaphoreType.DMA
    return pl.pallas_call(
        partial(embed_step, dp_size, vocab_size, block, room, owned),
        out_shape=[
            jax.ShapeDtypeStruct((length, width), jnp.bfloat16),
            jax.ShapeDtypeStruct((spots_here, width), jnp.float32),
            jax.ShapeDtypeStruct((8, spots_here), jnp.int32),
            jax.ShapeDtypeStruct((8, 128), jnp.float32),
            jax.ShapeDtypeStruct((1, 1), jnp.int32),
        ]
        + [
            jax.ShapeDtypeStruct(shape, jnp.bfloat16)
            for shape in (
                (width, NARROW), (NARROW, width), (width, NARROW), (NARROW, width),
                (width, NARROW), (NARROW, 4 * width), (4 * width, NARROW), (NARROW, width),
            )
        ],
        in_specs=[whole] * 4
        + [pl.BlockSpec(memory_space=pl.ANY), whole, whole, pl.BlockSpec(memory_space=pl.ANY)],
        out_specs=[whole] * 13,
        scratch_shapes=[
            pltpu.VMEM((held, width), jnp.bfloat16),
            pltpu.VMEM((span, width), jnp.bfloat16),
            pltpu.VMEM((length, 128), jnp.float32),
            pltpu.VMEM((length, 128), jnp.float32),
            pltpu.VMEM((length, 128), jnp.float32),
            pltpu.VMEM((vocab_size, length), jnp.float32),
            pltpu.VMEM((8, length), jnp.float32),
            pltpu.VMEM((vocab_size, 8, 128), jnp.float32),
            pltpu.VMEM((vocab_size, 8, 128), jnp.float32),
            pltpu.VMEM((2 * room, width), jnp.float32),
            pltpu.VMEM((vocab_size, room, width), jnp.bfloat16),
            pltpu.VMEM((vocab_size, 128, width), jnp.bfloat16),
            pltpu.VMEM((length, width), jnp.float32),
            pltpu.VMEM((dp_size, 8, 128), jnp.float32),
            dma((full + 1,)),
            dma,
            dma((vocab_size,)),
            dma((vocab_size,)),
            dma((vocab_size,)),
            dma((vocab_size,)),
            dma((dp_size,)),
            dma((dp_size,)),
        ],
        compiler_params=pltpu.CompilerParams(
            collective_id=1, has_side_effects=True, vmem_limit_bytes=60 << 20
        ),
        name="embed_step",
    )(tokens, segments, spots, flags, place_table, affine, flat.reshape(-1, 128), table)


def wide_loop(number, body):
    lax.fori_loop(0, number, lambda i, carry: (body(i), carry)[1], 0)


def norm_parts(rows):
    centred = rows - jnp.mean(rows, axis=-1, keepdims=True)
    return centred, lax.rsqrt(jnp.mean(centred * centred, axis=-1, keepdims=True) + NORM_EPS)


def norm_back(rows, gain, grad):
    centred, spread = norm_parts(rows)
    hat = centred * spread
    grad_hat = grad * gain
    return spread * (
        grad_hat
        - jnp.mean(grad_hat, axis=-1, keepdims=True)
        - hat * jnp.mean(grad_hat * hat, axis=-1, keepdims=True)
    )


GELU_RATE = math.sqrt(2.0 / math.pi)


def gelu_parts(pre):
    bend = jnp.tanh(GELU_RATE * (pre + 0.044715 * (pre * pre * pre)))
    return 0.5 * (1.0 + bend), bend


def gelu_slope(pre):
    half, bend = gelu_parts(pre)
    inner = GELU_RATE * (1.0 + 3.0 * 0.044715 * (pre * pre))
    return half + 0.5 * pre * (1.0 - bend * bend) * inner


def both_heads(pair):
    lanes = lax.broadcasted_iota(jnp.int32, pair.shape, 1)
    half = pair.shape[1] // 2
    wide = pair.astype(jnp.float32)
    return jnp.concatenate(
        [jnp.where(lanes < half, wide, 0.0), jnp.where(lanes < half, 0.0, wide)], axis=0
    ).astype(jnp.bfloat16)


def side_by_side(stacked):
    rows = stacked.shape[0] // 2
    lanes = lax.broadcasted_iota(jnp.int32, (rows, stacked.shape[1]), 1)
    return jnp.where(lanes < stacked.shape[1] // 2, stacked[:rows], stacked[rows:])


def third_of(rows, j):
    ids = lax.broadcasted_iota(jnp.int32, rows.shape, 0)
    wide = jnp.where((ids >= j * RANK) & (ids < (j + 1) * RANK), rows.astype(jnp.float32), 0.0)
    return wide.astype(jnp.bfloat16)


def attention_mask(spot_ref, segment_ref):
    spot = lane_columns(spot_ref[...].astype(jnp.float32))[:, 0:1]
    steps = lax.broadcasted_iota(jnp.int32, segment_ref.shape, 1).astype(jnp.float32)
    segment = segment_ref[...].astype(jnp.float32)
    here = jnp.sum(jnp.where(steps == spot, segment, 0.0), axis=1, keepdims=True)
    open_to = ones_where((steps <= spot) & (segment == here))
    return jnp.concatenate([open_to, open_to], axis=0)


def layer_up(h1_ref, rows_ref, segment_ref, spot_ref, affine_ref, bias_ref,
             a_qkv, b_qkv, a_o, b_o, a_fc, b_fc, a_p, b_p,
             qkv_hbm, o_hbm, in_hbm, out_hbm,
             final_ref, q_ref, k_ref, v_ref, u1_ref, u1_rows_ref, h1_rows_ref, lse_ref,
             o_ref, uo_ref, middle_ref, h2_ref, uf_ref, pre_ref, f_ref, up_ref, last_ref,
             wq, wk, wv, wo, win, wout, mask, sems):
    length, width = h1_ref.shape
    hidden = win.shape[1]
    quarter = hidden // 4

    def columns_of(source, j, number):
        return source.at[:, pl.ds(j * number, number)]

    copies = [
        pltpu.make_async_copy(columns_of(qkv_hbm, 1, width), wk, sems.at[0]),
        pltpu.make_async_copy(columns_of(qkv_hbm, 2, width), wv, sems.at[1]),
        pltpu.make_async_copy(columns_of(qkv_hbm, 0, width), wq, sems.at[2]),
        pltpu.make_async_copy(o_hbm, wo, sems.at[3]),
        pltpu.make_async_copy(in_hbm, win, sems.at[4]),
        pltpu.make_async_copy(out_hbm, wout, sems.at[5]),
    ]
    for copy in copies:
        copy.start()

    def bias(first, number):
        return bias_ref[0:1, first : first + number]

    mask[...] = attention_mask(spot_ref, segment_ref)
    h1_rows = layer_norm(rows_ref[...], affine_ref[0:1, :], affine_ref[3:4, :]).astype(
        jnp.bfloat16)
    h1_rows_ref[...] = h1_rows
    u1_ref[...] = matrix_multiply(h1_ref[...], a_qkv[...]).astype(jnp.bfloat16)
    u1_rows = matrix_multiply(h1_rows, a_qkv[...]).astype(jnp.bfloat16)
    u1_rows_ref[...] = u1_rows

    def project(normed, low, weight, j):
        return (
            matrix_multiply(normed, weight[...])
            + bias(j * width, width)
            + ADAPTER_SCALE * matrix_multiply(low, third_of(b_qkv[...], j))
        ).astype(jnp.bfloat16)

    chunk = 512
    for j, weight, out, copy in ((1, wk, k_ref, copies[0]), (2, wv, v_ref, copies[1])):
        copy.wait()

        def rows_of(i):
            rows = pl.ds(pl.multiple_of(i * chunk, chunk), chunk)
            out[rows, :] = project(h1_ref[rows, :], u1_ref[rows, :], weight, j)

        wide_loop(length // chunk, rows_of)
    copies[2].wait()
    q_ref[...] = project(h1_rows, u1_rows, wq, 0)
    scale = (width // HEADS) ** (-0.5)
    lanes = lax.broadcasted_iota(jnp.int32, lse_ref.shape, 1)
    lse_ref[...] = jnp.zeros(lse_ref.shape, jnp.float32)

    def heads(g):
        pair = pl.ds(pl.multiple_of(g * 128, 128), 128)
        scores = scale * matrix_multiply_transposed_right(both_heads(q_ref[:, pair]), k_ref[:, pair])
        scores = jnp.where(mask[...] > 0.0, scores, MASKED)
        top = jnp.max(scores, axis=1, keepdims=True)
        e = jnp.exp(scores - top)
        total = jnp.sum(e, axis=1, keepdims=True)
        probs = (e * (1.0 / total)).astype(jnp.bfloat16)
        o_ref[:, pair] = side_by_side(matrix_multiply(probs, v_ref[:, pair])).astype(jnp.bfloat16)
        lse_ref[...] = jnp.where(lanes == g, top + jnp.log(total), lse_ref[...])

    lax.fori_loop(0, HEADS // 2, lambda g, carry: (heads(g), carry)[1], 0, unroll=2)
    o = o_ref[...]
    uo = matrix_multiply(o, a_o[...]).astype(jnp.bfloat16)
    uo_ref[...] = uo
    copies[3].wait()
    middle = (
        rows_ref[...]
        + matrix_multiply(o, wo[...])
        + bias(3 * width, width)
        + ADAPTER_SCALE * matrix_multiply(uo, b_o[...])
    )
    middle_ref[...] = middle
    h2 = layer_norm(middle, affine_ref[1:2, :], affine_ref[4:5, :]).astype(jnp.bfloat16)
    h2_ref[...] = h2
    uf = matrix_multiply(h2, a_fc[...]).astype(jnp.bfloat16)
    uf_ref[...] = uf
    copies[4].wait()
    for j in range(4):
        part = slice(j * quarter, (j + 1) * quarter)
        pre = (
            matrix_multiply(h2, win[:, part])
            + bias(4 * width + j * quarter, quarter)
            + ADAPTER_SCALE * matrix_multiply(uf, b_fc[:, part])
        )
        pre_ref[:, part] = pre
        f_ref[:, part] = (pre * gelu_parts(pre)[0]).astype(jnp.bfloat16)
    f = f_ref[...]
    up = matrix_multiply(f, a_p[...]).astype(jnp.bfloat16)
    up_ref[...] = up
    copies[5].wait()
    last = (
        middle
        + matrix_multiply(f, wout[...])
        + bias(4 * width + hidden, width)
        + ADAPTER_SCALE * matrix_multiply(up, b_p[...])
    )
    last_ref[...] = last
    final_ref[...] = layer_norm(last, affine_ref[2:3, :], affine_ref[5:6, :]).astype(jnp.bfloat16)


def pack_up(out_ref, part, grad):
    ranks = 3 * RANK if part < 2 else RANK
    wide = grad.shape[1] // 128
    for c in range(wide):
        columns = slice(c * 128, (c + 1) * 128)
        if wide == 8 and ranks == RANK:
            for r in range(ranks):
                at = PARTS[part] + wide * r + c
                out_ref[at : at + 1, :] = grad[r : r + 1, columns]
        else:
            rows = pl.ds(PARTS[part] + c, ranks, stride=wide)
            out_ref[rows, :] = grad[0:ranks, columns]


def pack_down(out_ref, part, shift, grad):
    ranks = 3 * RANK if part < 2 else RANK
    slabs = ranks // RANK
    repeated = jnp.concatenate([grad[0:ranks]] * (128 * slabs // ranks), axis=0)
    for slab in range(slabs):
        spread = repeated[128 * slab : 128 * (slab + 1)].T
        spread = jnp.where(spread_places(ranks, slab), spread, 0.0)
        rows = pl.ds(PARTS[part] + shift + slab, 32, stride=slabs)
        out_ref[rows, :] = jnp.sum(spread.reshape(32, 32, 128), axis=1)


def layer_down(grad_ref, spot_ref, segment_ref, affine_ref, h1_ref,
               a_qkv, b_qkv, a_o, b_o, a_fc, b_fc, a_p, b_p,
               q_ref, k_ref, v_ref, u1_ref, u1_rows_ref, h1_rows_ref, lse_ref,
               o_ref, uo_ref, middle_ref, h2_ref, uf_ref, pre_ref, f_ref, up_ref, last_ref,
               o_hbm, in_hbm, out_hbm,
               grad_out,
               wo, win, wout, mask, dpre_ref, do_ref, dq_ref, dk_ref, dv_ref, sems):
    length, width = h1_ref.shape
    hidden = win.shape[1]
    quarter = hidden // 4
    rows_here = grad_ref.shape[0]
    copies = [
        pltpu.make_async_copy(out_hbm, wout, sems.at[0]),
        pltpu.make_async_copy(in_hbm, win, sems.at[1]),
        pltpu.make_async_copy(o_hbm, wo, sems.at[2]),
    ]
    for copy in copies:
        copy.start()
    mask[...] = attention_mask(spot_ref, segment_ref)
    spot_row = spot_ref[...].astype(jnp.float32)
    spot = lane_columns(spot_row)[:, 0:1]
    order_row = lax.broadcasted_iota(jnp.int32, (1, rows_here), 1)
    order = lax.broadcasted_iota(jnp.int32, (rows_here, 1), 0)
    same = spot == spot_row
    repeat = jnp.max(ones_where(same & (order_row < order)), axis=1, keepdims=True)
    merge = ones_where(same) * (1.0 - repeat)
    grad_final = jnp.dot(
        merge, grad_ref[...], precision=lax.Precision.HIGHEST,
        preferred_element_type=jnp.float32)
    dx3 = norm_back(last_ref[...], affine_ref[2:3, :], grad_final)
    dm = dx3.astype(jnp.bfloat16)
    pack_up(grad_out, 7, ADAPTER_SCALE * matrix_multiply_transposed_left(up_ref[...], dm))
    du_p = (ADAPTER_SCALE * matrix_multiply_transposed_right(dm, b_p[...])).astype(jnp.bfloat16)
    ga_p = matrix_multiply_transposed_left(du_p, f_ref[...])
    for b in range(hidden // 1024):
        pack_down(grad_out, 6, 32 * b, ga_p[:, 1024 * b : 1024 * (b + 1)])
    copies[0].wait()
    for j in range(4):
        part = slice(j * quarter, (j + 1) * quarter)
        df = matrix_multiply_transposed_right(dm, wout[part, :]) + matrix_multiply_transposed_right(
            du_p, a_p[part, :])
        dpre_ref[:, part] = (df * gelu_slope(pre_ref[:, part])).astype(jnp.bfloat16)
    dpre = dpre_ref[...]
    pack_up(grad_out, 5, ADAPTER_SCALE * matrix_multiply_transposed_left(uf_ref[...], dpre))
    du_f = (ADAPTER_SCALE * matrix_multiply_transposed_right(dpre, b_fc[...])).astype(jnp.bfloat16)
    pack_down(grad_out, 4, 0, matrix_multiply_transposed_left(du_f, h2_ref[...]))
    copies[1].wait()
    dh2 = matrix_multiply_transposed_right(dpre, win[...]) + matrix_multiply_transposed_right(
        du_f, a_fc[...])
    dx2 = dx3 + norm_back(middle_ref[...], affine_ref[1:2, :], dh2)
    da = dx2.astype(jnp.bfloat16)
    pack_up(grad_out, 3, ADAPTER_SCALE * matrix_multiply_transposed_left(uo_ref[...], da))
    du_o = (ADAPTER_SCALE * matrix_multiply_transposed_right(da, b_o[...])).astype(jnp.bfloat16)
    pack_down(grad_out, 2, 0, matrix_multiply_transposed_left(du_o, o_ref[...]))
    copies[2].wait()
    do_ref[...] = (
        matrix_multiply_transposed_right(da, wo[...])
        + matrix_multiply_transposed_right(du_o, a_o[...])
    ).astype(jnp.bfloat16)
    scale = (width // HEADS) ** (-0.5)
    lanes = lax.broadcasted_iota(jnp.int32, lse_ref.shape, 1)

    def heads(g):
        pair = pl.ds(pl.multiple_of(g * 128, 128), 128)
        q = both_heads(q_ref[:, pair])
        do = both_heads(do_ref[:, pair])
        lse = jnp.sum(jnp.where(lanes == g, lse_ref[...], 0.0), axis=1, keepdims=True)
        scores = scale * matrix_multiply_transposed_right(q, k_ref[:, pair])
        probs = jnp.where(mask[...] > 0.0, jnp.exp(jnp.minimum(scores - lse, 0.0)), 0.0)
        dp = matrix_multiply_transposed_right(do, v_ref[:, pair])
        ds = (probs * (dp - jnp.sum(probs * dp, axis=1, keepdims=True))).astype(jnp.bfloat16)
        dv_ref[:, pair] = matrix_multiply_transposed_left(
            probs.astype(jnp.bfloat16), do).astype(jnp.bfloat16)
        dk_ref[:, pair] = (scale * matrix_multiply_transposed_left(ds, q)).astype(jnp.bfloat16)
        dq_ref[:, pair] = side_by_side(scale * matrix_multiply(ds, k_ref[:, pair])).astype(
            jnp.bfloat16)

    lax.fori_loop(0, HEADS // 2, lambda g, carry: (heads(g), carry)[1], 0, unroll=2)
    b_all = b_qkv[...]
    gb = jnp.zeros((NARROW, width), jnp.float32)
    ids = lax.broadcasted_iota(jnp.int32, gb.shape, 0)
    dus = []
    for j, low, grad in ((0, u1_rows_ref, dq_ref), (1, u1_ref, dk_ref), (2, u1_ref, dv_ref)):
        mine = (ids >= j * RANK) & (ids < (j + 1) * RANK)
        gb = jnp.where(mine, ADAPTER_SCALE * matrix_multiply_transposed_left(
            low[...], grad[...]), gb)
        dus.append(ADAPTER_SCALE * matrix_multiply_transposed_right(grad[...], third_of(b_all, j)))
    pack_up(grad_out, 1, gb)
    ga = matrix_multiply_transposed_left(
        dus[0].astype(jnp.bfloat16), h1_rows_ref[...]
    ) + matrix_multiply_transposed_left((dus[1] + dus[2]).astype(jnp.bfloat16), h1_ref[...])
    pack_down(grad_out, 0, 0, ga)


def layer_kernels(rows_here, length, width, hidden):
    low, wide = jnp.bfloat16, jnp.float32
    whole = pl.BlockSpec(memory_space=pltpu.VMEM)
    away = pl.BlockSpec(memory_space=pl.ANY)
    dma = pltpu.SemaphoreType.DMA
    params = pltpu.CompilerParams(vmem_limit_bytes=60 << 20)
    kept = [
        ((rows_here, width), low),
        ((length, width), low),
        ((length, width), low),
        ((length, NARROW), low),
        ((rows_here, NARROW), low),
        ((rows_here, width), low),
        ((2 * rows_here, 128), wide),
        ((rows_here, width), low),
        ((rows_here, NARROW), low),
        ((rows_here, width), wide),
        ((rows_here, width), low),
        ((rows_here, NARROW), low),
        ((rows_here, hidden), wide),
        ((rows_here, hidden), low),
        ((rows_here, NARROW), low),
        ((rows_here, width), wide),
    ]
    up = pl.pallas_call(
        layer_up,
        out_shape=[jax.ShapeDtypeStruct(*k) for k in [((rows_here, width), low)] + kept],
        in_specs=[whole] * 14 + [away] * 4,
        out_specs=[whole] * 17,
        scratch_shapes=[pltpu.VMEM((width, width), low)] * 4
        + [
            pltpu.VMEM((width, hidden), low),
            pltpu.VMEM((hidden, width), low),
            pltpu.VMEM((2 * rows_here, length), wide),
            dma((6,)),
        ],
        compiler_params=params,
        name="layer_up",
    )
    down = pl.pallas_call(
        layer_down,
        out_shape=jax.ShapeDtypeStruct((PARTS[-1], 128), wide),
        in_specs=[whole] * 29 + [away] * 3,
        out_specs=whole,
        scratch_shapes=[
            pltpu.VMEM((width, width), low),
            pltpu.VMEM((width, hidden), low),
            pltpu.VMEM((hidden, width), low),
            pltpu.VMEM((2 * rows_here, length), wide),
            pltpu.VMEM((rows_here, hidden), low),
            pltpu.VMEM((rows_here, width), low),
            pltpu.VMEM((rows_here, width), low),
            pltpu.VMEM((length, width), low),
            pltpu.VMEM((length, width), low),
            dma((3,)),
        ],
        compiler_params=params,
        name="layer_down",
    )
    return up, down


def settle_step(held_ref, segment_ref, spot_ref, place_ref, affine_ref, h1_out, rows_out, place_cols):
    length = segment_ref.shape[1]
    span = place_ref.shape[0]
    segment = segment_ref[...].astype(jnp.float32)
    steps = lax.broadcasted_iota(jnp.int32, (1, length), 1).astype(jnp.float32)
    ids = lax.broadcasted_iota(jnp.int32, (32, length), 0).astype(jnp.float32)
    starts = jnp.sum(ones_where(segment < ids), axis=1, keepdims=True)
    place = steps - jnp.sum(jnp.where(segment == ids, starts, 0.0), axis=0, keepdims=True)
    place_cols[...] = lane_columns(place)
    spot = lane_columns(spot_ref[...].astype(jnp.float32))[:, 0:1]
    at_spot = steps == spot
    spot_place = jnp.sum(jnp.where(at_spot, place, 0.0), axis=1, keepdims=True)

    def placed(column):
        ids_here = lax.broadcasted_iota(jnp.int32, (column.shape[0], span), 1).astype(jnp.float32)
        return matrix_multiply(low_ones(ids_here == column), place_ref[...])

    rows_out[...] = matrix_multiply(low_ones(at_spot), held_ref[...]) + placed(spot_place)

    @pl.loop(0, length // 128)
    def _(a):
        rows = pl.ds(pl.multiple_of(a * 128, 128), 128)
        stream = held_ref[rows, :].astype(jnp.float32) + placed(place_cols[rows, 0:1])
        h1_out[rows, :] = layer_norm(stream, affine_ref[0:1, :], affine_ref[3:4, :]).astype(
            jnp.bfloat16)


def settle_rows(held, segments, spots, place_table, affine):
    length, width = held.shape
    whole = pl.BlockSpec(memory_space=pltpu.VMEM)
    return pl.pallas_call(
        settle_step,
        out_shape=[
            jax.ShapeDtypeStruct((length, width), jnp.bfloat16),
            jax.ShapeDtypeStruct((spots.shape[1], width), jnp.float32),
        ],
        in_specs=[whole] * 5,
        out_specs=[whole] * 2,
        scratch_shapes=[pltpu.VMEM((length, 128), jnp.float32)],
        compiler_params=pltpu.CompilerParams(vmem_limit_bytes=32 << 20),
        name="settle_step",
    )(held, segments, spots, place_table[:256], affine)


def visit_step(block, wanted_ref, held_ref, table_hbm, out_ref, table, columns, acc, sem):
    copy = pltpu.make_async_copy(table_hbm, table, sem)
    copy.start()
    columns[...] = lane_columns(wanted_ref[...].astype(jnp.float32))
    rows_here = table.shape[0]
    full = rows_here // block
    copy.wait()

    @pl.loop(0, held_ref.shape[0] // 256)
    def _(a):
        rows = pl.ds(pl.multiple_of(a * 256, 256), 256)
        acc[...] = held_ref[rows, :].astype(jnp.float32)

        def add(first, number):
            ids = lax.broadcasted_iota(jnp.int32, (256, number), 1) + first
            chosen = low_ones(ids.astype(jnp.float32) == columns[rows, 0:1])
            acc[...] += matrix_multiply(chosen, table[pl.ds(first, number), :])

        @pl.loop(0, full)
        def _(j):
            add(pl.multiple_of(j * block, block), block)

        add(full * block, rows_here - full * block)
        out_ref[rows, :] = acc[...].astype(jnp.bfloat16)


def visit_rows(wanted, held, table):
    length, width = held.shape
    whole = pl.BlockSpec(memory_space=pltpu.VMEM)
    return pl.pallas_call(
        partial(visit_step, 256),
        out_shape=jax.ShapeDtypeStruct((length, width), jnp.bfloat16),
        in_specs=[whole, whole, pl.BlockSpec(memory_space=pl.ANY)],
        out_specs=whole,
        scratch_shapes=[
            pltpu.VMEM(table.shape, jnp.bfloat16),
            pltpu.VMEM((length, 128), jnp.float32),
            pltpu.VMEM((256, width), jnp.float32),
            pltpu.SemaphoreType.DMA,
        ],
        compiler_params=pltpu.CompilerParams(vmem_limit_bytes=40 << 20),
        name="visit_step",
    )(wanted, held, table)


def local(
    mesh_sizes,
    packed_symbol_codes,
    article_numbering,
    target_spots,
    answer_flags,
    shared_embedding,
    spot_embedding,
    combined_qkv_weights,
    attend_outgoing_weights,
    dense_incoming_weights,
    dense_outgoing_weights,
    layernorm_affine,
    bias_terms,
    adaptor_float_copies,
    average_moments,
    squared_moments,
):
    rows_here = target_spots.shape[1]
    shard_rows = shared_embedding.shape[0]
    table = jnp.pad(shared_embedding, ((0, -shard_rows % 16), (0, 0)))
    fast_h1, fast_rows, labels, counts, crowded, *factors = embed(
        mesh_sizes,
        shard_rows,
        packed_symbol_codes,
        article_numbering,
        target_spots,
        answer_flags,
        spot_embedding,
        layernorm_affine,
        adaptor_float_copies,
        table,
    )

    sharers = mesh_sizes[1]
    ring = [(j, (j + 1) % sharers) for j in range(sharers)]

    def visit(carry):
        turns, tokens, held = carry
        wanted = tokens - lax.axis_index("vocab") * shard_rows
        wanted = jnp.where((wanted >= 0) & (wanted < shard_rows), wanted, -1)
        kept = jnp.where(turns == sharers, jnp.zeros((), jnp.bfloat16), held)
        held = visit_rows(wanted, kept, table)
        return turns - 1, lax.ppermute(tokens, "vocab", ring), lax.ppermute(held, "vocab", ring)

    def settle(carry):
        _, held, _ = carry
        settled, rows = settle_rows(
            held, article_numbering, target_spots, spot_embedding, layernorm_affine
        )
        return jnp.zeros((), jnp.int32), settled, rows

    overflow = crowded.reshape(())
    _, _, held = lax.while_loop(
        lambda carry: carry[0] > 0, visit, (overflow * sharers, packed_symbol_codes, fast_h1)
    )
    _, h1, stream_rows = lax.while_loop(
        lambda carry: carry[0] > 0, settle, (overflow, held, fast_rows)
    )
    length, width = h1.shape
    hidden = dense_incoming_weights.shape[1]
    layer_up_call, layer_down_call = layer_kernels(rows_here, length, width, hidden)
    final_rows, *kept = layer_up_call(
        h1,
        stream_rows,
        article_numbering,
        target_spots,
        layernorm_affine,
        bias_terms[None, :],
        *factors,
        combined_qkv_weights,
        attend_outgoing_weights,
        dense_incoming_weights,
        dense_outgoing_weights,
    )
    grad_rows, loss_part = head(
        mesh_sizes, shard_rows, final_rows, labels, counts, table
    )
    local_grad = layer_down_call(
        grad_rows,
        target_spots,
        article_numbering,
        layernorm_affine,
        h1,
        *factors,
        *kept,
        attend_outgoing_weights,
        dense_incoming_weights,
        dense_outgoing_weights,
    )
    (
        refreshed_thin_pairs,
        updated_first_moment,
        updated_second_moment,
        gradient_global_norm,
        smoothed_entropy_cost,
    ) = reduce_and_update(
        mesh_sizes, local_grad, adaptor_float_copies, average_moments, squared_moments, loss_part
    )
    return (
        refreshed_thin_pairs,
        updated_first_moment,
        updated_second_moment,
        gradient_global_norm,
        smoothed_entropy_cost,
    )


def solution(mesh):
    return jax.shard_map(
        partial(local, (mesh.shape["dp"], mesh.shape["vocab"])),
        mesh=mesh,
        in_specs=(
            P(("dp", "vocab"), None),
            P(("dp", "vocab"), None),
            P(("dp", "vocab"), None),
            P(("dp", "vocab"), None),
            P("vocab", None),
            P(),
            P(),
            P(),
            P(),
            P(),
            P(),
            P(),
            P(),
            P(),
            P(),
        ),
        out_specs=(P(), P(), P(), P(), P()),
        check_vma=False,
    )
```

```python
from functools import partial
import math

import jax
import jax.numpy as jnp
from jax import lax
from jax.experimental import pallas as pl
from jax.experimental.pallas import tpu as pltpu
from jax.sharding import PartitionSpec as P

MODEL_WIDTH = 1024
HEADS = 16
FEEDFWD_UNITS = 4096
VOCAB_SIZE = 50257
RANK = 4
STEP = 10


ADAPTER_SCALE = 8.0
NORM_EPS = 1e-05
GRAD_CLIP = 0.0001
STRIDE_LENGTH = 0.02
BETA_ONE = 0.9
BETA_TWO = 0.999
SHRINK_PENALTY = 0.01
STABILITY_FLOOR = 1e-08
MASKED = -1e30
MESH = pl.DeviceIdType.MESH


def matrix_multiply(left, right):
    return jnp.dot(left, right, preferred_element_type=jnp.float32)


def matrix_multiply_transposed_left(left, right):
    return lax.dot_general(
        left, right, (((0,), (0,)), ((), ())), preferred_element_type=jnp.float32
    )


def matrix_multiply_transposed_right(left, right):
    return lax.dot_general(
        left, right, (((1,), (1,)), ((), ())), preferred_element_type=jnp.float32
    )


def layer_norm(stream, gain, shift):
    centred = stream - jnp.mean(stream, axis=-1, keepdims=True)
    spread = lax.rsqrt(jnp.mean(centred * centred, axis=-1, keepdims=True) + NORM_EPS)
    return centred * spread * gain + shift


def adaptive_moment_update(grad, weight, first, second):
    first_new = BETA_ONE * first + (1.0 - BETA_ONE) * grad
    second_new = BETA_TWO * second + (1.0 - BETA_TWO) * grad * grad
    debiased_mean_estimate = first_new / (1.0 - BETA_ONE**STEP)
    debiased_variance_estimate = second_new / (1.0 - BETA_TWO**STEP)
    weight_new = weight - STRIDE_LENGTH * (
        debiased_mean_estimate / (jnp.sqrt(debiased_variance_estimate) + STABILITY_FLOOR)
        + SHRINK_PENALTY * weight
    )
    return (weight_new, first_new, second_new)


def sum_and_step(dp_size, vocab_size, grad_ref, weight_ref, first_ref, second_ref, loss_ref,
                 weight_out, first_out, second_out, norm_out, loss_out,
                 parts, planes, total, losses, send_a, recv_a, send_b, recv_b, send_c, recv_c,
                 send_d, recv_d):
    my_plane = lax.axis_index("dp")
    me = lax.axis_index("vocab")

    def across(j):
        return (my_plane, lax.rem(me + j, vocab_size))

    def along(i):
        return (lax.rem(my_plane + i, dp_size), me)

    barrier = pltpu.get_barrier_semaphore()

    @pl.loop(1, vocab_size)
    def _(j):
        pl.semaphore_signal(barrier, inc=1, device_id=across(j), device_id_type=MESH)

    @pl.loop(1, dp_size)
    def _(i):
        pl.semaphore_signal(barrier, inc=1, device_id=along(i), device_id_type=MESH)

    pl.semaphore_wait(barrier, vocab_size + dp_size - 2)

    def part_copy(j):
        peer = across(j)
        return pltpu.make_async_remote_copy(
            src_ref=grad_ref.at[peer[1]], dst_ref=parts.at[me],
            send_sem=send_a.at[peer[1]], recv_sem=recv_a.at[me],
            device_id=peer, device_id_type=MESH)

    def part_arrival(j):
        peer = across(j)
        return pltpu.make_async_remote_copy(
            src_ref=grad_ref.at[peer[1]], dst_ref=parts.at[peer[1]],
            send_sem=send_a.at[peer[1]], recv_sem=recv_a.at[peer[1]],
            device_id=peer, device_id_type=MESH)

    def plane_copy(i):
        peer = along(i)
        return pltpu.make_async_remote_copy(
            src_ref=planes.at[my_plane], dst_ref=planes.at[my_plane],
            send_sem=send_b.at[peer[0]], recv_sem=recv_b.at[my_plane],
            device_id=peer, device_id_type=MESH)

    def plane_arrival(i):
        peer = along(i)
        return pltpu.make_async_remote_copy(
            src_ref=planes.at[my_plane], dst_ref=planes.at[peer[0]],
            send_sem=send_b.at[peer[0]], recv_sem=recv_b.at[peer[0]],
            device_id=peer, device_id_type=MESH)

    def loss_copy(i):
        peer = along(i)
        return pltpu.make_async_remote_copy(
            src_ref=loss_ref, dst_ref=losses.at[my_plane],
            send_sem=send_d.at[peer[0]], recv_sem=recv_d.at[my_plane],
            device_id=peer, device_id_type=MESH)

    def loss_arrival(i):
        peer = along(i)
        return pltpu.make_async_remote_copy(
            src_ref=loss_ref, dst_ref=losses.at[peer[0]],
            send_sem=send_d.at[peer[0]], recv_sem=recv_d.at[peer[0]],
            device_id=peer, device_id_type=MESH)

    def total_copy(j):
        peer = across(j)
        return pltpu.make_async_remote_copy(
            src_ref=total.at[me], dst_ref=total.at[me],
            send_sem=send_c.at[peer[1]], recv_sem=recv_c.at[me],
            device_id=peer, device_id_type=MESH)

    def total_arrival(j):
        peer = across(j)
        return pltpu.make_async_remote_copy(
            src_ref=total.at[me], dst_ref=total.at[peer[1]],
            send_sem=send_c.at[peer[1]], recv_sem=recv_c.at[peer[1]],
            device_id=peer, device_id_type=MESH)

    @pl.loop(1, vocab_size)
    def _(j):
        part_copy(j).start()

    @pl.loop(1, dp_size)
    def _(i):
        loss_copy(i).start()

    losses[my_plane] = loss_ref[...]
    parts[me] = grad_ref[me]

    @pl.loop(1, vocab_size)
    def _(j):
        part_arrival(j).wait_recv()

    planes[my_plane] = lax.fori_loop(
        1, vocab_size, lambda j, held: held + parts[j], parts[0])

    @pl.loop(1, dp_size)
    def _(i):
        plane_copy(i).start()

    @pl.loop(1, dp_size)
    def _(i):
        plane_arrival(i).wait_recv()

    total[me] = lax.fori_loop(1, dp_size, lambda i, held: held + planes[i], planes[0])

    @pl.loop(1, vocab_size)
    def _(j):
        total_copy(j).start()

    @pl.loop(1, vocab_size)
    def _(j):
        part_copy(j).wait_send()

    @pl.loop(1, dp_size)
    def _(i):
        plane_copy(i).wait_send()

    @pl.loop(1, vocab_size)
    def _(j):
        total_arrival(j).wait_recv()

    @pl.loop(1, vocab_size)
    def _(j):
        total_copy(j).wait_send()

    def squares(j, held):
        piece = total[j]
        return held + piece * piece

    gathered = lax.fori_loop(0, vocab_size, squares, jnp.zeros(parts.shape[1:], jnp.float32))
    norm = jnp.sqrt(jnp.sum(gathered, keepdims=True))
    norm_out[...] = norm

    @pl.loop(1, dp_size)
    def _(i):
        loss_arrival(i).wait_recv()
        loss_copy(i).wait_send()

    loss_out[...] = jnp.sum(losses[...], axis=0)[0:1, 0:1]
    shrink = GRAD_CLIP / jnp.maximum(norm, GRAD_CLIP)

    @pl.loop(0, vocab_size)
    def _(j):
        weight, first, second = adaptive_moment_update(
            total[j] * shrink, weight_ref[j], first_ref[j], second_ref[j])
        weight_out[j] = weight
        first_out[j] = first
        second_out[j] = second


def reduce_and_update(mesh_sizes, local_grad, weights, first, second, loss):
    dp_size, vocab_size = mesh_sizes
    number = local_grad.size
    rows = number // (128 * vocab_size)
    shape = (vocab_size, rows, 128)
    block = pltpu.VMEM(shape, jnp.float32)
    whole = pl.BlockSpec(memory_space=pltpu.VMEM)
    weight_new, first_new, second_new, norm, total_loss = pl.pallas_call(
        partial(sum_and_step, dp_size, vocab_size),
        out_shape=[jax.ShapeDtypeStruct(shape, jnp.float32)] * 3
        + [jax.ShapeDtypeStruct((1, 1), jnp.float32)] * 2,
        in_specs=[whole] * 5,
        out_specs=[whole] * 5,
        scratch_shapes=[
            block,
            pltpu.VMEM((dp_size, rows, 128), jnp.float32),
            block,
            pltpu.VMEM((dp_size, 8, 128), jnp.float32),
            pltpu.SemaphoreType.DMA((vocab_size,)),
            pltpu.SemaphoreType.DMA((vocab_size,)),
            pltpu.SemaphoreType.DMA((dp_size,)),
            pltpu.SemaphoreType.DMA((dp_size,)),
            pltpu.SemaphoreType.DMA((vocab_size,)),
            pltpu.SemaphoreType.DMA((vocab_size,)),
            pltpu.SemaphoreType.DMA((dp_size,)),
            pltpu.SemaphoreType.DMA((dp_size,)),
        ],
        compiler_params=pltpu.CompilerParams(
            collective_id=5, has_side_effects=True, vmem_limit_bytes=24 << 20
        ),
        name="sum_and_step",
    )(*[piece.reshape(shape) for piece in (local_grad, weights, first, second)], loss)
    flat = [piece.reshape(-1) for piece in (weight_new, first_new, second_new)]
    return (*flat, norm.reshape(()), total_loss.reshape(()))


TILE = 32


def head_step(dp_size, vocab_size, block, owned, hf_ref, label_ref, count_ref, table_hbm, grad_out, loss_out,
              table, hf_all, label_all, exps, exps_rest, tops, run_top, run_sum, run_smooth,
              run_goal, offset, z_even, z_odd, z_rest, dz_even, dz_odd, rest_even, rest_odd,
              acc_even, acc_odd, lse_tile, share_tile, stats_all,
              from_core, from_chip, leaving,
              table_sem, label_send, label_recv, hf_send, hf_recv,
              stat_send, stat_recv, core_send, core_recv, chip_send, chip_recv):
    plane = lax.axis_index("dp")
    me = lax.axis_index("vocab")
    chips = vocab_size // 2
    chip = me // 2
    core = lax.rem(me, 2)
    other = 2 * chip + 1 - core
    sibling = (plane, other)
    held = table_hbm.shape[0]
    full = held // block
    rest = held - full * block
    padded = table.shape[0] - full * block
    base = me * owned
    rows_each = hf_ref.shape[0]
    pair = 2 * rows_each
    width = hf_ref.shape[1]

    def partner(k):
        out = 0
        bit = 1
        while bit < chips:
            out = out + lax.rem(chip // bit + lax.rem(k // bit, 2), 2) * bit
            bit *= 2
        return out

    def across(j):
        return (plane, lax.rem(me + j, vocab_size))

    def table_copy(j, number):
        rows = pl.ds(pl.multiple_of(j * block, 16), number)
        return pltpu.make_async_copy(table_hbm.at[rows], table.at[rows], table_sem.at[j])

    @pl.loop(0, full)
    def _(j):
        table_copy(j, block).start()

    table_copy(full, rest).start()

    table[held:, :] = jnp.zeros((padded - rest, width), jnp.bfloat16)
    barrier = pltpu.get_barrier_semaphore()

    @pl.loop(1, vocab_size)
    def _(j):
        pl.semaphore_signal(barrier, inc=1, device_id=across(j), device_id_type=MESH)

    pl.semaphore_wait(barrier, vocab_size - 1)

    def remote(src, dst, send, recv, peer):
        return pltpu.make_async_remote_copy(
            src_ref=src, dst_ref=dst, send_sem=send, recv_sem=recv,
            device_id=peer, device_id_type=MESH)

    def hf_to_sibling():
        return remote(hf_ref, hf_all.at[me], hf_send.at[0], hf_recv.at[me], sibling)

    def hf_copy(k):
        return remote(hf_ref, hf_all.at[me], hf_send.at[k], hf_recv.at[me],
                      (plane, 2 * partner(k) + core))

    def hf_arrival(source):
        return remote(hf_ref, hf_all.at[source], hf_send.at[0], hf_recv.at[source], sibling)

    def hf_forward(k):
        source = 2 * partner(k) + core
        return remote(hf_all.at[source], hf_all.at[source], hf_send.at[chips + k],
                      hf_recv.at[source], sibling)

    def label_copy(j):
        peer = across(j)
        return remote(label_ref, label_all.at[me], label_send.at[peer[1]], label_recv.at[me], peer)

    def label_arrival(source):
        return remote(label_ref, label_all.at[source], label_send.at[source],
                      label_recv.at[source], sibling)

    near = min(3, chips)
    hf_to_sibling().start()

    @pl.loop(1, near)
    def _(k):
        hf_copy(k).start()

    @pl.loop(1, vocab_size)
    def _(j):
        label_copy(j).start()

    hf_all[me] = hf_ref[...]
    label_all[me] = label_ref[...]
    lanes = lax.broadcasted_iota(jnp.int32, (pair, 128), 1)

    def label_row(c, i):
        rows = label_all[pl.ds(2 * c, 2), i : i + 1, :].astype(jnp.float32)
        return jnp.concatenate([rows[0], rows[1]], axis=1)

    def set_offset(c):
        offset[...] = lane_columns(label_row(c, 0)).astype(jnp.int32) - base - lanes

    def folded(x):
        return sum(x[:, i * 128 : (i + 1) * 128] for i in range(1, x.shape[1] // 128)) + x[:, :128]

    def chunk_up(k, first):
        c = partner(k)
        if first:
            hf_arrival(other).wait_recv()
            label_arrival(other).wait_recv()
        else:
            hf_arrival(2 * c + core).wait_recv()
            hf_forward(k).start()
            label_arrival(2 * c).wait_recv()
            label_arrival(2 * c + 1).wait_recv()
            hf_arrival(2 * c + 1 - core).wait_recv()
        set_offset(c)
        run_top[...] = jnp.full((pair, 128), MASKED, jnp.float32)
        for ref in (run_sum, run_smooth, run_goal):
            ref[...] = jnp.zeros((pair, 128), jnp.float32)
        start = pl.multiple_of(k * pair, pair)

        def multiply(j, z_ref):
            if first:
                table_copy(j, rest if z_ref is z_rest else block).wait()
            rows = pl.ds(pl.multiple_of(j * block, 16), z_ref.shape[1])
            hidden = hf_all[pl.ds(2 * c, 2)].reshape(pair, width)
            z_ref[...] = matrix_multiply_transposed_right(hidden, table[rows, :])

        def reduce_full(j, z_ref):
            for r in range(pair // TILE):
                rows = slice(r * TILE, (r + 1) * TILE)
                there = pl.ds(start + r * TILE, TILE)
                z = z_ref[rows, :]
                old = run_top[rows, :]
                top = jnp.maximum(old, jnp.max(z, axis=1, keepdims=True))
                run_top[rows, :] = top
                tops[k, j, rows, :] = top
                gap = offset[rows, :] - j * block
                total = jnp.zeros((TILE, 128), jnp.float32)
                smooth = jnp.zeros((TILE, 128), jnp.float32)
                goal = jnp.zeros((TILE, 128), jnp.float32)
                for i in range(block // 128):
                    part = slice(i * 128, (i + 1) * 128)
                    piece = z[:, part]
                    e = jnp.exp(piece - top)
                    exps[j, there, part] = e
                    total = total + e
                    smooth = smooth + piece
                    goal = goal + jnp.where(gap == i * 128, piece, 0.0)
                run_sum[rows, :] = run_sum[rows, :] * jnp.exp(old - top) + total
                run_smooth[rows, :] = run_smooth[rows, :] + smooth
                run_goal[rows, :] = run_goal[rows, :] + goal

        def reduce_rest():
            for r in range(pair // TILE):
                rows = slice(r * TILE, (r + 1) * TILE)
                there = pl.ds(start + r * TILE, TILE)
                spot = lanes[rows, :]
                limit = jnp.minimum(VOCAB_SIZE - base, owned) - full * block - spot
                gap = offset[rows, :] - full * block
                pieces = []
                for i in range(padded // 128):
                    piece = z_rest[rows, i * 128 : (i + 1) * 128]
                    pieces.append((i * 128 < limit, piece))
                highest = jnp.where(pieces[0][0], pieces[0][1], MASKED)
                for valid, piece in pieces[1:]:
                    highest = jnp.maximum(highest, jnp.where(valid, piece, MASKED))
                old = run_top[rows, :]
                top = jnp.maximum(old, jnp.max(highest, axis=1, keepdims=True))
                run_top[rows, :] = top
                tops[k, full, rows, :] = top
                total = jnp.zeros((TILE, 128), jnp.float32)
                smooth = jnp.zeros((TILE, 128), jnp.float32)
                goal = jnp.zeros((TILE, 128), jnp.float32)
                for i, (valid, piece) in enumerate(pieces):
                    e = jnp.where(valid, jnp.exp(piece - top), 0.0)
                    exps_rest[there, i * 128 : (i + 1) * 128] = e
                    total = total + e
                    smooth = smooth + jnp.where(valid, piece, 0.0)
                    goal = goal + jnp.where(valid & (gap == i * 128), piece, 0.0)
                run_sum[rows, :] = run_sum[rows, :] * jnp.exp(old - top) + total
                run_smooth[rows, :] = run_smooth[rows, :] + smooth
                run_goal[rows, :] = run_goal[rows, :] + goal

        multiply(0, z_even)
        turns = (full - 1) // 2

        if turns > 0:
            @pl.loop(0, turns)
            def _(t):
                multiply(2 * t + 1, z_odd)
                reduce_full(2 * t, z_even)
                multiply(2 * t + 2, z_even)
                reduce_full(2 * t + 1, z_odd)

        if full - 2 * turns == 2:
            multiply(full - 1, z_odd)
            reduce_full(full - 2, z_even)
            multiply(full, z_rest)
            reduce_full(full - 1, z_odd)
        else:
            multiply(full, z_rest)
            reduce_full(full - 1, z_even)
        reduce_rest()

        def row_sum(ref):
            return jnp.sum(ref[...].T, axis=0, keepdims=True)

        ids = lax.broadcasted_iota(jnp.int32, (8, pair), 0)
        packed = jnp.where(ids == 0, run_top[...].T[0:1, :], 0.0)
        for i, ref in enumerate((run_sum, run_smooth, run_goal)):
            packed = jnp.where(ids == i + 1, row_sum(ref), packed)
        stats_all[me, c] = packed

    chunk_up(0, True)

    @pl.loop(near, chips)
    def _(k):
        hf_copy(k).start()

    @pl.loop(1, chips)
    def _(k):
        chunk_up(k, False)

    def stat_copy(j):
        peer = across(j)
        return remote(stats_all.at[me], stats_all.at[me], stat_send.at[peer[1]],
                      stat_recv.at[me], peer)

    def stat_arrival(j):
        source = across(j)[1]
        return remote(stats_all.at[me], stats_all.at[source], stat_send.at[source],
                      stat_recv.at[source], across(j))

    @pl.loop(1, vocab_size)
    def _(j):
        stat_copy(j).start()

    @pl.loop(1, vocab_size)
    def _(j):
        stat_arrival(j).wait_recv()

    count = jnp.maximum(count_ref[1:2, 0:1], 1.0)

    def totals_of(c):
        here = stats_all[:, c]
        tops_here = here[:, 0:1, :]
        top = jnp.max(tops_here, axis=0)
        total = jnp.sum(here[:, 1:2, :] * jnp.exp(tops_here - top[None]), axis=0)
        return top + jnp.log(total), jnp.sum(here[:, 2:3, :], axis=0), jnp.sum(
            here[:, 3:4, :], axis=0)

    def chunk_loss(c, held_loss):
        lse, smooth, goal = totals_of(c)
        return held_loss + label_row(c, 1) * (lse - 0.9 * goal - 0.1 * smooth / VOCAB_SIZE)

    slots = from_core.shape[0]
    columns_each = width // 4

    def core_copy(k, n, acc):
        half = pl.ds(pl.multiple_of((1 - core) * rows_each, rows_each), rows_each)
        part = pl.ds(pl.multiple_of(n * columns_each, columns_each), columns_each)
        return remote(acc.at[half, part], from_core.at[lax.rem(k, slots), :, part],
                      core_send.at[k, n], core_recv.at[k, n], sibling)

    def chip_copy(k, n):
        part = pl.ds(pl.multiple_of(n * columns_each, columns_each), columns_each)
        return remote(leaving.at[k - 1, :, part], from_chip.at[k - 1, :, part],
                      chip_send.at[k, n], chip_recv.at[k, n], (plane, 2 * partner(k) + core))

    def prepare(k):
        c = partner(k)
        lse, _, _ = totals_of(c)
        lse_tile[...] = lane_columns(lse)
        share_tile[...] = lane_columns(label_row(c, 1) / count)
        set_offset(c)

    quarter = pair // 4

    def grads(k, n, dz_ref, rest_ref):
        for r in range(quarter // TILE):
            first = pl.multiple_of(n * quarter + r * TILE, TILE)
            rows = pl.ds(first, TILE)
            there = pl.ds(pl.multiple_of(k * pair + first, TILE), TILE)
            share = share_tile[rows, :]
            lse = lse_tile[rows, :]
            low = share * (0.1 / VOCAB_SIZE)
            high = low + 0.9 * share
            gap = offset[rows, :]
            for j in range(full):
                factor = share * jnp.exp(tops[k, j, rows, :] - lse)
                for i in range(block // 128):
                    at = j * block + i * 128
                    e = exps[j, there, i * 128 : (i + 1) * 128]
                    dz = e * factor - jnp.where(gap == at, high, low)
                    dz_ref[rows, at : at + 128] = dz.astype(jnp.bfloat16)
            factor = share * jnp.exp(tops[k, full, rows, :] - lse)
            limit = jnp.minimum(VOCAB_SIZE - base, owned) - full * block - lanes[0:TILE, :]
            for i in range(padded // 128):
                part = slice(i * 128, (i + 1) * 128)
                at = full * block + i * 128
                dz = exps_rest[there, part] * factor - jnp.where(gap == at, high, low)
                rest_ref[rows, part] = jnp.where(i * 128 < limit, dz, 0.0).astype(jnp.bfloat16)

    def gather(k, n, dz_ref, rest_ref, acc):
        part = pl.ds(pl.multiple_of(n * columns_each, columns_each), columns_each)
        acc[:, part] = matrix_multiply(
            dz_ref[...], table[pl.ds(0, full * block), part]
        ) + matrix_multiply(rest_ref[...], table[pl.ds(full * block, padded), part])

    def finish(k, n, acc):
        core_copy(k, n, acc).wait()
        own = pl.ds(pl.multiple_of(core * rows_each, rows_each), rows_each)
        part = pl.ds(pl.multiple_of(n * columns_each, columns_each), columns_each)
        return from_core[lax.rem(k, slots), :, part] + acc[own, part]

    def ship(k, n, acc):
        part = pl.ds(pl.multiple_of(n * columns_each, columns_each), columns_each)
        leaving[k - 1, :, part] = finish(k, n, acc).astype(jnp.bfloat16)
        chip_copy(k, n).start()

    def stage(k, now, later, acc, acc_before):
        if later is not None:
            prepare(k - 1)

        @pl.loop(0, 4)
        def _(n):
            gather(k, n, *now, acc)
            if later is not None:
                grads(k - 1, n, *later)
            core_copy(k, n, acc).start()
            if later is not None:
                @pl.when(n > 0)
                def _():
                    ship(k, n - 1, acc)

            if acc_before is not None:
                @pl.when((n == 0) & (k < chips - 1))
                def _():
                    ship(k + 1, 3, acc_before)

    evens = ((dz_even, rest_even), acc_even)
    odds = ((dz_odd, rest_odd), acc_odd)
    prepare(chips - 1)

    @pl.loop(0, 4)
    def _(n):
        grads(chips - 1, n, *odds[0])

    @pl.loop(0, chips // 2 - 1)
    def _(t):
        k = chips - 1 - 2 * t
        stage(k, odds[0], evens[0], acc_odd, acc_even)
        stage(k - 1, evens[0], odds[0], acc_even, acc_odd)

    stage(1, odds[0], evens[0], acc_odd, acc_even if chips > 2 else None)
    stage(0, evens[0], None, acc_even, acc_odd)

    loss = lax.fori_loop(0, chips, chunk_loss, jnp.zeros((1, pair), jnp.float32))
    loss_out[...] = jnp.broadcast_to(jnp.sum(loss, keepdims=True) / count, loss_out.shape)
    for n in range(4):
        grad_out[:, n * columns_each : (n + 1) * columns_each] = finish(0, n, acc_even)

    @pl.loop(1, chips)
    def _(t):
        k = chips - t
        for n in range(4):
            chip_copy(k, n).wait_recv()
        grad_out[...] += from_chip[k - 1].astype(jnp.float32)

    hf_to_sibling().wait_send()

    @pl.loop(1, chips)
    def _(k):
        hf_copy(k).wait_send()
        hf_forward(k).wait_send()
        for n in range(4):
            chip_copy(k, n).wait_send()

    @pl.loop(1, vocab_size)
    def _(j):
        label_copy(j).wait_send()
        stat_copy(j).wait_send()


def head(mesh_sizes, owned, final_rows, labels, counts, table):
    dp_size, vocab_size = mesh_sizes
    rows, width = final_rows.shape
    held = table.shape[0]
    block = 1024
    full = held // block
    rest = -(-(held - full * block) // 128) * 128
    chips = vocab_size // 2
    pair = 2 * rows
    low, wide = jnp.bfloat16, jnp.float32
    whole = pl.BlockSpec(memory_space=pltpu.VMEM)
    dma = pltpu.SemaphoreType.DMA
    tile = pltpu.VMEM((pair, 128), wide)
    grad, loss = pl.pallas_call(
        partial(head_step, dp_size, vocab_size, block, owned),
        out_shape=[
            jax.ShapeDtypeStruct((rows, width), wide),
            jax.ShapeDtypeStruct((8, 128), wide),
        ],
        in_specs=[whole, whole, whole, pl.BlockSpec(memory_space=pl.ANY)],
        out_specs=[whole, whole],
        scratch_shapes=[
            pltpu.VMEM((full * block + rest, width), low),
            pltpu.VMEM((vocab_size, rows, width), low),
            pltpu.VMEM((vocab_size, 8, rows), jnp.int32),
            pltpu.VMEM((full, vocab_size * rows, block), wide),
            pltpu.VMEM((vocab_size * rows, rest), wide),
            pltpu.VMEM((chips, full + 1, pair, 128), wide),
            tile,
            tile,
            tile,
            tile,
            pltpu.VMEM((pair, 128), jnp.int32),
            pltpu.VMEM((pair, block), wide),
            pltpu.VMEM((pair, block), wide),
            pltpu.VMEM((pair, rest), wide),
            pltpu.VMEM((pair, full * block), low),
            pltpu.VMEM((pair, full * block), low),
            pltpu.VMEM((pair, rest), low),
            pltpu.VMEM((pair, rest), low),
            pltpu.VMEM((pair, width), wide),
            pltpu.VMEM((pair, width), wide),
            tile,
            tile,
            pltpu.VMEM((vocab_size, chips, 8, pair), wide),
            pltpu.VMEM((3, rows, width), wide),
            pltpu.VMEM((chips - 1, rows, width), low),
            pltpu.VMEM((chips - 1, rows, width), low),
            dma((full + 1,)),
            dma((vocab_size,)),
            dma((vocab_size,)),
            dma((2 * chips,)),
            dma((vocab_size,)),
            dma((vocab_size,)),
            dma((vocab_size,)),
            dma((chips, 4)),
            dma((chips, 4)),
            dma((chips, 4)),
            dma((chips, 4)),
        ],
        compiler_params=pltpu.CompilerParams(
            collective_id=3, has_side_effects=True, vmem_limit_bytes=63 << 20
        ),
        name="head_step",
    )(final_rows, labels, counts, table)
    return grad, loss


NARROW = 16
PARTS = (0, 96, 192, 224, 256, 288, 416, 544, 576)


def floor_part(values, size):
    return jnp.floor((values + 0.5) * (1.0 / size))


def spread_places(ranks, slab):
    lanes = lax.broadcasted_iota(jnp.int32, (1024, 128), 1).astype(jnp.float32) + 128.0 * slab
    rows = lax.broadcasted_iota(jnp.int32, (1024, 128), 0).astype(jnp.float32)
    return floor_part(lanes, ranks) == rows - 32.0 * floor_part(rows, 32)


def unpack_down(flat_ref, first, ranks, out_ref, start):
    slabs = ranks // RANK
    total = None
    for slab in range(slabs):
        packed = flat_ref[pl.ds(first + slab, 32, stride=slabs), :]
        spread = jnp.broadcast_to(packed[:, None, :], (32, 32, 128)).reshape(1024, 128)
        spread = jnp.where(spread_places(ranks, slab), spread, 0.0).astype(jnp.bfloat16)
        lanes = lax.broadcasted_iota(jnp.int32, (128, NARROW), 0).astype(jnp.float32) + 128.0 * slab
        column = lax.broadcasted_iota(jnp.int32, (128, NARROW), 1).astype(jnp.float32)
        chosen = low_ones(lanes - ranks * floor_part(lanes, ranks) == column)
        part = matrix_multiply(spread, chosen)
        total = part if total is None else total + part
    out_ref[pl.ds(start, 1024), :] = total.astype(jnp.bfloat16)


def unpack_up(flat_ref, first, ranks, out_ref):
    wide = out_ref.shape[1] // 128
    for c in range(wide):
        if wide == 8 and ranks == RANK:
            rows = jnp.concatenate(
                [flat_ref[first + wide * r + c : first + wide * r + c + 1, :] for r in range(ranks)],
                axis=0)
        else:
            rows = flat_ref[pl.ds(first + c, ranks, stride=wide), :]
        rows = jnp.concatenate([rows, jnp.zeros((NARROW - ranks, 128), jnp.float32)], axis=0)
        out_ref[:, c * 128 : (c + 1) * 128] = rows.astype(jnp.bfloat16)


def unpack(flat_ref, outs):
    for i, out_ref in enumerate(outs):
        ranks = 3 * RANK if i < 2 else RANK
        if i % 2:
            unpack_up(flat_ref, PARTS[i], ranks, out_ref)
        else:
            for b in range(out_ref.shape[0] // 1024):
                unpack_down(flat_ref, PARTS[i] + 32 * b, ranks, out_ref, 1024 * b)


def lane_columns(row):
    return jnp.broadcast_to(row, (128, row.shape[1])).T


def ones_where(condition):
    return jnp.where(condition, 1.0, 0.0)


def low_ones(condition):
    return ones_where(condition).astype(jnp.bfloat16)


def embed_step(dp_size, vocab_size, block, room, owned, token_ref, segment_ref, spot_ref, flag_ref,
               place_hbm, affine_ref, flat_ref, table_hbm,
               h1_out, rows_out, label_out, full_out, crowd_out,
               a_qkv, b_qkv, a_o, b_o, a_fc, b_fc, a_p, b_p,
               table, place_table, key_cols, unique_cols, slot_cols, owners, asked, lists, lists_in,
               acc, leaving, arriving, stream, full_all,
               table_sem, place_sem, list_send, list_recv, row_send, row_recv, full_send, full_recv):
    plane = lax.axis_index("dp")
    me = lax.axis_index("vocab")
    chips = vocab_size // 2
    chip = me // 2
    held = table.shape[0]
    full = held // block
    rest = held - full * block
    length = token_ref.shape[1]
    width = table.shape[1]
    spots_here = spot_ref.shape[1]
    chunk = 128
    chunks = length // chunk

    def partner(k):
        out = 0
        bit = 1
        while bit < chips:
            out = out + lax.rem(chip // bit + (k // bit) % 2, 2) * bit
            bit *= 2
        return out

    def across(j):
        return (plane, lax.rem(me + j, vocab_size))

    def along(i):
        return (lax.rem(plane + i, dp_size), me)

    def remote(src, dst, send, recv, peer):
        return pltpu.make_async_remote_copy(
            src_ref=src, dst_ref=dst, send_sem=send, recv_sem=recv,
            device_id=peer, device_id_type=MESH)

    def table_copy(j, number):
        rows = pl.ds(pl.multiple_of(j * block, 16), number)
        return pltpu.make_async_copy(table_hbm.at[rows], table.at[rows], table_sem.at[j])

    @pl.loop(0, full)
    def _(j):
        table_copy(j, block).start()

    table_copy(full, rest).start()

    place_copy = pltpu.make_async_copy(
        place_hbm.at[pl.ds(0, place_table.shape[0])], place_table, place_sem)
    place_copy.start()
    barrier = pltpu.get_barrier_semaphore()

    @pl.loop(1, vocab_size)
    def _(j):
        pl.semaphore_signal(barrier, inc=1, device_id=across(j), device_id_type=MESH)

    @pl.loop(1, dp_size)
    def _(i):
        pl.semaphore_signal(barrier, inc=1, device_id=along(i), device_id_type=MESH)

    token = token_ref[...].astype(jnp.float32)
    segment = segment_ref[...].astype(jnp.float32)
    steps = lax.broadcasted_iota(jnp.int32, (1, length), 1).astype(jnp.float32)
    spot = lane_columns(spot_ref[...].astype(jnp.float32))[:, 0:1]
    flag = lane_columns(flag_ref[...].astype(jnp.float32))[:, 0:1]
    at_spot = steps == spot
    at_next = steps == spot + 1.0

    def picked(where_to, row):
        return jnp.sum(jnp.where(where_to, row, 0.0), axis=1, keepdims=True)

    segment_here = picked(at_spot, segment)
    weight = jnp.where(segment_here == picked(at_next, segment), flag, 0.0)
    heavy = jnp.sum(weight, axis=0, keepdims=True)
    target = picked(at_next, token)
    lanes = lax.broadcasted_iota(jnp.int32, (spots_here, 128), 1)
    label_tile = jnp.where(lanes == 0, target, jnp.where(lanes == 1, weight, 0.0))
    label_out[...] = label_tile.T[0:8, :].astype(jnp.int32)
    read = (steps <= spot) & (segment == segment_here) & (weight > 0.0)
    needed = jnp.max(ones_where(read), axis=0, keepdims=True) > 0.0

    key = jnp.where(needed, token, -1.0 - steps)
    key_cols[...] = lane_columns(key)

    def places(a):
        return (lax.broadcasted_iota(jnp.int32, (chunk, 1), 0) + a * chunk).astype(jnp.float32)

    def rows_at(a):
        return pl.ds(pl.multiple_of(a * chunk, chunk), chunk)

    def same(a):
        return key_cols[rows_at(a), 0:1] == key

    def seen(a, carry):
        return jnp.maximum(carry, jnp.max(
            ones_where(same(a) & (places(a) < steps)), axis=0, keepdims=True))

    again = lax.fori_loop(0, chunks, seen, jnp.zeros((1, length), jnp.float32))
    unique = ones_where(needed & (again == 0.0))
    unique_cols[...] = lane_columns(unique)
    owner = jnp.zeros((1, length), jnp.float32)
    for j in range(1, vocab_size):
        owner = owner + ones_where(token >= float(j * owned))
    owner_ids = lax.broadcasted_iota(jnp.int32, (vocab_size, length), 0).astype(jnp.float32)
    mine = jnp.where(owner_ids == owner, unique, 0.0)
    owners[...] = mine

    def ahead(a, carry):
        before = low_ones(places(a) < steps)
        return carry + matrix_multiply(owners[:, rows_at(a)].astype(jnp.bfloat16), before)

    ranks = lax.fori_loop(0, chunks, ahead, jnp.zeros((vocab_size, length), jnp.float32))
    rank = jnp.sum(jnp.where(owner_ids == owner, ranks, 0.0), axis=0, keepdims=True)
    too_many = jnp.max(unique * ones_where(rank >= float(room)), axis=1, keepdims=True)
    local_id = token - owner * float(owned)
    local_high = jnp.floor(local_id * (1.0 / 128.0))
    local_low = local_id - 128.0 * local_high
    row_ids = lax.broadcasted_iota(jnp.int32, (8, length), 0)

    def stacked(first, second):
        return jnp.where(row_ids == 0, first, jnp.where(row_ids == 1, second, 0.0))

    asked[...] = stacked(owner, jnp.minimum(rank, 127.0))

    def found(a, carry):
        match = low_ones(same(a) & (unique_cols[rows_at(a), 0:1] > 0.0))
        return carry + matrix_multiply(asked[:, rows_at(a)].astype(jnp.bfloat16), match)

    slots = lax.fori_loop(0, chunks, found, jnp.zeros((8, length), jnp.float32))
    slot = jnp.where(needed, slots[0:1, :] * 128.0 + slots[1:2, :], -1.0)
    slot_cols[...] = lane_columns(slot)
    local_parts = stacked(local_high, local_low).astype(jnp.bfloat16)
    rank_ids = lax.broadcasted_iota(jnp.int32, (128, length), 0).astype(jnp.float32)
    list_rows = lax.broadcasted_iota(jnp.int32, (8, 128), 0)

    @pl.loop(0, vocab_size)
    def _(j):
        theirs = (unique > 0.0) & (owner == j.astype(jnp.float32))
        chosen = low_ones(rank_ids == jnp.where(theirs, rank, -1.0))
        ids = matrix_multiply_transposed_right(local_parts, chosen)
        lists[j] = jnp.where(list_rows == 2, too_many, jnp.where(list_rows == 3, heavy, ids))

    @pl.loop(0, vocab_size)
    def _(j):
        arriving[j] = jnp.zeros(arriving.shape[1:], jnp.bfloat16)

    pl.semaphore_wait(barrier, vocab_size + dp_size - 2)

    def list_copy(j):
        peer = across(j)
        return remote(lists.at[peer[1]], lists_in.at[me], list_send.at[peer[1]],
                      list_recv.at[me], peer)

    def list_arrival(j):
        source = across(j)[1]
        return remote(lists.at[source], lists_in.at[source], list_send.at[source],
                      list_recv.at[source], across(j))

    @pl.loop(1, vocab_size)
    def _(j):
        list_copy(j).start()

    lists_in[me] = lists[me]

    ids = lax.broadcasted_iota(jnp.int32, (32, length), 0).astype(jnp.float32)
    starts = jnp.sum(ones_where(segment < ids), axis=1, keepdims=True)
    place = steps - jnp.sum(jnp.where(segment == ids, starts, 0.0), axis=0, keepdims=True)
    place_cols = lane_columns(place)[:, 0:1]
    span = place_table.shape[0]
    place_copy.wait()
    place_ids = lax.broadcasted_iota(jnp.int32, (length, span), 1).astype(jnp.float32)
    stream[...] = matrix_multiply(low_ones(place_ids == place_cols), place_table[...])
    spot_place = picked(at_spot, place)
    spot_slot = picked(at_spot, slot)
    unpack(flat_ref, (a_qkv, b_qkv, a_o, b_o, a_fc, b_fc, a_p, b_p))

    @pl.loop(1, vocab_size)
    def _(j):
        list_arrival(j).wait_recv()

    full_all[plane] = jnp.where(
        list_rows == 0, jnp.max(lists_in[:, 2:3, 0:1], axis=0),
        jnp.sum(lists_in[:, 3:4, 0:1], axis=0))

    def full_copy(i):
        peer = along(i)
        return remote(full_all.at[plane], full_all.at[plane], full_send.at[peer[0]],
                      full_recv.at[plane], peer)

    def full_arrival(i):
        source = along(i)[0]
        return remote(full_all.at[plane], full_all.at[source], full_send.at[source],
                      full_recv.at[source], along(i))

    @pl.loop(1, dp_size)
    def _(i):
        full_copy(i).start()

    def row_copy(d):
        return remote(leaving.at[d], arriving.at[me, pl.ds(0, room)], row_send.at[d],
                      row_recv.at[me], (plane, d))

    def row_arrival(d):
        return remote(leaving.at[d], arriving.at[d, pl.ds(0, room)], row_send.at[d],
                      row_recv.at[d], (plane, d))

    def wanted(d):
        here = lists_in[d]
        return lane_columns(here[0:1, :] * 128.0 + here[1:2, :])[0:room, 0:1]

    first = True
    for k in range(chips - 1, -1, -1):
        c = partner(k)
        wanted_here = jnp.concatenate([wanted(2 * c), wanted(2 * c + 1)], axis=0)

        def rows_of(j, number):
            if first:
                table_copy(j, number).wait()
            ids_here = (lax.broadcasted_iota(jnp.int32, (2 * room, number), 1)
                        + j * block).astype(jnp.float32)
            rows = pl.ds(pl.multiple_of(j * block, 16), number)
            return matrix_multiply(low_ones(ids_here == wanted_here), table[rows, :])

        acc[...] = rows_of(full, rest)

        @pl.loop(0, full)
        def _(j):
            acc[...] += rows_of(j, block)

        first = False
        for i in range(2):
            leaving[2 * c + i] = acc[pl.ds(i * room, room), :].astype(jnp.bfloat16)
        if k > 0:
            for i in range(2):
                row_copy(2 * c + i).start()
        else:
            row_copy(2 * c + 1 - lax.rem(me, 2)).start()
            arriving[me, pl.ds(0, room), :] = leaving[me]

    for k in range(chips):
        c = partner(k)
        if k > 0:
            for i in range(2):
                row_arrival(2 * c + i).wait_recv()
        else:
            row_arrival(2 * c + 1 - lax.rem(me, 2)).wait_recv()
        pair_rows = arriving[pl.ds(2 * c, 2)].reshape(256, width)
        offset = (2 * c * 128).astype(jnp.float32)

        def spread(column, ids_like):
            ids_here = lax.broadcasted_iota(jnp.int32, ids_like, 1).astype(jnp.float32)
            return low_ones(ids_here + offset == column)

        stream[...] += matrix_multiply(spread(slot_cols[:, 0:1], (length, 256)), pair_rows)
        spot_rows = matrix_multiply(spread(spot_slot, (spots_here, 256)), pair_rows)
        if k == 0:
            rows_out[...] = spot_rows
        else:
            rows_out[...] += spot_rows

    spot_ids = lax.broadcasted_iota(jnp.int32, (spots_here, span), 1).astype(jnp.float32)
    rows_out[...] += matrix_multiply(low_ones(spot_ids == spot_place), place_table[...])

    @pl.loop(0, length // 512)
    def _(a):
        rows = pl.ds(pl.multiple_of(a * 512, 512), 512)
        h1_out[rows, :] = layer_norm(
            stream[rows, :], affine_ref[0:1, :], affine_ref[3:4, :]).astype(jnp.bfloat16)

    @pl.loop(1, dp_size)
    def _(i):
        full_arrival(i).wait_recv()

    counts = jnp.where(
        list_rows == 0, jnp.max(full_all[...], axis=0), jnp.sum(full_all[...], axis=0))
    full_out[...] = counts
    crowd_out[...] = counts[0:1, 0:1].astype(jnp.int32)

    @pl.loop(1, vocab_size)
    def _(j):
        list_copy(j).wait_send()

    @pl.loop(1, dp_size)
    def _(i):
        full_copy(i).wait_send()

    for k in range(chips):
        if k > 0:
            for i in range(2):
                row_copy(2 * partner(k) + i).wait_send()
        else:
            row_copy(2 * chip + 1 - lax.rem(me, 2)).wait_send()


def embed(mesh_sizes, owned, tokens, segments, spots, flags, place_table, affine, flat, table):
    dp_size, vocab_size = mesh_sizes
    length = tokens.shape[1]
    spots_here = spots.shape[1]
    held, width = table.shape
    block = 1024
    full = held // block
    chips = vocab_size // 2
    room = 112 if vocab_size <= 8 else 64
    span = 256
    whole = pl.BlockSpec(memory_space=pltpu.VMEM)
    dma = pltpu.SemaphoreType.DMA
    return pl.pallas_call(
        partial(embed_step, dp_size, vocab_size, block, room, owned),
        out_shape=[
            jax.ShapeDtypeStruct((length, width), jnp.bfloat16),
            jax.ShapeDtypeStruct((spots_here, width), jnp.float32),
            jax.ShapeDtypeStruct((8, spots_here), jnp.int32),
            jax.ShapeDtypeStruct((8, 128), jnp.float32),
            jax.ShapeDtypeStruct((1, 1), jnp.int32),
        ]
        + [
            jax.ShapeDtypeStruct(shape, jnp.bfloat16)
            for shape in (
                (width, NARROW), (NARROW, width), (width, NARROW), (NARROW, width),
                (width, NARROW), (NARROW, 4 * width), (4 * width, NARROW), (NARROW, width),
            )
        ],
        in_specs=[whole] * 4
        + [pl.BlockSpec(memory_space=pl.ANY), whole, whole, pl.BlockSpec(memory_space=pl.ANY)],
        out_specs=[whole] * 13,
        scratch_shapes=[
            pltpu.VMEM((held, width), jnp.bfloat16),
            pltpu.VMEM((span, width), jnp.bfloat16),
            pltpu.VMEM((length, 128), jnp.float32),
            pltpu.VMEM((length, 128), jnp.float32),
            pltpu.VMEM((length, 128), jnp.float32),
            pltpu.VMEM((vocab_size, length), jnp.float32),
            pltpu.VMEM((8, length), jnp.float32),
            pltpu.VMEM((vocab_size, 8, 128), jnp.float32),
            pltpu.VMEM((vocab_size, 8, 128), jnp.float32),
            pltpu.VMEM((2 * room, width), jnp.float32),
            pltpu.VMEM((vocab_size, room, width), jnp.bfloat16),
            pltpu.VMEM((vocab_size, 128, width), jnp.bfloat16),
            pltpu.VMEM((length, width), jnp.float32),
            pltpu.VMEM((dp_size, 8, 128), jnp.float32),
            dma((full + 1,)),
            dma,
            dma((vocab_size,)),
            dma((vocab_size,)),
            dma((vocab_size,)),
            dma((vocab_size,)),
            dma((dp_size,)),
            dma((dp_size,)),
        ],
        compiler_params=pltpu.CompilerParams(
            collective_id=1, has_side_effects=True, vmem_limit_bytes=60 << 20
        ),
        name="embed_step",
    )(tokens, segments, spots, flags, place_table, affine, flat.reshape(-1, 128), table)


def wide_loop(number, body):
    lax.fori_loop(0, number, lambda i, carry: (body(i), carry)[1], 0)


def norm_parts(rows):
    centred = rows - jnp.mean(rows, axis=-1, keepdims=True)
    return centred, lax.rsqrt(jnp.mean(centred * centred, axis=-1, keepdims=True) + NORM_EPS)


def norm_back(rows, gain, grad):
    centred, spread = norm_parts(rows)
    hat = centred * spread
    grad_hat = grad * gain
    return spread * (
        grad_hat
        - jnp.mean(grad_hat, axis=-1, keepdims=True)
        - hat * jnp.mean(grad_hat * hat, axis=-1, keepdims=True)
    )


GELU_RATE = math.sqrt(2.0 / math.pi)


def gelu_parts(pre):
    bend = jnp.tanh(GELU_RATE * (pre + 0.044715 * (pre * pre * pre)))
    return 0.5 * (1.0 + bend), bend


def gelu_slope(pre):
    half, bend = gelu_parts(pre)
    inner = GELU_RATE * (1.0 + 3.0 * 0.044715 * (pre * pre))
    return half + 0.5 * pre * (1.0 - bend * bend) * inner


def both_heads(pair):
    lanes = lax.broadcasted_iota(jnp.int32, pair.shape, 1)
    half = pair.shape[1] // 2
    wide = pair.astype(jnp.float32)
    return jnp.concatenate(
        [jnp.where(lanes < half, wide, 0.0), jnp.where(lanes < half, 0.0, wide)], axis=0
    ).astype(jnp.bfloat16)


def side_by_side(stacked):
    rows = stacked.shape[0] // 2
    lanes = lax.broadcasted_iota(jnp.int32, (rows, stacked.shape[1]), 1)
    return jnp.where(lanes < stacked.shape[1] // 2, stacked[:rows], stacked[rows:])


def third_of(rows, j):
    ids = lax.broadcasted_iota(jnp.int32, rows.shape, 0)
    wide = jnp.where((ids >= j * RANK) & (ids < (j + 1) * RANK), rows.astype(jnp.float32), 0.0)
    return wide.astype(jnp.bfloat16)


def attention_mask(spot_ref, segment_ref):
    spot = lane_columns(spot_ref[...].astype(jnp.float32))[:, 0:1]
    steps = lax.broadcasted_iota(jnp.int32, segment_ref.shape, 1).astype(jnp.float32)
    segment = segment_ref[...].astype(jnp.float32)
    here = jnp.sum(jnp.where(steps == spot, segment, 0.0), axis=1, keepdims=True)
    open_to = ones_where((steps <= spot) & (segment == here))
    return jnp.concatenate([open_to, open_to], axis=0)


def layer_up(h1_ref, rows_ref, segment_ref, spot_ref, affine_ref, bias_ref,
             a_qkv, b_qkv, a_o, b_o, a_fc, b_fc, a_p, b_p,
             qkv_hbm, o_hbm, in_hbm, out_hbm,
             final_ref, q_ref, k_ref, v_ref, u1_ref, u1_rows_ref, h1_rows_ref, lse_ref,
             o_ref, uo_ref, middle_ref, h2_ref, uf_ref, pre_ref, f_ref, up_ref, last_ref,
             wq, wk, wv, wo, win, wout, mask, sems):
    length, width = h1_ref.shape
    hidden = win.shape[1]
    quarter = hidden // 4

    def columns_of(source, j, number):
        return source.at[:, pl.ds(j * number, number)]

    copies = [
        pltpu.make_async_copy(columns_of(qkv_hbm, 1, width), wk, sems.at[0]),
        pltpu.make_async_copy(columns_of(qkv_hbm, 2, width), wv, sems.at[1]),
        pltpu.make_async_copy(columns_of(qkv_hbm, 0, width), wq, sems.at[2]),
        pltpu.make_async_copy(o_hbm, wo, sems.at[3]),
        pltpu.make_async_copy(in_hbm, win, sems.at[4]),
        pltpu.make_async_copy(out_hbm, wout, sems.at[5]),
    ]
    for copy in copies:
        copy.start()

    def bias(first, number):
        return bias_ref[0:1, first : first + number]

    mask[...] = attention_mask(spot_ref, segment_ref)
    h1_rows = layer_norm(rows_ref[...], affine_ref[0:1, :], affine_ref[3:4, :]).astype(
        jnp.bfloat16)
    h1_rows_ref[...] = h1_rows
    u1_ref[...] = matrix_multiply(h1_ref[...], a_qkv[...]).astype(jnp.bfloat16)
    u1_rows = matrix_multiply(h1_rows, a_qkv[...]).astype(jnp.bfloat16)
    u1_rows_ref[...] = u1_rows

    def project(normed, low, weight, j):
        return (
            matrix_multiply(normed, weight[...])
            + bias(j * width, width)
            + ADAPTER_SCALE * matrix_multiply(low, third_of(b_qkv[...], j))
        ).astype(jnp.bfloat16)

    chunk = 512
    for j, weight, out, copy in ((1, wk, k_ref, copies[0]), (2, wv, v_ref, copies[1])):
        copy.wait()

        def rows_of(i):
            rows = pl.ds(pl.multiple_of(i * chunk, chunk), chunk)
            out[rows, :] = project(h1_ref[rows, :], u1_ref[rows, :], weight, j)

        wide_loop(length // chunk, rows_of)
    copies[2].wait()
    q_ref[...] = project(h1_rows, u1_rows, wq, 0)
    scale = (width // HEADS) ** (-0.5)
    lanes = lax.broadcasted_iota(jnp.int32, lse_ref.shape, 1)
    lse_ref[...] = jnp.zeros(lse_ref.shape, jnp.float32)

    def heads(g):
        pair = pl.ds(pl.multiple_of(g * 128, 128), 128)
        scores = scale * matrix_multiply_transposed_right(both_heads(q_ref[:, pair]), k_ref[:, pair])
        scores = jnp.where(mask[...] > 0.0, scores, MASKED)
        top = jnp.max(scores, axis=1, keepdims=True)
        e = jnp.exp(scores - top)
        total = jnp.sum(e, axis=1, keepdims=True)
        probs = (e * (1.0 / total)).astype(jnp.bfloat16)
        o_ref[:, pair] = side_by_side(matrix_multiply(probs, v_ref[:, pair])).astype(jnp.bfloat16)
        lse_ref[...] = jnp.where(lanes == g, top + jnp.log(total), lse_ref[...])

    lax.fori_loop(0, HEADS // 2, lambda g, carry: (heads(g), carry)[1], 0, unroll=2)
    o = o_ref[...]
    uo = matrix_multiply(o, a_o[...]).astype(jnp.bfloat16)
    uo_ref[...] = uo
    copies[3].wait()
    middle = (
        rows_ref[...]
        + matrix_multiply(o, wo[...])
        + bias(3 * width, width)
        + ADAPTER_SCALE * matrix_multiply(uo, b_o[...])
    )
    middle_ref[...] = middle
    h2 = layer_norm(middle, affine_ref[1:2, :], affine_ref[4:5, :]).astype(jnp.bfloat16)
    h2_ref[...] = h2
    uf = matrix_multiply(h2, a_fc[...]).astype(jnp.bfloat16)
    uf_ref[...] = uf
    copies[4].wait()
    for j in range(4):
        part = slice(j * quarter, (j + 1) * quarter)
        pre = (
            matrix_multiply(h2, win[:, part])
            + bias(4 * width + j * quarter, quarter)
            + ADAPTER_SCALE * matrix_multiply(uf, b_fc[:, part])
        )
        pre_ref[:, part] = pre
        f_ref[:, part] = (pre * gelu_parts(pre)[0]).astype(jnp.bfloat16)
    f = f_ref[...]
    up = matrix_multiply(f, a_p[...]).astype(jnp.bfloat16)
    up_ref[...] = up
    copies[5].wait()
    last = (
        middle
        + matrix_multiply(f, wout[...])
        + bias(4 * width + hidden, width)
        + ADAPTER_SCALE * matrix_multiply(up, b_p[...])
    )
    last_ref[...] = last
    final_ref[...] = layer_norm(last, affine_ref[2:3, :], affine_ref[5:6, :]).astype(jnp.bfloat16)


def pack_up(out_ref, part, grad):
    ranks = 3 * RANK if part < 2 else RANK
    wide = grad.shape[1] // 128
    for c in range(wide):
        columns = slice(c * 128, (c + 1) * 128)
        if wide == 8 and ranks == RANK:
            for r in range(ranks):
                at = PARTS[part] + wide * r + c
                out_ref[at : at + 1, :] = grad[r : r + 1, columns]
        else:
            rows = pl.ds(PARTS[part] + c, ranks, stride=wide)
            out_ref[rows, :] = grad[0:ranks, columns]


def pack_down(out_ref, part, shift, grad):
    ranks = 3 * RANK if part < 2 else RANK
    slabs = ranks // RANK
    repeated = jnp.concatenate([grad[0:ranks]] * (128 * slabs // ranks), axis=0)
    for slab in range(slabs):
        spread = repeated[128 * slab : 128 * (slab + 1)].T
        spread = jnp.where(spread_places(ranks, slab), spread, 0.0)
        rows = pl.ds(PARTS[part] + shift + slab, 32, stride=slabs)
        out_ref[rows, :] = jnp.sum(spread.reshape(32, 32, 128), axis=1)


def layer_down(grad_ref, spot_ref, segment_ref, affine_ref, h1_ref,
               a_qkv, b_qkv, a_o, b_o, a_fc, b_fc, a_p, b_p,
               q_ref, k_ref, v_ref, u1_ref, u1_rows_ref, h1_rows_ref, lse_ref,
               o_ref, uo_ref, middle_ref, h2_ref, uf_ref, pre_ref, f_ref, up_ref, last_ref,
               o_hbm, in_hbm, out_hbm,
               grad_out,
               wo, win, wout, mask, dpre_ref, do_ref, dq_ref, dk_ref, dv_ref, sems):
    length, width = h1_ref.shape
    hidden = win.shape[1]
    quarter = hidden // 4
    rows_here = grad_ref.shape[0]
    copies = [
        pltpu.make_async_copy(out_hbm, wout, sems.at[0]),
        pltpu.make_async_copy(in_hbm, win, sems.at[1]),
        pltpu.make_async_copy(o_hbm, wo, sems.at[2]),
    ]
    for copy in copies:
        copy.start()
    mask[...] = attention_mask(spot_ref, segment_ref)
    spot_row = spot_ref[...].astype(jnp.float32)
    spot = lane_columns(spot_row)[:, 0:1]
    order_row = lax.broadcasted_iota(jnp.int32, (1, rows_here), 1)
    order = lax.broadcasted_iota(jnp.int32, (rows_here, 1), 0)
    same = spot == spot_row
    repeat = jnp.max(ones_where(same & (order_row < order)), axis=1, keepdims=True)
    merge = ones_where(same) * (1.0 - repeat)
    grad_final = jnp.dot(
        merge, grad_ref[...], precision=lax.Precision.HIGHEST,
        preferred_element_type=jnp.float32)
    dx3 = norm_back(last_ref[...], affine_ref[2:3, :], grad_final)
    dm = dx3.astype(jnp.bfloat16)
    pack_up(grad_out, 7, ADAPTER_SCALE * matrix_multiply_transposed_left(up_ref[...], dm))
    du_p = (ADAPTER_SCALE * matrix_multiply_transposed_right(dm, b_p[...])).astype(jnp.bfloat16)
    ga_p = matrix_multiply_transposed_left(du_p, f_ref[...])
    for b in range(hidden // 1024):
        pack_down(grad_out, 6, 32 * b, ga_p[:, 1024 * b : 1024 * (b + 1)])
    copies[0].wait()
    for j in range(4):
        part = slice(j * quarter, (j + 1) * quarter)
        df = matrix_multiply_transposed_right(dm, wout[part, :]) + matrix_multiply_transposed_right(
            du_p, a_p[part, :])
        dpre_ref[:, part] = (df * gelu_slope(pre_ref[:, part])).astype(jnp.bfloat16)
    dpre = dpre_ref[...]
    pack_up(grad_out, 5, ADAPTER_SCALE * matrix_multiply_transposed_left(uf_ref[...], dpre))
    du_f = (ADAPTER_SCALE * matrix_multiply_transposed_right(dpre, b_fc[...])).astype(jnp.bfloat16)
    pack_down(grad_out, 4, 0, matrix_multiply_transposed_left(du_f, h2_ref[...]))
    copies[1].wait()
    dh2 = matrix_multiply_transposed_right(dpre, win[...]) + matrix_multiply_transposed_right(
        du_f, a_fc[...])
    dx2 = dx3 + norm_back(middle_ref[...], affine_ref[1:2, :], dh2)
    da = dx2.astype(jnp.bfloat16)
    pack_up(grad_out, 3, ADAPTER_SCALE * matrix_multiply_transposed_left(uo_ref[...], da))
    du_o = (ADAPTER_SCALE * matrix_multiply_transposed_right(da, b_o[...])).astype(jnp.bfloat16)
    pack_down(grad_out, 2, 0, matrix_multiply_transposed_left(du_o, o_ref[...]))
    copies[2].wait()
    do_ref[...] = (
        matrix_multiply_transposed_right(da, wo[...])
        + matrix_multiply_transposed_right(du_o, a_o[...])
    ).astype(jnp.bfloat16)
    scale = (width // HEADS) ** (-0.5)
    lanes = lax.broadcasted_iota(jnp.int32, lse_ref.shape, 1)

    def heads(g):
        pair = pl.ds(pl.multiple_of(g * 128, 128), 128)
        q = both_heads(q_ref[:, pair])
        do = both_heads(do_ref[:, pair])
        lse = jnp.sum(jnp.where(lanes == g, lse_ref[...], 0.0), axis=1, keepdims=True)
        scores = scale * matrix_multiply_transposed_right(q, k_ref[:, pair])
        probs = jnp.where(mask[...] > 0.0, jnp.exp(jnp.minimum(scores - lse, 0.0)), 0.0)
        dp = matrix_multiply_transposed_right(do, v_ref[:, pair])
        ds = (probs * (dp - jnp.sum(probs * dp, axis=1, keepdims=True))).astype(jnp.bfloat16)
        dv_ref[:, pair] = matrix_multiply_transposed_left(
            probs.astype(jnp.bfloat16), do).astype(jnp.bfloat16)
        dk_ref[:, pair] = (scale * matrix_multiply_transposed_left(ds, q)).astype(jnp.bfloat16)
        dq_ref[:, pair] = side_by_side(scale * matrix_multiply(ds, k_ref[:, pair])).astype(
            jnp.bfloat16)

    lax.fori_loop(0, HEADS // 2, lambda g, carry: (heads(g), carry)[1], 0, unroll=2)
    b_all = b_qkv[...]
    gb = jnp.zeros((NARROW, width), jnp.float32)
    ids = lax.broadcasted_iota(jnp.int32, gb.shape, 0)
    dus = []
    for j, low, grad in ((0, u1_rows_ref, dq_ref), (1, u1_ref, dk_ref), (2, u1_ref, dv_ref)):
        mine = (ids >= j * RANK) & (ids < (j + 1) * RANK)
        gb = jnp.where(mine, ADAPTER_SCALE * matrix_multiply_transposed_left(
            low[...], grad[...]), gb)
        dus.append(ADAPTER_SCALE * matrix_multiply_transposed_right(grad[...], third_of(b_all, j)))
    pack_up(grad_out, 1, gb)
    ga = matrix_multiply_transposed_left(
        dus[0].astype(jnp.bfloat16), h1_rows_ref[...]
    ) + matrix_multiply_transposed_left((dus[1] + dus[2]).astype(jnp.bfloat16), h1_ref[...])
    pack_down(grad_out, 0, 0, ga)


def layer_kernels(rows_here, length, width, hidden):
    low, wide = jnp.bfloat16, jnp.float32
    whole = pl.BlockSpec(memory_space=pltpu.VMEM)
    away = pl.BlockSpec(memory_space=pl.ANY)
    dma = pltpu.SemaphoreType.DMA
    params = pltpu.CompilerParams(vmem_limit_bytes=60 << 20)
    kept = [
        ((rows_here, width), low),
        ((length, width), low),
        ((length, width), low),
        ((length, NARROW), low),
        ((rows_here, NARROW), low),
        ((rows_here, width), low),
        ((2 * rows_here, 128), wide),
        ((rows_here, width), low),
        ((rows_here, NARROW), low),
        ((rows_here, width), wide),
        ((rows_here, width), low),
        ((rows_here, NARROW), low),
        ((rows_here, hidden), wide),
        ((rows_here, hidden), low),
        ((rows_here, NARROW), low),
        ((rows_here, width), wide),
    ]
    up = pl.pallas_call(
        layer_up,
        out_shape=[jax.ShapeDtypeStruct(*k) for k in [((rows_here, width), low)] + kept],
        in_specs=[whole] * 14 + [away] * 4,
        out_specs=[whole] * 17,
        scratch_shapes=[pltpu.VMEM((width, width), low)] * 4
        + [
            pltpu.VMEM((width, hidden), low),
            pltpu.VMEM((hidden, width), low),
            pltpu.VMEM((2 * rows_here, length), wide),
            dma((6,)),
        ],
        compiler_params=params,
        name="layer_up",
    )
    down = pl.pallas_call(
        layer_down,
        out_shape=jax.ShapeDtypeStruct((PARTS[-1], 128), wide),
        in_specs=[whole] * 29 + [away] * 3,
        out_specs=whole,
        scratch_shapes=[
            pltpu.VMEM((width, width), low),
            pltpu.VMEM((width, hidden), low),
            pltpu.VMEM((hidden, width), low),
            pltpu.VMEM((2 * rows_here, length), wide),
            pltpu.VMEM((rows_here, hidden), low),
            pltpu.VMEM((rows_here, width), low),
            pltpu.VMEM((rows_here, width), low),
            pltpu.VMEM((length, width), low),
            pltpu.VMEM((length, width), low),
            dma((3,)),
        ],
        compiler_params=params,
        name="layer_down",
    )
    return up, down


def settle_step(held_ref, segment_ref, spot_ref, place_ref, affine_ref, h1_out, rows_out, place_cols):
    length = segment_ref.shape[1]
    span = place_ref.shape[0]
    segment = segment_ref[...].astype(jnp.float32)
    steps = lax.broadcasted_iota(jnp.int32, (1, length), 1).astype(jnp.float32)
    ids = lax.broadcasted_iota(jnp.int32, (32, length), 0).astype(jnp.float32)
    starts = jnp.sum(ones_where(segment < ids), axis=1, keepdims=True)
    place = steps - jnp.sum(jnp.where(segment == ids, starts, 0.0), axis=0, keepdims=True)
    place_cols[...] = lane_columns(place)
    spot = lane_columns(spot_ref[...].astype(jnp.float32))[:, 0:1]
    at_spot = steps == spot
    spot_place = jnp.sum(jnp.where(at_spot, place, 0.0), axis=1, keepdims=True)

    def placed(column):
        ids_here = lax.broadcasted_iota(jnp.int32, (column.shape[0], span), 1).astype(jnp.float32)
        return matrix_multiply(low_ones(ids_here == column), place_ref[...])

    rows_out[...] = matrix_multiply(low_ones(at_spot), held_ref[...]) + placed(spot_place)

    @pl.loop(0, length // 128)
    def _(a):
        rows = pl.ds(pl.multiple_of(a * 128, 128), 128)
        stream = held_ref[rows, :].astype(jnp.float32) + placed(place_cols[rows, 0:1])
        h1_out[rows, :] = layer_norm(stream, affine_ref[0:1, :], affine_ref[3:4, :]).astype(
            jnp.bfloat16)


def settle_rows(held, segments, spots, place_table, affine):
    length, width = held.shape
    whole = pl.BlockSpec(memory_space=pltpu.VMEM)
    return pl.pallas_call(
        settle_step,
        out_shape=[
            jax.ShapeDtypeStruct((length, width), jnp.bfloat16),
            jax.ShapeDtypeStruct((spots.shape[1], width), jnp.float32),
        ],
        in_specs=[whole] * 5,
        out_specs=[whole] * 2,
        scratch_shapes=[pltpu.VMEM((length, 128), jnp.float32)],
        compiler_params=pltpu.CompilerParams(vmem_limit_bytes=32 << 20),
        name="settle_step",
    )(held, segments, spots, place_table[:256], affine)


def visit_step(block, wanted_ref, held_ref, table_hbm, out_ref, table, columns, acc, sem):
    copy = pltpu.make_async_copy(table_hbm, table, sem)
    copy.start()
    columns[...] = lane_columns(wanted_ref[...].astype(jnp.float32))
    rows_here = table.shape[0]
    full = rows_here // block
    copy.wait()

    @pl.loop(0, held_ref.shape[0] // 256)
    def _(a):
        rows = pl.ds(pl.multiple_of(a * 256, 256), 256)
        acc[...] = held_ref[rows, :].astype(jnp.float32)

        def add(first, number):
            ids = lax.broadcasted_iota(jnp.int32, (256, number), 1) + first
            chosen = low_ones(ids.astype(jnp.float32) == columns[rows, 0:1])
            acc[...] += matrix_multiply(chosen, table[pl.ds(first, number), :])

        @pl.loop(0, full)
        def _(j):
            add(pl.multiple_of(j * block, block), block)

        add(full * block, rows_here - full * block)
        out_ref[rows, :] = acc[...].astype(jnp.bfloat16)


def visit_rows(wanted, held, table):
    length, width = held.shape
    whole = pl.BlockSpec(memory_space=pltpu.VMEM)
    return pl.pallas_call(
        partial(visit_step, 256),
        out_shape=jax.ShapeDtypeStruct((length, width), jnp.bfloat16),
        in_specs=[whole, whole, pl.BlockSpec(memory_space=pl.ANY)],
        out_specs=whole,
        scratch_shapes=[
            pltpu.VMEM(table.shape, jnp.bfloat16),
            pltpu.VMEM((length, 128), jnp.float32),
            pltpu.VMEM((256, width), jnp.float32),
            pltpu.SemaphoreType.DMA,
        ],
        compiler_params=pltpu.CompilerParams(vmem_limit_bytes=40 << 20),
        name="visit_step",
    )(wanted, held, table)


def local(
    mesh_sizes,
    packed_symbol_codes,
    article_numbering,
    target_spots,
    answer_flags,
    shared_embedding,
    spot_embedding,
    combined_qkv_weights,
    attend_outgoing_weights,
    dense_incoming_weights,
    dense_outgoing_weights,
    layernorm_affine,
    bias_terms,
    adaptor_float_copies,
    average_moments,
    squared_moments,
):
    rows_here = target_spots.shape[1]
    shard_rows = shared_embedding.shape[0]
    table = jnp.pad(shared_embedding, ((0, -shard_rows % 16), (0, 0)))
    fast_h1, fast_rows, labels, counts, crowded, *factors = embed(
        mesh_sizes,
        shard_rows,
        packed_symbol_codes,
        article_numbering,
        target_spots,
        answer_flags,
        spot_embedding,
        layernorm_affine,
        adaptor_float_copies,
        table,
    )

    sharers = mesh_sizes[1]
    ring = [(j, (j + 1) % sharers) for j in range(sharers)]

    def visit(carry):
        turns, tokens, held = carry
        wanted = tokens - lax.axis_index("vocab") * shard_rows
        wanted = jnp.where((wanted >= 0) & (wanted < shard_rows), wanted, -1)
        kept = jnp.where(turns == sharers, jnp.zeros((), jnp.bfloat16), held)
        held = visit_rows(wanted, kept, table)
        return turns - 1, lax.ppermute(tokens, "vocab", ring), lax.ppermute(held, "vocab", ring)

    def settle(carry):
        _, held, _ = carry
        settled, rows = settle_rows(
            held, article_numbering, target_spots, spot_embedding, layernorm_affine
        )
        return jnp.zeros((), jnp.int32), settled, rows

    overflow = crowded.reshape(())
    _, _, held = lax.while_loop(
        lambda carry: carry[0] > 0, visit, (overflow * sharers, packed_symbol_codes, fast_h1)
    )
    _, h1, stream_rows = lax.while_loop(
        lambda carry: carry[0] > 0, settle, (overflow, held, fast_rows)
    )
    length, width = h1.shape
    hidden = dense_incoming_weights.shape[1]
    layer_up_call, layer_down_call = layer_kernels(rows_here, length, width, hidden)
    final_rows, *kept = layer_up_call(
        h1,
        stream_rows,
        article_numbering,
        target_spots,
        layernorm_affine,
        bias_terms[None, :],
        *factors,
        combined_qkv_weights,
        attend_outgoing_weights,
        dense_incoming_weights,
        dense_outgoing_weights,
    )
    grad_rows, loss_part = head(
        mesh_sizes, shard_rows, final_rows, labels, counts, table
    )
    local_grad = layer_down_call(
        grad_rows,
        target_spots,
        article_numbering,
        layernorm_affine,
        h1,
        *factors,
        *kept,
        attend_outgoing_weights,
        dense_incoming_weights,
        dense_outgoing_weights,
    )
    (
        refreshed_thin_pairs,
        updated_first_moment,
        updated_second_moment,
        gradient_global_norm,
        smoothed_entropy_cost,
    ) = reduce_and_update(
        mesh_sizes, local_grad, adaptor_float_copies, average_moments, squared_moments, loss_part
    )
    return (
        refreshed_thin_pairs,
        updated_first_moment,
        updated_second_moment,
        gradient_global_norm,
        smoothed_entropy_cost,
    )


def solution(mesh):
    return jax.shard_map(
        partial(local, (mesh.shape["dp"], mesh.shape["vocab"])),
        mesh=mesh,
        in_specs=(
            P(("dp", "vocab"), None),
            P(("dp", "vocab"), None),
            P(("dp", "vocab"), None),
            P(("dp", "vocab"), None),
            P("vocab", None),
            P(),
            P(),
            P(),
            P(),
            P(),
            P(),
            P(),
            P(),
            P(),
            P(),
        ),
        out_specs=(P(), P(), P(), P(), P()),
        check_vma=False,
    )
```
